32 devices in a mesh: seq: 8 (over z, x), wa: 4 (over y, core).
Axes of the slice: x: 2, y: 2, z: 4, core: 2. Of those that a mesh axis runs over, the one named last changes fastest.
Arguments:
- tokens: bfloat16 [8, 1024, 2048], P('wa', 'seq'), may hold values from -6 to 6
- lengths: int32 [8], P('wa'), may hold values from 256 to 1024, as said below
- norm_gain: float32 [2048], replicated, may hold values from 0.25 to 1.75
- in_weight: bfloat16 [2048, 8512], P('wa'), may hold values from -0.125 to 0.125
- conv_weight: float32 [4, 4352], replicated, may hold values from -3 to 3
- conv_bias: float32 [4352], replicated, may hold values from -1.8 to 1.8
- dt_bias: float32 [64], replicated, may hold values from -8 to -2
- a_log: float32 [64], replicated, may hold values from 0 to 2.77
- skip_gain: float32 [64], replicated, may hold values from 0.5 to 2
- out_gain: float32 [4096], replicated, may hold values from 0.25 to 1.75
- out_weight: bfloat16 [4096, 2048], P('wa'), may hold values from -0.09375 to 0.09375
- cotangent: bfloat16 [8, 1024, 2048], P('wa', 'seq'), may hold values from -6 to 6
Outputs:
- mixed_out: bfloat16 [8, 1024, 2048], P('wa', 'seq')
- grad_tokens: float32 [8, 1024, 2048], P('wa', 'seq')
- grad_norm_gain: float32 [2048], replicated
- grad_in_weight: float32 [2048, 8512], P('wa')
- grad_conv_weight: float32 [4, 4352], replicated
- grad_conv_bias: float32 [4352], replicated
- grad_dt_bias: float32 [64], replicated
- grad_a_log: float32 [64], replicated
- grad_skip: float32 [64], replicated
- grad_out_gain: float32 [4096], replicated
- grad_out_weight: float32 [4096, 2048], P('wa')
The draws below stay inside these ranges and needn't reach their ends.
Inputs may be any that keep to these rules, and one draw needn't show every extreme that they name: `lengths`: each sequence's used slots come first; in each group of 2 sequences laid out on one index of wa one sequence is full.
All inputs are finite; a program needn't handle non-finite values.
Results may differ from the reference program's by a relative error of at most 0.012.
Values may be sent and summed in bfloat16 or wider, within the bound.
A program may use at most 384 MiB of HBM per device.

```python
import jax
import jax.numpy as jnp
from jax import lax

D = 2048
H = 64
P_SIZE = 64
STATE = 128
KW = 4
BLOCK_LEN = 256
SEQS_GRP = 2
DI = 4096
CH = 4352
PROJ = 8512
SEQS = 8
SLOTS = 1024
N_WA = 4


def draw_lengths(key, part):
    first_key, second_key = jax.random.split(key)
    drawn = jax.random.randint(first_key, (SEQS,), SLOTS // 4, SLOTS + 1)
    chosen = jax.random.randint(second_key, (N_WA,), 0, SEQS_GRP)
    group_pos = jnp.arange(SEQS) % SEQS_GRP
    group_ids = jnp.arange(SEQS) // SEQS_GRP
    is_full = group_pos == chosen[group_ids]
    return jnp.where(is_full, SLOTS, drawn).astype(jnp.int32)


def levels(stream_key, extent, shards, smallest, top_value):
    gain, own = 1.0, jax.random.fold_in(stream_key, 6)
    for position, shards_of in shards:
        heights = jnp.exp(jax.random.uniform(jax.random.fold_in(own, position), (shards_of,), jnp.float32, smallest / len(shards), top_value / len(shards)))
        gain = gain * jnp.repeat(heights, extent[position] // shards_of).reshape([-1 if axis == position else 1 for axis in range(len(extent))])
    return gain


def bell_draw(stream_key, dims, deviation, limit, cuts=(), dtype=jnp.bfloat16):
    loudness = levels(stream_key, dims, cuts, -0.22, 0.18) if cuts else 1.0
    values = jax.random.normal(stream_key, dims, jnp.float32) * deviation * loudness
    return jnp.minimum(jnp.maximum(values, -limit), limit).astype(dtype)


def setup_inputs(seed: int = 0) -> dict:
    streams_of = jax.random.split(jax.random.key(seed), 13)
    return {
        "tokens": bell_draw(streams_of[0], (SEQS, SLOTS, D), 1.0, 6.0, ((0, 4), (1, 8))),
        "lengths": draw_lengths(jax.random.fold_in(streams_of[12], 71), 0),
        "norm_gain": jnp.clip(1.0 + 0.15 * jax.random.normal(streams_of[2], (D,), jnp.float32), 0.25, 1.75),
        "in_weight": bell_draw(streams_of[3], (D, PROJ), D ** -0.5, 0.125, ((0, 4),)),
        "conv_weight": bell_draw(streams_of[4], (KW, CH), KW ** -0.5, 3.0, (), jnp.float32),
        "conv_bias": bell_draw(streams_of[5], (CH,), 0.3, 1.8, (), jnp.float32),
        "dt_bias": jnp.clip(jax.random.uniform(streams_of[6], (H,), jnp.float32, -8.0, -2.0), -8.0, -2.0),
        "a_log": jnp.clip(jax.random.uniform(streams_of[7], (H,), jnp.float32, 0.0, 2.77), 0.0, 2.77),
        "skip_gain": jnp.clip(jax.random.uniform(streams_of[8], (H,), jnp.float32, 0.5, 2.0), 0.5, 2.0),
        "out_gain": jnp.clip(1.0 + 0.15 * jax.random.normal(streams_of[9], (DI,), jnp.float32), 0.25, 1.75),
        "out_weight": bell_draw(streams_of[10], (DI, D), DI ** -0.5, 0.09375, ((0, 4),)),
        "cotangent": bell_draw(streams_of[11], (SEQS, SLOTS, D), 1.0, 6.0, ((0, 4), (1, 8))),
    }


EPS = 1e-05
HIGH = lax.Precision.HIGHEST

@jax.custom_vjp
def low(v):
    return lax.optimization_barrier(v.astype(jnp.bfloat16)).astype(jnp.float32)

@jax.custom_vjp
def low_back(v):
    return v

def low_keep(v):
    return (low(v), None)

def low_pass(kept, grad):
    return (grad,)

def back_keep(v):
    return (v, None)

def back_low(kept, grad):
    return (low(grad),)
low.defvjp(low_keep, low_pass)
low_back.defvjp(back_keep, back_low)

def rms_scale(values, gain_vec):
    return values * lax.rsqrt(lax.optimization_barrier(jnp.mean(values * values, axis=-1, keepdims=True)) + EPS) * gain_vec

def block_step(carry_state, block_data):
    x_heads, dt_vals, rates, b_rows, c_rows = block_data
    cumulative = jnp.cumsum(rates, axis=0)
    cum_heads = cumulative.T
    rows_count = cumulative.shape[0]
    causal_mask = (jnp.arange(rows_count)[:, None] >= jnp.arange(rows_count)[None, :])[None]
    log_decay = cum_heads[:, :, None] - cum_heads[:, None, :]
    decay_matrix = jnp.where(causal_mask, jnp.exp(jnp.where(causal_mask, log_decay, 0.0)), 0.0)
    scores = jnp.dot(c_rows, b_rows.T, precision=HIGH)
    weights = scores[None] * decay_matrix * dt_vals.T[:, None, :]
    inner_part = jnp.einsum('hij,jhp->ihp', weights, x_heads, precision=HIGH)
    carried = jnp.exp(cumulative)[:, :, None] * jnp.einsum('in,hpn->ihp', c_rows, carry_state, precision=HIGH)
    tail_decay = jnp.exp(cum_heads[:, -1:] - cum_heads) * dt_vals.T
    new_state = jnp.exp(cum_heads[:, -1])[:, None, None] * carry_state + jnp.einsum('hj,jhp,jn->hpn', tail_decay, x_heads, b_rows, precision=HIGH)
    return (new_state, inner_part + carried)

def scan_sequence(x_heads, dt_vals, rates, b_rows, c_rows):
    length, head_total, head_size = x_heads.shape
    block_count = length // BLOCK_LEN
    blocks = (x_heads.reshape(block_count, BLOCK_LEN, head_total, head_size), dt_vals.reshape(block_count, BLOCK_LEN, head_total), rates.reshape(block_count, BLOCK_LEN, head_total), b_rows.reshape(block_count, BLOCK_LEN, b_rows.shape[1]), c_rows.reshape(block_count, BLOCK_LEN, c_rows.shape[1]))
    start_state = jnp.zeros((head_total, head_size, b_rows.shape[1]), jnp.float32)
    final_state, outputs = lax.scan(jax.checkpoint(block_step), start_state, blocks)
    return outputs.reshape(length, head_total, head_size)

def layer(params, tokens_seq, valid_rows):
    norm_gain, in_weight, conv_weight, conv_bias, dt_bias, a_log, skip_gain, out_gain, out_weight = params
    inner_width = H * P_SIZE
    channels = inner_width + 2 * STATE
    length = tokens_seq.shape[0]
    normed = low(rms_scale(tokens_seq, norm_gain))
    projected = low(low_back(jnp.dot(normed, in_weight, precision=HIGH)))
    gate_part = projected[:, :inner_width]
    conv_in = projected[:, inner_width:inner_width + channels]
    dt_raw = projected[:, inner_width + channels:]
    padded = jnp.concatenate([jnp.zeros((KW - 1, channels), jnp.float32), conv_in], axis=0)
    conv_sum = conv_bias[None, :]
    for offset in range(KW):
        conv_sum = conv_sum + conv_weight[offset][None, :] * padded[offset:offset + length]
    activated = jax.nn.silu(conv_sum)
    x_heads = activated[:, :inner_width].reshape(length, H, P_SIZE)
    b_rows = activated[:, inner_width:inner_width + STATE]
    c_rows = activated[:, inner_width + STATE:]
    dt_vals = jax.nn.softplus(dt_raw + dt_bias[None, :])
    rates = -jnp.exp(a_log)[None, :] * dt_vals
    y_heads = scan_sequence(x_heads, dt_vals, rates, b_rows, c_rows) + skip_gain[None, :, None] * x_heads
    gated_out = low(low_back(y_heads.reshape(length, inner_width) * jax.nn.silu(gate_part)))
    normed_out = low(rms_scale(gated_out, out_gain))
    branch = jnp.dot(normed_out, out_weight, precision=HIGH)
    return tokens_seq + valid_rows[:, None] * branch

def reference(tokens, lengths, norm_gain, in_weight, conv_weight, conv_bias, dt_bias, a_log, skip_gain, out_gain, out_weight, cotangent):
    params = (norm_gain, in_weight.astype(jnp.float32), conv_weight, conv_bias, dt_bias, a_log, skip_gain, out_gain, out_weight.astype(jnp.float32))
    positions = jnp.arange(SLOTS).astype(jnp.int32)

    def per_sequence(totals, inputs):
        tokens_seq, length_seq, cot_seq = inputs
        valid_rows = (positions < length_seq).astype(jnp.float32)

        def forward(param_tuple, row_values):
            return layer(param_tuple, row_values, valid_rows)
        result, pullback = jax.vjp(forward, params, tokens_seq.astype(jnp.float32))
        param_grads, token_grads = pullback(cot_seq.astype(jnp.float32))
        totals = jax.tree.map(jnp.add, totals, param_grads)
        return (totals, (result.astype(jnp.bfloat16), token_grads))
    zero_grads = jax.tree.map(jnp.zeros_like, params)
    totals, outputs = lax.scan(per_sequence, zero_grads, (tokens, lengths, cotangent))
    return (outputs[0], outputs[1], totals[0], totals[1], totals[2], totals[3], totals[4], totals[5], totals[6], totals[7], totals[8])
```

```python
import functools

import jax
import jax.numpy as jnp
from jax import lax
from jax.experimental import pallas as pl
from jax.experimental.pallas import tpu as pltpu
from jax.sharding import PartitionSpec as P

KW = 4
BLOCK_LEN = 128
MESH = pl.DeviceIdType.MESH


EPS = 1e-05
HIGH = lax.Precision.DEFAULT


def row_scale(values):
    return lax.rsqrt(jnp.mean(values * values, axis=-1, keepdims=True) + EPS)


def norm_backward(values, row_scales, gain_vec, grad_out):
    weighted = grad_out * gain_vec
    grad_gain = jnp.sum(grad_out * values * row_scales, axis=0)
    grad_values = row_scales * weighted - values * row_scales**3 * jnp.mean(
        weighted * values, axis=-1, keepdims=True
    )
    return (grad_values, grad_gain)


def block_chain(x_heads, dt_vals, rates, b_rows, c_rows, block_len):
    seqs_here, length, head_total, head_size = x_heads.shape
    block_count = length // block_len
    states_dim = b_rows.shape[-1]
    x_blocks = x_heads.reshape(seqs_here, block_count, block_len, head_total, head_size)
    dt_blocks = jnp.swapaxes(dt_vals.reshape(seqs_here, block_count, block_len, head_total), 2, 3)
    rate_blocks = jnp.swapaxes(rates.reshape(seqs_here, block_count, block_len, head_total), 2, 3)
    b_blocks = b_rows.reshape(seqs_here, block_count, block_len, states_dim)
    c_blocks = c_rows.reshape(seqs_here, block_count, block_len, states_dim)
    cumulative = jnp.cumsum(rate_blocks, axis=-1)
    causal_mask = jnp.arange(block_len)[:, None] >= jnp.arange(block_len)[None, :]
    log_decay = cumulative[..., :, None] - cumulative[..., None, :]
    decay_matrix = jnp.where(causal_mask, jnp.exp(jnp.where(causal_mask, log_decay, 0.0)), 0.0)
    scores = jnp.einsum("sbin,sbjn->sbij", c_blocks, b_blocks, precision=HIGH)
    weights = scores[:, :, None] * decay_matrix * dt_blocks[..., None, :]
    inner_part = jnp.einsum("sbhij,sbjhp->sbihp", weights, x_blocks, precision=HIGH)
    tail_decay = jnp.exp(cumulative[..., -1:] - cumulative) * dt_blocks
    block_states = jnp.einsum(
        "sbhj,sbjhp,sbjn->sbhpn", tail_decay, x_blocks, b_blocks, precision=HIGH
    )
    block_decay = jnp.exp(cumulative[..., -1])

    def carry_step(carry_state, pieces):
        decay_now, state_now = pieces
        return (decay_now[..., None, None] * carry_state + state_now, carry_state)

    start_state = jnp.zeros((seqs_here, head_total, head_size, states_dim), jnp.float32)
    final_state, entering = lax.scan(
        carry_step, start_state, (jnp.moveaxis(block_decay, 1, 0), jnp.moveaxis(block_states, 1, 0))
    )
    entering = jnp.moveaxis(entering, 0, 1)
    carried = jnp.swapaxes(jnp.exp(cumulative), 2, 3)[..., None] * jnp.einsum(
        "sbin,sbhpn->sbihp", c_blocks, entering, precision=HIGH
    )
    output = (inner_part + carried).reshape(seqs_here, length, head_total, head_size)
    return (output, final_state)


def mixer_front(
    extended, dt_raw, conv_w, conv_b, bias_part, log_rates, x_width, state_size, head_size
):
    seqs_here = extended.shape[0]
    length = extended.shape[1] - (KW - 1)
    conv_sum = conv_b
    for offset in range(KW):
        conv_sum = conv_sum + conv_w[offset] * extended[:, offset : offset + length]
    activated = jax.nn.silu(conv_sum)
    x_heads = activated[..., :x_width].reshape(seqs_here, length, x_width // head_size, head_size)
    b_rows = activated[..., x_width : x_width + state_size]
    c_rows = activated[..., x_width + state_size :]
    dt_vals = jax.nn.softplus(dt_raw + bias_part)
    rates = -jnp.exp(log_rates) * dt_vals
    block_len = min(BLOCK_LEN, length)
    y_local, local_state = block_chain(x_heads, dt_vals, rates, b_rows, c_rows, block_len)
    running = jnp.exp(jnp.cumsum(rates, axis=1))
    total_decay = running[:, -1]
    return (y_local, local_state, total_decay, x_heads, c_rows, running)


def mixer_finish(y_local, x_heads, gate_part, skip_part):
    y_heads = y_local + skip_part[:, None] * x_heads
    seqs_here, length = (y_heads.shape[0], y_heads.shape[1])
    return y_heads.reshape(seqs_here, length, -1) * jax.nn.silu(gate_part)


def ring_pos(index, size):
    row, side = index // 2, index % 2
    return row + side * (size - 1 - 2 * row)


def ring_index(pos, size):
    side = pos // (size // 2)
    row = pos + side * (size - 1 - 2 * pos)
    return row * 2 + side


def gather_kernel(size, chunks, x_ref, o_ref, local_sem, send_sem, recv_sem):
    me, group = lax.axis_index("seq"), lax.axis_index("wa")
    pos = ring_pos(me, size)
    right = ring_index((pos + 1) % size, size)
    left = ring_index((pos + size - 1) % size, size)
    barrier = pltpu.get_barrier_semaphore()
    for neighbour in (left, right):
        pl.semaphore_signal(barrier, inc=1, device_id=(neighbour, group), device_id_type=MESH)
    pl.semaphore_wait(barrier, 2)
    local = pltpu.make_async_copy(x_ref, o_ref.at[me], local_sem)
    local.start()
    copies = {}
    for step in range(size - 1):
        going_right = ring_index((pos - step + size) % size, size)
        going_left = ring_index((pos + step) % size, size)
        for chunk in range(chunks):
            for way, (block, target) in enumerate(((going_right, right), (going_left, left))):
                if step > 0:
                    copies[step - 1, chunk, way].wait_recv()
                source = x_ref.at[way, chunk] if step == 0 else o_ref.at[block, way, chunk]
                copy = pltpu.make_async_remote_copy(
                    source,
                    o_ref.at[block, way, chunk],
                    send_sem.at[step, chunk, way],
                    recv_sem.at[step, chunk, way],
                    device_id=(target, group),
                    device_id_type=MESH,
                )
                copy.start()
                copies[step, chunk, way] = copy
    for chunk in range(chunks):
        for way in range(2):
            copies[size - 2, chunk, way].wait_recv()
    for copy in copies.values():
        copy.wait_send()
    local.wait()


def ring_gather(x, collective_id):
    size = lax.axis_size("seq")
    rows, cols = x.shape
    chunks = 2
    parts = x.reshape(2, chunks, rows // (2 * chunks), cols)
    out = pl.pallas_call(
        functools.partial(gather_kernel, size, chunks),
        out_shape=jax.ShapeDtypeStruct((size,) + parts.shape, x.dtype),
        in_specs=[pl.BlockSpec(memory_space=pl.ANY)],
        out_specs=pl.BlockSpec(memory_space=pl.ANY),
        scratch_shapes=[
            pltpu.SemaphoreType.DMA,
            pltpu.SemaphoreType.DMA((size - 1, chunks, 2)),
            pltpu.SemaphoreType.DMA((size - 1, chunks, 2)),
        ],
        compiler_params=pltpu.CompilerParams(collective_id=collective_id, has_side_effects=True),
    )(parts)
    return out.reshape(size * rows, cols)


def body(
    tokens,
    lengths,
    norm_gain,
    in_weight,
    conv_weight,
    conv_bias,
    dt_bias,
    a_log,
    skip_gain,
    out_gain,
    out_weight,
    cotangent,
):
    seqs_here, slot_rows, width = tokens.shape
    row_count = seqs_here * slot_rows
    inner_width = out_gain.shape[0]
    channels = conv_bias.shape[0]
    bc_width = channels - inner_width
    state_size = bc_width // 2
    head_count = dt_bias.shape[0]
    head_size = inner_width // head_count
    seq_devices = lax.axis_size("seq")
    group_devices = lax.axis_size("wa")
    seq_index = lax.axis_index("seq")
    length = seq_devices * slot_rows
    local_heads = head_count // seq_devices
    local_width = local_heads * head_size
    channel_start = seq_index * local_width
    head_start = seq_index * local_heads
    bf16, f32 = jnp.bfloat16, jnp.float32

    def take(array, start, size, axis):
        return lax.dynamic_slice_in_dim(array, start, size, axis)

    def to_sequence(rows):
        blocks = rows.reshape(seq_devices, seqs_here, slot_rows, rows.shape[-1])
        return jnp.swapaxes(blocks, 0, 1).reshape(seqs_here, length, rows.shape[-1])

    def to_rows(values):
        blocks = values.reshape(seqs_here, seq_devices, slot_rows, values.shape[-1])
        return jnp.swapaxes(blocks, 0, 1).reshape(seq_devices * row_count, values.shape[-1])

    positions = seq_index * slot_rows + jnp.arange(slot_rows)
    valid_rows = (positions[None, :] < lengths[:, None]).astype(f32).reshape(row_count, 1)
    flat_tokens = tokens.reshape(row_count, width).astype(f32)
    in_scale = row_scale(flat_tokens)
    normed = (flat_tokens * in_scale * norm_gain).astype(bf16)
    normed_all = ring_gather(normed, 0)
    cot_rows = cotangent.reshape(row_count, width)
    branch_grad = ring_gather(cot_rows * valid_rows.astype(bf16), 1)

    local_columns = jnp.concatenate(
        [
            take(in_weight, channel_start, local_width, 1),
            take(in_weight, inner_width + channel_start, local_width, 1),
            in_weight[:, 2 * inner_width :],
        ],
        axis=1,
    )
    in_columns = lax.all_gather(local_columns, "wa", axis=0, tiled=True)
    projected = to_sequence(
        jnp.dot(normed_all, in_columns, preferred_element_type=f32).astype(bf16)
    )
    gate_part = projected[..., :local_width].astype(f32)
    joined = projected[..., local_width : 2 * local_width + bc_width].astype(f32)
    dt_raw = take(
        projected[..., 2 * local_width + bc_width :], head_start, local_heads, 2
    ).astype(f32)
    extended = jnp.concatenate(
        [jnp.zeros((seqs_here, KW - 1, joined.shape[2]), f32), joined], axis=1
    )
    conv_local = jnp.concatenate(
        [take(conv_weight, channel_start, local_width, 1), conv_weight[:, inner_width:]], axis=1
    )
    bias_local = jnp.concatenate(
        [take(conv_bias, channel_start, local_width, 0), conv_bias[inner_width:]], axis=0
    )
    shift_local = take(dt_bias, head_start, local_heads, 0)
    rates_local = take(a_log, head_start, local_heads, 0)
    skip_local = take(skip_gain, head_start, local_heads, 0)
    gain_local = take(out_gain, channel_start, local_width, 0)

    def front_fn(extended_in, dt_in, conv_w, conv_b, bias_part, log_rates):
        return mixer_front(
            extended_in, dt_in, conv_w, conv_b, bias_part, log_rates, local_width, state_size, head_size
        )

    front_out, front_pull = jax.vjp(
        front_fn, extended, dt_raw, conv_local, bias_local, shift_local, rates_local
    )
    y_local, local_state, total_decay, x_heads, c_rows, running = front_out
    gated_heads, finish_pull = jax.vjp(mixer_finish, y_local, x_heads, gate_part, skip_local)
    gated = to_rows(gated_heads.astype(bf16)).astype(f32)

    row_group = inner_width // group_devices
    owner = channel_start // row_group
    out_rows = lax.psum(
        jnp.where(
            lax.axis_index("wa") == owner,
            take(out_weight, channel_start - owner * row_group, local_width, 0),
            jnp.zeros((local_width, width), bf16),
        ),
        "wa",
    )
    out_grad = lax.dot_general(
        branch_grad, out_rows, (((1,), (1,)), ((), ())), preferred_element_type=f32
    )
    weighted = out_grad * gain_local
    sums = lax.psum(
        jnp.stack([jnp.sum(gated * gated, axis=-1), jnp.sum(weighted * gated, axis=-1)]), "seq"
    )
    out_scale = lax.rsqrt(sums[0] / inner_width + EPS)[:, None]
    mean_dot = (sums[1] / inner_width)[:, None]
    normed_out = (gated * out_scale * gain_local).astype(bf16)
    out_gain_part = jnp.sum(out_grad * gated * out_scale, axis=0)
    gated_grad = (out_scale * weighted - gated * out_scale**3 * mean_dot).astype(bf16)

    branch = lax.psum_scatter(
        jnp.dot(normed_out, out_rows, preferred_element_type=f32).astype(bf16),
        "seq",
        scatter_dimension=0,
        tiled=True,
    ).astype(f32)
    mixed_out = (flat_tokens + valid_rows * branch).astype(bf16).reshape(tokens.shape)
    out_weight_part = lax.psum_scatter(
        lax.dot_general(
            normed_out, branch_grad, (((0,), (0,)), ((), ())), preferred_element_type=f32
        ).astype(bf16),
        "wa",
        scatter_dimension=0,
        tiled=True,
    )
    piece = local_width // group_devices
    per_owner = seq_devices // group_devices
    pieces = lax.all_gather(out_weight_part, "seq", axis=0, tiled=False)
    pieces = lax.all_to_all(
        pieces.reshape(group_devices, per_owner, piece, width), "wa", 0, 0, tiled=True
    )
    out_weight_grad = jnp.swapaxes(pieces, 0, 1).reshape(row_group, width).astype(f32)

    y_grad, x_grad, gate_grad, skip_grad = finish_pull(to_sequence(gated_grad).astype(f32))
    extended_grad, dt_grad, conv_w_grad, conv_b_grad, shift_grad, rates_grad = front_pull(
        (
            y_grad,
            jnp.zeros_like(local_state),
            jnp.zeros_like(total_decay),
            x_grad,
            jnp.zeros_like(c_rows),
            jnp.zeros_like(running),
        )
    )
    dt_wide = lax.dynamic_update_slice_in_dim(
        jnp.zeros((seqs_here, length, head_count), f32), dt_grad, head_start, 2
    )
    proj_grad = to_rows(
        jnp.concatenate([gate_grad, extended_grad[:, KW - 1 :], dt_wide], axis=2).astype(bf16)
    )
    in_weight_part = lax.psum_scatter(
        lax.dot_general(
            normed_all, proj_grad, (((0,), (0,)), ((), ())), preferred_element_type=f32
        ).astype(bf16),
        "wa",
        scatter_dimension=0,
        tiled=True,
    )
    own = ring_gather(in_weight_part[:, : 2 * local_width], 2)
    own = own.reshape(seq_devices, in_weight.shape[0], 2, local_width)
    own = jnp.transpose(own, (1, 2, 0, 3)).reshape(in_weight.shape[0], 2 * inner_width)
    shared = lax.psum(in_weight_part[:, 2 * local_width :].astype(f32), "seq")
    in_weight_grad = jnp.concatenate([own.astype(f32), shared], axis=1)
    normed_grad = lax.psum_scatter(
        lax.dot_general(
            proj_grad, in_columns, (((1,), (1,)), ((), ())), preferred_element_type=f32
        ).astype(bf16),
        "seq",
        scatter_dimension=0,
        tiled=True,
    ).astype(f32)
    token_grad, norm_gain_grad = norm_backward(flat_tokens, in_scale, norm_gain, normed_grad)
    token_grad = token_grad + cot_rows.astype(f32)

    def place(part, total, start, axis):
        shape = list(part.shape)
        shape[axis] = total
        return lax.dynamic_update_slice_in_dim(jnp.zeros(shape, f32), part, start, axis)

    conv_weight_grad = jnp.concatenate(
        [place(conv_w_grad[:, :local_width], inner_width, channel_start, 1), conv_w_grad[:, local_width:]],
        axis=1,
    )
    conv_bias_grad = jnp.concatenate(
        [place(conv_b_grad[:local_width], inner_width, channel_start, 0), conv_b_grad[local_width:]],
        axis=0,
    )
    small = lax.psum(
        jnp.concatenate(
            [
                norm_gain_grad,
                conv_weight_grad.reshape(-1),
                conv_bias_grad,
                place(shift_grad, head_count, head_start, 0),
                place(rates_grad, head_count, head_start, 0),
                place(skip_grad, head_count, head_start, 0),
                place(out_gain_part, inner_width, channel_start, 0),
            ]
        ),
        ("seq", "wa"),
    )
    bounds, at = [], 0
    for extent in (width, KW * channels, channels, head_count, head_count, head_count, inner_width):
        bounds.append(small[at : at + extent])
        at += extent
    return (
        mixed_out,
        token_grad.reshape(tokens.shape),
        bounds[0],
        in_weight_grad,
        bounds[1].reshape(KW, channels),
        bounds[2],
        bounds[3],
        bounds[4],
        bounds[5],
        bounds[6],
        out_weight_grad,
    )


def solution(mesh):
    placed = (
        P("wa", "seq", None),
        P("wa"),
        P(),
        P("wa", None),
        P(),
        P(),
        P(),
        P(),
        P(),
        P(),
        P("wa", None),
        P("wa", "seq", None),
    )
    return jax.shard_map(
        body,
        mesh=mesh,
        in_specs=placed,
        out_specs=(
            P("wa", "seq", None),
            P("wa", "seq", None),
            P(),
            P("wa", None),
            P(),
            P(),
            P(),
            P(),
            P(),
            P(),
            P("wa", None),
        ),
        check_vma=False,
    )
```

```python
import functools

import jax
import jax.numpy as jnp
from jax import lax
from jax.experimental import pallas as pl
from jax.experimental.pallas import tpu as pltpu
from jax.sharding import PartitionSpec as P

KW = 4
EPS = 1e-05
HIGHEST = lax.Precision.HIGHEST
MESH = pl.DeviceIdType.MESH


def row_scale(values):
    return lax.rsqrt(jnp.mean(values * values, axis=-1, keepdims=True) + EPS)


def norm_backward(values, row_scales, gain_vec, grad_out):
    weighted = grad_out * gain_vec
    grad_gain = jnp.sum(grad_out * values * row_scales, axis=0)
    grad_values = row_scales * weighted - values * row_scales**3 * jnp.mean(
        weighted * values, axis=-1, keepdims=True
    )
    return (grad_values, grad_gain)


def dot(a, b, ca, cb, precision=None):
    return lax.dot_general(
        a, b, (((ca,), (cb,)), ((), ())), precision=precision, preferred_element_type=jnp.float32
    )


def chunk_front(proj_ref, ext, taps_ref, shift_ref, bias_ref, slope_ref, tri_ref, widths):
    lw, bc = widths
    rows = proj_ref.shape[2]
    ext[8:, :] = proj_ref[0, 0, :, lw : 2 * lw + bc].astype(jnp.float32)
    conv = shift_ref[0:1, :]
    for k in range(KW):
        conv = conv + taps_ref[k : k + 1, :] * ext[5 + k : 5 + k + rows, :]
    conv_sig = lax.logistic(conv)
    act = conv * conv_sig
    step_in = proj_ref[0, 0, :, 2 * lw + bc :].astype(jnp.float32) + bias_ref[0:1, :]
    steps = jnp.maximum(step_in, 0.0) + jnp.log1p(jnp.exp(-jnp.abs(step_in)))
    rates = slope_ref[0:1, :] * steps
    cum = dot(tri_ref[...], rates, 1, 0, HIGHEST)
    return conv, conv_sig, act, step_in, steps, rates, cum


def head_masks(rows, head_size):
    lane = lax.broadcasted_iota(jnp.int32, (rows, 128), 1)
    row = lax.broadcasted_iota(jnp.int32, (rows, rows), 0)
    col = lax.broadcasted_iota(jnp.int32, (rows, rows), 1)
    return lane, row >= col


def forward_kernel(
    widths,
    head_size,
    proj_ref,
    taps_ref,
    shift_ref,
    bias_ref,
    slope_ref,
    skip_ref,
    spread_ref,
    tri_ref,
    gated_ref,
    y_ref,
    enter_ref,
    state,
    ext,
    halo,
):
    lw, bc = widths
    bf16, f32 = jnp.bfloat16, jnp.float32
    rows = proj_ref.shape[2]
    per_tile = 128 // head_size

    @pl.when(pl.program_id(1) == 0)
    def _():
        state[...] = jnp.zeros_like(state)
        halo[...] = jnp.zeros_like(halo)

    ext[0:8, :] = halo[...]
    _, _, act, _, steps, _, cum = chunk_front(
        proj_ref, ext, taps_ref, shift_ref, bias_ref, slope_ref, tri_ref, widths
    )
    halo[...] = ext[rows : rows + 8, :]
    x = act[:, :lw]
    xb = x.astype(bf16)
    b_rows = act[:, lw : lw + bc // 2].astype(bf16)
    c_rows = act[:, lw + bc // 2 :].astype(bf16)
    cum_t, steps_t = cum.T, steps.T
    last = cum[rows - 1 : rows, :]
    grow = dot(jnp.exp(cum).astype(bf16), spread_ref[...], 1, 0)
    tail = dot((jnp.exp(last - cum) * steps).astype(bf16), spread_ref[...], 1, 0)
    scores = dot(c_rows, b_rows, 1, 1)
    entering = state[...].astype(bf16)
    enter_ref[0, 0] = entering
    y = dot(c_rows, entering, 1, 1) * grow + skip_ref[0:1, :] * x
    added = dot((x * tail).astype(bf16), b_rows, 0, 0)
    lane, causal = head_masks(rows, head_size)
    gate = proj_ref[0, 0, :, :lw].astype(f32)
    silu_gate = gate * lax.logistic(gate)
    for tile in range(lw // 128):
        cols = slice(tile * 128, (tile + 1) * 128)
        inner = None
        for sub in range(per_tile):
            head = tile * per_tile + sub
            log_decay = cum[:, head : head + 1] - cum_t[head : head + 1, :]
            decay = jnp.exp(jnp.where(causal, log_decay, -1e30))
            weights = (scores * decay * steps_t[head : head + 1, :]).astype(bf16)
            part = dot(weights, xb[:, cols], 1, 0)
            inner = part if inner is None else jnp.where(lane >= sub * head_size, part, inner)
            span = slice(head * head_size, (head + 1) * head_size)
            state[span, :] = (
                jnp.exp(cum[rows - 1 : rows, head : head + 1]) * state[span, :] + added[span, :]
            )
        y_tile = y[:, cols] + inner
        y_ref[0, 0, :, cols] = y_tile.astype(bf16)
        gated_ref[0, 0, :, cols] = (y_tile * silu_gate[:, cols]).astype(bf16)


def backward_kernel(
    widths,
    head_size,
    chunks,
    proj_ref,
    before_ref,
    y_ref,
    enter_ref,
    grad_ref,
    taps_ref,
    shift_ref,
    bias_ref,
    slope_ref,
    skip_ref,
    spread_ref,
    fold_ref,
    tri_ref,
    upper_ref,
    out_ref,
    taps_acc,
    skip_acc,
    head_acc,
    lam,
    ext,
    later,
    after,
):
    lw, bc = widths
    state_size = bc // 2
    bf16, f32 = jnp.bfloat16, jnp.float32
    rows = proj_ref.shape[2]
    per_tile = 128 // head_size
    chunk = chunks - 1 - pl.program_id(1)

    @pl.when((pl.program_id(0) == 0) & (pl.program_id(1) == 0))
    def _():
        taps_acc[...] = jnp.zeros_like(taps_acc)
        skip_acc[...] = jnp.zeros_like(skip_acc)
        head_acc[...] = jnp.zeros_like(head_acc)

    @pl.when(pl.program_id(1) == 0)
    def _():
        lam[...] = jnp.zeros_like(lam)
        after[...] = jnp.zeros_like(after)

    ext[0:8, :] = jnp.where(
        chunk > 0, before_ref[0, 0, 8:16, lw : 2 * lw + bc].astype(f32), 0.0
    )
    conv, conv_sig, act, step_in, steps, rates, cum = chunk_front(
        proj_ref, ext, taps_ref, shift_ref, bias_ref, slope_ref, tri_ref, widths
    )
    x = act[:, :lw]
    xb = x.astype(bf16)
    b_rows = act[:, lw : lw + state_size].astype(bf16)
    c_rows = act[:, lw + state_size :].astype(bf16)
    cum_t, steps_t = cum.T, steps.T
    last = cum[rows - 1 : rows, :]
    to_end = jnp.exp(last - cum)
    tail_heads = to_end * steps
    grow = dot(jnp.exp(cum).astype(bf16), spread_ref[...], 1, 0)
    tail = dot(tail_heads.astype(bf16), spread_ref[...], 1, 0)
    scores = dot(c_rows, b_rows, 1, 1)

    gate = proj_ref[0, 0, :, :lw].astype(f32)
    gate_sig = lax.logistic(gate)
    grad = grad_ref[0, 0].astype(f32)
    y_grad = grad * gate * gate_sig
    out_ref[0, 0, :, :lw] = (
        grad * y_ref[0, 0].astype(f32) * (gate_sig * (1.0 + gate * (1.0 - gate_sig)))
    ).astype(bf16)
    yb = y_grad.astype(bf16)

    entering = enter_ref[0, 0]
    grown = y_grad * grow
    grown_b = grown.astype(bf16)
    c_grad = dot(grown_b, entering, 1, 0)
    carried = dot((grown * dot(c_rows, entering, 1, 1)).astype(bf16), fold_ref[...], 1, 0)
    lam_now = lam[...]
    lam_b = lam_now.astype(bf16)
    from_lam = dot(b_rows, lam_b, 1, 1)
    b_grad = dot((x * tail).astype(bf16), lam_b, 1, 0)
    x_lam = dot((x * from_lam).astype(bf16), fold_ref[...], 1, 0)
    x_grad = skip_ref[0:1, :] * y_grad + tail * from_lam
    skip_acc[0:1, :] += jnp.sum(y_grad * x, axis=0, keepdims=True)
    ones = jnp.ones((8, state_size), bf16)
    kept = dot(
        dot(ones, (lam_now * entering.astype(f32)).astype(bf16), 1, 1),
        fold_ref[...].astype(f32),
        1,
        0,
        HIGHEST,
    )
    through = jnp.exp(last) * kept[0:1, :]
    lam_add = dot(grown_b, c_rows, 0, 0)

    lane, causal = head_masks(rows, head_size)
    score_grad = None
    row_sums = jnp.zeros((rows, 128), f32)
    col_sums = []
    x_tiles = []
    for tile in range(lw // 128):
        cols = slice(tile * 128, (tile + 1) * 128)
        inner = None
        for sub in range(per_tile):
            head = tile * per_tile + sub
            log_decay = cum[:, head : head + 1] - cum_t[head : head + 1, :]
            decay = jnp.exp(jnp.where(causal, log_decay, -1e30))
            step_row = steps_t[head : head + 1, :]
            weights = (scores * decay * step_row).astype(bf16)
            inside = (lane >= sub * head_size) & (lane < (sub + 1) * head_size)
            y_head = jnp.where(inside, yb[:, cols], jnp.zeros_like(yb[:, cols]))
            weights_grad = dot(y_head, xb[:, cols], 1, 1)
            part = dot(weights, yb[:, cols], 0, 0)
            inner = part if inner is None else jnp.where(lane >= sub * head_size, part, inner)
            decayed = weights_grad * decay
            stepped = decayed * step_row
            score_grad = stepped if score_grad is None else score_grad + stepped
            col_sums.append(jnp.sum(decayed * scores, axis=0, keepdims=True))
            row_sum = jnp.sum(stepped * scores, axis=1, keepdims=True)
            row_sums = row_sums + jnp.where(lane == head, row_sum, 0.0)
            span = slice(head * head_size, (head + 1) * head_size)
            lam[span, :] = (
                jnp.exp(cum[rows - 1 : rows, head : head + 1]) * lam_now[span, :] + lam_add[span, :]
            )
        x_tiles.append(x_grad[:, cols] + inner)
    col_sums.append(jnp.zeros((rows - len(col_sums), rows), f32))
    col_sum = jnp.concatenate(col_sums, axis=0).T
    source = row_sums - steps * col_sum + carried
    rates_grad = (
        dot(upper_ref[...], source, 1, 0, HIGHEST)
        + dot(1.0 - upper_ref[...], tail_heads * x_lam, 1, 0, HIGHEST)
        + through
    )
    steps_grad = col_sum + to_end * x_lam + rates_grad * slope_ref[0:1, :]
    raw_grad = steps_grad * lax.logistic(step_in)
    out_ref[0, 0, :, 2 * lw + bc :] = raw_grad.astype(bf16)
    head_acc[0:1, :] += jnp.sum(raw_grad, axis=0, keepdims=True)
    head_acc[1:2, :] += jnp.sum(rates_grad * rates, axis=0, keepdims=True)
    score_b = score_grad.astype(bf16)
    c_grad = c_grad + dot(score_b, b_rows, 1, 0)
    b_grad = b_grad + dot(score_b, c_rows, 0, 0)
    act_grad = jnp.concatenate(x_tiles + [b_grad, c_grad], axis=1)
    conv_grad = act_grad * (conv_sig * (1.0 + conv * (1.0 - conv_sig)))
    later[0:rows, :] = conv_grad
    later[rows : rows + 8, :] = after[...]
    after[...] = conv_grad[0:8, :]
    total = None
    for k in range(KW):
        term = taps_ref[k : k + 1, :] * later[3 - k : 3 - k + rows, :]
        total = term if total is None else total + term
        taps_acc[k : k + 1, :] += jnp.sum(conv_grad * ext[5 + k : 5 + k + rows, :], axis=0, keepdims=True)
    taps_acc[KW : KW + 1, :] += jnp.sum(conv_grad, axis=0, keepdims=True)
    out_ref[0, 0, :, lw : 2 * lw + bc] = total.astype(bf16)


def whole_spec(array):
    return pl.BlockSpec(array.shape, lambda q, c: (0,) * array.ndim)


def scan_tables(rows, local_width, head_size):
    head_of = jnp.arange(local_width) // head_size
    spread = (jnp.arange(128)[:, None] == head_of[None, :]).astype(jnp.bfloat16)
    tri = (jnp.arange(rows)[:, None] >= jnp.arange(rows)[None, :]).astype(jnp.float32)
    return spread, spread.T, tri, tri.T


def scan_forward(proj, taps, shift, bias, slope, skip, spread, tri, widths, head_size):
    chunks, seqs, rows, _ = proj.shape
    lw, bc = widths
    block = lambda *tail: pl.BlockSpec((1, 1) + tail, lambda q, c: (c, q, 0, 0))
    tables = (taps, shift, bias, slope, skip, spread, tri)
    return pl.pallas_call(
        functools.partial(forward_kernel, widths, head_size),
        grid=(seqs, chunks),
        in_specs=[block(rows, proj.shape[3])] + [whole_spec(t) for t in tables],
        out_specs=[block(rows, lw), block(rows, lw), block(lw, bc // 2)],
        out_shape=[
            jax.ShapeDtypeStruct((chunks, seqs, rows, lw), jnp.bfloat16),
            jax.ShapeDtypeStruct((chunks, seqs, rows, lw), jnp.bfloat16),
            jax.ShapeDtypeStruct((chunks, seqs, lw, bc // 2), jnp.bfloat16),
        ],
        scratch_shapes=[
            pltpu.VMEM((lw, bc // 2), jnp.float32),
            pltpu.VMEM((rows + 8, lw + bc), jnp.float32),
            pltpu.VMEM((8, lw + bc), jnp.float32),
        ],
        compiler_params=pltpu.CompilerParams(vmem_limit_bytes=48 * 2**20),
        name="scan_forward",
    )(proj, *tables)


def scan_backward(
    proj, y, enter, grad, taps, shift, bias, slope, skip, spread, fold, tri, upper, widths, head_size
):
    chunks, seqs, rows, cols = proj.shape
    lw, bc = widths
    block = lambda *tail: pl.BlockSpec((1, 1) + tail, lambda q, c: (chunks - 1 - c, q, 0, 0))
    before = pl.BlockSpec(
        (1, 1, 16, cols),
        lambda q, c: (jnp.maximum(chunks - 2 - c, 0), q, rows // 16 - 1, 0),
    )
    tables = (taps, shift, bias, slope, skip, spread, fold, tri, upper)
    sums = [(8, lw + bc), (8, lw), (8, 128)]
    return pl.pallas_call(
        functools.partial(backward_kernel, widths, head_size, chunks),
        grid=(seqs, chunks),
        in_specs=[block(rows, cols), before, block(rows, lw), block(lw, bc // 2), block(rows, lw)]
        + [whole_spec(t) for t in tables],
        out_specs=[block(rows, cols)] + [pl.BlockSpec(s, lambda q, c: (0, 0)) for s in sums],
        out_shape=[jax.ShapeDtypeStruct(proj.shape, jnp.bfloat16)]
        + [jax.ShapeDtypeStruct(s, jnp.float32) for s in sums],
        scratch_shapes=[
            pltpu.VMEM((lw, bc // 2), jnp.float32),
            pltpu.VMEM((rows + 8, lw + bc), jnp.float32),
            pltpu.VMEM((rows + 8, lw + bc), jnp.float32),
            pltpu.VMEM((8, lw + bc), jnp.float32),
        ],
        compiler_params=pltpu.CompilerParams(vmem_limit_bytes=48 * 2**20),
        name="scan_backward",
    )(proj, proj, y, enter, grad, *tables)


def ring_pos(index, size):
    row, side = index // 2, index % 2
    return row + side * (size - 1 - 2 * row)


def ring_index(pos, size):
    side = pos // (size // 2)
    row = pos + side * (size - 1 - 2 * pos)
    return row * 2 + side


def greet(peers):
    barrier = pltpu.get_barrier_semaphore()
    for peer in peers:
        pl.semaphore_signal(barrier, inc=1, device_id=peer, device_id_type=MESH)
    pl.semaphore_wait(barrier, len(peers))


def push(source, target, send_sem, recv_sem, peer):
    return pltpu.make_async_remote_copy(
        source, target, send_sem, recv_sem, device_id=peer, device_id_type=MESH
    )


def neighbours(size):
    me, group = lax.axis_index("seq"), lax.axis_index("wa")
    pos = ring_pos(me, size)
    right = (ring_index((pos + 1) % size, size), group)
    left = (ring_index((pos + size - 1) % size, size), group)
    return me, group, pos, right, left


def others(index, size):
    return [(index + offset) % size for offset in range(1, size)]


ANY = pl.BlockSpec(memory_space=pl.ANY)
VMEM = pl.BlockSpec(memory_space=pltpu.VMEM)


def comm_params(collective_id, megabytes=None):
    limit = None if megabytes is None else megabytes * 2**20
    return pltpu.CompilerParams(
        collective_id=collective_id, has_side_effects=True, vmem_limit_bytes=limit
    )


class RingGather:
    def __init__(self, size, x_ref, o_ref, send_sem, recv_sem, local_sem):
        self.size, self.x, self.o = size, x_ref, o_ref
        self.send, self.recv, self.local = send_sem, recv_sem, local_sem
        self.chunks = x_ref.shape[1]
        self.me, _, self.pos, self.right, self.left = neighbours(size)

    def copy(self, step, chunk, way, first=False):
        size = self.size
        if way == 0:
            block, peer = ring_index((self.pos - step + size) % size, size), self.right
        else:
            block, peer = ring_index((self.pos + step) % size, size), self.left
        source = self.x.at[way, chunk] if first else self.o.at[block, way, chunk]
        return push(
            source,
            self.o.at[block, way, chunk],
            self.send.at[step, chunk, way],
            self.recv.at[step, chunk, way],
            peer,
        )

    def start(self):
        self.kept = pltpu.make_async_copy(self.x, self.o.at[self.me], self.local)
        self.kept.start()
        for chunk in range(self.chunks):
            for way in range(2):
                self.copy(0, chunk, way, True).start()

    def advance(self, step):
        for chunk in range(self.chunks):
            for way in range(2):
                self.copy(step - 1, chunk, way).wait_recv()
                self.copy(step, chunk, way).start()

    def finish(self):
        last = self.size - 2
        for chunk in range(self.chunks):
            for way in range(2):
                self.copy(last, chunk, way).wait_recv()

        def drain(step, carry):
            for chunk in range(self.chunks):
                for way in range(2):
                    self.copy(step, chunk, way).wait_send()
            return carry

        lax.fori_loop(0, self.size - 1, drain, 0)
        self.kept.wait()


def ring_parts(x, chunks):
    return x.reshape(2, chunks, x.shape[0] // (2 * chunks), x.shape[1])


def ring_sems(size, chunks):
    return [
        pltpu.SemaphoreType.DMA((size - 1, chunks, 2)),
        pltpu.SemaphoreType.DMA((size - 1, chunks, 2)),
        pltpu.SemaphoreType.DMA,
    ]


def gather_kernel(size, x_ref, o_ref, send_sem, recv_sem, local_sem):
    _, _, _, right, left = neighbours(size)
    greet([right, left])
    ring = RingGather(size, x_ref, o_ref, send_sem, recv_sem, local_sem)
    ring.start()
    lax.fori_loop(1, size - 1, lambda step, carry: (ring.advance(step), carry)[1], 0)
    ring.finish()


def ring_gather(x, collective_id):
    size = lax.axis_size("seq")
    parts = ring_parts(x, 2)
    out = pl.pallas_call(
        functools.partial(gather_kernel, size),
        out_shape=jax.ShapeDtypeStruct((size,) + parts.shape, x.dtype),
        in_specs=[ANY],
        out_specs=ANY,
        scratch_shapes=ring_sems(size, 2),
        compiler_params=comm_params(collective_id),
        name="gather_rows",
    )(parts)
    return out.reshape(size * x.shape[0], x.shape[1])


def total_kernel(size, x_ref, o_ref, landing, send_sem, recv_sem):
    me, group = lax.axis_index("seq"), lax.axis_index("wa")
    peers = [(index, group) for index in others(me, size)]
    greet(peers)
    copies = [
        push(x_ref, landing.at[k], send_sem.at[k], recv_sem.at[k], peer)
        for k, peer in enumerate(peers)
    ]
    for copy in copies:
        copy.start()
    total = x_ref[...]
    for k, copy in enumerate(copies):
        copy.wait_recv()
        total = total + landing[k]
    o_ref[...] = total
    for copy in copies:
        copy.wait_send()


def seq_total(x, collective_id):
    size = lax.axis_size("seq")
    return pl.pallas_call(
        functools.partial(total_kernel, size),
        out_shape=jax.ShapeDtypeStruct(x.shape, x.dtype),
        in_specs=[VMEM],
        out_specs=VMEM,
        scratch_shapes=[
            pltpu.VMEM((size - 1,) + x.shape, x.dtype),
            pltpu.SemaphoreType.DMA((size - 1,)),
            pltpu.SemaphoreType.DMA((size - 1,)),
        ],
        compiler_params=comm_params(collective_id),
        name="seq_total",
    )(x)


def reduce_kernel(
    size,
    groups,
    grad_ref,
    weight_ref,
    piece_ref,
    part_ref,
    rows_ref,
    pieces_ref,
    landing_ref,
    slots,
    first,
    send_sem,
    recv_sem,
    piece_send,
    piece_recv,
    piece_local,
    part_send,
    part_recv,
):
    me, group, pos, right, left = neighbours(size)
    mates = [(me, index) for index in others(group, groups)]
    greet([right, left] + mates)
    tiles, tile = slots.shape[2], slots.shape[4]
    parts = [
        push(part_ref.at[mate[1]], landing_ref.at[k], part_send.at[k], part_recv.at[k], mate)
        for k, mate in enumerate(mates)
    ]
    for copy in parts:
        copy.start()
    ring = RingGather(size, piece_ref, pieces_ref, piece_send, piece_recv, piece_local)
    ring.start()

    def term(block, way, at):
        columns = pl.ds(pl.multiple_of(at * tile, tile), tile)
        return lax.dot_general(
            grad_ref[block, way],
            weight_ref[columns, :],
            (((1,), (1,)), ((), ())),
            preferred_element_type=jnp.float32,
        )

    def target(step, way):
        shift = (pos - 1 - step + 2 * size) if way == 0 else (pos + 1 + step)
        return ring_index(shift % size, size)

    def hop(step, way, at, source):
        return push(
            source,
            slots.at[step, way, at],
            send_sem.at[step, way, at],
            recv_sem.at[step, way, at],
            right if way == 0 else left,
        )

    def begin(at, carry):
        for way in range(2):
            first[way, at] = term(target(0, way), way, at).astype(jnp.bfloat16)
            hop(0, way, at, first.at[way, at]).start()
        return carry

    lax.fori_loop(0, tiles, begin, 0)

    def advance(step, carry):
        def one(at, inner):
            for way in range(2):
                own = term(target(step, way), way, at)
                hop(step - 1, way, at, first.at[way, at]).wait_recv()
                slots[step - 1, way, at] = (
                    slots[step - 1, way, at].astype(jnp.float32) + own
                ).astype(jnp.bfloat16)
                hop(step, way, at, slots.at[step - 1, way, at]).start()
            return inner

        lax.fori_loop(0, tiles, one, 0)
        ring.advance(step)
        return carry

    lax.fori_loop(1, size - 1, advance, 0)

    def end(at, carry):
        columns = pl.ds(pl.multiple_of(at * tile, tile), tile)
        for way in range(2):
            own = term(me, way, at)
            hop(size - 2, way, at, first.at[way, at]).wait_recv()
            rows_ref[way, :, columns] = slots[size - 2, way, at].astype(jnp.float32) + own
        return carry

    lax.fori_loop(0, tiles, end, 0)

    def drain(step, carry):
        def one(at, inner):
            for way in range(2):
                hop(step, way, at, first.at[way, at]).wait_send()
            return inner

        return lax.fori_loop(0, tiles, one, carry)

    lax.fori_loop(0, size - 1, drain, 0)
    ring.finish()
    for copy in parts:
        copy.wait()


def reduce_rows(grad, weight, piece, part, collective_id):
    size, groups = lax.axis_size("seq"), lax.axis_size("wa")
    _, ways, rows, _ = grad.shape
    width = weight.shape[0]
    tile = 512
    tiles = width // tile
    pieces = ring_parts(piece, 1)
    bf16 = jnp.bfloat16
    return pl.pallas_call(
        functools.partial(reduce_kernel, size, groups),
        out_shape=[
            jax.ShapeDtypeStruct((ways, rows, width), jnp.float32),
            jax.ShapeDtypeStruct((size,) + pieces.shape, bf16),
            jax.ShapeDtypeStruct((groups - 1,) + part.shape[1:], bf16),
        ],
        in_specs=[VMEM, VMEM, ANY, ANY],
        out_specs=[VMEM, ANY, ANY],
        scratch_shapes=[
            pltpu.VMEM((size - 1, 2, tiles, rows, tile), bf16),
            pltpu.VMEM((2, tiles, rows, tile), bf16),
            pltpu.SemaphoreType.DMA((size - 1, 2, tiles)),
            pltpu.SemaphoreType.DMA((size - 1, 2, tiles)),
        ]
        + ring_sems(size, 1)
        + [pltpu.SemaphoreType.DMA((groups - 1,)), pltpu.SemaphoreType.DMA((groups - 1,))],
        compiler_params=comm_params(collective_id, 60),
        name="reduce_rows",
    )(grad, weight, pieces, part)


def spread_kernel(
    size,
    groups,
    main_ref,
    pieces_ref,
    shared_ref,
    small_ref,
    gathered_ref,
    owned_ref,
    shared_out,
    small_out,
    shared_land,
    shared_sum,
    small_land,
    small_sum,
    main_send,
    main_recv,
    main_local,
    piece_send,
    piece_recv,
    piece_local,
    pair_send,
    pair_recv,
    mate_send,
    mate_recv,
):
    me, group, pos, right, left = neighbours(size)
    mates = [(me, index) for index in others(group, groups)]
    peers = [(index, group) for index in others(me, size)]
    greet(mates + peers)
    ring = RingGather(size, main_ref, gathered_ref, main_send, main_recv, main_local)
    ring.start()
    owned = [
        push(pieces_ref.at[mate[1]], owned_ref.at[group], piece_send.at[k], piece_recv.at[k], mate)
        for k, mate in enumerate(mates)
    ]
    kept = pltpu.make_async_copy(pieces_ref.at[group], owned_ref.at[group], piece_local)
    small_in = [
        push(small_ref, small_land.at[k], mate_send.at[k], mate_recv.at[k], mate)
        for k, mate in enumerate(mates)
    ]
    shared_in = [
        push(
            shared_ref.at[peer[0]], shared_land.at[k], pair_send.at[0, k], pair_recv.at[0, k], peer
        )
        for k, peer in enumerate(peers)
    ]
    for copy in small_in + shared_in:
        copy.start()
    kept.start()
    for copy in owned:
        copy.start()
    total = small_ref[...]
    for k, copy in enumerate(small_in):
        copy.wait_recv()
        total = total + small_land[k]
    small_sum[...] = total
    small_out[pl.ds(me, 1)] = total[None]
    total = shared_ref[me].astype(jnp.float32)
    for k, copy in enumerate(shared_in):
        copy.wait_recv()
        total = total + shared_land[k].astype(jnp.float32)
    shared_sum[...] = total.astype(jnp.bfloat16)
    shared_out[pl.ds(me, 1)] = total.astype(jnp.bfloat16)[None]
    second = []
    for k, peer in enumerate(peers):
        second.append(
            push(small_sum, small_out.at[me], pair_send.at[1, k], pair_recv.at[1, k], peer)
        )
        second.append(
            push(shared_sum, shared_out.at[me], pair_send.at[2, k], pair_recv.at[2, k], peer)
        )
    for copy in second:
        copy.start()
    lax.fori_loop(1, size - 1, lambda step, carry: (ring.advance(step), carry)[1], 0)
    ring.finish()
    for copy in small_in + shared_in:
        copy.wait_send()
    for copy in second + owned:
        copy.wait()
    kept.wait()


def spread_grads(main, pieces, shared, small, collective_id):
    size, groups = lax.axis_size("seq"), lax.axis_size("wa")
    parts = ring_parts(main, 2)
    bf16, f32 = jnp.bfloat16, jnp.float32
    DMA = pltpu.SemaphoreType.DMA
    return pl.pallas_call(
        functools.partial(spread_kernel, size, groups),
        out_shape=[
            jax.ShapeDtypeStruct((size,) + parts.shape, bf16),
            jax.ShapeDtypeStruct(pieces.shape, bf16),
            jax.ShapeDtypeStruct(shared.shape, bf16),
            jax.ShapeDtypeStruct((size,) + small.shape, f32),
        ],
        in_specs=[ANY, ANY, VMEM, VMEM],
        out_specs=[ANY, ANY, VMEM, VMEM],
        scratch_shapes=[
            pltpu.VMEM((size - 1,) + shared.shape[1:], bf16),
            pltpu.VMEM(shared.shape[1:], bf16),
            pltpu.VMEM((groups - 1,) + small.shape, f32),
            pltpu.VMEM(small.shape, f32),
        ]
        + ring_sems(size, 2)
        + [
            DMA((groups - 1,)),
            DMA((groups - 1,)),
            DMA,
            DMA((3, size - 1)),
            DMA((3, size - 1)),
            DMA((groups - 1,)),
            DMA((groups - 1,)),
        ],
        compiler_params=comm_params(collective_id, 32),
        name="spread_grads",
    )(parts, pieces, shared, small)


def assemble_kernel(lw, gathered_ref, shared_ref, o_ref):
    size = gathered_ref.shape[0]
    inner = size * lw
    for block in range(size):
        for half in range(2):
            at = half * inner + block * lw
            o_ref[:, at : at + lw] = gathered_ref[block, :, half * lw : (half + 1) * lw].astype(
                jnp.float32
            )
    tail = o_ref.shape[1] - 2 * inner
    o_ref[:, 2 * inner :] = shared_ref[:, :tail].astype(jnp.float32)


def assemble_in(gathered, shared, columns):
    size, rows, both = gathered.shape
    step = 64
    return pl.pallas_call(
        functools.partial(assemble_kernel, both // 2),
        grid=(rows // step,),
        in_specs=[
            pl.BlockSpec((size, step, both), lambda i: (0, i, 0)),
            pl.BlockSpec((step, shared.shape[1]), lambda i: (i, 0)),
        ],
        out_specs=pl.BlockSpec((step, columns), lambda i: (i, 0)),
        out_shape=jax.ShapeDtypeStruct((rows, columns), jnp.float32),
        compiler_params=pltpu.CompilerParams(vmem_limit_bytes=40 * 2**20),
        name="assemble_in",
    )(gathered, shared)


def widen_kernel(x_ref, o_ref):
    o_ref[...] = x_ref[0, 0].astype(jnp.float32)


def assemble_out(owned):
    groups, count, rows, width = owned.shape
    return pl.pallas_call(
        widen_kernel,
        grid=(count, groups),
        in_specs=[pl.BlockSpec((1, 1, rows, width), lambda t, g: (g, t, 0, 0))],
        out_specs=pl.BlockSpec((rows, width), lambda t, g: (t * groups + g, 0)),
        out_shape=jax.ShapeDtypeStruct((groups * count * rows, width), jnp.float32),
        name="assemble_out",
    )(owned)


def body(
    tokens,
    lengths,
    norm_gain,
    in_weight,
    conv_weight,
    conv_bias,
    dt_bias,
    a_log,
    skip_gain,
    out_gain,
    out_weight,
    cotangent,
):
    seqs_here, slot_rows, width = tokens.shape
    row_count = seqs_here * slot_rows
    inner_width = out_gain.shape[0]
    channels = conv_bias.shape[0]
    bc_width = channels - inner_width
    state_size = bc_width // 2
    head_count = dt_bias.shape[0]
    head_size = inner_width // head_count
    seq_devices = lax.axis_size("seq")
    group_devices = lax.axis_size("wa")
    seq_index = lax.axis_index("seq")
    length = seq_devices * slot_rows
    local_heads = head_count // seq_devices
    local_width = local_heads * head_size
    channel_start = seq_index * local_width
    head_start = seq_index * local_heads
    bf16, f32 = jnp.bfloat16, jnp.float32

    def take(array, start, size, axis):
        return lax.dynamic_slice_in_dim(array, start, size, axis)

    positions = seq_index * slot_rows + jnp.arange(slot_rows)
    valid_rows = (positions[None, :] < lengths[:, None]).astype(f32).reshape(row_count, 1)
    flat_tokens = tokens.reshape(row_count, width).astype(f32)
    in_scale = row_scale(flat_tokens)
    normed = (flat_tokens * in_scale * norm_gain).astype(bf16)
    normed_all = ring_gather(normed, 0)
    cot_rows = cotangent.reshape(row_count, width)
    branch_grad = ring_gather(cot_rows * valid_rows.astype(bf16), 1)

    dt_pad = jnp.zeros((in_weight.shape[0], 128 - local_heads), bf16)
    local_columns = jnp.concatenate(
        [
            take(in_weight, channel_start, local_width, 1),
            take(in_weight, inner_width + channel_start, local_width, 1),
            in_weight[:, 2 * inner_width : 2 * inner_width + bc_width],
            take(in_weight, 2 * inner_width + bc_width + head_start, local_heads, 1),
            dt_pad,
        ],
        axis=1,
    )
    in_columns = lax.all_gather(local_columns, "wa", axis=0, tiled=True)
    columns_here = in_columns.shape[1]
    blocks = (seq_devices, seqs_here, slot_rows)
    projected = (
        jnp.dot(normed_all, in_columns, preferred_element_type=f32)
        .astype(bf16)
        .reshape(blocks + (columns_here,))
    )

    def lanes(part):
        return jnp.pad(part[None], ((0, 7), (0, 128 - local_heads)))

    taps = jnp.pad(
        jnp.concatenate(
            [take(conv_weight, channel_start, local_width, 1), conv_weight[:, inner_width:]], axis=1
        ),
        ((0, 8 - KW), (0, 0)),
    )
    shift = jnp.concatenate(
        [take(conv_bias, channel_start, local_width, 0), conv_bias[inner_width:]]
    )[None]
    bias = lanes(take(dt_bias, head_start, local_heads, 0))
    slope = lanes(-jnp.exp(take(a_log, head_start, local_heads, 0)))
    skip = jnp.repeat(take(skip_gain, head_start, local_heads, 0), head_size)[None]
    gain_local = take(out_gain, channel_start, local_width, 0)
    spread, fold, tri, upper = scan_tables(slot_rows, local_width, head_size)
    widths = (local_width, bc_width)
    gated_heads, y_heads, entering = scan_forward(
        projected, taps, shift, bias, slope, skip, spread, tri, widths, head_size
    )
    gated = gated_heads.reshape(-1, local_width).astype(f32)

    out_full = lax.all_gather(out_weight, "wa", axis=0, tiled=True)
    out_rows = take(out_full, channel_start, local_width, 0)
    out_grad = lax.dot_general(
        branch_grad, out_rows, (((1,), (1,)), ((), ())), preferred_element_type=f32
    )
    weighted = out_grad * gain_local
    sums = seq_total(
        jnp.stack(
            [jnp.sum(gated * gated, axis=-1), jnp.sum(weighted * gated, axis=-1)]
        ).reshape(-1, 128),
        2,
    ).reshape(2, -1)
    out_scale = lax.rsqrt(sums[0] / inner_width + EPS)[:, None]
    mean_dot = (sums[1] / inner_width)[:, None]
    normed_out = (gated * out_scale * gain_local).astype(bf16)
    out_gain_part = jnp.sum(out_grad * gated * out_scale, axis=0)
    gated_grad = (out_scale * weighted - gated * out_scale**3 * mean_dot).astype(bf16)

    swapped = lax.all_to_all(
        normed_out.reshape(seq_devices, row_count, local_width), "seq", 0, 0, tiled=True
    )
    out_weight_part = lax.psum_scatter(
        lax.dot_general(
            normed_out, branch_grad, (((0,), (0,)), ((), ())), preferred_element_type=f32
        ).astype(bf16),
        "wa",
        scatter_dimension=0,
        tiled=True,
    )
    proj_grad, taps_sum, skip_sum, head_sum = scan_backward(
        projected,
        y_heads,
        entering,
        gated_grad.reshape(blocks + (local_width,)),
        taps,
        shift,
        bias,
        slope,
        skip,
        spread,
        fold,
        tri,
        upper,
        widths,
        head_size,
    )
    proj_grad = proj_grad.reshape(-1, columns_here)
    conv_w_grad, conv_b_grad = taps_sum[:KW], taps_sum[KW]
    skip_grad = jnp.sum(skip_sum[0].reshape(local_heads, head_size), axis=1)
    shift_grad, rates_grad = head_sum[0, :local_heads], head_sum[1, :local_heads]
    in_rows = in_weight.shape[0]
    in_weight_part = (
        lax.dot_general(
            normed_all, proj_grad, (((0,), (0,)), ((), ())), preferred_element_type=f32
        )
        .astype(bf16)
        .reshape(group_devices, in_rows, columns_here)
    )
    branch = jnp.dot(
        jnp.swapaxes(swapped, 0, 1).reshape(row_count, inner_width),
        out_full,
        preferred_element_type=f32,
    )
    mixed_out = (flat_tokens + valid_rows * branch).astype(bf16).reshape(tokens.shape)
    normed_grad, pieces, landed = reduce_rows(
        proj_grad.reshape(blocks + (columns_here,)),
        in_columns,
        out_weight_part,
        in_weight_part,
        3,
    )
    normed_grad = normed_grad.reshape(row_count, width)
    in_weight_sum = lax.dynamic_index_in_dim(
        in_weight_part, lax.axis_index("wa"), 0, keepdims=False
    ).astype(f32) + jnp.sum(landed.astype(f32), axis=0)
    token_grad, norm_gain_grad = norm_backward(flat_tokens, in_scale, norm_gain, normed_grad)
    token_grad = token_grad + cot_rows.astype(f32)

    dt_wide = lax.dynamic_update_slice_in_dim(
        jnp.zeros((in_rows, 128), f32),
        in_weight_sum[:, 2 * local_width + bc_width :][:, :local_heads],
        head_start,
        1,
    )
    shared = jnp.concatenate(
        [in_weight_sum[:, 2 * local_width : 2 * local_width + bc_width], dt_wide], axis=1
    ).astype(bf16)
    shared_columns = shared.shape[1]
    heads = jnp.stack(
        [
            jnp.pad(part, (0, 128 - local_heads))
            for part in (shift_grad, rates_grad, skip_grad)
        ]
    )
    own_parts = [conv_w_grad[:, :local_width], conv_b_grad[:local_width], out_gain_part, heads]
    sum_parts = [conv_w_grad[:, local_width:], conv_b_grad[local_width:], norm_gain_grad]
    packed = jnp.concatenate([part.reshape(-1, 128) for part in own_parts + sum_parts])
    packed_rows = packed.shape[0]
    packed = jnp.pad(packed, ((0, -packed_rows % 8), (0, 0)))
    per_owner = seq_devices // group_devices
    gathered, owned, shared_all, small_all = spread_grads(
        in_weight_sum[:, : 2 * local_width].astype(bf16),
        pieces.reshape(group_devices, per_owner, local_width // group_devices, width),
        shared.reshape(seq_devices, in_rows // seq_devices, shared_columns),
        packed,
        4,
    )
    in_weight_grad = assemble_in(
        gathered.reshape(seq_devices, in_rows, 2 * local_width),
        shared_all.reshape(in_rows, shared_columns),
        in_weight.shape[1],
    )
    out_weight_grad = assemble_out(owned)

    tile_rows = local_width // 128
    own_rows = (KW + 2) * tile_rows
    own_all = small_all[:, :own_rows].reshape(seq_devices, KW + 2, local_width)
    own_all = jnp.swapaxes(own_all, 0, 1).reshape(KW + 2, inner_width)
    head_all = jnp.swapaxes(small_all[:, own_rows : own_rows + 3, :local_heads], 0, 1)
    head_all = head_all.reshape(3, head_count)
    summed = jnp.sum(small_all[:, own_rows + 3 : packed_rows], axis=0).reshape(-1)
    conv_weight_grad = jnp.concatenate(
        [own_all[:KW], summed[: KW * bc_width].reshape(KW, bc_width)], axis=1
    )
    conv_bias_grad = jnp.concatenate(
        [own_all[KW], summed[KW * bc_width : (KW + 1) * bc_width]]
    )
    norm_gain_total = summed[(KW + 1) * bc_width :]
    return (
        mixed_out,
        token_grad.reshape(tokens.shape),
        norm_gain_total,
        in_weight_grad,
        conv_weight_grad,
        conv_bias_grad,
        head_all[0],
        head_all[1],
        head_all[2],
        own_all[KW + 1],
        out_weight_grad,
    )


def solution(mesh):
    placed = (
        P("wa", "seq", None),
        P("wa"),
        P(),
        P("wa", None),
        P(),
        P(),
        P(),
        P(),
        P(),
        P(),
        P("wa", None),
        P("wa", "seq", None),
    )
    return jax.shard_map(
        body,
        mesh=mesh,
        in_specs=placed,
        out_specs=(
            P("wa", "seq", None),
            P("wa", "seq", None),
            P(),
            P("wa", None),
            P(),
            P(),
            P(),
            P(),
            P(),
            P(),
            P("wa", None),
        ),
        check_vma=False,
    )
```

```python
import functools

import jax
import jax.numpy as jnp
from jax import lax
from jax.experimental import pallas as pl
from jax.experimental.pallas import tpu as pltpu
from jax.sharding import PartitionSpec as P

KW = 4
EPS = 1e-05
HIGHEST = lax.Precision.HIGHEST
MESH = pl.DeviceIdType.MESH


def row_scale(values):
    return lax.rsqrt(jnp.mean(values * values, axis=-1, keepdims=True) + EPS)


def norm_backward(values, row_scales, gain_vec, grad_out):
    weighted = grad_out * gain_vec
    grad_gain = jnp.sum(grad_out * values * row_scales, axis=0)
    grad_values = row_scales * weighted - values * row_scales**3 * jnp.mean(
        weighted * values, axis=-1, keepdims=True
    )
    return (grad_values, grad_gain)


def dot(a, b, ca, cb, precision=None):
    return lax.dot_general(
        a, b, (((ca,), (cb,)), ((), ())), precision=precision, preferred_element_type=jnp.float32
    )


def chunk_front(proj_ref, ext, taps_ref, shift_ref, bias_ref, slope_ref, tri_ref, widths):
    lw, bc = widths
    rows = proj_ref.shape[2]
    ext[8:, :] = proj_ref[0, 0, :, lw : 2 * lw + bc].astype(jnp.float32)
    conv = shift_ref[0:1, :]
    for k in range(KW):
        conv = conv + taps_ref[k : k + 1, :] * ext[5 + k : 5 + k + rows, :]
    conv_sig = lax.logistic(conv)
    act = conv * conv_sig
    step_in = proj_ref[0, 0, :, 2 * lw + bc :].astype(jnp.float32) + bias_ref[0:1, :]
    steps = jnp.maximum(step_in, 0.0) + jnp.log1p(jnp.exp(-jnp.abs(step_in)))
    rates = slope_ref[0:1, :] * steps
    cum = dot(tri_ref[...], rates, 1, 0, HIGHEST)
    return conv, conv_sig, act, step_in, steps, rates, cum


def head_masks(rows, head_size):
    lane = lax.broadcasted_iota(jnp.int32, (rows, 128), 1)
    row = lax.broadcasted_iota(jnp.int32, (rows, rows), 0)
    col = lax.broadcasted_iota(jnp.int32, (rows, rows), 1)
    return lane, row >= col


def forward_chunk(
    widths,
    head_size,
    start,
    proj_ref,
    taps_ref,
    shift_ref,
    bias_ref,
    slope_ref,
    skip_ref,
    spread_ref,
    tri_ref,
    gated_ref,
    y_ref,
    enter_ref,
    state,
    ext,
    halo,
):
    lw, bc = widths
    bf16, f32 = jnp.bfloat16, jnp.float32
    rows = proj_ref.shape[2]
    per_tile = 128 // head_size

    @pl.when(start)
    def _():
        state[...] = jnp.zeros_like(state)
        halo[...] = jnp.zeros_like(halo)

    ext[0:8, :] = halo[...]
    _, _, act, _, steps, _, cum = chunk_front(
        proj_ref, ext, taps_ref, shift_ref, bias_ref, slope_ref, tri_ref, widths
    )
    halo[...] = ext[rows : rows + 8, :]
    x = act[:, :lw]
    xb = x.astype(bf16)
    b_rows = act[:, lw : lw + bc // 2].astype(bf16)
    c_rows = act[:, lw + bc // 2 :].astype(bf16)
    cum_t, steps_t = cum.T, steps.T
    last = cum[rows - 1 : rows, :]
    grow = dot(jnp.exp(cum).astype(bf16), spread_ref[...], 1, 0)
    tail = dot((jnp.exp(last - cum) * steps).astype(bf16), spread_ref[...], 1, 0)
    scores = dot(c_rows, b_rows, 1, 1)
    entering = state[...].astype(bf16)
    enter_ref[0, 0] = entering
    y = dot(c_rows, entering, 1, 1) * grow + skip_ref[0:1, :] * x
    added = dot((x * tail).astype(bf16), b_rows, 0, 0)
    lane, causal = head_masks(rows, head_size)
    gate = proj_ref[0, 0, :, :lw].astype(f32)
    silu_gate = gate * lax.logistic(gate)
    for tile in range(lw // 128):
        cols = slice(tile * 128, (tile + 1) * 128)
        inner = None
        for sub in range(per_tile):
            head = tile * per_tile + sub
            log_decay = cum[:, head : head + 1] - cum_t[head : head + 1, :]
            decay = jnp.exp(jnp.where(causal, log_decay, -1e30))
            weights = (scores * decay * steps_t[head : head + 1, :]).astype(bf16)
            part = dot(weights, xb[:, cols], 1, 0)
            inner = part if inner is None else jnp.where(lane >= sub * head_size, part, inner)
            span = slice(head * head_size, (head + 1) * head_size)
            state[span, :] = (
                jnp.exp(cum[rows - 1 : rows, head : head + 1]) * state[span, :] + added[span, :]
            )
        y_tile = y[:, cols] + inner
        y_ref[0, 0, :, cols] = y_tile.astype(bf16)
        gated_ref[:, cols] = (y_tile * silu_gate[:, cols]).astype(bf16)


def backward_kernel(
    widths,
    head_size,
    chunks,
    proj_ref,
    before_ref,
    y_ref,
    enter_ref,
    grad_ref,
    taps_ref,
    shift_ref,
    bias_ref,
    slope_ref,
    skip_ref,
    spread_ref,
    fold_ref,
    tri_ref,
    upper_ref,
    out_ref,
    turned_ref,
    taps_acc,
    skip_acc,
    head_acc,
    lam,
    ext,
    later,
    after,
):
    lw, bc = widths
    state_size = bc // 2
    bf16, f32 = jnp.bfloat16, jnp.float32
    rows = proj_ref.shape[2]
    per_tile = 128 // head_size
    chunk = chunks - 1 - pl.program_id(1)

    @pl.when((pl.program_id(0) == 0) & (pl.program_id(1) == 0))
    def _():
        taps_acc[...] = jnp.zeros_like(taps_acc)
        skip_acc[...] = jnp.zeros_like(skip_acc)
        head_acc[...] = jnp.zeros_like(head_acc)

    @pl.when(pl.program_id(1) == 0)
    def _():
        lam[...] = jnp.zeros_like(lam)
        after[...] = jnp.zeros_like(after)

    ext[0:8, :] = jnp.where(
        chunk > 0, before_ref[0, 0, 8:16, lw : 2 * lw + bc].astype(f32), 0.0
    )
    conv, conv_sig, act, step_in, steps, rates, cum = chunk_front(
        proj_ref, ext, taps_ref, shift_ref, bias_ref, slope_ref, tri_ref, widths
    )
    x = act[:, :lw]
    xb = x.astype(bf16)
    b_rows = act[:, lw : lw + state_size].astype(bf16)
    c_rows = act[:, lw + state_size :].astype(bf16)
    cum_t, steps_t = cum.T, steps.T
    last = cum[rows - 1 : rows, :]
    to_end = jnp.exp(last - cum)
    tail_heads = to_end * steps
    grow = dot(jnp.exp(cum).astype(bf16), spread_ref[...], 1, 0)
    tail = dot(tail_heads.astype(bf16), spread_ref[...], 1, 0)
    scores = dot(c_rows, b_rows, 1, 1)

    gate = proj_ref[0, 0, :, :lw].astype(f32)
    gate_sig = lax.logistic(gate)
    grad = grad_ref[0, 0].astype(f32)
    y_grad = grad * gate * gate_sig
    out_ref[0, 0, :, :lw] = (
        grad * y_ref[0, 0].astype(f32) * (gate_sig * (1.0 + gate * (1.0 - gate_sig)))
    ).astype(bf16)
    yb = y_grad.astype(bf16)

    entering = enter_ref[0, 0]
    grown = y_grad * grow
    grown_b = grown.astype(bf16)
    c_grad = dot(grown_b, entering, 1, 0)
    carried = dot((grown * dot(c_rows, entering, 1, 1)).astype(bf16), fold_ref[...], 1, 0)
    lam_now = lam[...]
    lam_b = lam_now.astype(bf16)
    from_lam = dot(b_rows, lam_b, 1, 1)
    b_grad = dot((x * tail).astype(bf16), lam_b, 1, 0)
    x_lam = dot((x * from_lam).astype(bf16), fold_ref[...], 1, 0)
    x_grad = skip_ref[0:1, :] * y_grad + tail * from_lam
    skip_acc[0:1, :] += jnp.sum(y_grad * x, axis=0, keepdims=True)
    ones = jnp.ones((8, state_size), bf16)
    kept = dot(
        dot(ones, (lam_now * entering.astype(f32)).astype(bf16), 1, 1),
        fold_ref[...].astype(f32),
        1,
        0,
        HIGHEST,
    )
    through = jnp.exp(last) * kept[0:1, :]
    lam_add = dot(grown_b, c_rows, 0, 0)

    lane, causal = head_masks(rows, head_size)
    score_grad = None
    row_sums = jnp.zeros((rows, 128), f32)
    col_sums = []
    x_tiles = []
    for tile in range(lw // 128):
        cols = slice(tile * 128, (tile + 1) * 128)
        inner = None
        for sub in range(per_tile):
            head = tile * per_tile + sub
            log_decay = cum[:, head : head + 1] - cum_t[head : head + 1, :]
            decay = jnp.exp(jnp.where(causal, log_decay, -1e30))
            step_row = steps_t[head : head + 1, :]
            weights = (scores * decay * step_row).astype(bf16)
            inside = (lane >= sub * head_size) & (lane < (sub + 1) * head_size)
            y_head = jnp.where(inside, yb[:, cols], jnp.zeros_like(yb[:, cols]))
            weights_grad = dot(y_head, xb[:, cols], 1, 1)
            part = dot(weights, yb[:, cols], 0, 0)
            inner = part if inner is None else jnp.where(lane >= sub * head_size, part, inner)
            decayed = weights_grad * decay
            stepped = decayed * step_row
            score_grad = stepped if score_grad is None else score_grad + stepped
            col_sums.append(jnp.sum(decayed * scores, axis=0, keepdims=True))
            row_sum = jnp.sum(stepped * scores, axis=1, keepdims=True)
            row_sums = row_sums + jnp.where(lane == head, row_sum, 0.0)
            span = slice(head * head_size, (head + 1) * head_size)
            lam[span, :] = (
                jnp.exp(cum[rows - 1 : rows, head : head + 1]) * lam_now[span, :] + lam_add[span, :]
            )
        x_tiles.append(x_grad[:, cols] + inner)
    col_sums.append(jnp.zeros((rows - len(col_sums), rows), f32))
    col_sum = jnp.concatenate(col_sums, axis=0).T
    source = row_sums - steps * col_sum + carried
    rates_grad = (
        dot(upper_ref[...], source, 1, 0, HIGHEST)
        + dot(1.0 - upper_ref[...], tail_heads * x_lam, 1, 0, HIGHEST)
        + through
    )
    steps_grad = col_sum + to_end * x_lam + rates_grad * slope_ref[0:1, :]
    raw_grad = steps_grad * lax.logistic(step_in)
    out_ref[0, 0, :, 2 * lw + bc :] = raw_grad.astype(bf16)
    head_acc[0:1, :] += jnp.sum(raw_grad, axis=0, keepdims=True)
    head_acc[1:2, :] += jnp.sum(rates_grad * rates, axis=0, keepdims=True)
    score_b = score_grad.astype(bf16)
    c_grad = c_grad + dot(score_b, b_rows, 1, 0)
    b_grad = b_grad + dot(score_b, c_rows, 0, 0)
    act_grad = jnp.concatenate(x_tiles + [b_grad, c_grad], axis=1)
    conv_grad = act_grad * (conv_sig * (1.0 + conv * (1.0 - conv_sig)))
    later[0:rows, :] = conv_grad
    later[rows : rows + 8, :] = after[...]
    after[...] = conv_grad[0:8, :]
    total = None
    for k in range(KW):
        term = taps_ref[k : k + 1, :] * later[3 - k : 3 - k + rows, :]
        total = term if total is None else total + term
        taps_acc[k : k + 1, :] += jnp.sum(conv_grad * ext[5 + k : 5 + k + rows, :], axis=0, keepdims=True)
    taps_acc[KW : KW + 1, :] += jnp.sum(conv_grad, axis=0, keepdims=True)
    out_ref[0, 0, :, lw : 2 * lw + bc] = total.astype(bf16)
    turned_ref[...] = out_ref[0, 0].T


def whole_spec(array):
    return pl.BlockSpec(array.shape, lambda q, c: (0,) * array.ndim)


def scan_tables(rows, local_width, head_size):
    head_of = jnp.arange(local_width) // head_size
    spread = (jnp.arange(128)[:, None] == head_of[None, :]).astype(jnp.bfloat16)
    tri = (jnp.arange(rows)[:, None] >= jnp.arange(rows)[None, :]).astype(jnp.float32)
    return spread, spread.T, tri, tri.T


def scan_backward(
    proj, y, enter, grad, taps, shift, bias, slope, skip, spread, fold, tri, upper, widths, head_size
):
    chunks, seqs, rows, cols = proj.shape
    lw, bc = widths
    block = lambda *tail: pl.BlockSpec((1, 1) + tail, lambda q, c: (chunks - 1 - c, q, 0, 0))
    before = pl.BlockSpec(
        (1, 1, 16, cols),
        lambda q, c: (jnp.maximum(chunks - 2 - c, 0), q, rows // 16 - 1, 0),
    )
    tables = (taps, shift, bias, slope, skip, spread, fold, tri, upper)
    sums = [(8, lw + bc), (8, lw), (8, 128)]
    return pl.pallas_call(
        functools.partial(backward_kernel, widths, head_size, chunks),
        grid=(seqs, chunks),
        in_specs=[block(rows, cols), before, block(rows, lw), block(lw, bc // 2), block(rows, lw)]
        + [whole_spec(t) for t in tables],
        out_specs=[
            block(rows, cols),
            pl.BlockSpec((cols, rows), lambda q, c: (0, (chunks - 1 - c) * seqs + q)),
        ]
        + [pl.BlockSpec(s, lambda q, c: (0, 0)) for s in sums],
        out_shape=[
            jax.ShapeDtypeStruct(proj.shape, jnp.bfloat16),
            jax.ShapeDtypeStruct((cols, chunks * seqs * rows), jnp.bfloat16),
        ]
        + [jax.ShapeDtypeStruct(s, jnp.float32) for s in sums],
        scratch_shapes=[
            pltpu.VMEM((lw, bc // 2), jnp.float32),
            pltpu.VMEM((rows + 8, lw + bc), jnp.float32),
            pltpu.VMEM((rows + 8, lw + bc), jnp.float32),
            pltpu.VMEM((8, lw + bc), jnp.float32),
        ],
        compiler_params=pltpu.CompilerParams(vmem_limit_bytes=48 * 2**20),
        name="scan_backward",
    )(proj, proj, y, enter, grad, *tables)


def ring_pos(index, size):
    row, side = index // 2, index % 2
    return row + side * (size - 1 - 2 * row)


def ring_index(pos, size):
    side = pos // (size // 2)
    row = pos + side * (size - 1 - 2 * pos)
    return row * 2 + side


def greet(peers):
    barrier = pltpu.get_barrier_semaphore()
    for peer in peers:
        pl.semaphore_signal(barrier, inc=1, device_id=peer, device_id_type=MESH)
    pl.semaphore_wait(barrier, len(peers))


def push(source, target, send_sem, recv_sem, peer):
    return pltpu.make_async_remote_copy(
        source, target, send_sem, recv_sem, device_id=peer, device_id_type=MESH
    )


def neighbours(size):
    me, group = lax.axis_index("seq"), lax.axis_index("wa")
    pos = ring_pos(me, size)
    right = (ring_index((pos + 1) % size, size), group)
    left = (ring_index((pos + size - 1) % size, size), group)
    return me, group, pos, right, left


def others(index, size):
    return [(index + offset) % size for offset in range(1, size)]


ANY = pl.BlockSpec(memory_space=pl.ANY)
VMEM = pl.BlockSpec(memory_space=pltpu.VMEM)


def comm_params(collective_id, megabytes=None):
    limit = None if megabytes is None else megabytes * 2**20
    return pltpu.CompilerParams(
        collective_id=collective_id, has_side_effects=True, vmem_limit_bytes=limit
    )


class RingGather:
    def __init__(self, size, x_ref, o_ref, send_sem, recv_sem, local_sem):
        self.size, self.x, self.o = size, x_ref, o_ref
        self.send, self.recv, self.local = send_sem, recv_sem, local_sem
        self.chunks = x_ref.shape[1]
        self.me, _, self.pos, self.right, self.left = neighbours(size)

    def copy(self, step, chunk, way, first=False):
        size = self.size
        if way == 0:
            block, peer = ring_index((self.pos - step + size) % size, size), self.right
        else:
            block, peer = ring_index((self.pos + step) % size, size), self.left
        source = self.x.at[way, chunk] if first else self.o.at[block, way, chunk]
        return push(
            source,
            self.o.at[block, way, chunk],
            self.send.at[step, chunk, way],
            self.recv.at[step, chunk, way],
            peer,
        )

    def kept(self):
        return pltpu.make_async_copy(self.x, self.o.at[self.me], self.local)

    def start(self):
        self.kept().start()
        for chunk in range(self.chunks):
            for way in range(2):
                self.copy(0, chunk, way, True).start()

    def advance(self, step):
        for chunk in range(self.chunks):
            for way in range(2):
                self.copy(step - 1, chunk, way).wait_recv()
                self.copy(step, chunk, way).start()

    def finish(self):
        last = self.size - 2
        for chunk in range(self.chunks):
            for way in range(2):
                self.copy(last, chunk, way).wait_recv()

        def drain(step, carry):
            for chunk in range(self.chunks):
                for way in range(2):
                    self.copy(step, chunk, way).wait_send()
            return carry

        lax.fori_loop(0, self.size - 1, drain, 0)
        self.kept().wait()


def ring_parts(x, chunks):
    return x.reshape(2, chunks, x.shape[0] // (2 * chunks), x.shape[1])


def ring_sems(size, chunks):
    return [
        pltpu.SemaphoreType.DMA((size - 1, chunks, 2)),
        pltpu.SemaphoreType.DMA((size - 1, chunks, 2)),
        pltpu.SemaphoreType.DMA,
    ]


def project_kernel(
    size,
    groups,
    x_ref,
    w_ref,
    rows_ref,
    weights_ref,
    proj_ref,
    taken,
    weights,
    made,
    send_sem,
    recv_sem,
    local_sem,
    weight_send,
    weight_recv,
    weight_local,
    take_sem,
    made_sem,
):
    me, group, pos, right, left = neighbours(size)
    mates = [(me, index) for index in others(group, groups)]
    greet([right, left] + mates)
    ring = RingGather(size, x_ref, rows_ref, send_sem, recv_sem, local_sem)
    ring.start()
    sent = [
        push(w_ref, weights.at[group], weight_send.at[k], weight_recv.at[k], mate)
        for k, mate in enumerate(mates)
    ]
    for copy in sent:
        copy.start()
    kept = pltpu.make_async_copy(w_ref, weights.at[group], weight_local.at[0])
    kept.start()
    depth = weights.shape[2]

    def block_of(pair, way):
        return ring_index((pos - pair + size) % size if way == 0 else (pos + pair) % size, size)

    def take(pair, slot, way, own=False):
        source = x_ref.at[way] if own else rows_ref.at[block_of(pair, way), way]
        return pltpu.make_async_copy(source, taken.at[slot, way], take_sem.at[slot, way])

    def put(pair, slot, way):
        return pltpu.make_async_copy(
            made.at[slot, way], proj_ref.at[block_of(pair, way), way], made_sem.at[slot, way]
        )

    def compute(pair, slot):
        for way in range(2):
            x = taken[slot, way].reshape(made.shape[2], taken.shape[4])
            total = None
            for part in range(groups):
                term = lax.dot_general(
                    x[:, part * depth : (part + 1) * depth],
                    weights[part],
                    (((1,), (1,)), ((), ())),
                    preferred_element_type=jnp.float32,
                )
                total = term if total is None else total + term
            made[slot, way] = total.astype(jnp.bfloat16)
            put(pair, slot, way).start()

    def advance(step, carry):
        ring.advance(step)
        return carry

    middle = size // 2 + 1
    lax.fori_loop(1, middle, advance, 0)
    for way in range(2):
        take(0, 0, way, True).start()
    kept.wait()
    for copy in sent:
        copy.wait_recv()
    flushed = pltpu.make_async_copy(weights, weights_ref, weight_local.at[1])
    flushed.start()
    for way in range(2):
        take(0, 0, way, True).wait()
    compute(0, 0)

    def pairs(low, high):
        for way in range(2):
            take(low, lax.rem(low, 2), way).start()

        def one(pair, carry):
            slot = lax.rem(pair, 2)
            for way in range(2):
                take(pair, slot, way).wait()

            @pl.when(pair + 1 < high)
            def _():
                for way in range(2):
                    take(pair + 1, 1 - slot, way).start()

            @pl.when(pair >= 2)
            def _():
                for way in range(2):
                    put(pair - 2, slot, way).wait()

            compute(pair, slot)
            return carry

        lax.fori_loop(low, high, one, 0)

    count = size - 1 - middle

    def late(step, carry):
        ring.advance(step)
        turn = step - middle
        pairs(1 + (turn * (size - 2)) // count, 1 + ((turn + 1) * (size - 2)) // count)
        return carry

    lax.fori_loop(middle, size - 1, late, 0)
    ring.finish()
    pairs(size - 1, size)
    for pair in (size - 2, size - 1):
        for way in range(2):
            put(pair, pair % 2, way).wait()
    for copy in sent:
        copy.wait_send()
    flushed.wait()


def project(x, weight, collective_id):
    size, groups = lax.axis_size("seq"), lax.axis_size("wa")
    parts = ring_parts(x, 2)
    cols, depth = weight.shape
    rows = x.shape[0] // 2
    bf16, DMA = jnp.bfloat16, pltpu.SemaphoreType.DMA
    return pl.pallas_call(
        functools.partial(project_kernel, size, groups),
        out_shape=[
            jax.ShapeDtypeStruct((size,) + parts.shape, bf16),
            jax.ShapeDtypeStruct((groups, cols, depth), bf16),
            jax.ShapeDtypeStruct((size, 2, rows, cols), bf16),
        ],
        in_specs=[ANY, ANY],
        out_specs=[ANY, ANY, ANY],
        scratch_shapes=[
            pltpu.VMEM((2,) + parts.shape, bf16),
            pltpu.VMEM((groups, cols, depth), bf16),
            pltpu.VMEM((2, 2, rows, cols), bf16),
        ]
        + ring_sems(size, 2)
        + [DMA((groups - 1,)), DMA((groups - 1,)), DMA((2,)), DMA((2, 2)), DMA((2, 2))],
        compiler_params=comm_params(collective_id, 60),
        name="project",
    )(parts, weight)


def middle_kernel(
    widths,
    head_size,
    size,
    groups,
    inner,
    proj_ref,
    taps_ref,
    shift_ref,
    bias_ref,
    slope_ref,
    skip_ref,
    spread_ref,
    tri_ref,
    gain_ref,
    cot_ref,
    shard_ref,
    y_ref,
    enter_ref,
    normed_ref,
    grad_ref,
    gain_acc,
    branch_ref,
    part_ref,
    state,
    ext,
    halo,
    gated,
    out_grad,
    sums,
    landing,
    taken,
    weights,
    turned,
    send_sem,
    recv_sem,
    local_sem,
    pair_send,
    pair_recv,
    shard_send,
    shard_recv,
    shard_local,
    take_sem,
):
    bf16, f32 = jnp.bfloat16, jnp.float32
    index = pl.program_id(0)
    seq, chunk = index // size, lax.rem(index, size)
    me, group, pos, right, left = neighbours(size)
    rows, lw = gated.shape[2:]
    peers = [(other, group) for other in others(me, size)]
    sibling = (me, group + 1 - 2 * lax.rem(group, 2))
    across = (me, lax.rem(group + 2, groups))
    ring = RingGather(size, cot_ref, branch_ref, send_sem, recv_sem, local_sem)
    chosen = lax.rem(me, size // groups)
    owner = me // (size // groups)

    def shard(step, source, slot, peer):
        return push(
            source, part_ref.at[slot], shard_send.at[step], shard_recv.at[step], peer
        )

    def shards(step):
        if step == 2:
            return shard(2, part_ref.at[across[1]], across[1], sibling)
        return shard(step, shard_ref.at[chosen], group, across if step == 0 else sibling)

    @pl.when(index == 0)
    def _():
        greet([right, left, across, sibling] + [p for p in peers])
        ring.start()
        shards(0).start()
        shards(1).start()

    forward_chunk(
        widths,
        head_size,
        chunk == 0,
        proj_ref,
        taps_ref,
        shift_ref,
        bias_ref,
        slope_ref,
        skip_ref,
        spread_ref,
        tri_ref,
        gated.at[chunk, seq],
        y_ref,
        enter_ref,
        state,
        ext,
        halo,
    )

    @pl.when(index == size + 2)
    def _():
        ring.advance(1)

    def block_of(pair, way):
        return ring_index((pos - pair + size) % size if way == 0 else (pos + pair) % size, size)

    def take(pair, slot, way, own=False):
        source = cot_ref.at[way] if own else branch_ref.at[block_of(pair, way), way]
        return pltpu.make_async_copy(source, taken.at[slot, way], take_sem.at[slot, way])

    ones = jnp.ones((8, lw), bf16)

    def compute(pair, slot):
        for way in range(2):
            block = block_of(pair, way)
            values = dot(taken[slot, way].reshape(rows, taken.shape[4]), turned[...], 1, 0)
            out_grad[block, way] = values
            here = gated[block, way].astype(f32)
            weighted = values * gain_ref[0:1, :] * here
            at = pl.ds(block * 2 + way, 1)
            sums[0, at, :] = dot(ones, (here * here).astype(bf16), 1, 1)[0:1, :]
            sums[1, at, :] = dot(ones, weighted.astype(bf16), 1, 1)[0:1, :]

    def pairs(low, high):
        for way in range(2):
            take(low, lax.rem(low, 2), way).start()

        def one(pair, carry):
            slot = lax.rem(pair, 2)
            for way in range(2):
                take(pair, slot, way).wait()

            @pl.when(pair + 1 < high)
            def _():
                for way in range(2):
                    take(pair + 1, 1 - slot, way).start()

            compute(pair, slot)
            return carry

        lax.fori_loop(low, high, one, 0)

    @pl.when(index == 2 * size - 1)
    def _():
        def advance(step, carry):
            ring.advance(step)
            return carry

        middle = size // 2 + 1
        lax.fori_loop(2, middle, advance, 0)
        for way in range(2):
            take(0, 0, way, True).start()
        first, second, third = (shards(step) for step in range(3))
        first.wait_recv()
        third.start()
        second.wait_recv()
        ring.advance(middle)
        third.wait_recv()

        @pl.when(owner == group)
        def _():
            loaded = pltpu.make_async_copy(shard_ref.at[chosen], weights, shard_local.at[0])
            loaded.start()
            loaded.wait()

        @pl.when(owner != group)
        def _():
            loaded = pltpu.make_async_copy(part_ref.at[owner], weights, shard_local.at[1])
            loaded.start()
            loaded.wait()

        turned[...] = weights[...].T
        for way in range(2):
            take(0, 0, way, True).wait()
        compute(0, 0)
        count = size - 1 - middle

        def batch(turn):
            pairs(1 + (turn * (size - 2)) // count, 1 + ((turn + 1) * (size - 2)) // count)

        batch(0)

        def late(step, carry):
            ring.advance(step)
            batch(step - middle)
            return carry

        lax.fori_loop(middle + 1, size - 1, late, 0)
        ring.finish()
        pairs(size - 1, size)
        copies = [
            push(sums, landing.at[k], pair_send.at[k], pair_recv.at[k], peer)
            for k, peer in enumerate(peers)
        ]
        for copy in copies:
            copy.start()
        total = sums[...]
        for k, copy in enumerate(copies):
            copy.wait_recv()
            total = total + landing[k]
        scale = lax.rsqrt(total[0] / inner + EPS)
        pull = scale * scale * scale * (total[1] / inner)
        fill = jnp.zeros((128 - 2 * size, rows), f32)
        scale_turned = jnp.concatenate([scale, fill]).T
        pull_turned = jnp.concatenate([pull, fill]).T
        lane = lax.broadcasted_iota(jnp.int32, (rows, 128), 1)
        gain_acc[...] = jnp.zeros_like(gain_acc)

        def finish(block, carry):
            for way in range(2):
                mask = lane == block * 2 + way
                by = jnp.sum(jnp.where(mask, scale_turned, 0.0), axis=1, keepdims=True)
                less = jnp.sum(jnp.where(mask, pull_turned, 0.0), axis=1, keepdims=True)
                here = gated[block, way].astype(f32)
                values = out_grad[block, way]
                scaled = here * by
                normed_ref[block, way] = (scaled * gain_ref[0:1, :]).astype(bf16)
                grad_ref[block, way] = (values * gain_ref[0:1, :] * by - here * less).astype(bf16)
                gain_acc[0:1, :] += jnp.sum(values * scaled, axis=0, keepdims=True)
            return carry

        lax.fori_loop(0, size, finish, 0)
        for copy in copies:
            copy.wait_send()
        for copy in (first, second, third):
            copy.wait_send()


def middle(proj, tables, gain, cot, shard, inner, widths, head_size, collective_id):
    size, groups = lax.axis_size("seq"), lax.axis_size("wa")
    chunks, seqs, rows, cols = proj.shape
    lw, bc = widths
    parts = ring_parts(cot, 2)
    bf16, f32, DMA = jnp.bfloat16, jnp.float32, pltpu.SemaphoreType.DMA
    width = shard.shape[2]

    def block(*tail):
        return pl.BlockSpec((1, 1) + tail, lambda i: (lax.rem(i, chunks), i // chunks, 0, 0))

    def fixed(shape):
        return pl.BlockSpec(shape, lambda i: (0,) * len(shape))

    whole = (chunks, seqs, rows, lw)
    return pl.pallas_call(
        functools.partial(middle_kernel, widths, head_size, size, groups, inner),
        grid=(seqs * chunks,),
        in_specs=[block(rows, cols)] + [fixed(t.shape) for t in tables + (gain,)] + [ANY, ANY],
        out_specs=[
            block(rows, lw),
            block(lw, bc // 2),
            fixed(whole),
            fixed(whole),
            fixed((8, lw)),
            ANY,
            ANY,
        ],
        out_shape=[
            jax.ShapeDtypeStruct(whole, bf16),
            jax.ShapeDtypeStruct((chunks, seqs, lw, bc // 2), bf16),
            jax.ShapeDtypeStruct(whole, bf16),
            jax.ShapeDtypeStruct(whole, bf16),
            jax.ShapeDtypeStruct((8, lw), f32),
            jax.ShapeDtypeStruct((size,) + parts.shape, bf16),
            jax.ShapeDtypeStruct((groups, lw, width), bf16),
        ],
        scratch_shapes=[
            pltpu.VMEM((lw, bc // 2), f32),
            pltpu.VMEM((rows + 8, lw + bc), f32),
            pltpu.VMEM((8, lw + bc), f32),
            pltpu.VMEM(whole, bf16),
            pltpu.VMEM(whole, f32),
            pltpu.VMEM((2, 2 * chunks, rows), f32),
            pltpu.VMEM((size - 1, 2, 2 * chunks, rows), f32),
            pltpu.VMEM((2,) + parts.shape, bf16),
            pltpu.VMEM((lw, width), bf16),
            pltpu.VMEM((width, lw), bf16),
        ]
        + ring_sems(size, 2)
        + [
            DMA((size - 1,)),
            DMA((size - 1,)),
            DMA((3,)),
            DMA((3,)),
            DMA((2,)),
            DMA((2, 2)),
        ],
        compiler_params=comm_params(collective_id, 60),
        name="middle",
    )(proj, *tables, gain, parts, shard)


def reduce_kernel(
    size,
    groups,
    grad_ref,
    weight_ref,
    piece_ref,
    normed_ref,
    turned_ref,
    rows_ref,
    pieces_ref,
    main_ref,
    shared_ref,
    own_ref,
    slots,
    first,
    landing,
    parts,
    total,
    taken,
    turned,
    send_sem,
    recv_sem,
    piece_send,
    piece_recv,
    piece_local,
    part_send,
    part_recv,
    take_sem,
):
    me, group, pos, right, left = neighbours(size)
    mates = [(me, index) for index in others(group, groups)]
    greet([right, left] + mates)
    tiles, rows, tile = slots.shape[2:]
    cols = total.shape[0]
    bf16, f32 = jnp.bfloat16, jnp.float32
    ring = RingGather(size, piece_ref, pieces_ref, piece_send, piece_recv, piece_local)
    ring.start()

    def term(block, way, at):
        return dot(grad_ref[block, way], weight_ref[at], 1, 0)

    def target(step, way):
        shift = (pos - 1 - step + 2 * size) if way == 0 else (pos + 1 + step)
        return ring_index(shift % size, size)

    def hop(step, way, at, source):
        return push(
            source,
            slots.at[step, way, at],
            send_sem.at[step, way, at],
            recv_sem.at[step, way, at],
            right if way == 0 else left,
        )

    def begin(at, carry):
        for way in range(2):
            first[way, at] = term(target(0, way), way, at).astype(bf16)
            hop(0, way, at, first.at[way, at]).start()
        return carry

    lax.fori_loop(0, tiles, begin, 0)

    def send_part(offset):
        mate = (group + offset) % groups
        return push(
            parts.at[offset - 1],
            landing.at[offset - 1],
            part_send.at[offset - 1],
            part_recv.at[offset - 1],
            (me, mate),
        )

    def weight_part(offset):
        mate = (group + offset) % groups
        columns = pl.ds(pl.multiple_of(mate * tile, tile), tile)

        def take(block, slot):
            tokens = pl.ds(pl.multiple_of(block * 2 * rows, 2 * rows), 2 * rows)
            return [
                pltpu.make_async_copy(
                    normed_ref.at[block, :, :, columns], taken.at[slot], take_sem.at[slot, 0]
                ),
                pltpu.make_async_copy(
                    turned_ref.at[:, tokens], turned.at[slot], take_sem.at[slot, 1]
                ),
            ]

        for copy in take(0, 0):
            copy.start()

        def one(block, carry):
            slot = lax.rem(block, 2)

            @pl.when(block + 1 < size)
            def _():
                for copy in take(block + 1, 1 - slot):
                    copy.start()

            for copy in take(block, slot):
                copy.wait()
            values = dot(turned[slot], taken[slot].reshape(2 * rows, tile), 1, 0)

            @pl.when(block == 0)
            def _():
                total[...] = values

            @pl.when(block > 0)
            def _():
                total[...] += values

            return carry

        lax.fori_loop(0, size, one, 0)

    def advance(step, carry):
        def one(at, inner):
            for way in range(2):
                own = term(target(step, way), way, at)
                hop(step - 1, way, at, first.at[way, at]).wait_recv()
                slots[step - 1, way, at] = (slots[step - 1, way, at].astype(f32) + own).astype(bf16)
                hop(step, way, at, slots.at[step - 1, way, at]).start()
            return inner

        lax.fori_loop(0, tiles, one, 0)
        ring.advance(step)

        @pl.when(step <= groups)
        def _():
            weight_part(step)

        @pl.when(step < groups)
        def _():
            parts[step - 1] = total[...].astype(bf16)
            send_part(step).start()

        return carry

    lax.fori_loop(1, size - 1, advance, 0)
    for offset in range(1, groups):
        send_part(offset).wait_recv()
        total[...] += landing[offset - 1].astype(f32)
    at = 0
    for out_ref in (main_ref, shared_ref, own_ref):
        count = out_ref.shape[0]
        out_ref[...] = total[at : at + count].astype(bf16)
        at += count

    def end(at, carry):
        columns = pl.ds(pl.multiple_of(at * tile, tile), tile)
        for way in range(2):
            own = term(me, way, at)
            hop(size - 2, way, at, first.at[way, at]).wait_recv()
            rows_ref[way, :, columns] = slots[size - 2, way, at].astype(f32) + own
        return carry

    lax.fori_loop(0, tiles, end, 0)

    def drain(step, carry):
        def one(at, inner):
            for way in range(2):
                hop(step, way, at, first.at[way, at]).wait_send()
            return inner

        return lax.fori_loop(0, tiles, one, carry)

    lax.fori_loop(0, size - 1, drain, 0)
    ring.finish()
    for offset in range(1, groups):
        send_part(offset).wait_send()


def reduce_rows(grad, weight, piece, normed, turned, counts, collective_id):
    size, groups = lax.axis_size("seq"), lax.axis_size("wa")
    _, ways, rows, cols = grad.shape
    tile = weight.shape[2]
    tiles = groups
    pieces = ring_parts(piece, 1)
    bf16, f32, DMA = jnp.bfloat16, jnp.float32, pltpu.SemaphoreType.DMA
    return pl.pallas_call(
        functools.partial(reduce_kernel, size, groups),
        out_shape=[
            jax.ShapeDtypeStruct((ways, rows, tiles * tile), f32),
            jax.ShapeDtypeStruct((size,) + pieces.shape, bf16),
        ]
        + [jax.ShapeDtypeStruct((count, tile), bf16) for count in counts],
        in_specs=[VMEM, VMEM, ANY, ANY, ANY],
        out_specs=[VMEM, ANY] + [VMEM] * len(counts),
        scratch_shapes=[
            pltpu.VMEM((size - 1, 2, tiles, rows, tile), bf16),
            pltpu.VMEM((2, tiles, rows, tile), bf16),
            pltpu.VMEM((groups - 1, cols, tile), bf16),
            pltpu.VMEM((groups - 1, cols, tile), bf16),
            pltpu.VMEM((cols, tile), f32),
            pltpu.VMEM((2, ways, rows, tile), bf16),
            pltpu.VMEM((2, cols, 2 * rows), bf16),
            DMA((size - 1, 2, tiles)),
            DMA((size - 1, 2, tiles)),
        ]
        + ring_sems(size, 1)
        + [DMA((groups - 1,)), DMA((groups - 1,)), DMA((2, 2))],
        compiler_params=comm_params(collective_id, 62),
        name="reduce_rows",
    )(grad, weight, pieces, normed, turned)


def spread_kernel(
    size,
    groups,
    main_ref,
    pieces_ref,
    shared_ref,
    own_ref,
    small_ref,
    tokens_ref,
    weight_ref,
    gathered_ref,
    owned_ref,
    shared_out,
    small_out,
    branch_ref,
    shared_land,
    shared_sum,
    small_land,
    small_sum,
    taken,
    main_send,
    main_recv,
    main_local,
    piece_send,
    piece_recv,
    piece_local,
    pair_send,
    pair_recv,
    mate_send,
    mate_recv,
    take_sem,
):
    me, group, pos, right, left = neighbours(size)
    mates = [(me, index) for index in others(group, groups)]
    peers = [(index, group) for index in others(me, size)]
    greet(mates + peers)
    f32, bf16 = jnp.float32, jnp.bfloat16
    ring = RingGather(size, main_ref, gathered_ref, main_send, main_recv, main_local)
    owned = [
        push(pieces_ref.at[mate[1]], owned_ref.at[group], piece_send.at[k], piece_recv.at[k], mate)
        for k, mate in enumerate(mates)
    ]
    kept = pltpu.make_async_copy(pieces_ref.at[group], owned_ref.at[group], piece_local)
    small_in = [
        push(small_ref, small_land.at[k], mate_send.at[k], mate_recv.at[k], mate)
        for k, mate in enumerate(mates)
    ]
    shared_in = [
        push(
            shared_ref.at[peer[0]], shared_land.at[k], pair_send.at[0, k], pair_recv.at[0, k], peer
        )
        for k, peer in enumerate(peers)
    ]
    for copy in small_in + shared_in:
        copy.start()
    ring.start()
    kept.start()
    for copy in owned:
        copy.start()

    def take(block, slot):
        return pltpu.make_async_copy(weight_ref.at[block], taken.at[slot], take_sem.at[slot])

    take(0, 0).start()
    branch_ref[...] = jnp.zeros_like(branch_ref)

    def multiply(block, carry):
        slot = lax.rem(block, 2)

        @pl.when(block + 1 < size)
        def _():
            take(block + 1, 1 - slot).start()

        take(block, slot).wait()
        branch_ref[...] += dot(tokens_ref[block], taken[slot], 1, 0)
        return carry

    count = size - 2

    def advance(step, carry):
        ring.advance(step)
        lax.fori_loop(((step - 1) * size) // count, (step * size) // count, multiply, 0)
        return carry

    lax.fori_loop(1, 2, advance, 0)
    total = small_ref[...]
    for k, copy in enumerate(small_in):
        copy.wait_recv()
        total = total + small_land[k]
    small_sum[...] = total
    small_out[pl.ds(me, 1)] = total[None]
    total = shared_ref[me].astype(f32)
    for k, copy in enumerate(shared_in):
        copy.wait_recv()
        total = total + shared_land[k].astype(f32)
    shared_rows = total.shape[0]
    shared_sum[:shared_rows] = total.astype(bf16)
    shared_sum[shared_rows:] = own_ref[...]
    shared_out[pl.ds(me, 1)] = shared_sum[...][None]
    second = []
    for k, peer in enumerate(peers):
        second.append(
            push(small_sum, small_out.at[me], pair_send.at[1, k], pair_recv.at[1, k], peer)
        )
        second.append(
            push(shared_sum, shared_out.at[me], pair_send.at[2, k], pair_recv.at[2, k], peer)
        )
    for copy in second:
        copy.start()
    lax.fori_loop(2, size - 1, advance, 0)
    ring.finish()
    for copy in small_in + shared_in:
        copy.wait_send()
    for copy in second + owned:
        copy.wait()
    kept.wait()


def spread_grads(main, pieces, shared, own, small, tokens, weight, collective_id):
    size, groups = lax.axis_size("seq"), lax.axis_size("wa")
    parts = ring_parts(main, 2)
    bf16, f32 = jnp.bfloat16, jnp.float32
    DMA = pltpu.SemaphoreType.DMA
    both = (shared.shape[1] + own.shape[0], shared.shape[2])
    return pl.pallas_call(
        functools.partial(spread_kernel, size, groups),
        out_shape=[
            jax.ShapeDtypeStruct((size,) + parts.shape, bf16),
            jax.ShapeDtypeStruct(pieces.shape, bf16),
            jax.ShapeDtypeStruct((size,) + both, bf16),
            jax.ShapeDtypeStruct((size,) + small.shape, f32),
            jax.ShapeDtypeStruct((tokens.shape[1], weight.shape[2]), f32),
        ],
        in_specs=[ANY, ANY, VMEM, VMEM, VMEM, VMEM, ANY],
        out_specs=[ANY, ANY, VMEM, VMEM, VMEM],
        scratch_shapes=[
            pltpu.VMEM((size - 1,) + shared.shape[1:], bf16),
            pltpu.VMEM(both, bf16),
            pltpu.VMEM((groups - 1,) + small.shape, f32),
            pltpu.VMEM(small.shape, f32),
            pltpu.VMEM((2,) + weight.shape[1:], bf16),
        ]
        + ring_sems(size, 2)
        + [
            DMA((groups - 1,)),
            DMA((groups - 1,)),
            DMA,
            DMA((3, size - 1)),
            DMA((3, size - 1)),
            DMA((groups - 1,)),
            DMA((groups - 1,)),
            DMA((2,)),
        ],
        compiler_params=comm_params(collective_id, 60),
        name="spread_grads",
    )(parts, pieces, shared, own, small, tokens, weight)


def assemble_kernel(blocks, gathered_ref, tail_ref, o_ref):
    @pl.when(pl.program_id(0) < blocks)
    def _():
        o_ref[...] = gathered_ref[0, 0].reshape(o_ref.shape).astype(jnp.float32)

    @pl.when(pl.program_id(0) == blocks)
    def _():
        o_ref[...] = tail_ref[...].astype(jnp.float32)


def assemble_in(gathered, tail):
    size, ways, chunks, rows, width = gathered.shape
    step = chunks * rows
    blocks = size * ways
    total = blocks * step + tail.shape[0]
    steps = blocks + 1
    pad = -tail.shape[0] % step
    if tail.shape[0] > step:
        out = jnp.swapaxes(gathered, 0, 1).reshape(blocks * step, width)
        return jnp.concatenate([out, tail]).astype(jnp.float32)
    return pl.pallas_call(
        functools.partial(assemble_kernel, blocks),
        grid=(steps,),
        in_specs=[
            pl.BlockSpec(
                (1, 1, chunks, rows, width),
                lambda i: (lax.rem(i, size), jnp.minimum(i // size, ways - 1), 0, 0, 0),
            ),
            pl.BlockSpec((step, width), lambda i: (0, 0)),
        ],
        out_specs=pl.BlockSpec((step, width), lambda i: (i, 0)),
        out_shape=jax.ShapeDtypeStruct((total, width), jnp.float32),
        compiler_params=pltpu.CompilerParams(vmem_limit_bytes=32 * 2**20),
        name="assemble_in",
    )(gathered, jnp.pad(tail, ((0, pad), (0, 0))))


def widen_kernel(x_ref, o_ref):
    o_ref[...] = x_ref[0, 0].astype(jnp.float32)


def assemble_out(owned):
    groups, count, rows, width = owned.shape
    return pl.pallas_call(
        widen_kernel,
        grid=(count, groups),
        in_specs=[pl.BlockSpec((1, 1, rows, width), lambda t, g: (g, t, 0, 0))],
        out_specs=pl.BlockSpec((rows, width), lambda t, g: (t * groups + g, 0)),
        out_shape=jax.ShapeDtypeStruct((groups * count * rows, width), jnp.float32),
        name="assemble_out",
    )(owned)


def body(
    tokens,
    lengths,
    norm_gain,
    in_weight,
    conv_weight,
    conv_bias,
    dt_bias,
    a_log,
    skip_gain,
    out_gain,
    out_weight,
    cotangent,
):
    seqs_here, slot_rows, width = tokens.shape
    row_count = seqs_here * slot_rows
    inner_width = out_gain.shape[0]
    channels = conv_bias.shape[0]
    bc_width = channels - inner_width
    state_size = bc_width // 2
    head_count = dt_bias.shape[0]
    head_size = inner_width // head_count
    seq_devices = lax.axis_size("seq")
    group_devices = lax.axis_size("wa")
    seq_index = lax.axis_index("seq")
    length = seq_devices * slot_rows
    local_heads = head_count // seq_devices
    local_width = local_heads * head_size
    channel_start = seq_index * local_width
    head_start = seq_index * local_heads
    bf16, f32 = jnp.bfloat16, jnp.float32

    def take(array, start, size, axis):
        return lax.dynamic_slice_in_dim(array, start, size, axis)

    positions = seq_index * slot_rows + jnp.arange(slot_rows)
    valid_rows = (positions[None, :] < lengths[:, None]).astype(f32).reshape(row_count, 1)
    flat_tokens = tokens.reshape(row_count, width).astype(f32)
    in_scale = row_scale(flat_tokens)
    normed = (flat_tokens * in_scale * norm_gain).astype(bf16)
    cot_rows = cotangent.reshape(row_count, width)

    in_turned = in_weight.T
    local_columns = jnp.concatenate(
        [
            take(in_turned, channel_start, local_width, 0),
            take(in_turned, inner_width + channel_start, local_width, 0),
            in_turned[2 * inner_width : 2 * inner_width + bc_width],
            take(in_turned, 2 * inner_width + bc_width + head_start, local_heads, 0),
            jnp.zeros((128 - local_heads, in_weight.shape[0]), bf16),
        ]
    )
    columns_here = local_columns.shape[0]
    blocks = (seq_devices, seqs_here, slot_rows)
    normed_all, in_columns, projected = project(normed, local_columns, 0)

    def lanes(part):
        return jnp.pad(part[None], ((0, 7), (0, 128 - local_heads)))

    taps = jnp.pad(
        jnp.concatenate(
            [take(conv_weight, channel_start, local_width, 1), conv_weight[:, inner_width:]], axis=1
        ),
        ((0, 8 - KW), (0, 0)),
    )
    shift = jnp.concatenate(
        [take(conv_bias, channel_start, local_width, 0), conv_bias[inner_width:]]
    )[None]
    bias = lanes(take(dt_bias, head_start, local_heads, 0))
    slope = lanes(-jnp.exp(take(a_log, head_start, local_heads, 0)))
    skip = jnp.repeat(take(skip_gain, head_start, local_heads, 0), head_size)[None]
    gain_local = take(out_gain, channel_start, local_width, 0)
    spread, fold, tri, upper = scan_tables(slot_rows, local_width, head_size)
    widths = (local_width, bc_width)
    per_owner = seq_devices // group_devices
    y_heads, entering, normed_out, gated_grad, gain_sum, branch_grad, out_part = middle(
        projected,
        (taps, shift, bias, slope, skip, spread, tri),
        gain_local[None],
        cot_rows * valid_rows.astype(bf16),
        out_weight.reshape(per_owner, local_width, width),
        inner_width,
        widths,
        head_size,
        1,
    )
    normed_out = normed_out.reshape(-1, local_width)
    branch_grad = branch_grad.reshape(-1, width)
    out_gain_part = gain_sum[0]
    out_full = lax.all_gather(
        lax.optimization_barrier((out_weight, gain_sum))[0], "wa", axis=0, tiled=True
    )

    swapped = lax.all_to_all(
        normed_out.reshape(seq_devices, row_count, local_width), "seq", 0, 0, tiled=True
    )
    out_weight_part = lax.psum_scatter(
        lax.dot_general(
            normed_out, branch_grad, (((0,), (0,)), ((), ())), preferred_element_type=f32
        ).astype(bf16),
        "wa",
        scatter_dimension=0,
        tiled=True,
    )
    proj_grad, turned_grad, taps_sum, skip_sum, head_sum = scan_backward(
        projected,
        y_heads,
        entering,
        gated_grad,
        taps,
        shift,
        bias,
        slope,
        skip,
        spread,
        fold,
        tri,
        upper,
        widths,
        head_size,
    )
    proj_grad = proj_grad.reshape(-1, columns_here)
    conv_w_grad, conv_b_grad = taps_sum[:KW], taps_sum[KW]
    skip_grad = jnp.sum(skip_sum[0].reshape(local_heads, head_size), axis=1)
    shift_grad, rates_grad = head_sum[0, :local_heads], head_sum[1, :local_heads]
    in_rows = in_weight.shape[0]
    at_shared = 2 * local_width
    normed_grad, pieces, main_part, shared_part, own_part = reduce_rows(
        proj_grad.reshape(blocks + (columns_here,)),
        in_columns,
        out_weight_part,
        normed_all.reshape(blocks + (width,)),
        turned_grad,
        (at_shared, bc_width, 16),
        3,
    )
    normed_grad = normed_grad.reshape(row_count, width)
    token_grad, norm_gain_grad = norm_backward(flat_tokens, in_scale, norm_gain, normed_grad)
    token_grad = token_grad + cot_rows.astype(f32)

    shared_rows = bc_width // seq_devices
    heads = jnp.stack(
        [
            jnp.pad(part, (0, 128 - local_heads))
            for part in (shift_grad, rates_grad, skip_grad)
        ]
    )
    own_parts = [conv_w_grad[:, :local_width], conv_b_grad[:local_width], out_gain_part, heads]
    sum_parts = [conv_w_grad[:, local_width:], conv_b_grad[local_width:], norm_gain_grad]
    packed = jnp.concatenate([part.reshape(-1, 128) for part in own_parts + sum_parts])
    packed_rows = packed.shape[0]
    packed = jnp.pad(packed, ((0, -packed_rows % 8), (0, 0)))
    gathered, owned, shared_all, small_all, branch = spread_grads(
        main_part,
        pieces.reshape(group_devices, per_owner, local_width // group_devices, width),
        shared_part.reshape(seq_devices, shared_rows, in_rows),
        own_part,
        packed,
        swapped,
        out_full.reshape(seq_devices, local_width, width),
        4,
    )
    mixed_out = (flat_tokens + valid_rows * branch).astype(bf16).reshape(tokens.shape)
    tail = jnp.concatenate(
        [
            shared_all[:, :shared_rows].reshape(bc_width, in_rows),
            shared_all[:, shared_rows : shared_rows + local_heads].reshape(head_count, in_rows),
        ]
    )
    in_weight_grad = assemble_in(gathered, tail).T
    out_weight_grad = assemble_out(owned)

    tile_rows = local_width // 128
    own_rows = (KW + 2) * tile_rows
    own_all = small_all[:, :own_rows].reshape(seq_devices, KW + 2, local_width)
    own_all = jnp.swapaxes(own_all, 0, 1).reshape(KW + 2, inner_width)
    head_all = jnp.swapaxes(small_all[:, own_rows : own_rows + 3, :local_heads], 0, 1)
    head_all = head_all.reshape(3, head_count)
    summed = jnp.sum(small_all[:, own_rows + 3 : packed_rows], axis=0).reshape(-1)
    conv_weight_grad = jnp.concatenate(
        [own_all[:KW], summed[: KW * bc_width].reshape(KW, bc_width)], axis=1
    )
    conv_bias_grad = jnp.concatenate(
        [own_all[KW], summed[KW * bc_width : (KW + 1) * bc_width]]
    )
    norm_gain_total = summed[(KW + 1) * bc_width :]
    return (
        mixed_out,
        token_grad.reshape(tokens.shape),
        norm_gain_total,
        in_weight_grad,
        conv_weight_grad,
        conv_bias_grad,
        head_all[0],
        head_all[1],
        head_all[2],
        own_all[KW + 1],
        out_weight_grad,
    )


def solution(mesh):
    placed = (
        P("wa", "seq", None),
        P("wa"),
        P(),
        P("wa", None),
        P(),
        P(),
        P(),
        P(),
        P(),
        P(),
        P("wa", None),
        P("wa", "seq", None),
    )
    return jax.shard_map(
        body,
        mesh=mesh,
        in_specs=placed,
        out_specs=(
            P("wa", "seq", None),
            P("wa", "seq", None),
            P(),
            P("wa", None),
            P(),
            P(),
            P(),
            P(),
            P(),
            P(),
            P("wa", None),
        ),
        check_vma=False,
    )
```

```python
import functools

import jax
import jax.numpy as jnp
from jax import lax
from jax.experimental import pallas as pl
from jax.experimental.pallas import tpu as pltpu
from jax.sharding import PartitionSpec as P

KW = 4
EPS = 1e-05
HIGHEST = lax.Precision.HIGHEST
MESH = pl.DeviceIdType.MESH


def row_scale(values):
    return lax.rsqrt(jnp.mean(values * values, axis=-1, keepdims=True) + EPS)


def norm_backward(values, row_scales, gain_vec, grad_out):
    weighted = grad_out * gain_vec
    return row_scales * weighted - values * row_scales**3 * jnp.mean(
        weighted * values, axis=-1, keepdims=True
    )


def dot(a, b, ca, cb, precision=None):
    return lax.dot_general(
        a, b, (((ca,), (cb,)), ((), ())), precision=precision, preferred_element_type=jnp.float32
    )


def chunk_front(proj_ref, ext, taps_ref, shift_ref, bias_ref, slope_ref, tri_ref, widths):
    lw, bc = widths
    rows = proj_ref.shape[2]
    ext[8:, :] = proj_ref[0, 0, :, lw : 2 * lw + bc].astype(jnp.float32)
    conv = shift_ref[0:1, :]
    for k in range(KW):
        conv = conv + taps_ref[k : k + 1, :] * ext[5 + k : 5 + k + rows, :]
    conv_sig = lax.logistic(conv)
    act = conv * conv_sig
    step_in = proj_ref[0, 0, :, 2 * lw + bc :].astype(jnp.float32) + bias_ref[0:1, :]
    steps = jnp.maximum(step_in, 0.0) + jnp.log1p(jnp.exp(-jnp.abs(step_in)))
    rates = slope_ref[0:1, :] * steps
    cum = dot(tri_ref[...], rates, 1, 0, HIGHEST)
    return conv, conv_sig, act, step_in, steps, rates, cum


def head_masks(rows, head_size):
    lane = lax.broadcasted_iota(jnp.int32, (rows, 128), 1)
    row = lax.broadcasted_iota(jnp.int32, (rows, rows), 0)
    col = lax.broadcasted_iota(jnp.int32, (rows, rows), 1)
    return lane, row >= col


def forward_chunk(
    widths,
    head_size,
    start,
    proj_ref,
    taps_ref,
    shift_ref,
    bias_ref,
    slope_ref,
    skip_ref,
    spread_ref,
    tri_ref,
    gated_ref,
    y_ref,
    enter_ref,
    state,
    ext,
    halo,
):
    lw, bc = widths
    bf16, f32 = jnp.bfloat16, jnp.float32
    rows = proj_ref.shape[2]
    per_tile = 128 // head_size

    @pl.when(start)
    def _():
        state[...] = jnp.zeros_like(state)
        halo[...] = jnp.zeros_like(halo)

    ext[0:8, :] = halo[...]
    _, _, act, _, steps, _, cum = chunk_front(
        proj_ref, ext, taps_ref, shift_ref, bias_ref, slope_ref, tri_ref, widths
    )
    halo[...] = ext[rows : rows + 8, :]
    x = act[:, :lw]
    xb = x.astype(bf16)
    b_rows = act[:, lw : lw + bc // 2].astype(bf16)
    c_rows = act[:, lw + bc // 2 :].astype(bf16)
    cum_t, steps_t = cum.T, steps.T
    last = cum[rows - 1 : rows, :]
    grow = dot(jnp.exp(cum).astype(bf16), spread_ref[...], 1, 0)
    tail = dot((jnp.exp(last - cum) * steps).astype(bf16), spread_ref[...], 1, 0)
    scores = dot(c_rows, b_rows, 1, 1)
    entering = state[...].astype(bf16)
    enter_ref[0, 0] = entering
    y = dot(c_rows, entering, 1, 1) * grow + skip_ref[0:1, :] * x
    added = dot((x * tail).astype(bf16), b_rows, 0, 0)
    lane, causal = head_masks(rows, head_size)
    gate = proj_ref[0, 0, :, :lw].astype(f32)
    silu_gate = gate * lax.logistic(gate)
    for tile in range(lw // 128):
        cols = slice(tile * 128, (tile + 1) * 128)
        inner = None
        for sub in range(per_tile):
            head = tile * per_tile + sub
            log_decay = cum[:, head : head + 1] - cum_t[head : head + 1, :]
            decay = jnp.exp(jnp.where(causal, log_decay, -1e30))
            weights = (scores * decay * steps_t[head : head + 1, :]).astype(bf16)
            part = dot(weights, xb[:, cols], 1, 0)
            inner = part if inner is None else jnp.where(lane >= sub * head_size, part, inner)
            span = slice(head * head_size, (head + 1) * head_size)
            state[span, :] = (
                jnp.exp(cum[rows - 1 : rows, head : head + 1]) * state[span, :] + added[span, :]
            )
        y_tile = y[:, cols] + inner
        y_ref[0, 0, :, cols] = y_tile.astype(bf16)
        gated_ref[:, cols] = (y_tile * silu_gate[:, cols]).astype(bf16)


def backward_kernel(
    widths,
    head_size,
    chunks,
    proj_ref,
    before_ref,
    y_ref,
    enter_ref,
    grad_ref,
    taps_ref,
    shift_ref,
    bias_ref,
    slope_ref,
    skip_ref,
    spread_ref,
    fold_ref,
    tri_ref,
    upper_ref,
    out_ref,
    turned_ref,
    taps_acc,
    skip_acc,
    head_acc,
    lam,
    ext,
    later,
    after,
):
    lw, bc = widths
    state_size = bc // 2
    bf16, f32 = jnp.bfloat16, jnp.float32
    rows = proj_ref.shape[2]
    per_tile = 128 // head_size
    chunk = chunks - 1 - pl.program_id(1)

    @pl.when((pl.program_id(0) == 0) & (pl.program_id(1) == 0))
    def _():
        taps_acc[...] = jnp.zeros_like(taps_acc)
        skip_acc[...] = jnp.zeros_like(skip_acc)
        head_acc[...] = jnp.zeros_like(head_acc)

    @pl.when(pl.program_id(1) == 0)
    def _():
        lam[...] = jnp.zeros_like(lam)
        after[...] = jnp.zeros_like(after)

    ext[0:8, :] = jnp.where(
        chunk > 0, before_ref[0, 0, 8:16, lw : 2 * lw + bc].astype(f32), 0.0
    )
    conv, conv_sig, act, step_in, steps, rates, cum = chunk_front(
        proj_ref, ext, taps_ref, shift_ref, bias_ref, slope_ref, tri_ref, widths
    )
    x = act[:, :lw]
    xb = x.astype(bf16)
    b_rows = act[:, lw : lw + state_size].astype(bf16)
    c_rows = act[:, lw + state_size :].astype(bf16)
    cum_t, steps_t = cum.T, steps.T
    last = cum[rows - 1 : rows, :]
    to_end = jnp.exp(last - cum)
    tail_heads = to_end * steps
    grow = dot(jnp.exp(cum).astype(bf16), spread_ref[...], 1, 0)
    tail = dot(tail_heads.astype(bf16), spread_ref[...], 1, 0)
    scores = dot(c_rows, b_rows, 1, 1)

    gate = proj_ref[0, 0, :, :lw].astype(f32)
    gate_sig = lax.logistic(gate)
    grad = grad_ref[0, 0].astype(f32)
    y_grad = grad * gate * gate_sig
    out_ref[0, 0, :, :lw] = (
        grad * y_ref[0, 0].astype(f32) * (gate_sig * (1.0 + gate * (1.0 - gate_sig)))
    ).astype(bf16)
    yb = y_grad.astype(bf16)

    entering = enter_ref[0, 0]
    grown = y_grad * grow
    grown_b = grown.astype(bf16)
    c_grad = dot(grown_b, entering, 1, 0)
    carried = dot((grown * dot(c_rows, entering, 1, 1)).astype(bf16), fold_ref[...], 1, 0)
    lam_now = lam[...]
    lam_b = lam_now.astype(bf16)
    from_lam = dot(b_rows, lam_b, 1, 1)
    b_grad = dot((x * tail).astype(bf16), lam_b, 1, 0)
    x_lam = dot((x * from_lam).astype(bf16), fold_ref[...], 1, 0)
    x_grad = skip_ref[0:1, :] * y_grad + tail * from_lam
    skip_acc[0:1, :] += jnp.sum(y_grad * x, axis=0, keepdims=True)
    ones = jnp.ones((8, state_size), bf16)
    kept = dot(
        dot(ones, (lam_now * entering.astype(f32)).astype(bf16), 1, 1),
        fold_ref[...].astype(f32),
        1,
        0,
        HIGHEST,
    )
    through = jnp.exp(last) * kept[0:1, :]
    lam_add = dot(grown_b, c_rows, 0, 0)

    lane, causal = head_masks(rows, head_size)
    score_grad = None
    row_sums = jnp.zeros((rows, 128), f32)
    col_sums = []
    x_tiles = []
    for tile in range(lw // 128):
        cols = slice(tile * 128, (tile + 1) * 128)
        inner = None
        for sub in range(per_tile):
            head = tile * per_tile + sub
            log_decay = cum[:, head : head + 1] - cum_t[head : head + 1, :]
            decay = jnp.exp(jnp.where(causal, log_decay, -1e30))
            step_row = steps_t[head : head + 1, :]
            weights = (scores * decay * step_row).astype(bf16)
            inside = (lane >= sub * head_size) & (lane < (sub + 1) * head_size)
            y_head = jnp.where(inside, yb[:, cols], jnp.zeros_like(yb[:, cols]))
            weights_grad = dot(y_head, xb[:, cols], 1, 1)
            part = dot(weights, yb[:, cols], 0, 0)
            inner = part if inner is None else jnp.where(lane >= sub * head_size, part, inner)
            decayed = weights_grad * decay
            stepped = decayed * step_row
            score_grad = stepped if score_grad is None else score_grad + stepped
            col_sums.append(jnp.sum(decayed * scores, axis=0, keepdims=True))
            row_sum = jnp.sum(stepped * scores, axis=1, keepdims=True)
            row_sums = row_sums + jnp.where(lane == head, row_sum, 0.0)
            span = slice(head * head_size, (head + 1) * head_size)
            lam[span, :] = (
                jnp.exp(cum[rows - 1 : rows, head : head + 1]) * lam_now[span, :] + lam_add[span, :]
            )
        x_tiles.append(x_grad[:, cols] + inner)
    col_sums.append(jnp.zeros((rows - len(col_sums), rows), f32))
    col_sum = jnp.concatenate(col_sums, axis=0).T
    source = row_sums - steps * col_sum + carried
    rates_grad = (
        dot(upper_ref[...], source, 1, 0, HIGHEST)
        + dot(1.0 - upper_ref[...], tail_heads * x_lam, 1, 0, HIGHEST)
        + through
    )
    steps_grad = col_sum + to_end * x_lam + rates_grad * slope_ref[0:1, :]
    raw_grad = steps_grad * lax.logistic(step_in)
    out_ref[0, 0, :, 2 * lw + bc :] = raw_grad.astype(bf16)
    head_acc[0:1, :] += jnp.sum(raw_grad, axis=0, keepdims=True)
    head_acc[1:2, :] += jnp.sum(rates_grad * rates, axis=0, keepdims=True)
    score_b = score_grad.astype(bf16)
    c_grad = c_grad + dot(score_b, b_rows, 1, 0)
    b_grad = b_grad + dot(score_b, c_rows, 0, 0)
    act_grad = jnp.concatenate(x_tiles + [b_grad, c_grad], axis=1)
    conv_grad = act_grad * (conv_sig * (1.0 + conv * (1.0 - conv_sig)))
    later[0:rows, :] = conv_grad
    later[rows : rows + 8, :] = after[...]
    after[...] = conv_grad[0:8, :]
    total = None
    for k in range(KW):
        term = taps_ref[k : k + 1, :] * later[3 - k : 3 - k + rows, :]
        total = term if total is None else total + term
        taps_acc[k : k + 1, :] += jnp.sum(conv_grad * ext[5 + k : 5 + k + rows, :], axis=0, keepdims=True)
    taps_acc[KW : KW + 1, :] += jnp.sum(conv_grad, axis=0, keepdims=True)

    @pl.when((pl.program_id(0) == pl.num_programs(0) - 1) & (chunk == 0))
    def _():
        head_acc[2:3, :] = dot(
            skip_acc[...], fold_ref[...].astype(f32), 1, 0, HIGHEST
        )[0:1, :]
    out_ref[0, 0, :, lw : 2 * lw + bc] = total.astype(bf16)
    turned_ref[...] = out_ref[0, 0].T


def whole_spec(array):
    return pl.BlockSpec(array.shape, lambda q, c: (0,) * array.ndim)


def scan_tables(rows, local_width, head_size):
    head_of = jnp.arange(local_width) // head_size
    spread = (jnp.arange(128)[:, None] == head_of[None, :]).astype(jnp.bfloat16)
    tri = (jnp.arange(rows)[:, None] >= jnp.arange(rows)[None, :]).astype(jnp.float32)
    return spread, spread.T, tri, tri.T


def scan_backward(
    proj, y, enter, grad, taps, shift, bias, slope, skip, spread, fold, tri, upper, widths, head_size
):
    chunks, seqs, rows, cols = proj.shape
    lw, bc = widths
    block = lambda *tail: pl.BlockSpec((1, 1) + tail, lambda q, c: (chunks - 1 - c, q, 0, 0))
    before = pl.BlockSpec(
        (1, 1, 16, cols),
        lambda q, c: (jnp.maximum(chunks - 2 - c, 0), q, rows // 16 - 1, 0),
    )
    tables = (taps, shift, bias, slope, skip, spread, fold, tri, upper)
    sums = [(8, lw + bc), (8, lw), (8, 128)]
    return pl.pallas_call(
        functools.partial(backward_kernel, widths, head_size, chunks),
        grid=(seqs, chunks),
        in_specs=[block(rows, cols), before, block(rows, lw), block(lw, bc // 2), block(rows, lw)]
        + [whole_spec(t) for t in tables],
        out_specs=[
            block(rows, cols),
            pl.BlockSpec((cols, rows), lambda q, c: (0, (chunks - 1 - c) * seqs + q)),
        ]
        + [pl.BlockSpec(s, lambda q, c: (0, 0)) for s in sums],
        out_shape=[
            jax.ShapeDtypeStruct(proj.shape, jnp.bfloat16),
            jax.ShapeDtypeStruct((cols, chunks * seqs * rows), jnp.bfloat16),
        ]
        + [jax.ShapeDtypeStruct(s, jnp.float32) for s in sums],
        scratch_shapes=[
            pltpu.VMEM((lw, bc // 2), jnp.float32),
            pltpu.VMEM((rows + 8, lw + bc), jnp.float32),
            pltpu.VMEM((rows + 8, lw + bc), jnp.float32),
            pltpu.VMEM((8, lw + bc), jnp.float32),
        ],
        compiler_params=pltpu.CompilerParams(vmem_limit_bytes=48 * 2**20),
        name="scan_backward",
    )(proj, proj, y, enter, grad, *tables)


def ring_pos(index, size):
    row, side = index // 2, index % 2
    return row + side * (size - 1 - 2 * row)


def ring_index(pos, size):
    side = pos // (size // 2)
    row = pos + side * (size - 1 - 2 * pos)
    return row * 2 + side


def greet(peers):
    barrier = pltpu.get_barrier_semaphore()
    for peer in peers:
        pl.semaphore_signal(barrier, inc=1, device_id=peer, device_id_type=MESH)
    pl.semaphore_wait(barrier, len(peers))


def push(source, target, send_sem, recv_sem, peer):
    return pltpu.make_async_remote_copy(
        source, target, send_sem, recv_sem, device_id=peer, device_id_type=MESH
    )


def neighbours(size):
    me, group = lax.axis_index("seq"), lax.axis_index("wa")
    pos = ring_pos(me, size)
    right = (ring_index((pos + 1) % size, size), group)
    left = (ring_index((pos + size - 1) % size, size), group)
    return me, group, pos, right, left


def others(index, size):
    return [(index + offset) % size for offset in range(1, size)]


ANY = pl.BlockSpec(memory_space=pl.ANY)
VMEM = pl.BlockSpec(memory_space=pltpu.VMEM)


def comm_params(collective_id, megabytes=None):
    limit = None if megabytes is None else megabytes * 2**20
    return pltpu.CompilerParams(
        collective_id=collective_id, has_side_effects=True, vmem_limit_bytes=limit
    )


class RingGather:
    def __init__(self, size, x_ref, o_ref, send_sem, recv_sem, local_sem):
        self.size, self.x, self.o = size, x_ref, o_ref
        self.send, self.recv, self.local = send_sem, recv_sem, local_sem
        self.chunks = x_ref.shape[1]
        self.me, _, self.pos, self.right, self.left = neighbours(size)

    def copy(self, step, chunk, way, first=False):
        size = self.size
        if way == 0:
            block, peer = ring_index((self.pos - step + size) % size, size), self.right
        else:
            block, peer = ring_index((self.pos + step) % size, size), self.left
        source = self.x.at[way, chunk] if first else self.o.at[block, way, chunk]
        return push(
            source,
            self.o.at[block, way, chunk],
            self.send.at[step, chunk, way],
            self.recv.at[step, chunk, way],
            peer,
        )

    def kept(self):
        return pltpu.make_async_copy(self.x, self.o.at[self.me], self.local)

    def start(self):
        self.kept().start()
        for chunk in range(self.chunks):
            for way in range(2):
                self.copy(0, chunk, way, True).start()

    def advance(self, step):
        for chunk in range(self.chunks):
            for way in range(2):
                self.copy(step - 1, chunk, way).wait_recv()
                self.copy(step, chunk, way).start()

    def arrive(self):
        last = self.size - 2
        for chunk in range(self.chunks):
            for way in range(2):
                self.copy(last, chunk, way).wait_recv()

    def finish(self):
        self.arrive()
        self.settle()

    def settle(self):
        def drain(step, carry):
            for chunk in range(self.chunks):
                for way in range(2):
                    self.copy(step, chunk, way).wait_send()
            return carry

        lax.fori_loop(0, self.size - 1, drain, 0)
        self.kept().wait()


def ring_parts(x, chunks):
    return x.reshape(2, chunks, x.shape[0] // (2 * chunks), x.shape[1])


def ring_sems(size, chunks):
    return [
        pltpu.SemaphoreType.DMA((size - 1, chunks, 2)),
        pltpu.SemaphoreType.DMA((size - 1, chunks, 2)),
        pltpu.SemaphoreType.DMA,
    ]


def front_kernel(
    widths,
    head_size,
    size,
    groups,
    inner,
    x_ref,
    w_ref,
    cot_ref,
    shard_ref,
    taps_ref,
    shift_ref,
    bias_ref,
    slope_ref,
    skip_ref,
    spread_ref,
    tri_ref,
    gain_ref,
    rows_ref,
    weights_ref,
    proj_ref,
    y_ref,
    enter_ref,
    normed_ref,
    turned_ref,
    grad_ref,
    gain_acc,
    branch_ref,
    part_ref,
    weights,
    projected,
    taken,
    state,
    ext,
    halo,
    gated,
    out_grad,
    y_held,
    enter_held,
    out_rows,
    out_turned,
    sums,
    landing,
    weight_send,
    weight_recv,
    weight_local,
    take_sem,
    proj_sem,
    held_sem,
    shard_send,
    shard_recv,
    shard_local,
    pair_send,
    pair_recv,
    *ring_refs,
):
    bf16, f32 = jnp.bfloat16, jnp.float32
    me, group, pos, right, left = neighbours(size)
    rows, lw = gated.shape[2:]
    depth = weights.shape[2]
    peers = [(other, group) for other in others(me, size)]
    mates = [(me, other) for other in others(group, groups)]
    sibling = (me, group + 1 - 2 * lax.rem(group, 2))
    across = (me, lax.rem(group + 2, groups))
    per_owner = size // groups
    chosen = lax.rem(me, per_owner)
    owner = me // per_owner
    greet(mates + peers)
    ring = RingGather(size, x_ref, rows_ref, *ring_refs[0:3])
    cot_ring = RingGather(size, cot_ref, branch_ref, *ring_refs[3:6])
    ring.start()
    sent = [
        push(w_ref, weights.at[group], weight_send.at[k], weight_recv.at[k], mate)
        for k, mate in enumerate(mates)
    ]
    for copy in sent:
        copy.start()
    kept = pltpu.make_async_copy(w_ref, weights.at[group], weight_local.at[0])
    kept.start()

    def shards(step, offset=0):
        at = lax.rem(chosen + offset, per_owner)
        held_by = across[1] if step == 2 else group
        source = part_ref.at[held_by, at] if step == 2 else shard_ref.at[at]
        return push(
            source,
            part_ref.at[held_by, at],
            shard_send.at[step, offset],
            shard_recv.at[step, offset],
            across if step == 0 else sibling,
        )

    def block_of(pair, way):
        return ring_index((pos - pair + size) % size if way == 0 else (pos + pair) % size, size)

    def stream(source_ref, landed_ref, low, high, compute, own=False):
        def take(pair, slot, way):
            source = source_ref.at[way] if own else landed_ref.at[block_of(pair, way), way]
            return pltpu.make_async_copy(source, taken.at[slot, way], take_sem.at[slot, way])

        for way in range(2):
            take(low, lax.rem(low, 2), way).start()

        def one(pair, carry):
            slot = lax.rem(pair, 2)
            for way in range(2):
                take(pair, slot, way).wait()

            @pl.when(pair + 1 < high)
            def _():
                for way in range(2):
                    take(pair + 1, 1 - slot, way).start()

            compute(pair, slot)
            return carry

        lax.fori_loop(low, high, one, 0)

    def put(pair, way):
        block = block_of(pair, way)
        return pltpu.make_async_copy(
            projected.at[block, way], proj_ref.at[block, way], proj_sem.at[pair, way]
        )

    def project(pair, slot):
        for way in range(2):
            x = taken[slot, way].reshape(rows, taken.shape[4])
            total = None
            for part in range(groups):
                term = dot(x[:, part * depth : (part + 1) * depth], weights[part], 1, 1)
                total = term if total is None else total + term
            projected[block_of(pair, way), way] = total.astype(bf16)
            put(pair, way).start()

    def advance(step, carry):
        ring.advance(step)
        return carry

    def turns(turn, count):
        return 1 + (turn * (size - 2)) // count, 1 + ((turn + 1) * (size - 2)) // count

    middle = size // 2 + 1
    lax.fori_loop(1, middle, advance, 0)
    kept.wait()
    for copy in sent:
        copy.wait_recv()
    flushed = pltpu.make_async_copy(weights, weights_ref, weight_local.at[1])
    flushed.start()
    shards(0).start()
    shards(1).start()
    stream(x_ref, rows_ref, 0, 1, project, own=True)

    def late(step, carry):
        ring.advance(step)
        stream(x_ref, rows_ref, *turns(step - middle, size - 1 - middle), project)
        return carry

    lax.fori_loop(middle, size - 2, late, 0)
    ring.advance(size - 2)
    cot_ring.start()
    stream(x_ref, rows_ref, *turns(size - 2 - middle, size - 1 - middle), project)
    ring.arrive()
    stream(x_ref, rows_ref, size - 1, size, project)
    cot_ring.advance(1)

    def keep(index, slot):
        seq, chunk = index // size, lax.rem(index, size)
        return [
            pltpu.make_async_copy(y_held.at[slot, 0], y_ref.at[chunk, seq], held_sem.at[slot, 0]),
            pltpu.make_async_copy(
                enter_held.at[slot, 0], enter_ref.at[chunk, seq], held_sem.at[slot, 1]
            ),
        ]

    def scan(index, carry):
        seq, chunk = index // size, lax.rem(index, size)
        slot = lax.rem(index, 2)

        @pl.when(index >= 2)
        def _():
            for copy in keep(index - 2, slot):
                copy.wait()

        forward_chunk(
            widths,
            head_size,
            chunk == 0,
            projected.at[pl.ds(chunk, 1), pl.ds(seq, 1)],
            taps_ref,
            shift_ref,
            bias_ref,
            slope_ref,
            skip_ref,
            spread_ref,
            tri_ref,
            gated.at[chunk, seq],
            y_held.at[pl.ds(slot, 1)],
            enter_held.at[pl.ds(slot, 1)],
            state,
            ext,
            halo,
        )
        for copy in keep(index, slot):
            copy.start()

        @pl.when(index == size + 2)
        def _():
            cot_ring.advance(2)

        return carry

    lax.fori_loop(0, 2 * size, scan, 0)
    first, second, third = (shards(step) for step in range(3))
    first.wait_recv()
    third.start()
    for offset in range(1, per_owner):
        shards(0, offset).start()
        shards(1, offset).start()
    second.wait_recv()
    cot_ring.advance(3)
    third.wait_recv()

    @pl.when(owner == group)
    def _():
        loaded = pltpu.make_async_copy(shard_ref.at[chosen], out_rows, shard_local)
        loaded.start()
        loaded.wait()

    @pl.when(owner != group)
    def _():
        loaded = pltpu.make_async_copy(part_ref.at[owner, chosen], out_rows, shard_local)
        loaded.start()
        loaded.wait()

    out_turned[...] = out_rows[...].T
    ones = jnp.ones((8, lw), bf16)

    def compute(pair, slot):
        for way in range(2):
            block = block_of(pair, way)
            values = dot(taken[slot, way].reshape(rows, taken.shape[4]), out_turned[...], 1, 0)
            out_grad[block, way] = values
            here = gated[block, way].astype(f32)
            weighted = values * gain_ref[0:1, :] * here
            at = pl.ds(block * 2 + way, 1)
            sums[0, at, :] = dot(ones, (here * here).astype(bf16), 1, 1)[0:1, :]
            sums[1, at, :] = dot(ones, weighted.astype(bf16), 1, 1)[0:1, :]

    stream(cot_ref, branch_ref, 0, 1, compute, own=True)
    stream(cot_ref, branch_ref, *turns(0, size - 4), compute)

    def cot_late(step, carry):
        cot_ring.advance(step)
        stream(cot_ref, branch_ref, *turns(step - 3, size - 4), compute)
        return carry

    lax.fori_loop(4, size - 1, cot_late, 0)
    cot_ring.arrive()
    stream(cot_ref, branch_ref, size - 1, size, compute)
    copies = [
        push(sums, landing.at[k], pair_send.at[k], pair_recv.at[k], peer)
        for k, peer in enumerate(peers)
    ]
    for copy in copies:
        copy.start()
    total = sums[...]
    for k, copy in enumerate(copies):
        copy.wait_recv()
        total = total + landing[k]
    scale = lax.rsqrt(total[0] / inner + EPS)
    pull = scale * scale * scale * (total[1] / inner)
    fill = jnp.zeros((128 - 2 * size, rows), f32)
    scale_turned = jnp.concatenate([scale, fill]).T
    pull_turned = jnp.concatenate([pull, fill]).T
    lane = lax.broadcasted_iota(jnp.int32, (rows, 128), 1)
    gain_acc[...] = jnp.zeros_like(gain_acc)

    def finish(block, carry):
        for way in range(2):
            mask = lane == block * 2 + way
            by = jnp.sum(jnp.where(mask, scale_turned, 0.0), axis=1, keepdims=True)
            less = jnp.sum(jnp.where(mask, pull_turned, 0.0), axis=1, keepdims=True)
            here = gated[block, way].astype(f32)
            values = out_grad[block, way]
            scaled = here * by
            normed = (scaled * gain_ref[0:1, :]).astype(bf16)
            normed_ref[block, way] = normed
            turned_ref[block, :, way * rows : (way + 1) * rows] = normed.T
            grad_ref[block, way] = (values * gain_ref[0:1, :] * by - here * less).astype(bf16)
            gain_acc[0:1, :] += jnp.sum(values * scaled, axis=0, keepdims=True)
        return carry

    lax.fori_loop(0, size, finish, 0)
    for offset in range(1, per_owner):
        shards(0, offset).wait_recv()
        shards(2, offset).start()
    for copy in sent + copies + [first, second, third]:
        copy.wait_send()
    flushed.wait()
    for index in (2 * size - 2, 2 * size - 1):
        for copy in keep(index, index % 2):
            copy.wait()

    def settle(pair, carry):
        for way in range(2):
            put(pair, way).wait()
        return carry

    lax.fori_loop(0, size, settle, 0)
    ring.settle()
    cot_ring.settle()
    for offset in range(1, per_owner):
        shards(1, offset).wait_recv()
        shards(2, offset).wait_recv()
        for step in range(3):
            shards(step, offset).wait_send()


def front(x, weight, cot, shard, tables, gain, inner, widths, head_size, collective_id):
    size, groups = lax.axis_size("seq"), lax.axis_size("wa")
    parts, cot_parts = ring_parts(x, 2), ring_parts(cot, 2)
    cols, depth = weight.shape
    rows = x.shape[0] // 2
    width = x.shape[1]
    lw, bc = widths
    per_owner = size // groups
    bf16, f32, DMA, vmem = jnp.bfloat16, jnp.float32, pltpu.SemaphoreType.DMA, pltpu.VMEM
    whole = (size, 2, rows, lw)
    shape = jax.ShapeDtypeStruct
    return pl.pallas_call(
        functools.partial(front_kernel, widths, head_size, size, groups, inner),
        out_shape=[
            shape((size,) + parts.shape, bf16),
            shape((groups, cols, depth), bf16),
            shape((size, 2, rows, cols), bf16),
            shape(whole, bf16),
            shape((size, 2, lw, bc // 2), bf16),
            shape(whole, bf16),
            shape((size, lw, 2 * rows), bf16),
            shape(whole, bf16),
            shape((8, lw), f32),
            shape((size,) + parts.shape, bf16),
            shape((groups, per_owner, lw, width), bf16),
        ],
        in_specs=[ANY] * 4 + [VMEM] * 8,
        out_specs=[ANY] * 5 + [VMEM] * 4 + [ANY] * 2,
        scratch_shapes=[
            vmem((groups, cols, depth), bf16),
            vmem((size, 2, rows, cols), bf16),
            vmem((2,) + parts.shape, bf16),
            vmem((lw, bc // 2), f32),
            vmem((rows + 8, lw + bc), f32),
            vmem((8, lw + bc), f32),
            vmem(whole, bf16),
            vmem(whole, f32),
            vmem((2, 1, rows, lw), bf16),
            vmem((2, 1, lw, bc // 2), bf16),
            vmem((lw, width), bf16),
            vmem((width, lw), bf16),
            vmem((2, 2 * size, rows), f32),
            vmem((size - 1, 2, 2 * size, rows), f32),
            DMA((groups - 1,)),
            DMA((groups - 1,)),
            DMA((2,)),
            DMA((2, 2)),
            DMA((size, 2)),
            DMA((2, 2)),
            DMA((3, per_owner)),
            DMA((3, per_owner)),
            DMA,
            DMA((size - 1,)),
            DMA((size - 1,)),
        ]
        + ring_sems(size, 2)
        + ring_sems(size, 2),
        compiler_params=comm_params(collective_id, 62),
        name="front",
    )(parts, weight, cot_parts, shard, *tables, gain)


def finish_kernel(
    size,
    groups,
    counts,
    grad_ref,
    weight_ref,
    normed_ref,
    turned_ref,
    out_ref,
    branch_grad_ref,
    tokens_ref,
    scale_ref,
    taps_ref,
    gain_ref,
    heads_ref,
    swapped_ref,
    shard_ref,
    out_full_ref,
    rows_ref,
    gathered_ref,
    pieces_ref,
    owned_ref,
    shared_out,
    small_out,
    branch_ref,
    landing,
    slots,
    first,
    parts,
    total,
    taken,
    turned,
    out_total,
    out_parts,
    out_landing,
    out_taken,
    piece,
    main,
    shared,
    shared_land,
    shared_sum,
    small,
    small_land,
    send_sem,
    recv_sem,
    part_send,
    part_recv,
    take_sem,
    out_send,
    out_recv,
    owned_send,
    owned_recv,
    owned_local,
    pair_send,
    pair_recv,
    mate_send,
    mate_recv,
    *ring_refs,
):
    me, group, pos, right, left = neighbours(size)
    mates = [(me, index) for index in others(group, groups)]
    peers = [(index, group) for index in others(me, size)]
    greet(mates + peers)
    tiles, rows, tile = slots.shape[2:]
    cols = total.shape[0]
    bf16, f32 = jnp.bfloat16, jnp.float32
    out_ring = RingGather(size, piece, pieces_ref, *ring_refs[0:3])
    main_ring = RingGather(size, main, gathered_ref, *ring_refs[3:6])
    shared_ring = RingGather(size, shared_sum, shared_out, *ring_refs[6:9])
    small_ring = RingGather(size, small, small_out, *ring_refs[9:12])
    fetch_sem, weights_taken, held, held_sem, out_turned = ring_refs[12:17]

    def target(step, way):
        shift = (pos - 1 - step + 2 * size) if way == 0 else (pos + 1 + step)
        return ring_index(shift % size, size)

    def fetch(step, way):
        slot = lax.rem(step, 2)
        return pltpu.make_async_copy(
            grad_ref.at[target(step, way), way], held.at[slot, way], held_sem.at[slot, way]
        )

    def term(step, way, at):
        return dot(held[lax.rem(step, 2), way], weight_ref[at], 1, 0)

    def hop(step, way, at, source):
        return push(
            source,
            slots.at[step, way, at],
            send_sem.at[step, way, at],
            recv_sem.at[step, way, at],
            right if way == 0 else left,
        )

    def begin(at, carry):
        for way in range(2):
            first[way, at] = term(0, way, at).astype(bf16)
            hop(0, way, at, first.at[way, at]).start()
        return carry

    for way in range(2):
        fetch(0, way).start()
    for way in range(2):
        fetch(1, way).start()
    for way in range(2):
        fetch(0, way).wait()
    lax.fori_loop(0, tiles, begin, 0)

    def mate_of(offset):
        return lax.rem(group + offset, groups)

    def send_part(offset):
        return push(
            parts.at[offset - 1],
            landing.at[offset - 1],
            part_send.at[offset - 1],
            part_recv.at[offset - 1],
            (me, mate_of(offset)),
        )

    def send_out(offset):
        return push(
            out_parts.at[mate_of(offset)],
            out_landing.at[offset - 1],
            out_send.at[offset - 1],
            out_recv.at[offset - 1],
            (me, mate_of(offset)),
        )

    def stream(count, take, use):
        for copy in take(0, 0):
            copy.start()

        def one(block, carry):
            slot = lax.rem(block, 2)

            @pl.when(block + 1 < count)
            def _():
                for copy in take(block + 1, 1 - slot):
                    copy.start()

            for copy in take(block, slot):
                copy.wait()
            use(block, slot)
            return carry

        lax.fori_loop(0, count, one, 0)

    def tokens_of(block):
        return pl.ds(pl.multiple_of(block * 2 * rows, 2 * rows), 2 * rows)

    def weight_part(offset):
        columns = pl.ds(pl.multiple_of(mate_of(offset) * tile, tile), tile)

        def take(block, slot):
            return [
                pltpu.make_async_copy(
                    normed_ref.at[block, :, :, columns], taken.at[slot], take_sem.at[slot, 0]
                ),
                pltpu.make_async_copy(
                    turned_ref.at[:, tokens_of(block)], turned.at[slot], take_sem.at[slot, 1]
                ),
            ]

        def use(block, slot):
            values = dot(turned[slot], taken[slot].reshape(2 * rows, tile), 1, 0)

            @pl.when(block == 0)
            def _():
                total[...] = values

            @pl.when(block > 0)
            def _():
                total[...] += values

        stream(size, take, use)

    def out_part(low, count):
        piece_rows = out_parts.shape[1]

        def take(block, slot):
            return [
                pltpu.make_async_copy(
                    branch_grad_ref.at[tokens_of(low + block)],
                    out_taken.at[slot],
                    take_sem.at[slot, 0],
                ),
                pltpu.make_async_copy(
                    out_ref.at[low + block], out_turned.at[slot], take_sem.at[slot, 1]
                ),
            ]

        def use(block, slot):
            values = dot(out_turned[slot], out_taken[slot], 1, 0)

            @pl.when(low + block == 0)
            def _():
                out_total[...] = values

            @pl.when(low + block > 0)
            def _():
                out_total[...] += values

        stream(count, take, use)

    def out_sends():
        piece_rows = out_parts.shape[1]
        for index in range(groups):
            out_parts[index] = out_total[index * piece_rows : (index + 1) * piece_rows].astype(bf16)
        for offset in range(1, groups):
            send_out(offset).start()

    def advance(step, carry):
        for way in range(2):
            fetch(step + 1, way).start()
        for way in range(2):
            fetch(step, way).wait()

        def one(at, inner):
            for way in range(2):
                own = term(step, way, at)
                hop(step - 1, way, at, first.at[way, at]).wait_recv()
                slots[step - 1, way, at] = (slots[step - 1, way, at].astype(f32) + own).astype(bf16)
                hop(step, way, at, slots.at[step - 1, way, at]).start()
            return inner

        lax.fori_loop(0, tiles, one, 0)

        @pl.when(step < 3)
        def _():
            out_part((step - 1) * (size // 2), size // 2)

        @pl.when(step == 2)
        def _():
            out_sends()

        @pl.when((step > 2) & (step <= groups + 2))
        def _():
            weight_part(step - 2)

        @pl.when((step > 2) & (step <= groups + 1))
        def _():
            parts[step - 3] = total[...].astype(bf16)
            send_part(step - 2).start()

        return carry

    lax.fori_loop(1, size - 1, advance, 0)
    for offset in range(1, groups):
        send_out(offset).wait_recv()
    summed = out_parts[group].astype(f32)
    for offset in range(1, groups):
        summed = summed + out_landing[offset - 1].astype(f32)
    piece[...] = summed.astype(bf16).reshape(piece.shape)
    out_ring.start()

    for way in range(2):
        fetch(size - 1, way).wait()

    def end(at, carry):
        columns = pl.ds(pl.multiple_of(at * tile, tile), tile)
        for way in range(2):
            own = term(size - 1, way, at)
            hop(size - 2, way, at, first.at[way, at]).wait_recv()
            rows_ref[way, :, columns] = slots[size - 2, way, at].astype(f32) + own
        return carry

    lax.fori_loop(0, tiles, end, 0)
    width = rows_ref.shape[2]
    own_width = gain_ref.shape[1]
    flat = jnp.zeros((1, width), f32)
    for way in range(2):
        values = tokens_ref[way].astype(f32) * scale_ref[way, :, 0:1]
        flat = flat + jnp.sum(rows_ref[way] * values, axis=0, keepdims=True)
    half = small.shape[2]
    listed = [
        taps_ref[k : k + 1, at : at + 128] for k in range(KW + 1) for at in range(0, own_width, 128)
    ]
    listed += [gain_ref[0:1, at : at + 128] for at in range(0, own_width, 128)]
    listed += [heads_ref[k : k + 1, :] for k in range(3)]
    listed += [
        taps_ref[k : k + 1, at : at + 128]
        for k in range(KW + 1)
        for at in range(own_width, taps_ref.shape[1], 128)
    ]
    listed += [flat[:, at : at + 128] for at in range(0, width, 128)]
    for at, row in enumerate(listed):
        small[at // half, 0, at % half : at % half + 1, :] = row
    small_in = [
        push(small, small_land.at[k], mate_send.at[k], mate_recv.at[k], mate)
        for k, mate in enumerate(mates)
    ]
    for copy in small_in:
        copy.start()

    def out_advance(step, carry):
        out_ring.advance(step)
        return carry

    lax.fori_loop(1, size // 2, out_advance, 0)
    fetched = []
    for offset in range(1, groups):
        send_part(offset).wait()
        fetched.append(
            pltpu.make_async_copy(
                landing.at[offset - 1], parts.at[offset - 1], fetch_sem.at[offset - 1]
            )
        )
        fetched[-1].start()
    for copy, part in zip(fetched, range(groups - 1)):
        copy.wait()
        total[...] += parts[part].astype(f32)
    main[...] = total[: counts[0]].astype(bf16).reshape(main.shape)
    shared[...] = total[counts[0] : counts[0] + counts[1]].astype(bf16).reshape(shared.shape)
    shared_in = [
        push(shared.at[peer[0]], shared_land.at[k], pair_send.at[k], pair_recv.at[k], peer)
        for k, peer in enumerate(peers)
    ]
    lax.fori_loop(size // 2, size - 1, out_advance, 0)
    for copy in shared_in:
        copy.start()
    main_ring.start()
    out_ring.finish()
    owned = [
        push(pieces_by_owner(pieces_ref, mate[1], groups), owned_ref.at[group], owned_send.at[k], owned_recv.at[k], mate)
        for k, mate in enumerate(mates)
    ]
    kept = pltpu.make_async_copy(
        pieces_by_owner(pieces_ref, group, groups), owned_ref.at[group], owned_local
    )
    for copy in owned:
        copy.start()
    kept.start()
    main_ring.advance(1)
    for copy in small_in + shared_in:
        copy.wait()
    values = small[...]
    for k in range(groups - 1):
        values = values + small_land[k]
    small[...] = values
    values = shared[me].astype(f32)
    for k in range(size - 1):
        values = values + shared_land[k].astype(f32)
    shared_rows = values.shape[0]
    own_rows = shared_sum.shape[0] * shared_sum.shape[2] - shared_rows
    tail = jnp.concatenate([values, total[counts[0] + counts[1] :][:own_rows]]).astype(bf16)
    shared_sum[...] = tail.reshape(shared_sum.shape)
    small_ring.start()
    shared_ring.start()
    branch_ref[...] = jnp.zeros_like(branch_ref)

    per_owner = size // groups

    def weight_take(block, slot):
        owner, at = block // per_owner, lax.rem(block, per_owner)

        @pl.when(owner == group)
        def _():
            pltpu.make_async_copy(
                shard_ref.at[at], weights_taken.at[slot], take_sem.at[slot, 0]
            ).start()

        @pl.when(owner != group)
        def _():
            pltpu.make_async_copy(
                out_full_ref.at[owner, at], weights_taken.at[slot], take_sem.at[slot, 0]
            ).start()

    def multiply(block, carry):
        slot = lax.rem(block, 2)

        @pl.when(block + 1 < size)
        def _():
            weight_take(block + 1, 1 - slot)

        pltpu.make_async_copy(
            shard_ref.at[0], weights_taken.at[slot], take_sem.at[slot, 0]
        ).wait()
        branch_ref[...] += dot(swapped_ref[block], weights_taken[slot], 1, 0)
        return carry

    weight_take(0, 0)
    count = size - 3

    def main_advance(step, carry):
        main_ring.advance(step)
        small_ring.advance(step - 1)
        shared_ring.advance(step - 1)
        lax.fori_loop(((step - 2) * size) // count, ((step - 1) * size) // count, multiply, 0)
        return carry

    lax.fori_loop(2, size - 1, main_advance, 0)
    small_ring.advance(size - 2)
    shared_ring.advance(size - 2)

    def drain(step, carry):
        def one(at, inner):
            for way in range(2):
                hop(step, way, at, first.at[way, at]).wait_send()
            return inner

        return lax.fori_loop(0, tiles, one, carry)

    lax.fori_loop(0, size - 1, drain, 0)
    for offset in range(1, groups):
        send_out(offset).wait_send()
    main_ring.finish()
    small_ring.finish()
    shared_ring.finish()
    for copy in owned:
        copy.wait()
    kept.wait()


def pieces_by_owner(pieces_ref, owner, groups):
    count = pieces_ref.shape[0] // groups
    return pieces_ref.at[pl.ds(owner * count, count)]


def finish(
    grad,
    weight,
    normed,
    turned,
    out,
    branch_grad,
    tokens,
    scale,
    taps,
    gain,
    heads,
    swapped,
    shard,
    out_full,
    counts,
    collective_id,
):
    size, groups = lax.axis_size("seq"), lax.axis_size("wa")
    _, ways, rows, cols = grad.shape
    tile, tiles = weight.shape[2], groups
    width = tiles * tile
    lw = out.shape[1]
    bc = taps.shape[1] - lw
    piece_rows = lw // groups
    per_owner = size // groups
    bf16, f32, DMA = jnp.bfloat16, jnp.float32, pltpu.SemaphoreType.DMA
    total_small = ((KW + 2) * lw + (KW + 1) * bc + width) // 128 + 3
    half = -(-total_small // 16) * 8
    piece = (2, 1, piece_rows // 2, width)
    main = (2, 2, counts[0] // 4, tile)
    shared_rows = counts[1] // size
    both = (2, 1, (shared_rows + counts[2]) // 2, tile)
    small_shape = (2, 1, half, 128)
    vmem = pltpu.VMEM
    return pl.pallas_call(
        functools.partial(finish_kernel, size, groups, counts),
        out_shape=[
            jax.ShapeDtypeStruct((ways, rows, width), f32),
            jax.ShapeDtypeStruct((size,) + main, bf16),
            jax.ShapeDtypeStruct((size,) + piece, bf16),
            jax.ShapeDtypeStruct((groups, per_owner) + piece, bf16),
            jax.ShapeDtypeStruct((size,) + both, bf16),
            jax.ShapeDtypeStruct((size,) + small_shape, f32),
            jax.ShapeDtypeStruct((ways * rows, width), f32),
            jax.ShapeDtypeStruct((groups - 1, cols, tile), bf16),
        ],
        in_specs=[ANY, VMEM, ANY, ANY, ANY, ANY] + [VMEM] * 6 + [ANY, ANY],
        out_specs=[VMEM, ANY, ANY, ANY, ANY, ANY, VMEM, ANY],
        scratch_shapes=[
            vmem((size - 1, 2, tiles, rows, tile), bf16),
            vmem((2, tiles, rows, tile), bf16),
            vmem((groups - 1, cols, tile), bf16),
            vmem((cols, tile), f32),
            vmem((2, ways, rows, tile), bf16),
            vmem((2, cols, 2 * rows), bf16),
            vmem((lw, width), f32),
            vmem((groups, piece_rows, width), bf16),
            vmem((groups - 1, piece_rows, width), bf16),
            vmem((2, 2 * rows, width), bf16),
            vmem(piece, bf16),
            vmem(main, bf16),
            vmem((size, shared_rows, tile), bf16),
            vmem((size - 1, shared_rows, tile), bf16),
            vmem(both, bf16),
            vmem(small_shape, f32),
            vmem((groups - 1,) + small_shape, f32),
            DMA((size - 1, 2, tiles)),
            DMA((size - 1, 2, tiles)),
            DMA((groups - 1,)),
            DMA((groups - 1,)),
            DMA((2, 2)),
            DMA((groups - 1,)),
            DMA((groups - 1,)),
            DMA((groups - 1,)),
            DMA((groups - 1,)),
            DMA,
            DMA((size - 1,)),
            DMA((size - 1,)),
            DMA((groups - 1,)),
            DMA((groups - 1,)),
        ]
        + ring_sems(size, 1)
        + ring_sems(size, 2)
        + ring_sems(size, 1)
        + ring_sems(size, 1)
        + [DMA((groups - 1,)), vmem((2, lw, width), bf16)]
        + [vmem((2, 2, rows, cols), bf16), DMA((2, 2)), vmem((2, lw, 2 * rows), bf16)],
        compiler_params=comm_params(collective_id, 63),
        name="finish",
    )(
        grad,
        weight,
        normed,
        turned,
        out,
        branch_grad,
        tokens,
        scale,
        taps,
        gain,
        heads,
        swapped,
        shard,
        out_full,
    )


def assemble_kernel(blocks, gathered_ref, tail_ref, o_ref):
    @pl.when(pl.program_id(0) < blocks)
    def _():
        o_ref[...] = gathered_ref[0, 0].reshape(o_ref.shape).astype(jnp.float32)

    @pl.when(pl.program_id(0) == blocks)
    def _():
        o_ref[...] = tail_ref[...].astype(jnp.float32)


def assemble_in(gathered, tail):
    size, ways, chunks, rows, width = gathered.shape
    step = chunks * rows
    blocks = size * ways
    total = blocks * step + tail.shape[0]
    steps = blocks + 1
    pad = -tail.shape[0] % step
    if tail.shape[0] > step:
        out = jnp.swapaxes(gathered, 0, 1).reshape(blocks * step, width)
        return jnp.concatenate([out, tail]).astype(jnp.float32)
    return pl.pallas_call(
        functools.partial(assemble_kernel, blocks),
        grid=(steps,),
        in_specs=[
            pl.BlockSpec(
                (1, 1, chunks, rows, width),
                lambda i: (lax.rem(i, size), jnp.minimum(i // size, ways - 1), 0, 0, 0),
            ),
            pl.BlockSpec((step, width), lambda i: (0, 0)),
        ],
        out_specs=pl.BlockSpec((step, width), lambda i: (i, 0)),
        out_shape=jax.ShapeDtypeStruct((total, width), jnp.float32),
        compiler_params=pltpu.CompilerParams(vmem_limit_bytes=32 * 2**20),
        name="assemble_in",
    )(gathered, jnp.pad(tail, ((0, pad), (0, 0))))


def widen_kernel(x_ref, o_ref):
    o_ref[...] = x_ref[0, 0].astype(jnp.float32)


def assemble_out(owned):
    groups, count, rows, width = owned.shape
    return pl.pallas_call(
        widen_kernel,
        grid=(count, groups),
        in_specs=[pl.BlockSpec((1, 1, rows, width), lambda t, g: (g, t, 0, 0))],
        out_specs=pl.BlockSpec((rows, width), lambda t, g: (t * groups + g, 0)),
        out_shape=jax.ShapeDtypeStruct((groups * count * rows, width), jnp.float32),
        name="assemble_out",
    )(owned)


def body(
    tokens,
    lengths,
    norm_gain,
    in_weight,
    conv_weight,
    conv_bias,
    dt_bias,
    a_log,
    skip_gain,
    out_gain,
    out_weight,
    cotangent,
):
    seqs_here, slot_rows, width = tokens.shape
    row_count = seqs_here * slot_rows
    inner_width = out_gain.shape[0]
    channels = conv_bias.shape[0]
    bc_width = channels - inner_width
    state_size = bc_width // 2
    head_count = dt_bias.shape[0]
    head_size = inner_width // head_count
    seq_devices = lax.axis_size("seq")
    group_devices = lax.axis_size("wa")
    seq_index = lax.axis_index("seq")
    length = seq_devices * slot_rows
    local_heads = head_count // seq_devices
    local_width = local_heads * head_size
    channel_start = seq_index * local_width
    head_start = seq_index * local_heads
    bf16, f32 = jnp.bfloat16, jnp.float32

    def take(array, start, size, axis):
        return lax.dynamic_slice_in_dim(array, start, size, axis)

    positions = seq_index * slot_rows + jnp.arange(slot_rows)
    valid_rows = (positions[None, :] < lengths[:, None]).astype(f32).reshape(row_count, 1)
    flat_tokens = tokens.reshape(row_count, width).astype(f32)
    in_scale = row_scale(flat_tokens)
    normed = (flat_tokens * in_scale * norm_gain).astype(bf16)
    cot_rows = cotangent.reshape(row_count, width)

    in_turned = in_weight.T
    local_columns = jnp.concatenate(
        [
            take(in_turned, channel_start, local_width, 0),
            take(in_turned, inner_width + channel_start, local_width, 0),
            in_turned[2 * inner_width : 2 * inner_width + bc_width],
            take(in_turned, 2 * inner_width + bc_width + head_start, local_heads, 0),
            jnp.zeros((128 - local_heads, in_weight.shape[0]), bf16),
        ]
    )
    columns_here = local_columns.shape[0]
    blocks = (seq_devices, seqs_here, slot_rows)
    def lanes(part):
        return jnp.pad(part[None], ((0, 7), (0, 128 - local_heads)))

    taps = jnp.pad(
        jnp.concatenate(
            [take(conv_weight, channel_start, local_width, 1), conv_weight[:, inner_width:]], axis=1
        ),
        ((0, 8 - KW), (0, 0)),
    )
    shift = jnp.concatenate(
        [take(conv_bias, channel_start, local_width, 0), conv_bias[inner_width:]]
    )[None]
    bias = lanes(take(dt_bias, head_start, local_heads, 0))
    slope = lanes(-jnp.exp(take(a_log, head_start, local_heads, 0)))
    skip = jnp.repeat(take(skip_gain, head_start, local_heads, 0), head_size)[None]
    gain_local = take(out_gain, channel_start, local_width, 0)
    spread, fold, tri, upper = scan_tables(slot_rows, local_width, head_size)
    widths = (local_width, bc_width)
    per_owner = seq_devices // group_devices
    (
        normed_all,
        in_columns,
        projected,
        y_heads,
        entering,
        normed_out,
        turned_out,
        gated_grad,
        gain_sum,
        branch_grad,
        out_full,
    ) = front(
        normed,
        local_columns,
        cot_rows * valid_rows.astype(bf16),
        out_weight.reshape(per_owner, local_width, width),
        (taps, shift, bias, slope, skip, spread, tri),
        gain_local[None],
        inner_width,
        widths,
        head_size,
        0,
    )
    normed_out = normed_out.reshape(-1, local_width)
    branch_grad = branch_grad.reshape(-1, width)
    swapped = lax.all_to_all(
        normed_out.reshape(seq_devices, row_count, local_width), "seq", 0, 0, tiled=True
    )
    proj_grad, turned_grad, taps_sum, _, head_sum = scan_backward(
        projected,
        y_heads,
        entering,
        gated_grad,
        taps,
        shift,
        bias,
        slope,
        skip,
        spread,
        fold,
        tri,
        upper,
        widths,
        head_size,
    )
    proj_grad = proj_grad.reshape(-1, columns_here)
    in_rows = in_weight.shape[0]
    own_rows = (KW + 2) * (local_width // 128)
    packed_rows = own_rows + 3 + ((KW + 1) * bc_width + width) // 128
    shared_rows = bc_width // seq_devices
    normed_grad, gathered, _, owned, shared_all, small_all, branch, _ = finish(
        proj_grad.reshape(blocks + (columns_here,)),
        in_columns,
        normed_all.reshape(blocks + (width,)),
        turned_grad,
        turned_out,
        branch_grad,
        tokens,
        jnp.broadcast_to(in_scale.reshape(seqs_here, slot_rows, 1), (seqs_here, slot_rows, 128)),
        taps_sum,
        gain_sum,
        head_sum,
        swapped,
        out_weight.reshape(per_owner, local_width, width),
        out_full,
        (2 * local_width, bc_width, 16),
        2,
    )
    normed_grad = normed_grad.reshape(row_count, width)
    token_grad = norm_backward(flat_tokens, in_scale, norm_gain, normed_grad)
    token_grad = token_grad + cot_rows.astype(f32)
    owned = owned.reshape(
        group_devices, per_owner, local_width // group_devices, width
    )
    shared_all = shared_all.reshape(seq_devices, shared_rows + 16, in_rows)
    small_all = small_all.reshape(seq_devices, -1, 128)
    mixed_out = (flat_tokens + valid_rows * branch).astype(bf16).reshape(tokens.shape)
    tail = jnp.concatenate(
        [
            shared_all[:, :shared_rows].reshape(bc_width, in_rows),
            shared_all[:, shared_rows : shared_rows + local_heads].reshape(head_count, in_rows),
        ]
    )
    in_weight_grad = assemble_in(gathered, tail).T
    out_weight_grad = assemble_out(owned)

    own_all = small_all[:, :own_rows].reshape(seq_devices, KW + 2, local_width)
    own_all = jnp.swapaxes(own_all, 0, 1).reshape(KW + 2, inner_width)
    head_all = jnp.swapaxes(small_all[:, own_rows : own_rows + 3, :local_heads], 0, 1)
    head_all = head_all.reshape(3, head_count)
    summed = jnp.sum(small_all[:, own_rows + 3 : packed_rows], axis=0).reshape(-1)
    conv_weight_grad = jnp.concatenate(
        [own_all[:KW], summed[: KW * bc_width].reshape(KW, bc_width)], axis=1
    )
    conv_bias_grad = jnp.concatenate(
        [own_all[KW], summed[KW * bc_width : (KW + 1) * bc_width]]
    )
    norm_gain_total = summed[(KW + 1) * bc_width :]
    return (
        mixed_out,
        token_grad.reshape(tokens.shape),
        norm_gain_total,
        in_weight_grad,
        conv_weight_grad,
        conv_bias_grad,
        head_all[0],
        head_all[1],
        head_all[2],
        own_all[KW + 1],
        out_weight_grad,
    )


def solution(mesh):
    placed = (
        P("wa", "seq", None),
        P("wa"),
        P(),
        P("wa", None),
        P(),
        P(),
        P(),
        P(),
        P(),
        P(),
        P("wa", None),
        P("wa", "seq", None),
    )
    return jax.shard_map(
        body,
        mesh=mesh,
        in_specs=placed,
        out_specs=(
            P("wa", "seq", None),
            P("wa", "seq", None),
            P(),
            P("wa", None),
            P(),
            P(),
            P(),
            P(),
            P(),
            P(),
            P("wa", None),
        ),
        check_vma=False,
    )
```

```python
import functools

import jax
import jax.numpy as jnp
import numpy as np
from jax import lax
from jax.experimental import pallas as pl
from jax.experimental.pallas import tpu as pltpu
from jax.sharding import PartitionSpec as P

KW = 4
EPS = 1e-05
HIGHEST = lax.Precision.HIGHEST
MESH = pl.DeviceIdType.MESH


def row_scale(values):
    return lax.rsqrt(jnp.mean(values * values, axis=-1, keepdims=True) + EPS)


def norm_backward(values, row_scales, gain_vec, grad_out):
    weighted = grad_out * gain_vec
    return row_scales * weighted - values * row_scales**3 * jnp.mean(
        weighted * values, axis=-1, keepdims=True
    )


def dot(a, b, ca, cb, precision=None):
    return lax.dot_general(
        a, b, (((ca,), (cb,)), ((), ())), precision=precision, preferred_element_type=jnp.float32
    )


def chunk_front(proj_ref, ext, taps_ref, heads_ref, tri_ref, widths, head_start):
    lw, bc = widths
    rows = proj_ref.shape[2]
    ext[8:, :] = proj_ref[0, 0, :, lw : 2 * lw + bc].astype(jnp.float32)
    conv = taps_ref[KW : KW + 1, :]
    for k in range(KW):
        conv = conv + taps_ref[k : k + 1, :] * ext[5 + k : 5 + k + rows, :]
    conv_sig = lax.logistic(conv)
    act = conv * conv_sig
    raw = proj_ref[0, 0, :, 2 * lw + bc :].astype(jnp.float32)
    step_in = pltpu.roll(raw, lax.rem(128 - head_start, 128), 1) + heads_ref[0:1, :]
    steps = jnp.maximum(step_in, 0.0) + jnp.log1p(jnp.exp(-jnp.abs(step_in)))
    rates = heads_ref[1:2, :] * steps
    cum = dot(tri_ref[...], rates, 1, 0, HIGHEST)
    return conv, conv_sig, act, step_in, steps, rates, cum


def head_masks(rows, head_size):
    lane = lax.broadcasted_iota(jnp.int32, (rows, 128), 1)
    row = lax.broadcasted_iota(jnp.int32, (rows, rows), 0)
    col = lax.broadcasted_iota(jnp.int32, (rows, rows), 1)
    return lane, row >= col


def forward_chunk(
    widths,
    head_size,
    head_start,
    start,
    proj_ref,
    taps_ref,
    heads_ref,
    wide_ref,
    spread_ref,
    tri_ref,
    gated_ref,
    y_ref,
    enter_ref,
    state,
    ext,
    halo,
):
    lw, bc = widths
    bf16, f32 = jnp.bfloat16, jnp.float32
    rows = proj_ref.shape[2]
    per_tile = 128 // head_size

    @pl.when(start)
    def _():
        state[...] = jnp.zeros_like(state)
        halo[...] = jnp.zeros_like(halo)

    ext[0:8, :] = halo[...]
    _, _, act, _, steps, _, cum = chunk_front(
        proj_ref, ext, taps_ref, heads_ref, tri_ref, widths, head_start
    )
    halo[...] = ext[rows : rows + 8, :]
    x = act[:, :lw]
    xb = x.astype(bf16)
    b_rows = act[:, lw : lw + bc // 2].astype(bf16)
    c_rows = act[:, lw + bc // 2 :].astype(bf16)
    cum_t, steps_t = cum.T, steps.T
    last = cum[rows - 1 : rows, :]
    grow = dot(jnp.exp(cum).astype(bf16), spread_ref[...], 1, 0)
    tail = dot((jnp.exp(last - cum) * steps).astype(bf16), spread_ref[...], 1, 0)
    scores = dot(c_rows, b_rows, 1, 1)
    entering = state[...].astype(bf16)
    enter_ref[0, 0] = entering
    y = dot(c_rows, entering, 1, 1) * grow + wide_ref[1:2, :] * x
    added = dot((x * tail).astype(bf16), b_rows, 0, 0)
    lane, causal = head_masks(rows, head_size)
    gate = proj_ref[0, 0, :, :lw].astype(f32)
    silu_gate = gate * lax.logistic(gate)
    for tile in range(lw // 128):
        cols = slice(tile * 128, (tile + 1) * 128)
        inner = None
        for sub in range(per_tile):
            head = tile * per_tile + sub
            log_decay = cum[:, head : head + 1] - cum_t[head : head + 1, :]
            decay = jnp.exp(jnp.where(causal, log_decay, -1e30))
            weights = (scores * decay * steps_t[head : head + 1, :]).astype(bf16)
            part = dot(weights, xb[:, cols], 1, 0)
            inner = part if inner is None else jnp.where(lane >= sub * head_size, part, inner)
            span = slice(head * head_size, (head + 1) * head_size)
            state[span, :] = (
                jnp.exp(cum[rows - 1 : rows, head : head + 1]) * state[span, :] + added[span, :]
            )
        y_tile = y[:, cols] + inner
        y_ref[0, 0, :, cols] = y_tile.astype(bf16)
        gated_ref[:, cols] = (y_tile * silu_gate[:, cols]).astype(bf16)


def backward_kernel(
    widths,
    head_size,
    chunks,
    proj_ref,
    before_ref,
    y_ref,
    enter_ref,
    grad_ref,
    taps_ref,
    heads_ref,
    wide_ref,
    spread_ref,
    fold_ref,
    tri_ref,
    upper_ref,
    out_ref,
    turned_ref,
    taps_acc,
    skip_acc,
    head_acc,
    lam,
    ext,
    later,
    after,
):
    lw, bc = widths
    state_size = bc // 2
    bf16, f32 = jnp.bfloat16, jnp.float32
    rows = proj_ref.shape[2]
    per_tile = 128 // head_size
    chunk = chunks - 1 - pl.program_id(1)
    head_start = lax.axis_index("seq") * (lw // head_size)

    @pl.when((pl.program_id(0) == 0) & (pl.program_id(1) == 0))
    def _():
        taps_acc[...] = jnp.zeros_like(taps_acc)
        skip_acc[...] = jnp.zeros_like(skip_acc)
        head_acc[...] = jnp.zeros_like(head_acc)

    @pl.when(pl.program_id(1) == 0)
    def _():
        lam[...] = jnp.zeros_like(lam)
        after[...] = jnp.zeros_like(after)

    ext[0:8, :] = jnp.where(
        chunk > 0, before_ref[0, 0, 8:16, lw : 2 * lw + bc].astype(f32), 0.0
    )
    conv, conv_sig, act, step_in, steps, rates, cum = chunk_front(
        proj_ref, ext, taps_ref, heads_ref, tri_ref, widths, head_start
    )
    x = act[:, :lw]
    xb = x.astype(bf16)
    b_rows = act[:, lw : lw + state_size].astype(bf16)
    c_rows = act[:, lw + state_size :].astype(bf16)
    cum_t, steps_t = cum.T, steps.T
    last = cum[rows - 1 : rows, :]
    to_end = jnp.exp(last - cum)
    tail_heads = to_end * steps
    grow = dot(jnp.exp(cum).astype(bf16), spread_ref[...], 1, 0)
    tail = dot(tail_heads.astype(bf16), spread_ref[...], 1, 0)
    scores = dot(c_rows, b_rows, 1, 1)

    gate = proj_ref[0, 0, :, :lw].astype(f32)
    gate_sig = lax.logistic(gate)
    grad = grad_ref[0, 0].astype(f32)
    y_grad = grad * gate * gate_sig
    out_ref[0, 0, :, :lw] = (
        grad * y_ref[0, 0].astype(f32) * (gate_sig * (1.0 + gate * (1.0 - gate_sig)))
    ).astype(bf16)
    yb = y_grad.astype(bf16)

    entering = enter_ref[0, 0]
    grown = y_grad * grow
    grown_b = grown.astype(bf16)
    c_grad = dot(grown_b, entering, 1, 0)
    carried = dot((grown * dot(c_rows, entering, 1, 1)).astype(bf16), fold_ref[...], 1, 0)
    lam_now = lam[...]
    lam_b = lam_now.astype(bf16)
    from_lam = dot(b_rows, lam_b, 1, 1)
    b_grad = dot((x * tail).astype(bf16), lam_b, 1, 0)
    x_lam = dot((x * from_lam).astype(bf16), fold_ref[...], 1, 0)
    x_grad = wide_ref[1:2, :] * y_grad + tail * from_lam
    skip_acc[0:1, :] += jnp.sum(y_grad * x, axis=0, keepdims=True)
    ones = jnp.ones((8, state_size), bf16)
    kept = dot(
        dot(ones, (lam_now * entering.astype(f32)).astype(bf16), 1, 1),
        fold_ref[...].astype(f32),
        1,
        0,
        HIGHEST,
    )
    through = jnp.exp(last) * kept[0:1, :]
    lam_add = dot(grown_b, c_rows, 0, 0)

    lane, causal = head_masks(rows, head_size)
    score_grad = None
    row_sums = jnp.zeros((rows, 128), f32)
    col_sums = []
    x_tiles = []
    for tile in range(lw // 128):
        cols = slice(tile * 128, (tile + 1) * 128)
        inner = None
        for sub in range(per_tile):
            head = tile * per_tile + sub
            log_decay = cum[:, head : head + 1] - cum_t[head : head + 1, :]
            decay = jnp.exp(jnp.where(causal, log_decay, -1e30))
            step_row = steps_t[head : head + 1, :]
            weights = (scores * decay * step_row).astype(bf16)
            inside = (lane >= sub * head_size) & (lane < (sub + 1) * head_size)
            y_head = jnp.where(inside, yb[:, cols], jnp.zeros_like(yb[:, cols]))
            weights_grad = dot(y_head, xb[:, cols], 1, 1)
            part = dot(weights, yb[:, cols], 0, 0)
            inner = part if inner is None else jnp.where(lane >= sub * head_size, part, inner)
            decayed = weights_grad * decay
            stepped = decayed * step_row
            score_grad = stepped if score_grad is None else score_grad + stepped
            col_sums.append(jnp.sum(decayed * scores, axis=0, keepdims=True))
            row_sum = jnp.sum(stepped * scores, axis=1, keepdims=True)
            row_sums = row_sums + jnp.where(lane == head, row_sum, 0.0)
            span = slice(head * head_size, (head + 1) * head_size)
            lam[span, :] = (
                jnp.exp(cum[rows - 1 : rows, head : head + 1]) * lam_now[span, :] + lam_add[span, :]
            )
        x_tiles.append(x_grad[:, cols] + inner)
    col_sums.append(jnp.zeros((rows - len(col_sums), rows), f32))
    col_sum = jnp.concatenate(col_sums, axis=0).T
    source = row_sums - steps * col_sum + carried
    rates_grad = (
        dot(upper_ref[...], source, 1, 0, HIGHEST)
        + dot(1.0 - upper_ref[...], tail_heads * x_lam, 1, 0, HIGHEST)
        + through
    )
    steps_grad = col_sum + to_end * x_lam + rates_grad * heads_ref[1:2, :]
    raw_grad = steps_grad * lax.logistic(step_in)
    out_ref[0, 0, :, 2 * lw + bc :] = pltpu.roll(raw_grad, head_start, 1).astype(bf16)
    head_acc[0:1, :] += jnp.sum(raw_grad, axis=0, keepdims=True)
    head_acc[1:2, :] += jnp.sum(rates_grad * rates, axis=0, keepdims=True)
    score_b = score_grad.astype(bf16)
    c_grad = c_grad + dot(score_b, b_rows, 1, 0)
    b_grad = b_grad + dot(score_b, c_rows, 0, 0)
    act_grad = jnp.concatenate(x_tiles + [b_grad, c_grad], axis=1)
    conv_grad = act_grad * (conv_sig * (1.0 + conv * (1.0 - conv_sig)))
    later[0:rows, :] = conv_grad
    later[rows : rows + 8, :] = after[...]
    after[...] = conv_grad[0:8, :]
    total = None
    for k in range(KW):
        term = taps_ref[k : k + 1, :] * later[3 - k : 3 - k + rows, :]
        total = term if total is None else total + term
        taps_acc[k : k + 1, :] += jnp.sum(conv_grad * ext[5 + k : 5 + k + rows, :], axis=0, keepdims=True)
    taps_acc[KW : KW + 1, :] += jnp.sum(conv_grad, axis=0, keepdims=True)

    @pl.when((pl.program_id(0) == pl.num_programs(0) - 1) & (chunk == 0))
    def _():
        head_acc[2:3, :] = dot(
            skip_acc[...], fold_ref[...].astype(f32), 1, 0, HIGHEST
        )[0:1, :]
    out_ref[0, 0, :, lw : 2 * lw + bc] = total.astype(bf16)
    turned_ref[...] = out_ref[0, 0].T


def whole_spec(array):
    return pl.BlockSpec(array.shape, lambda q, c: (0,) * array.ndim)


def scan_tables(rows, local_width, head_size):
    head_of = np.arange(local_width) // head_size
    spread = (np.arange(128)[:, None] == head_of[None, :]).astype(jnp.bfloat16)
    tri = (np.arange(rows)[:, None] >= np.arange(rows)[None, :]).astype(np.float32)
    return [jnp.asarray(t) for t in (spread, spread.T.copy(), tri, tri.T.copy())]


def scan_backward(
    proj, y, enter, grad, taps, heads, wide, spread, fold, tri, upper, widths, head_size
):
    chunks, seqs, rows, cols = proj.shape
    lw, bc = widths
    block = lambda *tail: pl.BlockSpec((1, 1) + tail, lambda q, c: (chunks - 1 - c, q, 0, 0))
    before = pl.BlockSpec(
        (1, 1, 16, cols),
        lambda q, c: (jnp.maximum(chunks - 2 - c, 0), q, rows // 16 - 1, 0),
    )
    tables = (taps, heads, wide, spread, fold, tri, upper)
    sums = [(8, lw + bc), (8, lw), (8, 128)]
    return pl.pallas_call(
        functools.partial(backward_kernel, widths, head_size, chunks),
        grid=(seqs, chunks),
        in_specs=[block(rows, cols), before, block(rows, lw), block(lw, bc // 2), block(rows, lw)]
        + [whole_spec(t) for t in tables],
        out_specs=[
            block(rows, cols),
            pl.BlockSpec((cols, rows), lambda q, c: (0, (chunks - 1 - c) * seqs + q)),
        ]
        + [pl.BlockSpec(s, lambda q, c: (0, 0)) for s in sums],
        out_shape=[
            jax.ShapeDtypeStruct(proj.shape, jnp.bfloat16),
            jax.ShapeDtypeStruct((cols, chunks * seqs * rows), jnp.bfloat16),
        ]
        + [jax.ShapeDtypeStruct(s, jnp.float32) for s in sums],
        scratch_shapes=[
            pltpu.VMEM((lw, bc // 2), jnp.float32),
            pltpu.VMEM((rows + 8, lw + bc), jnp.float32),
            pltpu.VMEM((rows + 8, lw + bc), jnp.float32),
            pltpu.VMEM((8, lw + bc), jnp.float32),
        ],
        compiler_params=pltpu.CompilerParams(vmem_limit_bytes=48 * 2**20),
        name="scan_backward",
    )(proj, proj, y, enter, grad, *tables)


def ring_pos(index, size):
    row, side = index // 2, index % 2
    return row + side * (size - 1 - 2 * row)


def ring_index(pos, size):
    side = pos // (size // 2)
    row = pos + side * (size - 1 - 2 * pos)
    return row * 2 + side


def greet(peers):
    barrier = pltpu.get_barrier_semaphore()
    for peer in peers:
        pl.semaphore_signal(barrier, inc=1, device_id=peer, device_id_type=MESH)
    pl.semaphore_wait(barrier, len(peers))


def push(source, target, send_sem, recv_sem, peer):
    return pltpu.make_async_remote_copy(
        source, target, send_sem, recv_sem, device_id=peer, device_id_type=MESH
    )


def neighbours(size):
    me, group = lax.axis_index("seq"), lax.axis_index("wa")
    pos = ring_pos(me, size)
    right = (ring_index((pos + 1) % size, size), group)
    left = (ring_index((pos + size - 1) % size, size), group)
    return me, group, pos, right, left


def others(index, size):
    return [(index + offset) % size for offset in range(1, size)]


ANY = pl.BlockSpec(memory_space=pl.ANY)
VMEM = pl.BlockSpec(memory_space=pltpu.VMEM)


def comm_params(collective_id, megabytes=None):
    limit = None if megabytes is None else megabytes * 2**20
    return pltpu.CompilerParams(
        collective_id=collective_id, has_side_effects=True, vmem_limit_bytes=limit
    )


class RingGather:
    def __init__(self, size, x_ref, o_ref, send_sem, recv_sem, local_sem):
        self.size, self.x, self.o = size, x_ref, o_ref
        self.send, self.recv, self.local = send_sem, recv_sem, local_sem
        self.chunks = x_ref.shape[1]
        self.me, _, self.pos, self.right, self.left = neighbours(size)

    def copy(self, step, chunk, way, first=False):
        size = self.size
        if way == 0:
            block, peer = ring_index((self.pos - step + size) % size, size), self.right
        else:
            block, peer = ring_index((self.pos + step) % size, size), self.left
        source = self.x.at[way, chunk] if first else self.o.at[block, way, chunk]
        return push(
            source,
            self.o.at[block, way, chunk],
            self.send.at[step, chunk, way],
            self.recv.at[step, chunk, way],
            peer,
        )

    def kept(self):
        return pltpu.make_async_copy(self.x, self.o.at[self.me], self.local)

    def start(self):
        self.kept().start()
        for chunk in range(self.chunks):
            for way in range(2):
                self.copy(0, chunk, way, True).start()

    def advance(self, step):
        for chunk in range(self.chunks):
            for way in range(2):
                self.copy(step - 1, chunk, way).wait_recv()
                self.copy(step, chunk, way).start()

    def arrive(self):
        last = self.size - 2
        for chunk in range(self.chunks):
            for way in range(2):
                self.copy(last, chunk, way).wait_recv()

    def finish(self):
        self.arrive()
        self.settle()

    def settle(self):
        def drain(step, carry):
            for chunk in range(self.chunks):
                for way in range(2):
                    self.copy(step, chunk, way).wait_send()
            return carry

        lax.fori_loop(0, self.size - 1, drain, 0)
        self.kept().wait()


def ring_parts(x, chunks):
    return x.reshape(2, chunks, x.shape[0] // (2 * chunks), x.shape[1])


def ring_sems(size, chunks):
    return [
        pltpu.SemaphoreType.DMA((size - 1, chunks, 2)),
        pltpu.SemaphoreType.DMA((size - 1, chunks, 2)),
        pltpu.SemaphoreType.DMA,
    ]


def front_kernel(
    widths,
    head_size,
    size,
    groups,
    inner,
    x_ref,
    w_ref,
    cot_ref,
    shard_ref,
    conv_ref,
    conv_bias_ref,
    params_ref,
    out_gain_ref,
    spread_ref,
    tri_ref,
    rows_ref,
    weights_ref,
    proj_ref,
    y_ref,
    enter_ref,
    normed_ref,
    turned_ref,
    grad_ref,
    gain_acc,
    taps_ref,
    heads_ref,
    wide_ref,
    branch_ref,
    part_ref,
    weights,
    projected,
    taken,
    state,
    ext,
    halo,
    gated,
    out_grad,
    y_held,
    enter_held,
    out_rows,
    out_turned,
    sums,
    landing,
    weight_send,
    weight_recv,
    weight_local,
    take_sem,
    proj_sem,
    held_sem,
    shard_send,
    shard_recv,
    shard_local,
    pair_send,
    pair_recv,
    *ring_refs,
):
    bf16, f32 = jnp.bfloat16, jnp.float32
    me, group, pos, right, left = neighbours(size)
    rows, lw = gated.shape[2:]
    depth = weights.shape[2]
    peers = [(other, group) for other in others(me, size)]
    mates = [(me, other) for other in others(group, groups)]
    sibling = (me, group + 1 - 2 * lax.rem(group, 2))
    across = (me, lax.rem(group + 2, groups))
    per_owner = size // groups
    chosen = lax.rem(me, per_owner)
    owner = me // per_owner
    greet(mates + peers)
    ring = RingGather(size, x_ref, rows_ref, *ring_refs[0:3])
    cot_ring = RingGather(size, cot_ref, branch_ref, *ring_refs[3:6])
    ring.start()
    bc = widths[1]
    used = w_ref.shape[0] - 2 * inner
    lane_at = pl.multiple_of(me * lw, 128)
    spans = (
        (pl.ds(lane_at, lw), pl.ds(0, lw)),
        (pl.ds(pl.multiple_of(inner + me * lw, 128), lw), pl.ds(lw, lw)),
        (pl.ds(2 * inner, used), pl.ds(2 * lw, used)),
    )
    sent = [
        push(
            w_ref.at[here],
            weights.at[group, there],
            weight_send.at[k, part],
            weight_recv.at[k, part],
            mate,
        )
        for k, mate in enumerate(mates)
        for part, (here, there) in enumerate(spans)
    ]
    for copy in sent:
        copy.start()
    kept = [
        pltpu.make_async_copy(w_ref.at[here], weights.at[group, there], weight_local.at[part])
        for part, (here, there) in enumerate(spans)
    ]
    for copy in kept:
        copy.start()
    blank = weights.shape[1] - 2 * lw - used
    for part in range(groups):
        weights[part, 2 * lw + used :, :] = jnp.zeros((blank, depth), bf16)
    heads_here = lw // head_size
    head_start = me * heads_here
    taps_ref[...] = jnp.zeros_like(taps_ref)
    taps_ref[0:KW, :lw] = conv_ref[:, pl.ds(lane_at, lw)]
    taps_ref[0:KW, lw:] = conv_ref[:, inner:]
    taps_ref[KW : KW + 1, :lw] = conv_bias_ref[:, pl.ds(lane_at, lw)]
    taps_ref[KW : KW + 1, lw:] = conv_bias_ref[:, inner:]
    params = pltpu.roll(params_ref[...], lax.rem(128 - head_start, 128), 1)
    params = jnp.where(
        lax.broadcasted_iota(jnp.int32, params.shape, 1) < heads_here, params, 0.0
    )
    at_row = lax.broadcasted_iota(jnp.int32, params.shape, 0)
    at_lane = lax.broadcasted_iota(jnp.int32, params.shape, 1)
    slopes = jnp.where(at_lane < heads_here, -jnp.exp(params), 0.0)
    heads_ref[...] = jnp.where(at_row == 1, slopes, params)
    wide_ref[...] = jnp.zeros_like(wide_ref)
    wide_ref[0:1, :] = out_gain_ref[:, pl.ds(lane_at, lw)]
    wide_ref[1:2, :] = dot(params, spread_ref[...].astype(f32), 1, 0, HIGHEST)[2:3, :]

    def shards(step, offset=0):
        at = lax.rem(chosen + offset, per_owner)
        held_by = across[1] if step == 2 else group
        source = part_ref.at[held_by, at] if step == 2 else shard_ref.at[at]
        return push(
            source,
            part_ref.at[held_by, at],
            shard_send.at[step, offset],
            shard_recv.at[step, offset],
            across if step == 0 else sibling,
        )

    def block_of(pair, way):
        return ring_index((pos - pair + size) % size if way == 0 else (pos + pair) % size, size)

    def stream(source_ref, landed_ref, low, high, compute, own=False):
        def take(pair, slot, way):
            source = source_ref.at[way] if own else landed_ref.at[block_of(pair, way), way]
            return pltpu.make_async_copy(source, taken.at[slot, way], take_sem.at[slot, way])

        for way in range(2):
            take(low, lax.rem(low, 2), way).start()

        def one(pair, carry):
            slot = lax.rem(pair, 2)
            for way in range(2):
                take(pair, slot, way).wait()

            @pl.when(pair + 1 < high)
            def _():
                for way in range(2):
                    take(pair + 1, 1 - slot, way).start()

            compute(pair, slot)
            return carry

        lax.fori_loop(low, high, one, 0)

    def put(pair, way):
        block = block_of(pair, way)
        return pltpu.make_async_copy(
            projected.at[block, way], proj_ref.at[block, way], proj_sem.at[pair, way]
        )

    def project(pair, slot):
        for way in range(2):
            x = taken[slot, way].reshape(rows, taken.shape[4])
            total = None
            for part in range(groups):
                term = dot(x[:, part * depth : (part + 1) * depth], weights[part], 1, 1)
                total = term if total is None else total + term
            projected[block_of(pair, way), way] = total.astype(bf16)
            put(pair, way).start()

    def advance(step, carry):
        ring.advance(step)
        return carry

    def turns(turn, count):
        return 1 + (turn * (size - 2)) // count, 1 + ((turn + 1) * (size - 2)) // count

    middle = size // 2 + 1
    lax.fori_loop(1, middle, advance, 0)
    for copy in kept:
        copy.wait()
    for copy in sent:
        copy.wait_recv()
    flushed = pltpu.make_async_copy(weights, weights_ref, weight_local.at[0])
    flushed.start()
    shards(0).start()
    shards(1).start()
    stream(x_ref, rows_ref, 0, 1, project, own=True)

    def late(step, carry):
        ring.advance(step)
        stream(x_ref, rows_ref, *turns(step - middle, size - 1 - middle), project)
        return carry

    lax.fori_loop(middle, size - 2, late, 0)
    ring.advance(size - 2)
    cot_ring.start()
    stream(x_ref, rows_ref, *turns(size - 2 - middle, size - 1 - middle), project)
    ring.arrive()
    stream(x_ref, rows_ref, size - 1, size, project)
    cot_ring.advance(1)

    def keep(index, slot):
        seq, chunk = index // size, lax.rem(index, size)
        return [
            pltpu.make_async_copy(y_held.at[slot, 0], y_ref.at[chunk, seq], held_sem.at[slot, 0]),
            pltpu.make_async_copy(
                enter_held.at[slot, 0], enter_ref.at[chunk, seq], held_sem.at[slot, 1]
            ),
        ]

    def scan(index, carry):
        seq, chunk = index // size, lax.rem(index, size)
        slot = lax.rem(index, 2)

        @pl.when(index >= 2)
        def _():
            for copy in keep(index - 2, slot):
                copy.wait()

        forward_chunk(
            widths,
            head_size,
            head_start,
            chunk == 0,
            projected.at[pl.ds(chunk, 1), pl.ds(seq, 1)],
            taps_ref,
            heads_ref,
            wide_ref,
            spread_ref,
            tri_ref,
            gated.at[chunk, seq],
            y_held.at[pl.ds(slot, 1)],
            enter_held.at[pl.ds(slot, 1)],
            state,
            ext,
            halo,
        )
        for copy in keep(index, slot):
            copy.start()

        @pl.when(index == size + 2)
        def _():
            cot_ring.advance(2)

        return carry

    lax.fori_loop(0, 2 * size, scan, 0)
    first, second, third = (shards(step) for step in range(3))
    first.wait_recv()
    third.start()
    for offset in range(1, per_owner):
        shards(0, offset).start()
        shards(1, offset).start()
    second.wait_recv()
    cot_ring.advance(3)
    third.wait_recv()

    @pl.when(owner == group)
    def _():
        loaded = pltpu.make_async_copy(shard_ref.at[chosen], out_rows, shard_local)
        loaded.start()
        loaded.wait()

    @pl.when(owner != group)
    def _():
        loaded = pltpu.make_async_copy(part_ref.at[owner, chosen], out_rows, shard_local)
        loaded.start()
        loaded.wait()

    out_turned[...] = out_rows[...].T
    ones = jnp.ones((8, lw), bf16)

    def compute(pair, slot):
        for way in range(2):
            block = block_of(pair, way)
            values = dot(taken[slot, way].reshape(rows, taken.shape[4]), out_turned[...], 1, 0)
            out_grad[block, way] = values
            here = gated[block, way].astype(f32)
            weighted = values * wide_ref[0:1, :] * here
            at = pl.ds(block * 2 + way, 1)
            sums[0, at, :] = dot(ones, (here * here).astype(bf16), 1, 1)[0:1, :]
            sums[1, at, :] = dot(ones, weighted.astype(bf16), 1, 1)[0:1, :]

    stream(cot_ref, branch_ref, 0, 1, compute, own=True)
    stream(cot_ref, branch_ref, *turns(0, size - 4), compute)

    def cot_late(step, carry):
        cot_ring.advance(step)
        stream(cot_ref, branch_ref, *turns(step - 3, size - 4), compute)
        return carry

    lax.fori_loop(4, size - 1, cot_late, 0)
    cot_ring.arrive()
    stream(cot_ref, branch_ref, size - 1, size, compute)
    copies = [
        push(sums, landing.at[k], pair_send.at[k], pair_recv.at[k], peer)
        for k, peer in enumerate(peers)
    ]
    for copy in copies:
        copy.start()
    total = sums[...]
    for k, copy in enumerate(copies):
        copy.wait_recv()
        total = total + landing[k]
    scale = lax.rsqrt(total[0] / inner + EPS)
    pull = scale * scale * scale * (total[1] / inner)
    fill = jnp.zeros((128 - 2 * size, rows), f32)
    scale_turned = jnp.concatenate([scale, fill]).T
    pull_turned = jnp.concatenate([pull, fill]).T
    lane = lax.broadcasted_iota(jnp.int32, (rows, 128), 1)
    gain_acc[...] = jnp.zeros_like(gain_acc)

    def finish(block, carry):
        for way in range(2):
            mask = lane == block * 2 + way
            by = jnp.sum(jnp.where(mask, scale_turned, 0.0), axis=1, keepdims=True)
            less = jnp.sum(jnp.where(mask, pull_turned, 0.0), axis=1, keepdims=True)
            here = gated[block, way].astype(f32)
            values = out_grad[block, way]
            scaled = here * by
            normed = (scaled * wide_ref[0:1, :]).astype(bf16)
            normed_ref[block, way] = normed
            turned_ref[block, :, way * rows : (way + 1) * rows] = normed.T
            grad_ref[block, way] = (values * wide_ref[0:1, :] * by - here * less).astype(bf16)
            gain_acc[0:1, :] += jnp.sum(values * scaled, axis=0, keepdims=True)
        return carry

    lax.fori_loop(0, size, finish, 0)
    for offset in range(1, per_owner):
        shards(0, offset).wait_recv()
        shards(2, offset).start()
    for copy in sent + copies + [first, second, third]:
        copy.wait_send()
    flushed.wait()
    for index in (2 * size - 2, 2 * size - 1):
        for copy in keep(index, index % 2):
            copy.wait()

    def settle(pair, carry):
        for way in range(2):
            put(pair, way).wait()
        return carry

    lax.fori_loop(0, size, settle, 0)
    ring.settle()
    cot_ring.settle()
    for offset in range(1, per_owner):
        shards(1, offset).wait_recv()
        shards(2, offset).wait_recv()
        for step in range(3):
            shards(step, offset).wait_send()


def front(x, weight, cot, shard, params, inner, widths, head_size, collective_id):
    size, groups = lax.axis_size("seq"), lax.axis_size("wa")
    parts, cot_parts = ring_parts(x, 2), ring_parts(cot, 2)
    depth = weight.shape[1]
    rows = x.shape[0] // 2
    width = x.shape[1]
    lw, bc = widths
    cols = 2 * lw + bc + 128
    per_owner = size // groups
    bf16, f32, DMA, vmem = jnp.bfloat16, jnp.float32, pltpu.SemaphoreType.DMA, pltpu.VMEM
    whole = (size, 2, rows, lw)
    shape = jax.ShapeDtypeStruct
    return pl.pallas_call(
        functools.partial(front_kernel, widths, head_size, size, groups, inner),
        out_shape=[
            shape((size,) + parts.shape, bf16),
            shape((groups, cols, depth), bf16),
            shape((size, 2, rows, cols), bf16),
            shape(whole, bf16),
            shape((size, 2, lw, bc // 2), bf16),
            shape(whole, bf16),
            shape((size, lw, 2 * rows), bf16),
            shape(whole, bf16),
            shape((8, lw), f32),
            shape((8, lw + bc), f32),
            shape((8, 128), f32),
            shape((8, lw), f32),
            shape((size,) + parts.shape, bf16),
            shape((groups, per_owner, lw, width), bf16),
        ],
        in_specs=[ANY] * 4 + [VMEM] * 6,
        out_specs=[ANY] * 5 + [VMEM] * 7 + [ANY] * 2,
        scratch_shapes=[
            vmem((groups, cols, depth), bf16),
            vmem((size, 2, rows, cols), bf16),
            vmem((2,) + parts.shape, bf16),
            vmem((lw, bc // 2), f32),
            vmem((rows + 8, lw + bc), f32),
            vmem((8, lw + bc), f32),
            vmem(whole, bf16),
            vmem(whole, f32),
            vmem((2, 1, rows, lw), bf16),
            vmem((2, 1, lw, bc // 2), bf16),
            vmem((lw, width), bf16),
            vmem((width, lw), bf16),
            vmem((2, 2 * size, rows), f32),
            vmem((size - 1, 2, 2 * size, rows), f32),
            DMA((groups - 1, 3)),
            DMA((groups - 1, 3)),
            DMA((3,)),
            DMA((2, 2)),
            DMA((size, 2)),
            DMA((2, 2)),
            DMA((3, per_owner)),
            DMA((3, per_owner)),
            DMA,
            DMA((size - 1,)),
            DMA((size - 1,)),
        ]
        + ring_sems(size, 2)
        + ring_sems(size, 2),
        compiler_params=comm_params(collective_id, 62),
        name="front",
    )(parts, weight, cot_parts, shard, *params)


def finish_kernel(
    size,
    groups,
    counts,
    grad_ref,
    weight_ref,
    normed_ref,
    turned_ref,
    out_ref,
    branch_grad_ref,
    tokens_ref,
    scale_ref,
    taps_ref,
    gain_ref,
    heads_ref,
    swapped_ref,
    shard_ref,
    out_full_ref,
    rows_ref,
    gathered_ref,
    pieces_ref,
    owned_ref,
    shared_out,
    small_out,
    branch_ref,
    landing,
    slots,
    first,
    parts,
    total,
    taken,
    turned,
    out_total,
    out_parts,
    out_landing,
    out_taken,
    piece,
    main,
    shared,
    shared_land,
    shared_sum,
    small,
    small_land,
    send_sem,
    recv_sem,
    part_send,
    part_recv,
    take_sem,
    out_send,
    out_recv,
    owned_send,
    owned_recv,
    owned_local,
    pair_send,
    pair_recv,
    mate_send,
    mate_recv,
    *ring_refs,
):
    me, group, pos, right, left = neighbours(size)
    mates = [(me, index) for index in others(group, groups)]
    peers = [(index, group) for index in others(me, size)]
    tiles, rows, tile = slots.shape[2:]
    cols = total.shape[0]
    bf16, f32 = jnp.bfloat16, jnp.float32
    out_ring = RingGather(size, piece, pieces_ref, *ring_refs[0:3])
    main_ring = RingGather(size, main, gathered_ref, *ring_refs[3:6])
    shared_ring = RingGather(size, shared_sum, shared_out, *ring_refs[6:9])
    small_ring = RingGather(size, small, small_out, *ring_refs[9:12])
    fetch_sem, weights_taken, held, held_sem, out_turned = ring_refs[12:17]
    weight_held, swapped_held, load_sem = ring_refs[17:20]
    loads = [
        pltpu.make_async_copy(weight_ref.at[part], weight_held.at[part], load_sem.at[part])
        for part in range(groups)
    ]
    swapped_load = pltpu.make_async_copy(swapped_ref, swapped_held, load_sem.at[groups])

    def target(step, way):
        shift = (pos - 1 - step + 2 * size) if way == 0 else (pos + 1 + step)
        return ring_index(shift % size, size)

    def fetch(step, way):
        slot = lax.rem(step, 2)
        return pltpu.make_async_copy(
            grad_ref.at[target(step, way), way], held.at[slot, way], held_sem.at[slot, way]
        )

    def term(step, way, at):
        return dot(held[lax.rem(step, 2), way], weight_held[at], 1, 0)

    def hop(step, way, at, source):
        return push(
            source,
            slots.at[step, way, at],
            send_sem.at[step, way, at],
            recv_sem.at[step, way, at],
            right if way == 0 else left,
        )

    def begin(at, carry):
        for way in range(2):
            first[way, at] = term(0, way, at).astype(bf16)
            hop(0, way, at, first.at[way, at]).start()
        return carry

    for way in range(2):
        fetch(0, way).start()
    for copy in loads:
        copy.start()
    for way in range(2):
        fetch(1, way).start()
    swapped_load.start()
    greet(mates + peers)
    for way in range(2):
        fetch(0, way).wait()
    for part in range(groups):
        loads[part].wait()
        begin(part, 0)

    def mate_of(offset):
        return lax.rem(group + offset, groups)

    def send_part(offset):
        return push(
            parts.at[offset - 1],
            landing.at[offset - 1],
            part_send.at[offset - 1],
            part_recv.at[offset - 1],
            (me, mate_of(offset)),
        )

    def send_out(offset):
        return push(
            out_parts.at[mate_of(offset)],
            out_landing.at[offset - 1],
            out_send.at[offset - 1],
            out_recv.at[offset - 1],
            (me, mate_of(offset)),
        )

    def stream(count, take, use):
        for copy in take(0, 0):
            copy.start()

        def one(block, carry):
            slot = lax.rem(block, 2)

            @pl.when(block + 1 < count)
            def _():
                for copy in take(block + 1, 1 - slot):
                    copy.start()

            for copy in take(block, slot):
                copy.wait()
            use(block, slot)
            return carry

        lax.fori_loop(0, count, one, 0)

    def tokens_of(block):
        return pl.ds(pl.multiple_of(block * 2 * rows, 2 * rows), 2 * rows)

    def weight_part(offset):
        columns = pl.ds(pl.multiple_of(mate_of(offset) * tile, tile), tile)

        def take(block, slot):
            return [
                pltpu.make_async_copy(
                    normed_ref.at[block, :, :, columns], taken.at[slot], take_sem.at[slot, 0]
                ),
                pltpu.make_async_copy(
                    turned_ref.at[:, tokens_of(block)], turned.at[slot], take_sem.at[slot, 1]
                ),
            ]

        def use(block, slot):
            values = dot(turned[slot], taken[slot].reshape(2 * rows, tile), 1, 0)

            @pl.when(block == 0)
            def _():
                total[...] = values

            @pl.when(block > 0)
            def _():
                total[...] += values

        stream(size, take, use)

    def out_part(low, count):
        piece_rows = out_parts.shape[1]

        def take(block, slot):
            return [
                pltpu.make_async_copy(
                    branch_grad_ref.at[tokens_of(low + block)],
                    out_taken.at[slot],
                    take_sem.at[slot, 0],
                ),
                pltpu.make_async_copy(
                    out_ref.at[low + block], out_turned.at[slot], take_sem.at[slot, 1]
                ),
            ]

        def use(block, slot):
            values = dot(out_turned[slot], out_taken[slot], 1, 0)

            @pl.when(low + block == 0)
            def _():
                out_total[...] = values

            @pl.when(low + block > 0)
            def _():
                out_total[...] += values

        stream(count, take, use)

    def out_sends():
        piece_rows = out_parts.shape[1]
        for index in range(groups):
            out_parts[index] = out_total[index * piece_rows : (index + 1) * piece_rows].astype(bf16)
        for offset in range(1, groups):
            send_out(offset).start()

    def advance(step, carry):
        for way in range(2):
            fetch(step + 1, way).start()
        for way in range(2):
            fetch(step, way).wait()

        def one(at, inner):
            for way in range(2):
                own = term(step, way, at)
                hop(step - 1, way, at, first.at[way, at]).wait_recv()
                slots[step - 1, way, at] = (slots[step - 1, way, at].astype(f32) + own).astype(bf16)
                hop(step, way, at, slots.at[step - 1, way, at]).start()
            return inner

        lax.fori_loop(0, tiles, one, 0)

        @pl.when(step < 3)
        def _():
            out_part((step - 1) * (size // 2), size // 2)

        @pl.when(step == 2)
        def _():
            out_sends()

        @pl.when((step > 2) & (step <= groups + 2))
        def _():
            weight_part(step - 2)

        @pl.when((step > 2) & (step <= groups + 1))
        def _():
            parts[step - 3] = total[...].astype(bf16)
            send_part(step - 2).start()

        return carry

    lax.fori_loop(1, size - 1, advance, 0)
    for offset in range(1, groups):
        send_out(offset).wait_recv()
    summed = out_parts[group].astype(f32)
    for offset in range(1, groups):
        summed = summed + out_landing[offset - 1].astype(f32)
    piece[...] = summed.astype(bf16).reshape(piece.shape)
    out_ring.start()

    for way in range(2):
        fetch(size - 1, way).wait()

    def end(at, carry):
        columns = pl.ds(pl.multiple_of(at * tile, tile), tile)
        for way in range(2):
            own = term(size - 1, way, at)
            hop(size - 2, way, at, first.at[way, at]).wait_recv()
            rows_ref[way, :, columns] = slots[size - 2, way, at].astype(f32) + own
        return carry

    lax.fori_loop(0, tiles, end, 0)
    width = rows_ref.shape[2]
    own_width = gain_ref.shape[1]
    flat = jnp.zeros((1, width), f32)
    for way in range(2):
        values = tokens_ref[way].astype(f32) * scale_ref[way, :, 0:1]
        flat = flat + jnp.sum(rows_ref[way] * values, axis=0, keepdims=True)
    half = small.shape[2]
    listed = [
        taps_ref[k : k + 1, at : at + 128] for k in range(KW + 1) for at in range(0, own_width, 128)
    ]
    listed += [gain_ref[0:1, at : at + 128] for at in range(0, own_width, 128)]
    listed += [heads_ref[k : k + 1, :] for k in range(3)]
    listed += [
        taps_ref[k : k + 1, at : at + 128]
        for k in range(KW + 1)
        for at in range(own_width, taps_ref.shape[1], 128)
    ]
    listed += [flat[:, at : at + 128] for at in range(0, width, 128)]
    for at, row in enumerate(listed):
        small[at // half, 0, at % half : at % half + 1, :] = row
    small_in = [
        push(small, small_land.at[k], mate_send.at[k], mate_recv.at[k], mate)
        for k, mate in enumerate(mates)
    ]
    for copy in small_in:
        copy.start()

    def out_advance(step, carry):
        out_ring.advance(step)
        return carry

    lax.fori_loop(1, size // 2, out_advance, 0)
    fetched = []
    for offset in range(1, groups):
        send_part(offset).wait()
        fetched.append(
            pltpu.make_async_copy(
                landing.at[offset - 1], parts.at[offset - 1], fetch_sem.at[offset - 1]
            )
        )
        fetched[-1].start()
    for copy, part in zip(fetched, range(groups - 1)):
        copy.wait()
        total[...] += parts[part].astype(f32)
    main[...] = total[: counts[0]].astype(bf16).reshape(main.shape)
    shared[...] = total[counts[0] : counts[0] + counts[1]].astype(bf16).reshape(shared.shape)
    shared_in = [
        push(shared.at[peer[0]], shared_land.at[k], pair_send.at[k], pair_recv.at[k], peer)
        for k, peer in enumerate(peers)
    ]
    lax.fori_loop(size // 2, size - 1, out_advance, 0)
    for copy in shared_in:
        copy.start()
    main_ring.start()
    out_ring.finish()
    owned = [
        push(pieces_by_owner(pieces_ref, mate[1], groups), owned_ref.at[group], owned_send.at[k], owned_recv.at[k], mate)
        for k, mate in enumerate(mates)
    ]
    kept = pltpu.make_async_copy(
        pieces_by_owner(pieces_ref, group, groups), owned_ref.at[group], owned_local
    )
    for copy in owned:
        copy.start()
    kept.start()
    main_ring.advance(1)
    for copy in small_in + shared_in:
        copy.wait()
    values = small[...]
    for k in range(groups - 1):
        values = values + small_land[k]
    small[...] = values
    values = shared[me].astype(f32)
    for k in range(size - 1):
        values = values + shared_land[k].astype(f32)
    across = shared_sum.shape[3]
    for way in range(2):
        shared_sum[way, 0] = values[:, way * across : (way + 1) * across].astype(bf16)
    small_ring.start()
    shared_ring.start()
    branch_ref[...] = jnp.zeros_like(branch_ref)

    per_owner = size // groups

    def weight_take(block, slot):
        owner, at = block // per_owner, lax.rem(block, per_owner)

        @pl.when(owner == group)
        def _():
            pltpu.make_async_copy(
                shard_ref.at[at], weights_taken.at[slot], take_sem.at[slot, 0]
            ).start()

        @pl.when(owner != group)
        def _():
            pltpu.make_async_copy(
                out_full_ref.at[owner, at], weights_taken.at[slot], take_sem.at[slot, 0]
            ).start()

    def multiply(block, carry):
        slot = lax.rem(block, 2)

        @pl.when(block + 1 < size)
        def _():
            weight_take(block + 1, 1 - slot)

        pltpu.make_async_copy(
            shard_ref.at[0], weights_taken.at[slot], take_sem.at[slot, 0]
        ).wait()
        branch_ref[...] += dot(swapped_held[block], weights_taken[slot], 1, 0)
        return carry

    weight_take(0, 0)
    swapped_load.wait()
    count = size - 3

    def main_advance(step, carry):
        main_ring.advance(step)
        small_ring.advance(step - 1)
        shared_ring.advance(step - 1)
        lax.fori_loop(((step - 2) * size) // count, ((step - 1) * size) // count, multiply, 0)
        return carry

    lax.fori_loop(2, size - 1, main_advance, 0)
    small_ring.advance(size - 2)
    shared_ring.advance(size - 2)

    def drain(step, carry):
        def one(at, inner):
            for way in range(2):
                hop(step, way, at, first.at[way, at]).wait_send()
            return inner

        return lax.fori_loop(0, tiles, one, carry)

    lax.fori_loop(0, size - 1, drain, 0)
    for offset in range(1, groups):
        send_out(offset).wait_send()
    main_ring.finish()
    small_ring.finish()
    shared_ring.finish()
    for copy in owned:
        copy.wait()
    kept.wait()


def pieces_by_owner(pieces_ref, owner, groups):
    count = pieces_ref.shape[0] // groups
    return pieces_ref.at[pl.ds(owner * count, count)]


def finish(
    grad,
    weight,
    normed,
    turned,
    out,
    branch_grad,
    tokens,
    scale,
    taps,
    gain,
    heads,
    swapped,
    shard,
    out_full,
    counts,
    collective_id,
):
    size, groups = lax.axis_size("seq"), lax.axis_size("wa")
    _, ways, rows, cols = grad.shape
    tile, tiles = weight.shape[2], groups
    width = tiles * tile
    lw = out.shape[1]
    bc = taps.shape[1] - lw
    piece_rows = lw // groups
    per_owner = size // groups
    bf16, f32, DMA = jnp.bfloat16, jnp.float32, pltpu.SemaphoreType.DMA
    total_small = ((KW + 2) * lw + (KW + 1) * bc + width) // 128 + 3
    half = -(-total_small // 16) * 8
    piece = (2, 2, piece_rows // 4, width)
    main = (2, 2, counts[0] // 4, tile)
    shared_rows = counts[1] // size
    both = (2, 1, shared_rows, tile // 2)
    small_shape = (2, 1, half, 128)
    vmem = pltpu.VMEM
    return pl.pallas_call(
        functools.partial(finish_kernel, size, groups, counts),
        out_shape=[
            jax.ShapeDtypeStruct((ways, rows, width), f32),
            jax.ShapeDtypeStruct((size,) + main, bf16),
            jax.ShapeDtypeStruct((size,) + piece, bf16),
            jax.ShapeDtypeStruct((groups, per_owner) + piece, bf16),
            jax.ShapeDtypeStruct((size,) + both, bf16),
            jax.ShapeDtypeStruct((size,) + small_shape, f32),
            jax.ShapeDtypeStruct((ways * rows, width), f32),
            jax.ShapeDtypeStruct((groups - 1, cols, tile), bf16),
        ],
        in_specs=[ANY] * 6 + [VMEM] * 5 + [ANY] * 3,
        out_specs=[VMEM, ANY, ANY, ANY, ANY, ANY, VMEM, ANY],
        scratch_shapes=[
            vmem((size - 1, 2, tiles, rows, tile), bf16),
            vmem((2, tiles, rows, tile), bf16),
            vmem((groups - 1, cols, tile), bf16),
            vmem((cols, tile), f32),
            vmem((2, ways, rows, tile), bf16),
            vmem((2, cols, 2 * rows), bf16),
            vmem((lw, width), f32),
            vmem((groups, piece_rows, width), bf16),
            vmem((groups - 1, piece_rows, width), bf16),
            vmem((2, 2 * rows, width), bf16),
            vmem(piece, bf16),
            vmem(main, bf16),
            vmem((size, shared_rows, tile), bf16),
            vmem((size - 1, shared_rows, tile), bf16),
            vmem(both, bf16),
            vmem(small_shape, f32),
            vmem((groups - 1,) + small_shape, f32),
            DMA((size - 1, 2, tiles)),
            DMA((size - 1, 2, tiles)),
            DMA((groups - 1,)),
            DMA((groups - 1,)),
            DMA((2, 2)),
            DMA((groups - 1,)),
            DMA((groups - 1,)),
            DMA((groups - 1,)),
            DMA((groups - 1,)),
            DMA,
            DMA((size - 1,)),
            DMA((size - 1,)),
            DMA((groups - 1,)),
            DMA((groups - 1,)),
        ]
        + ring_sems(size, 2)
        + ring_sems(size, 2)
        + ring_sems(size, 1)
        + ring_sems(size, 1)
        + [DMA((groups - 1,)), vmem((2, lw, width), bf16)]
        + [vmem((2, 2, rows, cols), bf16), DMA((2, 2)), vmem((2, lw, 2 * rows), bf16)]
        + [vmem(weight.shape, bf16), vmem(swapped.shape, bf16), DMA((groups + 1,))],
        compiler_params=comm_params(collective_id, 63),
        name="finish",
    )(
        grad,
        weight,
        normed,
        turned,
        out,
        branch_grad,
        tokens,
        scale,
        taps,
        gain,
        heads,
        swapped,
        shard,
        out_full,
    )


def assemble_kernel(blocks, gathered_ref, tail_ref, o_ref):
    @pl.when(pl.program_id(0) < blocks)
    def _():
        o_ref[...] = gathered_ref[0, 0].reshape(o_ref.shape).astype(jnp.float32)

    @pl.when(pl.program_id(0) == blocks)
    def _():
        o_ref[...] = tail_ref[...].astype(jnp.float32)


def assemble_in(gathered, tail):
    size, ways, chunks, rows, width = gathered.shape
    step = chunks * rows
    blocks = size * ways
    total = blocks * step + tail.shape[0]
    steps = blocks + 1
    pad = -tail.shape[0] % step
    if tail.shape[0] > step:
        out = jnp.swapaxes(gathered, 0, 1).reshape(blocks * step, width)
        return jnp.concatenate([out, tail]).astype(jnp.float32)
    return pl.pallas_call(
        functools.partial(assemble_kernel, blocks),
        grid=(steps,),
        in_specs=[
            pl.BlockSpec(
                (1, 1, chunks, rows, width),
                lambda i: (lax.rem(i, size), jnp.minimum(i // size, ways - 1), 0, 0, 0),
            ),
            pl.BlockSpec((step, width), lambda i: (0, 0)),
        ],
        out_specs=pl.BlockSpec((step, width), lambda i: (i, 0)),
        out_shape=jax.ShapeDtypeStruct((total, width), jnp.float32),
        compiler_params=pltpu.CompilerParams(vmem_limit_bytes=32 * 2**20),
        name="assemble_in",
    )(gathered, jnp.pad(tail, ((0, pad), (0, 0))))


def widen_kernel(
    widths, heads, x_ref, small_ref, o_ref, conv_ref, bias_ref, gain_ref, heads_ref, norm_ref
):
    o_ref[...] = x_ref[0, 0].astype(jnp.float32)

    @pl.when((pl.program_id(0) == 0) & (pl.program_id(1) == 0))
    def _():
        lw, bc = widths
        size = small_ref.shape[0]
        tiles, shared = lw // 128, bc // 128
        inner = size * lw
        found = jnp.zeros((8, 128), jnp.float32)
        first = (KW + 2) * tiles
        for block in range(size):
            for tile in range(tiles):
                at = slice(block * lw + tile * 128, block * lw + (tile + 1) * 128)
                for k in range(KW):
                    row = k * tiles + tile
                    conv_ref[k : k + 1, at] = small_ref[block, row : row + 1, :]
                row = KW * tiles + tile
                bias_ref[:, at] = small_ref[block, row : row + 1, :]
                row = (KW + 1) * tiles + tile
                gain_ref[:, at] = small_ref[block, row : row + 1, :]
            found = found + pltpu.roll(small_ref[block, first : first + 8, :], block * heads, 1)
        heads_ref[...] = found
        total = small_ref[0]
        for block in range(1, size):
            total = total + small_ref[block]
        row = first + 3
        for k in range(KW + 1):
            for tile in range(shared):
                at = slice(inner + tile * 128, inner + (tile + 1) * 128)
                if k < KW:
                    conv_ref[k : k + 1, at] = total[row : row + 1, :]
                else:
                    bias_ref[:, at] = total[row : row + 1, :]
                row += 1
        for tile in range(norm_ref.shape[1] // 128):
            norm_ref[:, tile * 128 : (tile + 1) * 128] = total[row : row + 1, :]
            row += 1


def assemble_out(owned, small, widths, heads):
    groups, count, rows, width = owned.shape
    size = small.shape[0]
    lw, bc = widths
    inner = size * lw
    f32 = jnp.float32
    shapes = [(KW, inner + bc), (1, inner + bc), (1, inner), (8, 128), (1, width)]
    return pl.pallas_call(
        functools.partial(widen_kernel, widths, heads),
        grid=(count, groups),
        in_specs=[
            pl.BlockSpec((1, 1, rows, width), lambda t, g: (g, t, 0, 0)),
            pl.BlockSpec(small.shape, lambda t, g: (0, 0, 0)),
        ],
        out_specs=[pl.BlockSpec((rows, width), lambda t, g: (t * groups + g, 0))]
        + [pl.BlockSpec(s, lambda t, g: (0, 0)) for s in shapes],
        out_shape=[jax.ShapeDtypeStruct((groups * count * rows, width), f32)]
        + [jax.ShapeDtypeStruct(s, f32) for s in shapes],
        name="assemble_out",
    )(owned, small)


def body(
    tokens,
    lengths,
    norm_gain,
    in_weight,
    conv_weight,
    conv_bias,
    dt_bias,
    a_log,
    skip_gain,
    out_gain,
    out_weight,
    cotangent,
):
    seqs_here, slot_rows, width = tokens.shape
    row_count = seqs_here * slot_rows
    inner_width = out_gain.shape[0]
    channels = conv_bias.shape[0]
    bc_width = channels - inner_width
    state_size = bc_width // 2
    head_count = dt_bias.shape[0]
    head_size = inner_width // head_count
    seq_devices = lax.axis_size("seq")
    group_devices = lax.axis_size("wa")
    seq_index = lax.axis_index("seq")
    length = seq_devices * slot_rows
    local_heads = head_count // seq_devices
    local_width = local_heads * head_size
    channel_start = seq_index * local_width
    head_start = seq_index * local_heads
    bf16, f32 = jnp.bfloat16, jnp.float32

    def take(array, start, size, axis):
        return lax.dynamic_slice_in_dim(array, start, size, axis)

    positions = seq_index * slot_rows + jnp.arange(slot_rows)
    valid_rows = (positions[None, :] < lengths[:, None]).astype(f32).reshape(row_count, 1)
    flat_tokens = tokens.reshape(row_count, width).astype(f32)
    in_scale = row_scale(flat_tokens)
    normed = (flat_tokens * in_scale * norm_gain).astype(bf16)
    cot_rows = cotangent.reshape(row_count, width)

    blocks = (seq_devices, seqs_here, slot_rows)
    params = jnp.pad(jnp.stack([dt_bias, a_log, skip_gain]), ((0, 5), (0, 128 - head_count)))
    spread, fold, tri, upper = scan_tables(slot_rows, local_width, head_size)
    widths = (local_width, bc_width)
    per_owner = seq_devices // group_devices
    (
        normed_all,
        in_columns,
        projected,
        y_heads,
        entering,
        normed_out,
        turned_out,
        gated_grad,
        gain_sum,
        taps,
        heads,
        wide,
        branch_grad,
        out_full,
    ) = front(
        normed,
        in_weight.T,
        cot_rows * valid_rows.astype(bf16),
        out_weight.reshape(per_owner, local_width, width),
        (conv_weight, conv_bias[None], params, out_gain[None], spread, tri),
        inner_width,
        widths,
        head_size,
        0,
    )
    normed_out = normed_out.reshape(-1, local_width)
    branch_grad = branch_grad.reshape(-1, width)
    swapped = lax.all_to_all(
        normed_out.reshape(seq_devices, row_count, local_width), "seq", 0, 0, tiled=True
    )
    proj_grad, turned_grad, taps_sum, _, head_sum = scan_backward(
        projected,
        y_heads,
        entering,
        gated_grad,
        taps,
        heads,
        wide,
        spread,
        fold,
        tri,
        upper,
        widths,
        head_size,
    )
    columns_here = proj_grad.shape[3]
    proj_grad = proj_grad.reshape(-1, columns_here)
    in_rows = in_weight.shape[0]
    shared_count = bc_width + head_count
    shared_rows = shared_count // seq_devices
    normed_grad, gathered, _, owned, shared_all, small_all, branch, _ = finish(
        proj_grad.reshape(blocks + (columns_here,)),
        in_columns,
        normed_all.reshape(blocks + (width,)),
        turned_grad,
        turned_out,
        branch_grad,
        tokens,
        jnp.broadcast_to(in_scale.reshape(seqs_here, slot_rows, 1), (seqs_here, slot_rows, 128)),
        taps_sum,
        gain_sum,
        head_sum,
        swapped,
        out_weight.reshape(per_owner, local_width, width),
        out_full,
        (2 * local_width, shared_count),
        2,
    )
    normed_grad = normed_grad.reshape(row_count, width)
    token_grad = norm_backward(flat_tokens, in_scale, norm_gain, normed_grad)
    token_grad = token_grad + cot_rows.astype(f32)
    owned = owned.reshape(
        group_devices, per_owner, local_width // group_devices, width
    )
    shared_all = shared_all.reshape(seq_devices, 2, shared_rows, in_rows // 2)
    small_all = small_all.reshape(seq_devices, -1, 128)
    mixed_out = (flat_tokens + valid_rows * branch).astype(bf16).reshape(tokens.shape)
    tail = jnp.transpose(shared_all, (0, 2, 1, 3)).reshape(shared_count, in_rows)
    in_weight_grad = assemble_in(gathered, tail).T
    out_weight_grad, conv_weight_grad, conv_bias_grad, gain_grad, head_all, norm_grad = (
        assemble_out(owned, small_all, widths, local_heads)
    )
    return (
        mixed_out,
        token_grad.reshape(tokens.shape),
        norm_grad[0],
        in_weight_grad,
        conv_weight_grad,
        conv_bias_grad[0],
        head_all[0, :head_count],
        head_all[1, :head_count],
        head_all[2, :head_count],
        gain_grad[0],
        out_weight_grad,
    )


def solution(mesh):
    placed = (
        P("wa", "seq", None),
        P("wa"),
        P(),
        P("wa", None),
        P(),
        P(),
        P(),
        P(),
        P(),
        P(),
        P("wa", None),
        P("wa", "seq", None),
    )
    return jax.shard_map(
        body,
        mesh=mesh,
        in_specs=placed,
        out_specs=(
            P("wa", "seq", None),
            P("wa", "seq", None),
            P(),
            P("wa", None),
            P(),
            P(),
            P(),
            P(),
            P(),
            P(),
            P("wa", None),
        ),
        check_vma=False,
    )
```

```python
import functools

import jax
import jax.numpy as jnp
import numpy as np
from jax import lax
from jax.experimental import pallas as pl
from jax.experimental.pallas import tpu as pltpu
from jax.sharding import PartitionSpec as P

KW = 4
EPS = 1e-05
HIGHEST = lax.Precision.HIGHEST
MESH = pl.DeviceIdType.MESH


def row_scale(values):
    return lax.rsqrt(jnp.mean(values * values, axis=-1, keepdims=True) + EPS)


def norm_backward(values, row_scales, gain_vec, grad_out):
    weighted = grad_out * gain_vec
    return row_scales * weighted - values * row_scales**3 * jnp.mean(
        weighted * values, axis=-1, keepdims=True
    )


def dot(a, b, ca, cb, precision=None):
    return lax.dot_general(
        a, b, (((ca,), (cb,)), ((), ())), precision=precision, preferred_element_type=jnp.float32
    )


def chunk_front(proj_ref, ext, taps_ref, heads_ref, tri_ref, widths, head_start):
    lw, bc = widths
    rows = proj_ref.shape[2]
    ext[8:, :] = proj_ref[0, 0, :, lw : 2 * lw + bc].astype(jnp.float32)
    conv = taps_ref[KW : KW + 1, :]
    for k in range(KW):
        conv = conv + taps_ref[k : k + 1, :] * ext[5 + k : 5 + k + rows, :]
    conv_sig = lax.logistic(conv)
    act = conv * conv_sig
    raw = proj_ref[0, 0, :, 2 * lw + bc :].astype(jnp.float32)
    step_in = pltpu.roll(raw, lax.rem(128 - head_start, 128), 1) + heads_ref[0:1, :]
    steps = jnp.maximum(step_in, 0.0) + jnp.log1p(jnp.exp(-jnp.abs(step_in)))
    rates = heads_ref[1:2, :] * steps
    cum = dot(tri_ref[...], rates, 1, 0, HIGHEST)
    return conv, conv_sig, act, step_in, steps, rates, cum


def head_masks(rows, head_size):
    lane = lax.broadcasted_iota(jnp.int32, (rows, 128), 1)
    row = lax.broadcasted_iota(jnp.int32, (rows, rows), 0)
    col = lax.broadcasted_iota(jnp.int32, (rows, rows), 1)
    return lane, row >= col


def forward_chunk(
    widths,
    head_size,
    head_start,
    start,
    proj_ref,
    taps_ref,
    heads_ref,
    wide_ref,
    spread_ref,
    tri_ref,
    gated_ref,
    y_ref,
    enter_ref,
    state,
    ext,
    halo,
):
    lw, bc = widths
    bf16, f32 = jnp.bfloat16, jnp.float32
    rows = proj_ref.shape[2]
    per_tile = 128 // head_size

    @pl.when(start)
    def _():
        state[...] = jnp.zeros_like(state)
        halo[...] = jnp.zeros_like(halo)

    ext[0:8, :] = halo[...]
    _, _, act, _, steps, _, cum = chunk_front(
        proj_ref, ext, taps_ref, heads_ref, tri_ref, widths, head_start
    )
    halo[...] = ext[rows : rows + 8, :]
    x = act[:, :lw]
    xb = x.astype(bf16)
    b_rows = act[:, lw : lw + bc // 2].astype(bf16)
    c_rows = act[:, lw + bc // 2 :].astype(bf16)
    cum_t, steps_t = cum.T, steps.T
    last = cum[rows - 1 : rows, :]
    grow = dot(jnp.exp(cum).astype(bf16), spread_ref[...], 1, 0)
    tail = dot((jnp.exp(last - cum) * steps).astype(bf16), spread_ref[...], 1, 0)
    scores = dot(c_rows, b_rows, 1, 1)
    entering = state[...].astype(bf16)
    enter_ref[0, 0] = entering
    y = dot(c_rows, entering, 1, 1) * grow + wide_ref[1:2, :] * x
    added = dot((x * tail).astype(bf16), b_rows, 0, 0)
    lane, causal = head_masks(rows, head_size)
    gate = proj_ref[0, 0, :, :lw].astype(f32)
    silu_gate = gate * lax.logistic(gate)
    for tile in range(lw // 128):
        cols = slice(tile * 128, (tile + 1) * 128)
        inner = None
        for sub in range(per_tile):
            head = tile * per_tile + sub
            log_decay = cum[:, head : head + 1] - cum_t[head : head + 1, :]
            decay = jnp.exp(jnp.where(causal, log_decay, -1e30))
            weights = (scores * decay * steps_t[head : head + 1, :]).astype(bf16)
            part = dot(weights, xb[:, cols], 1, 0)
            inner = part if inner is None else jnp.where(lane >= sub * head_size, part, inner)
            span = slice(head * head_size, (head + 1) * head_size)
            state[span, :] = (
                jnp.exp(cum[rows - 1 : rows, head : head + 1]) * state[span, :] + added[span, :]
            )
        y_tile = y[:, cols] + inner
        y_ref[0, 0, :, cols] = y_tile.astype(bf16)
        gated_ref[:, cols] = (y_tile * silu_gate[:, cols]).astype(bf16)


def backward_kernel(
    widths,
    head_size,
    chunks,
    proj_ref,
    before_ref,
    y_ref,
    enter_ref,
    grad_ref,
    taps_ref,
    heads_ref,
    wide_ref,
    spread_ref,
    fold_ref,
    tri_ref,
    upper_ref,
    normed_ref,
    out_ref,
    turned_ref,
    taps_acc,
    skip_acc,
    head_acc,
    swapped_ref,
    lam,
    ext,
    later,
    after,
    swap_send,
    swap_recv,
    swap_local,
):
    lw, bc = widths
    state_size = bc // 2
    bf16, f32 = jnp.bfloat16, jnp.float32
    rows = proj_ref.shape[2]
    per_tile = 128 // head_size
    chunk = chunks - 1 - pl.program_id(1)
    head_start = lax.axis_index("seq") * (lw // head_size)

    me, group = lax.axis_index("seq"), lax.axis_index("wa")
    swaps = [
        push(
            normed_ref.at[other],
            swapped_ref.at[me],
            swap_send.at[k],
            swap_recv.at[k],
            (other, group),
        )
        for k, other in enumerate(others(me, chunks))
    ]
    swap_kept = pltpu.make_async_copy(normed_ref.at[me], swapped_ref.at[me], swap_local)

    @pl.when((pl.program_id(0) == 0) & (pl.program_id(1) == 0))
    def _():
        greet([(other, group) for other in others(me, chunks)])
        for copy in swaps:
            copy.start()
        swap_kept.start()
        taps_acc[...] = jnp.zeros_like(taps_acc)
        skip_acc[...] = jnp.zeros_like(skip_acc)
        head_acc[...] = jnp.zeros_like(head_acc)

    @pl.when(pl.program_id(1) == 0)
    def _():
        lam[...] = jnp.zeros_like(lam)
        after[...] = jnp.zeros_like(after)

    ext[0:8, :] = jnp.where(
        chunk > 0, before_ref[0, 0, 8:16, lw : 2 * lw + bc].astype(f32), 0.0
    )
    conv, conv_sig, act, step_in, steps, rates, cum = chunk_front(
        proj_ref, ext, taps_ref, heads_ref, tri_ref, widths, head_start
    )
    x = act[:, :lw]
    xb = x.astype(bf16)
    b_rows = act[:, lw : lw + state_size].astype(bf16)
    c_rows = act[:, lw + state_size :].astype(bf16)
    cum_t, steps_t = cum.T, steps.T
    last = cum[rows - 1 : rows, :]
    to_end = jnp.exp(last - cum)
    tail_heads = to_end * steps
    grow = dot(jnp.exp(cum).astype(bf16), spread_ref[...], 1, 0)
    tail = dot(tail_heads.astype(bf16), spread_ref[...], 1, 0)
    scores = dot(c_rows, b_rows, 1, 1)

    gate = proj_ref[0, 0, :, :lw].astype(f32)
    gate_sig = lax.logistic(gate)
    grad = grad_ref[0, 0].astype(f32)
    y_grad = grad * gate * gate_sig
    out_ref[0, 0, :, :lw] = (
        grad * y_ref[0, 0].astype(f32) * (gate_sig * (1.0 + gate * (1.0 - gate_sig)))
    ).astype(bf16)
    yb = y_grad.astype(bf16)

    entering = enter_ref[0, 0]
    grown = y_grad * grow
    grown_b = grown.astype(bf16)
    c_grad = dot(grown_b, entering, 1, 0)
    carried = dot((grown * dot(c_rows, entering, 1, 1)).astype(bf16), fold_ref[...], 1, 0)
    lam_now = lam[...]
    lam_b = lam_now.astype(bf16)
    from_lam = dot(b_rows, lam_b, 1, 1)
    b_grad = dot((x * tail).astype(bf16), lam_b, 1, 0)
    x_lam = dot((x * from_lam).astype(bf16), fold_ref[...], 1, 0)
    x_grad = wide_ref[1:2, :] * y_grad + tail * from_lam
    skip_acc[0:1, :] += jnp.sum(y_grad * x, axis=0, keepdims=True)
    ones = jnp.ones((8, state_size), bf16)
    kept = dot(
        dot(ones, (lam_now * entering.astype(f32)).astype(bf16), 1, 1),
        fold_ref[...].astype(f32),
        1,
        0,
        HIGHEST,
    )
    through = jnp.exp(last) * kept[0:1, :]
    lam_add = dot(grown_b, c_rows, 0, 0)

    lane, causal = head_masks(rows, head_size)
    score_grad = None
    row_sums = jnp.zeros((rows, 128), f32)
    col_sums = []
    x_tiles = []
    for tile in range(lw // 128):
        cols = slice(tile * 128, (tile + 1) * 128)
        inner = None
        for sub in range(per_tile):
            head = tile * per_tile + sub
            log_decay = cum[:, head : head + 1] - cum_t[head : head + 1, :]
            decay = jnp.exp(jnp.where(causal, log_decay, -1e30))
            step_row = steps_t[head : head + 1, :]
            weights = (scores * decay * step_row).astype(bf16)
            inside = (lane >= sub * head_size) & (lane < (sub + 1) * head_size)
            y_head = jnp.where(inside, yb[:, cols], jnp.zeros_like(yb[:, cols]))
            weights_grad = dot(y_head, xb[:, cols], 1, 1)
            part = dot(weights, yb[:, cols], 0, 0)
            inner = part if inner is None else jnp.where(lane >= sub * head_size, part, inner)
            decayed = weights_grad * decay
            stepped = decayed * step_row
            score_grad = stepped if score_grad is None else score_grad + stepped
            col_sums.append(jnp.sum(decayed * scores, axis=0, keepdims=True))
            row_sum = jnp.sum(stepped * scores, axis=1, keepdims=True)
            row_sums = row_sums + jnp.where(lane == head, row_sum, 0.0)
            span = slice(head * head_size, (head + 1) * head_size)
            lam[span, :] = (
                jnp.exp(cum[rows - 1 : rows, head : head + 1]) * lam_now[span, :] + lam_add[span, :]
            )
        x_tiles.append(x_grad[:, cols] + inner)
    col_sums.append(jnp.zeros((rows - len(col_sums), rows), f32))
    col_sum = jnp.concatenate(col_sums, axis=0).T
    source = row_sums - steps * col_sum + carried
    rates_grad = (
        dot(upper_ref[...], source, 1, 0, HIGHEST)
        + dot(1.0 - upper_ref[...], tail_heads * x_lam, 1, 0, HIGHEST)
        + through
    )
    steps_grad = col_sum + to_end * x_lam + rates_grad * heads_ref[1:2, :]
    raw_grad = steps_grad * lax.logistic(step_in)
    out_ref[0, 0, :, 2 * lw + bc :] = pltpu.roll(raw_grad, head_start, 1).astype(bf16)
    head_acc[0:1, :] += jnp.sum(raw_grad, axis=0, keepdims=True)
    head_acc[1:2, :] += jnp.sum(rates_grad * rates, axis=0, keepdims=True)
    score_b = score_grad.astype(bf16)
    c_grad = c_grad + dot(score_b, b_rows, 1, 0)
    b_grad = b_grad + dot(score_b, c_rows, 0, 0)
    act_grad = jnp.concatenate(x_tiles + [b_grad, c_grad], axis=1)
    conv_grad = act_grad * (conv_sig * (1.0 + conv * (1.0 - conv_sig)))
    later[0:rows, :] = conv_grad
    later[rows : rows + 8, :] = after[...]
    after[...] = conv_grad[0:8, :]
    total = None
    for k in range(KW):
        term = taps_ref[k : k + 1, :] * later[3 - k : 3 - k + rows, :]
        total = term if total is None else total + term
        taps_acc[k : k + 1, :] += jnp.sum(conv_grad * ext[5 + k : 5 + k + rows, :], axis=0, keepdims=True)
    taps_acc[KW : KW + 1, :] += jnp.sum(conv_grad, axis=0, keepdims=True)

    @pl.when((pl.program_id(0) == pl.num_programs(0) - 1) & (chunk == 0))
    def _():
        head_acc[2:3, :] = dot(
            skip_acc[...], fold_ref[...].astype(f32), 1, 0, HIGHEST
        )[0:1, :]
        for copy in swaps:
            copy.wait()
        swap_kept.wait()
    out_ref[0, 0, :, lw : 2 * lw + bc] = total.astype(bf16)
    turned_ref[...] = out_ref[0, 0].T


def whole_spec(array):
    return pl.BlockSpec(array.shape, lambda q, c: (0,) * array.ndim)


def scan_tables(rows, local_width, head_size):
    head_of = np.arange(local_width) // head_size
    spread = (np.arange(128)[:, None] == head_of[None, :]).astype(jnp.bfloat16)
    tri = (np.arange(rows)[:, None] >= np.arange(rows)[None, :]).astype(np.float32)
    return [jnp.asarray(t) for t in (spread, spread.T.copy(), tri, tri.T.copy())]


def scan_backward(
    proj, y, enter, grad, taps, heads, wide, spread, fold, tri, upper, normed, widths, head_size, collective_id
):
    chunks, seqs, rows, cols = proj.shape
    lw, bc = widths
    block = lambda *tail: pl.BlockSpec((1, 1) + tail, lambda q, c: (chunks - 1 - c, q, 0, 0))
    before = pl.BlockSpec(
        (1, 1, 16, cols),
        lambda q, c: (jnp.maximum(chunks - 2 - c, 0), q, rows // 16 - 1, 0),
    )
    tables = (taps, heads, wide, spread, fold, tri, upper)
    sums = [(8, lw + bc), (8, lw), (8, 128)]
    return pl.pallas_call(
        functools.partial(backward_kernel, widths, head_size, chunks),
        grid=(seqs, chunks),
        in_specs=[block(rows, cols), before, block(rows, lw), block(lw, bc // 2), block(rows, lw)]
        + [whole_spec(t) for t in tables]
        + [ANY],
        out_specs=[
            block(rows, cols),
            pl.BlockSpec((cols, rows), lambda q, c: (0, (chunks - 1 - c) * seqs + q)),
        ]
        + [pl.BlockSpec(s, lambda q, c: (0, 0)) for s in sums]
        + [ANY],
        out_shape=[
            jax.ShapeDtypeStruct(proj.shape, jnp.bfloat16),
            jax.ShapeDtypeStruct((cols, chunks * seqs * rows), jnp.bfloat16),
        ]
        + [jax.ShapeDtypeStruct(s, jnp.float32) for s in sums]
        + [jax.ShapeDtypeStruct(normed.shape, normed.dtype)],
        scratch_shapes=[
            pltpu.VMEM((lw, bc // 2), jnp.float32),
            pltpu.VMEM((rows + 8, lw + bc), jnp.float32),
            pltpu.VMEM((rows + 8, lw + bc), jnp.float32),
            pltpu.VMEM((8, lw + bc), jnp.float32),
            pltpu.SemaphoreType.DMA((chunks - 1,)),
            pltpu.SemaphoreType.DMA((chunks - 1,)),
            pltpu.SemaphoreType.DMA,
        ],
        compiler_params=comm_params(collective_id, 60),
        name="scan_backward",
    )(proj, proj, y, enter, grad, *tables, normed)


def ring_pos(index, size):
    row, side = index // 2, index % 2
    return row + side * (size - 1 - 2 * row)


def ring_index(pos, size):
    side = pos // (size // 2)
    row = pos + side * (size - 1 - 2 * pos)
    return row * 2 + side


def greet(peers):
    barrier = pltpu.get_barrier_semaphore()
    for peer in peers:
        pl.semaphore_signal(barrier, inc=1, device_id=peer, device_id_type=MESH)
    pl.semaphore_wait(barrier, len(peers))


def push(source, target, send_sem, recv_sem, peer):
    return pltpu.make_async_remote_copy(
        source, target, send_sem, recv_sem, device_id=peer, device_id_type=MESH
    )


def neighbours(size):
    me, group = lax.axis_index("seq"), lax.axis_index("wa")
    pos = ring_pos(me, size)
    right = (ring_index((pos + 1) % size, size), group)
    left = (ring_index((pos + size - 1) % size, size), group)
    return me, group, pos, right, left


def others(index, size):
    return [(index + offset) % size for offset in range(1, size)]


ANY = pl.BlockSpec(memory_space=pl.ANY)
VMEM = pl.BlockSpec(memory_space=pltpu.VMEM)


def comm_params(collective_id, megabytes=None):
    limit = None if megabytes is None else megabytes * 2**20
    return pltpu.CompilerParams(
        collective_id=collective_id, has_side_effects=True, vmem_limit_bytes=limit
    )


class RingGather:
    def __init__(self, size, x_ref, o_ref, send_sem, recv_sem, local_sem):
        self.size, self.x, self.o = size, x_ref, o_ref
        self.send, self.recv, self.local = send_sem, recv_sem, local_sem
        self.chunks = x_ref.shape[1]
        self.me, _, self.pos, self.right, self.left = neighbours(size)

    def copy(self, step, chunk, way, first=False):
        size = self.size
        if way == 0:
            block, peer = ring_index((self.pos - step + size) % size, size), self.right
        else:
            block, peer = ring_index((self.pos + step) % size, size), self.left
        source = self.x.at[way, chunk] if first else self.o.at[block, way, chunk]
        return push(
            source,
            self.o.at[block, way, chunk],
            self.send.at[step, chunk, way],
            self.recv.at[step, chunk, way],
            peer,
        )

    def kept(self):
        return pltpu.make_async_copy(self.x, self.o.at[self.me], self.local)

    def start(self):
        self.kept().start()
        for chunk in range(self.chunks):
            for way in range(2):
                self.copy(0, chunk, way, True).start()

    def advance(self, step):
        for chunk in range(self.chunks):
            for way in range(2):
                self.copy(step - 1, chunk, way).wait_recv()
                self.copy(step, chunk, way).start()

    def arrive(self):
        last = self.size - 2
        for chunk in range(self.chunks):
            for way in range(2):
                self.copy(last, chunk, way).wait_recv()

    def finish(self):
        self.arrive()
        self.settle()

    def settle(self):
        def drain(step, carry):
            for chunk in range(self.chunks):
                for way in range(2):
                    self.copy(step, chunk, way).wait_send()
            return carry

        lax.fori_loop(0, self.size - 1, drain, 0)
        self.kept().wait()


def ring_parts(x, chunks):
    return x.reshape(2, chunks, x.shape[0] // (2 * chunks), x.shape[1])


def ring_sems(size, chunks):
    return [
        pltpu.SemaphoreType.DMA((size - 1, chunks, 2)),
        pltpu.SemaphoreType.DMA((size - 1, chunks, 2)),
        pltpu.SemaphoreType.DMA,
    ]


def front_kernel(
    widths,
    head_size,
    size,
    groups,
    inner,
    x_ref,
    w_ref,
    cot_ref,
    shard_ref,
    conv_ref,
    conv_bias_ref,
    params_ref,
    out_gain_ref,
    spread_ref,
    tri_ref,
    rows_ref,
    weights_ref,
    proj_ref,
    y_ref,
    enter_ref,
    normed_ref,
    turned_ref,
    grad_ref,
    gain_acc,
    taps_ref,
    heads_ref,
    wide_ref,
    branch_ref,
    part_ref,
    weights,
    projected,
    taken,
    state,
    ext,
    halo,
    gated,
    out_grad,
    y_held,
    enter_held,
    out_rows,
    out_turned,
    sums,
    landing,
    normed_held,
    turned_held,
    grad_held,
    result_sem,
    weight_send,
    weight_recv,
    weight_local,
    take_sem,
    proj_sem,
    held_sem,
    shard_send,
    shard_recv,
    shard_local,
    pair_send,
    pair_recv,
    *ring_refs,
):
    bf16, f32 = jnp.bfloat16, jnp.float32
    me, group, pos, right, left = neighbours(size)
    rows, lw = gated.shape[2:]
    depth = weights.shape[2]
    peers = [(other, group) for other in others(me, size)]
    mates = [(me, other) for other in others(group, groups)]
    sibling = (me, group + 1 - 2 * lax.rem(group, 2))
    across = (me, lax.rem(group + 2, groups))
    per_owner = size // groups
    chosen = lax.rem(me, per_owner)
    owner = me // per_owner
    greet(mates + peers)
    ring = RingGather(size, x_ref, rows_ref, *ring_refs[0:3])
    cot_ring = RingGather(size, cot_ref, branch_ref, *ring_refs[3:6])
    ring.start()
    bc = widths[1]
    used = w_ref.shape[0] - 2 * inner
    lane_at = pl.multiple_of(me * lw, 128)
    spans = (
        (pl.ds(lane_at, lw), pl.ds(0, lw)),
        (pl.ds(pl.multiple_of(inner + me * lw, 128), lw), pl.ds(lw, lw)),
        (pl.ds(2 * inner, used), pl.ds(2 * lw, used)),
    )
    sent = [
        push(
            w_ref.at[here],
            weights.at[group, there],
            weight_send.at[k, part],
            weight_recv.at[k, part],
            mate,
        )
        for k, mate in enumerate(mates)
        for part, (here, there) in enumerate(spans)
    ]
    for copy in sent:
        copy.start()
    kept = [
        pltpu.make_async_copy(w_ref.at[here], weights.at[group, there], weight_local.at[part])
        for part, (here, there) in enumerate(spans)
    ]
    for copy in kept:
        copy.start()
    blank = weights.shape[1] - 2 * lw - used
    for part in range(groups):
        weights[part, 2 * lw + used :, :] = jnp.zeros((blank, depth), bf16)
    heads_here = lw // head_size
    head_start = me * heads_here
    taps_ref[...] = jnp.zeros_like(taps_ref)
    taps_ref[0:KW, :lw] = conv_ref[:, pl.ds(lane_at, lw)]
    taps_ref[0:KW, lw:] = conv_ref[:, inner:]
    taps_ref[KW : KW + 1, :lw] = conv_bias_ref[:, pl.ds(lane_at, lw)]
    taps_ref[KW : KW + 1, lw:] = conv_bias_ref[:, inner:]
    params = pltpu.roll(params_ref[...], lax.rem(128 - head_start, 128), 1)
    params = jnp.where(
        lax.broadcasted_iota(jnp.int32, params.shape, 1) < heads_here, params, 0.0
    )
    at_row = lax.broadcasted_iota(jnp.int32, params.shape, 0)
    at_lane = lax.broadcasted_iota(jnp.int32, params.shape, 1)
    slopes = jnp.where(at_lane < heads_here, -jnp.exp(params), 0.0)
    heads_ref[...] = jnp.where(at_row == 1, slopes, params)
    wide_ref[...] = jnp.zeros_like(wide_ref)
    wide_ref[0:1, :] = out_gain_ref[:, pl.ds(lane_at, lw)]
    wide_ref[1:2, :] = dot(params, spread_ref[...].astype(f32), 1, 0, HIGHEST)[2:3, :]

    def shards(step, offset=0):
        at = lax.rem(chosen + offset, per_owner)
        held_by = across[1] if step == 2 else group
        source = part_ref.at[held_by, at] if step == 2 else shard_ref.at[at]
        return push(
            source,
            part_ref.at[held_by, at],
            shard_send.at[step, offset],
            shard_recv.at[step, offset],
            across if step == 0 else sibling,
        )

    def block_of(pair, way):
        return ring_index((pos - pair + size) % size if way == 0 else (pos + pair) % size, size)

    def stream(source_ref, landed_ref, low, high, compute, own=False):
        def take(pair, slot, way):
            source = source_ref.at[way] if own else landed_ref.at[block_of(pair, way), way]
            return pltpu.make_async_copy(source, taken.at[slot, way], take_sem.at[slot, way])

        for way in range(2):
            take(low, lax.rem(low, 2), way).start()

        def one(pair, carry):
            slot = lax.rem(pair, 2)
            for way in range(2):
                take(pair, slot, way).wait()

            @pl.when(pair + 1 < high)
            def _():
                for way in range(2):
                    take(pair + 1, 1 - slot, way).start()

            compute(pair, slot)
            return carry

        lax.fori_loop(low, high, one, 0)

    def put(pair, way):
        block = block_of(pair, way)
        return pltpu.make_async_copy(
            projected.at[block, way], proj_ref.at[block, way], proj_sem.at[pair, way]
        )

    def project(pair, slot):
        for way in range(2):
            x = taken[slot, way].reshape(rows, taken.shape[4])
            total = None
            for part in range(groups):
                term = dot(x[:, part * depth : (part + 1) * depth], weights[part], 1, 1)
                total = term if total is None else total + term
            projected[block_of(pair, way), way] = total.astype(bf16)
            put(pair, way).start()

    def advance(step, carry):
        ring.advance(step)
        return carry

    def turns(turn, count):
        return 1 + (turn * (size - 2)) // count, 1 + ((turn + 1) * (size - 2)) // count

    middle = size // 2 + 1
    lax.fori_loop(1, middle, advance, 0)
    for copy in kept:
        copy.wait()
    for copy in sent:
        copy.wait_recv()
    flushed = pltpu.make_async_copy(weights, weights_ref, weight_local.at[0])
    flushed.start()
    shards(0).start()
    shards(1).start()
    stream(x_ref, rows_ref, 0, 1, project, own=True)

    def late(step, carry):
        ring.advance(step)
        stream(x_ref, rows_ref, *turns(step - middle, size - 1 - middle), project)
        return carry

    lax.fori_loop(middle, size - 2, late, 0)
    ring.advance(size - 2)
    cot_ring.start()
    stream(x_ref, rows_ref, *turns(size - 2 - middle, size - 1 - middle), project)
    ring.arrive()
    stream(x_ref, rows_ref, size - 1, size, project)
    cot_ring.advance(1)

    def keep(index, slot):
        seq, chunk = index // size, lax.rem(index, size)
        return [
            pltpu.make_async_copy(y_held.at[slot, 0], y_ref.at[chunk, seq], held_sem.at[slot, 0]),
            pltpu.make_async_copy(
                enter_held.at[slot, 0], enter_ref.at[chunk, seq], held_sem.at[slot, 1]
            ),
        ]

    def scan(index, carry):
        seq, chunk = index // size, lax.rem(index, size)
        slot = lax.rem(index, 2)

        @pl.when(index >= 2)
        def _():
            for copy in keep(index - 2, slot):
                copy.wait()

        forward_chunk(
            widths,
            head_size,
            head_start,
            chunk == 0,
            projected.at[pl.ds(chunk, 1), pl.ds(seq, 1)],
            taps_ref,
            heads_ref,
            wide_ref,
            spread_ref,
            tri_ref,
            gated.at[chunk, seq],
            y_held.at[pl.ds(slot, 1)],
            enter_held.at[pl.ds(slot, 1)],
            state,
            ext,
            halo,
        )
        for copy in keep(index, slot):
            copy.start()

        @pl.when(index == size + 2)
        def _():
            cot_ring.advance(2)

        return carry

    lax.fori_loop(0, 2 * size, scan, 0)
    first, second, third = (shards(step) for step in range(3))
    first.wait_recv()
    third.start()
    for offset in range(1, per_owner):
        shards(0, offset).start()
        shards(1, offset).start()
    second.wait_recv()
    cot_ring.advance(3)
    third.wait_recv()

    @pl.when(owner == group)
    def _():
        loaded = pltpu.make_async_copy(shard_ref.at[chosen], out_rows, shard_local)
        loaded.start()
        loaded.wait()

    @pl.when(owner != group)
    def _():
        loaded = pltpu.make_async_copy(part_ref.at[owner, chosen], out_rows, shard_local)
        loaded.start()
        loaded.wait()

    out_turned[...] = out_rows[...].T
    ones = jnp.ones((8, lw), bf16)

    def compute(pair, slot):
        for way in range(2):
            block = block_of(pair, way)
            values = dot(taken[slot, way].reshape(rows, taken.shape[4]), out_turned[...], 1, 0)
            out_grad[block, way] = values
            here = gated[block, way].astype(f32)
            weighted = values * wide_ref[0:1, :] * here
            at = pl.ds(block * 2 + way, 1)
            sums[0, at, :] = dot(ones, (here * here).astype(bf16), 1, 1)[0:1, :]
            sums[1, at, :] = dot(ones, weighted.astype(bf16), 1, 1)[0:1, :]

    stream(cot_ref, branch_ref, 0, 1, compute, own=True)
    stream(cot_ref, branch_ref, *turns(0, size - 4), compute)

    def cot_late(step, carry):
        cot_ring.advance(step)
        stream(cot_ref, branch_ref, *turns(step - 3, size - 4), compute)
        return carry

    lax.fori_loop(4, size - 1, cot_late, 0)
    cot_ring.arrive()
    stream(cot_ref, branch_ref, size - 1, size, compute)
    copies = [
        push(sums, landing.at[k], pair_send.at[k], pair_recv.at[k], peer)
        for k, peer in enumerate(peers)
    ]
    for copy in copies:
        copy.start()
    total = sums[...]
    for k, copy in enumerate(copies):
        copy.wait_recv()
        total = total + landing[k]
    scale = lax.rsqrt(total[0] / inner + EPS)
    pull = scale * scale * scale * (total[1] / inner)
    fill = jnp.zeros((128 - 2 * size, rows), f32)
    scale_turned = jnp.concatenate([scale, fill]).T
    pull_turned = jnp.concatenate([pull, fill]).T
    lane = lax.broadcasted_iota(jnp.int32, (rows, 128), 1)
    gain_acc[...] = jnp.zeros_like(gain_acc)

    def results(block):
        pairs = ((normed_held, normed_ref), (turned_held, turned_ref), (grad_held, grad_ref))
        return [
            pltpu.make_async_copy(held.at[block], out.at[block], result_sem.at[k, block])
            for k, (held, out) in enumerate(pairs)
        ]

    def finish(block, carry):
        for way in range(2):
            mask = lane == block * 2 + way
            by = jnp.sum(jnp.where(mask, scale_turned, 0.0), axis=1, keepdims=True)
            less = jnp.sum(jnp.where(mask, pull_turned, 0.0), axis=1, keepdims=True)
            here = gated[block, way].astype(f32)
            values = out_grad[block, way]
            scaled = here * by
            normed = (scaled * wide_ref[0:1, :]).astype(bf16)
            normed_held[block, way] = normed
            turned_held[block, :, way * rows : (way + 1) * rows] = normed.T
            grad_held[block, way] = (values * wide_ref[0:1, :] * by - here * less).astype(bf16)
            gain_acc[0:1, :] += jnp.sum(values * scaled, axis=0, keepdims=True)
        for copy in results(block):
            copy.start()
        return carry

    lax.fori_loop(0, size, finish, 0)
    for offset in range(1, per_owner):
        shards(0, offset).wait_recv()
        shards(2, offset).start()
    for copy in sent + copies + [first, second, third]:
        copy.wait_send()
    flushed.wait()
    for index in (2 * size - 2, 2 * size - 1):
        for copy in keep(index, index % 2):
            copy.wait()

    def settle(pair, carry):
        for way in range(2):
            put(pair, way).wait()
        for copy in results(pair):
            copy.wait()
        return carry

    lax.fori_loop(0, size, settle, 0)
    ring.settle()
    cot_ring.settle()
    for offset in range(1, per_owner):
        shards(1, offset).wait_recv()
        shards(2, offset).wait_recv()
        for step in range(3):
            shards(step, offset).wait_send()


def front(x, weight, cot, shard, params, inner, widths, head_size, collective_id):
    size, groups = lax.axis_size("seq"), lax.axis_size("wa")
    parts, cot_parts = ring_parts(x, 2), ring_parts(cot, 2)
    depth = weight.shape[1]
    rows = x.shape[0] // 2
    width = x.shape[1]
    lw, bc = widths
    cols = 2 * lw + bc + 128
    per_owner = size // groups
    bf16, f32, DMA, vmem = jnp.bfloat16, jnp.float32, pltpu.SemaphoreType.DMA, pltpu.VMEM
    whole = (size, 2, rows, lw)
    shape = jax.ShapeDtypeStruct
    return pl.pallas_call(
        functools.partial(front_kernel, widths, head_size, size, groups, inner),
        out_shape=[
            shape((size,) + parts.shape, bf16),
            shape((groups, cols, depth), bf16),
            shape((size, 2, rows, cols), bf16),
            shape(whole, bf16),
            shape((size, 2, lw, bc // 2), bf16),
            shape(whole, bf16),
            shape((size, lw, 2 * rows), bf16),
            shape(whole, bf16),
            shape((8, lw), f32),
            shape((8, lw + bc), f32),
            shape((8, 128), f32),
            shape((8, lw), f32),
            shape((size,) + parts.shape, bf16),
            shape((groups, per_owner, lw, width), bf16),
        ],
        in_specs=[ANY] * 4 + [VMEM] * 6,
        out_specs=[ANY] * 8 + [VMEM] * 4 + [ANY] * 2,
        scratch_shapes=[
            vmem((groups, cols, depth), bf16),
            vmem((size, 2, rows, cols), bf16),
            vmem((2,) + parts.shape, bf16),
            vmem((lw, bc // 2), f32),
            vmem((rows + 8, lw + bc), f32),
            vmem((8, lw + bc), f32),
            vmem(whole, bf16),
            vmem(whole, f32),
            vmem((2, 1, rows, lw), bf16),
            vmem((2, 1, lw, bc // 2), bf16),
            vmem((lw, width), bf16),
            vmem((width, lw), bf16),
            vmem((2, 2 * size, rows), f32),
            vmem((size - 1, 2, 2 * size, rows), f32),
            vmem(whole, bf16),
            vmem((size, lw, 2 * rows), bf16),
            vmem(whole, bf16),
            DMA((3, size)),
            DMA((groups - 1, 3)),
            DMA((groups - 1, 3)),
            DMA((3,)),
            DMA((2, 2)),
            DMA((size, 2)),
            DMA((2, 2)),
            DMA((3, per_owner)),
            DMA((3, per_owner)),
            DMA,
            DMA((size - 1,)),
            DMA((size - 1,)),
        ]
        + ring_sems(size, 2)
        + ring_sems(size, 2),
        compiler_params=comm_params(collective_id, 62),
        name="front",
    )(parts, weight, cot_parts, shard, *params)


def finish_kernel(
    size,
    groups,
    counts,
    grad_ref,
    weight_ref,
    normed_ref,
    turned_ref,
    out_ref,
    branch_grad_ref,
    tokens_ref,
    scale_ref,
    taps_ref,
    gain_ref,
    heads_ref,
    swapped_ref,
    shard_ref,
    out_full_ref,
    rows_ref,
    gathered_ref,
    pieces_ref,
    owned_ref,
    shared_out,
    small_out,
    branch_ref,
    landing,
    slots,
    first,
    parts,
    total,
    taken,
    turned,
    out_total,
    out_parts,
    out_landing,
    out_taken,
    piece,
    main,
    shared,
    shared_land,
    shared_sum,
    small,
    small_land,
    send_sem,
    recv_sem,
    part_send,
    part_recv,
    take_sem,
    out_send,
    out_recv,
    owned_send,
    owned_recv,
    owned_local,
    pair_send,
    pair_recv,
    mate_send,
    mate_recv,
    *ring_refs,
):
    me, group, pos, right, left = neighbours(size)
    mates = [(me, index) for index in others(group, groups)]
    peers = [(index, group) for index in others(me, size)]
    tiles, rows, tile = slots.shape[2:]
    cols = total.shape[0]
    bf16, f32 = jnp.bfloat16, jnp.float32
    out_ring = RingGather(size, piece, pieces_ref, *ring_refs[0:3])
    main_ring = RingGather(size, main, gathered_ref, *ring_refs[3:6])
    shared_ring = RingGather(size, shared_sum, shared_out, *ring_refs[6:9])
    small_ring = RingGather(size, small, small_out, *ring_refs[9:12])
    fetch_sem, weights_taken, held, held_sem, out_turned = ring_refs[12:17]
    weight_held, swapped_held, load_sem = ring_refs[17:20]
    loads = [
        pltpu.make_async_copy(weight_ref.at[part], weight_held.at[part], load_sem.at[part])
        for part in range(groups)
    ]
    swapped_load = pltpu.make_async_copy(swapped_ref, swapped_held, load_sem.at[groups])

    def target(step, way):
        shift = (pos - 1 - step + 2 * size) if way == 0 else (pos + 1 + step)
        return ring_index(shift % size, size)

    def fetch(step, way):
        slot = lax.rem(step, 2)
        return pltpu.make_async_copy(
            grad_ref.at[target(step, way), way], held.at[slot, way], held_sem.at[slot, way]
        )

    def term(step, way, at):
        return dot(held[lax.rem(step, 2), way], weight_held[at], 1, 0)

    def hop(step, way, at, source):
        return push(
            source,
            slots.at[step, way, at],
            send_sem.at[step, way, at],
            recv_sem.at[step, way, at],
            right if way == 0 else left,
        )

    def begin(at, carry):
        for way in range(2):
            first[way, at] = term(0, way, at).astype(bf16)
            hop(0, way, at, first.at[way, at]).start()
        return carry

    for way in range(2):
        fetch(0, way).start()
    for copy in loads:
        copy.start()
    for way in range(2):
        fetch(1, way).start()
    swapped_load.start()
    greet(mates + peers)
    for way in range(2):
        fetch(0, way).wait()
    for part in range(groups):
        loads[part].wait()
        begin(part, 0)

    def mate_of(offset):
        return lax.rem(group + offset, groups)

    def send_part(offset):
        return push(
            parts.at[offset - 1],
            landing.at[offset - 1],
            part_send.at[offset - 1],
            part_recv.at[offset - 1],
            (me, mate_of(offset)),
        )

    def send_out(offset):
        return push(
            out_parts.at[mate_of(offset)],
            out_landing.at[offset - 1],
            out_send.at[offset - 1],
            out_recv.at[offset - 1],
            (me, mate_of(offset)),
        )

    def stream(count, take, use):
        for copy in take(0, 0):
            copy.start()

        def one(block, carry):
            slot = lax.rem(block, 2)

            @pl.when(block + 1 < count)
            def _():
                for copy in take(block + 1, 1 - slot):
                    copy.start()

            for copy in take(block, slot):
                copy.wait()
            use(block, slot)
            return carry

        lax.fori_loop(0, count, one, 0)

    def tokens_of(block):
        return pl.ds(pl.multiple_of(block * 2 * rows, 2 * rows), 2 * rows)

    def weight_part(offset):
        columns = pl.ds(pl.multiple_of(mate_of(offset) * tile, tile), tile)

        def take(block, slot):
            return [
                pltpu.make_async_copy(
                    normed_ref.at[block, :, :, columns], taken.at[slot], take_sem.at[slot, 0]
                ),
                pltpu.make_async_copy(
                    turned_ref.at[:, tokens_of(block)], turned.at[slot], take_sem.at[slot, 1]
                ),
            ]

        def use(block, slot):
            values = dot(turned[slot], taken[slot].reshape(2 * rows, tile), 1, 0)

            @pl.when(block == 0)
            def _():
                total[...] = values

            @pl.when(block > 0)
            def _():
                total[...] += values

        stream(size, take, use)

    def out_part(low, count):
        piece_rows = out_parts.shape[1]

        def take(block, slot):
            return [
                pltpu.make_async_copy(
                    branch_grad_ref.at[tokens_of(low + block)],
                    out_taken.at[slot],
                    take_sem.at[slot, 0],
                ),
                pltpu.make_async_copy(
                    out_ref.at[low + block], out_turned.at[slot], take_sem.at[slot, 1]
                ),
            ]

        def use(block, slot):
            values = dot(out_turned[slot], out_taken[slot], 1, 0)

            @pl.when(low + block == 0)
            def _():
                out_total[...] = values

            @pl.when(low + block > 0)
            def _():
                out_total[...] += values

        stream(count, take, use)

    def out_sends():
        piece_rows = out_parts.shape[1]
        for index in range(groups):
            out_parts[index] = out_total[index * piece_rows : (index + 1) * piece_rows].astype(bf16)
        for offset in range(1, groups):
            send_out(offset).start()

    def advance(step, carry):
        for way in range(2):
            fetch(step + 1, way).start()
        for way in range(2):
            fetch(step, way).wait()

        def one(at, inner):
            for way in range(2):
                own = term(step, way, at)
                hop(step - 1, way, at, first.at[way, at]).wait_recv()
                slots[step - 1, way, at] = (slots[step - 1, way, at].astype(f32) + own).astype(bf16)
                hop(step, way, at, slots.at[step - 1, way, at]).start()
            return inner

        lax.fori_loop(0, tiles, one, 0)

        @pl.when(step < 3)
        def _():
            out_part((step - 1) * (size // 2), size // 2)

        @pl.when(step == 2)
        def _():
            out_sends()

        @pl.when((step > 2) & (step <= groups + 2))
        def _():
            weight_part(step - 2)

        @pl.when((step > 2) & (step <= groups + 1))
        def _():
            parts[step - 3] = total[...].astype(bf16)
            send_part(step - 2).start()

        return carry

    lax.fori_loop(1, size - 1, advance, 0)
    for offset in range(1, groups):
        send_out(offset).wait_recv()
    summed = out_parts[group].astype(f32)
    for offset in range(1, groups):
        summed = summed + out_landing[offset - 1].astype(f32)
    piece[...] = summed.astype(bf16).reshape(piece.shape)
    out_ring.start()

    for way in range(2):
        fetch(size - 1, way).wait()

    def end(at, carry):
        columns = pl.ds(pl.multiple_of(at * tile, tile), tile)
        for way in range(2):
            own = term(size - 1, way, at)
            hop(size - 2, way, at, first.at[way, at]).wait_recv()
            rows_ref[way, :, columns] = slots[size - 2, way, at].astype(f32) + own
        return carry

    lax.fori_loop(0, tiles, end, 0)
    width = rows_ref.shape[2]
    own_width = gain_ref.shape[1]
    flat = jnp.zeros((1, width), f32)
    for way in range(2):
        values = tokens_ref[way].astype(f32) * scale_ref[way, :, 0:1]
        flat = flat + jnp.sum(rows_ref[way] * values, axis=0, keepdims=True)
    half = small.shape[2]
    listed = [
        taps_ref[k : k + 1, at : at + 128] for k in range(KW + 1) for at in range(0, own_width, 128)
    ]
    listed += [gain_ref[0:1, at : at + 128] for at in range(0, own_width, 128)]
    listed += [heads_ref[k : k + 1, :] for k in range(3)]
    listed += [
        taps_ref[k : k + 1, at : at + 128]
        for k in range(KW + 1)
        for at in range(own_width, taps_ref.shape[1], 128)
    ]
    listed += [flat[:, at : at + 128] for at in range(0, width, 128)]
    for at, row in enumerate(listed):
        small[at // half, 0, at % half : at % half + 1, :] = row
    small_in = [
        push(small, small_land.at[k], mate_send.at[k], mate_recv.at[k], mate)
        for k, mate in enumerate(mates)
    ]
    for copy in small_in:
        copy.start()

    def out_advance(step, carry):
        out_ring.advance(step)
        return carry

    lax.fori_loop(1, size // 2, out_advance, 0)
    fetched = []
    for offset in range(1, groups):
        send_part(offset).wait()
        fetched.append(
            pltpu.make_async_copy(
                landing.at[offset - 1], parts.at[offset - 1], fetch_sem.at[offset - 1]
            )
        )
        fetched[-1].start()
    for copy, part in zip(fetched, range(groups - 1)):
        copy.wait()
        total[...] += parts[part].astype(f32)
    main[...] = total[: counts[0]].astype(bf16).reshape(main.shape)
    shared[...] = total[counts[0] : counts[0] + counts[1]].astype(bf16).reshape(shared.shape)
    shared_in = [
        push(shared.at[peer[0]], shared_land.at[k], pair_send.at[k], pair_recv.at[k], peer)
        for k, peer in enumerate(peers)
    ]
    lax.fori_loop(size // 2, size - 1, out_advance, 0)
    for copy in shared_in:
        copy.start()
    main_ring.start()
    out_ring.finish()
    owned = [
        push(pieces_by_owner(pieces_ref, mate[1], groups), owned_ref.at[group], owned_send.at[k], owned_recv.at[k], mate)
        for k, mate in enumerate(mates)
    ]
    kept = pltpu.make_async_copy(
        pieces_by_owner(pieces_ref, group, groups), owned_ref.at[group], owned_local
    )
    for copy in owned:
        copy.start()
    kept.start()
    main_ring.advance(1)
    for copy in small_in + shared_in:
        copy.wait()
    values = small[...]
    for k in range(groups - 1):
        values = values + small_land[k]
    small[...] = values
    values = shared[me].astype(f32)
    for k in range(size - 1):
        values = values + shared_land[k].astype(f32)
    across = shared_sum.shape[3]
    for way in range(2):
        shared_sum[way, 0] = values[:, way * across : (way + 1) * across].astype(bf16)
    small_ring.start()
    shared_ring.start()
    branch_ref[...] = jnp.zeros_like(branch_ref)

    per_owner = size // groups

    def weight_take(block, slot):
        owner, at = block // per_owner, lax.rem(block, per_owner)

        @pl.when(owner == group)
        def _():
            pltpu.make_async_copy(
                shard_ref.at[at], weights_taken.at[slot], take_sem.at[slot, 0]
            ).start()

        @pl.when(owner != group)
        def _():
            pltpu.make_async_copy(
                out_full_ref.at[owner, at], weights_taken.at[slot], take_sem.at[slot, 0]
            ).start()

    def multiply(block, carry):
        slot = lax.rem(block, 2)

        @pl.when(block + 1 < size)
        def _():
            weight_take(block + 1, 1 - slot)

        pltpu.make_async_copy(
            shard_ref.at[0], weights_taken.at[slot], take_sem.at[slot, 0]
        ).wait()
        branch_ref[...] += dot(swapped_held[block], weights_taken[slot], 1, 0)
        return carry

    weight_take(0, 0)
    swapped_load.wait()
    count = size - 3

    def main_advance(step, carry):
        main_ring.advance(step)
        small_ring.advance(step - 1)
        shared_ring.advance(step - 1)
        lax.fori_loop(((step - 2) * size) // count, ((step - 1) * size) // count, multiply, 0)
        return carry

    lax.fori_loop(2, size - 1, main_advance, 0)
    small_ring.advance(size - 2)
    shared_ring.advance(size - 2)

    def drain(step, carry):
        def one(at, inner):
            for way in range(2):
                hop(step, way, at, first.at[way, at]).wait_send()
            return inner

        return lax.fori_loop(0, tiles, one, carry)

    lax.fori_loop(0, size - 1, drain, 0)
    for offset in range(1, groups):
        send_out(offset).wait_send()
    main_ring.finish()
    small_ring.finish()
    shared_ring.finish()
    for copy in owned:
        copy.wait()
    kept.wait()


def pieces_by_owner(pieces_ref, owner, groups):
    count = pieces_ref.shape[0] // groups
    return pieces_ref.at[pl.ds(owner * count, count)]


def finish(
    grad,
    weight,
    normed,
    turned,
    out,
    branch_grad,
    tokens,
    scale,
    taps,
    gain,
    heads,
    swapped,
    shard,
    out_full,
    counts,
    collective_id,
):
    size, groups = lax.axis_size("seq"), lax.axis_size("wa")
    _, ways, rows, cols = grad.shape
    tile, tiles = weight.shape[2], groups
    width = tiles * tile
    lw = out.shape[1]
    bc = taps.shape[1] - lw
    piece_rows = lw // groups
    per_owner = size // groups
    bf16, f32, DMA = jnp.bfloat16, jnp.float32, pltpu.SemaphoreType.DMA
    total_small = ((KW + 2) * lw + (KW + 1) * bc + width) // 128 + 3
    half = -(-total_small // 16) * 8
    piece = (2, 2, piece_rows // 4, width)
    main = (2, 2, counts[0] // 4, tile)
    shared_rows = counts[1] // size
    both = (2, 1, shared_rows, tile // 2)
    small_shape = (2, 1, half, 128)
    vmem = pltpu.VMEM
    return pl.pallas_call(
        functools.partial(finish_kernel, size, groups, counts),
        out_shape=[
            jax.ShapeDtypeStruct((ways, rows, width), f32),
            jax.ShapeDtypeStruct((size,) + main, bf16),
            jax.ShapeDtypeStruct((size,) + piece, bf16),
            jax.ShapeDtypeStruct((groups, per_owner) + piece, bf16),
            jax.ShapeDtypeStruct((size,) + both, bf16),
            jax.ShapeDtypeStruct((size,) + small_shape, f32),
            jax.ShapeDtypeStruct((ways * rows, width), f32),
            jax.ShapeDtypeStruct((groups - 1, cols, tile), bf16),
        ],
        in_specs=[ANY] * 6 + [VMEM] * 5 + [ANY] * 3,
        out_specs=[VMEM, ANY, ANY, ANY, ANY, ANY, VMEM, ANY],
        scratch_shapes=[
            vmem((size - 1, 2, tiles, rows, tile), bf16),
            vmem((2, tiles, rows, tile), bf16),
            vmem((groups - 1, cols, tile), bf16),
            vmem((cols, tile), f32),
            vmem((2, ways, rows, tile), bf16),
            vmem((2, cols, 2 * rows), bf16),
            vmem((lw, width), f32),
            vmem((groups, piece_rows, width), bf16),
            vmem((groups - 1, piece_rows, width), bf16),
            vmem((2, 2 * rows, width), bf16),
            vmem(piece, bf16),
            vmem(main, bf16),
            vmem((size, shared_rows, tile), bf16),
            vmem((size - 1, shared_rows, tile), bf16),
            vmem(both, bf16),
            vmem(small_shape, f32),
            vmem((groups - 1,) + small_shape, f32),
            DMA((size - 1, 2, tiles)),
            DMA((size - 1, 2, tiles)),
            DMA((groups - 1,)),
            DMA((groups - 1,)),
            DMA((2, 2)),
            DMA((groups - 1,)),
            DMA((groups - 1,)),
            DMA((groups - 1,)),
            DMA((groups - 1,)),
            DMA,
            DMA((size - 1,)),
            DMA((size - 1,)),
            DMA((groups - 1,)),
            DMA((groups - 1,)),
        ]
        + ring_sems(size, 2)
        + ring_sems(size, 2)
        + ring_sems(size, 1)
        + ring_sems(size, 1)
        + [DMA((groups - 1,)), vmem((2, lw, width), bf16)]
        + [vmem((2, 2, rows, cols), bf16), DMA((2, 2)), vmem((2, lw, 2 * rows), bf16)]
        + [vmem(weight.shape, bf16), vmem(swapped.shape, bf16), DMA((groups + 1,))],
        compiler_params=comm_params(collective_id, 63),
        name="finish",
    )(
        grad,
        weight,
        normed,
        turned,
        out,
        branch_grad,
        tokens,
        scale,
        taps,
        gain,
        heads,
        swapped,
        shard,
        out_full,
    )


def assemble_kernel(blocks, gathered_ref, tail_ref, o_ref):
    @pl.when(pl.program_id(0) < blocks)
    def _():
        o_ref[...] = gathered_ref[0, 0].reshape(o_ref.shape).astype(jnp.float32)

    @pl.when(pl.program_id(0) == blocks)
    def _():
        o_ref[...] = tail_ref[...].astype(jnp.float32)


def assemble_in(gathered, tail):
    size, ways, chunks, rows, width = gathered.shape
    step = chunks * rows
    blocks = size * ways
    total = blocks * step + tail.shape[0]
    steps = blocks + 1
    pad = -tail.shape[0] % step
    if tail.shape[0] > step:
        out = jnp.swapaxes(gathered, 0, 1).reshape(blocks * step, width)
        return jnp.concatenate([out, tail]).astype(jnp.float32)
    return pl.pallas_call(
        functools.partial(assemble_kernel, blocks),
        grid=(steps,),
        in_specs=[
            pl.BlockSpec(
                (1, 1, chunks, rows, width),
                lambda i: (lax.rem(i, size), jnp.minimum(i // size, ways - 1), 0, 0, 0),
            ),
            pl.BlockSpec((step, width), lambda i: (0, 0)),
        ],
        out_specs=pl.BlockSpec((step, width), lambda i: (i, 0)),
        out_shape=jax.ShapeDtypeStruct((total, width), jnp.float32),
        compiler_params=pltpu.CompilerParams(vmem_limit_bytes=32 * 2**20),
        name="assemble_in",
    )(gathered, jnp.pad(tail, ((0, pad), (0, 0))))


def widen_kernel(
    widths, heads, x_ref, small_ref, o_ref, conv_ref, bias_ref, gain_ref, heads_ref, norm_ref
):
    o_ref[...] = x_ref[0, 0].astype(jnp.float32)

    @pl.when((pl.program_id(0) == 0) & (pl.program_id(1) == 0))
    def _():
        lw, bc = widths
        size = small_ref.shape[0]
        tiles, shared = lw // 128, bc // 128
        inner = size * lw
        found = jnp.zeros((8, 128), jnp.float32)
        first = (KW + 2) * tiles
        for block in range(size):
            for tile in range(tiles):
                at = slice(block * lw + tile * 128, block * lw + (tile + 1) * 128)
                for k in range(KW):
                    row = k * tiles + tile
                    conv_ref[k : k + 1, at] = small_ref[block, row : row + 1, :]
                row = KW * tiles + tile
                bias_ref[:, at] = small_ref[block, row : row + 1, :]
                row = (KW + 1) * tiles + tile
                gain_ref[:, at] = small_ref[block, row : row + 1, :]
            found = found + pltpu.roll(small_ref[block, first : first + 8, :], block * heads, 1)
        heads_ref[...] = found
        total = small_ref[0]
        for block in range(1, size):
            total = total + small_ref[block]
        row = first + 3
        for k in range(KW + 1):
            for tile in range(shared):
                at = slice(inner + tile * 128, inner + (tile + 1) * 128)
                if k < KW:
                    conv_ref[k : k + 1, at] = total[row : row + 1, :]
                else:
                    bias_ref[:, at] = total[row : row + 1, :]
                row += 1
        for tile in range(norm_ref.shape[1] // 128):
            norm_ref[:, tile * 128 : (tile + 1) * 128] = total[row : row + 1, :]
            row += 1


def assemble_out(owned, small, widths, heads):
    groups, count, rows, width = owned.shape
    size = small.shape[0]
    lw, bc = widths
    inner = size * lw
    f32 = jnp.float32
    shapes = [(KW, inner + bc), (1, inner + bc), (1, inner), (8, 128), (1, width)]
    return pl.pallas_call(
        functools.partial(widen_kernel, widths, heads),
        grid=(count, groups),
        in_specs=[
            pl.BlockSpec((1, 1, rows, width), lambda t, g: (g, t, 0, 0)),
            pl.BlockSpec(small.shape, lambda t, g: (0, 0, 0)),
        ],
        out_specs=[pl.BlockSpec((rows, width), lambda t, g: (t * groups + g, 0))]
        + [pl.BlockSpec(s, lambda t, g: (0, 0)) for s in shapes],
        out_shape=[jax.ShapeDtypeStruct((groups * count * rows, width), f32)]
        + [jax.ShapeDtypeStruct(s, f32) for s in shapes],
        name="assemble_out",
    )(owned, small)


def body(
    tokens,
    lengths,
    norm_gain,
    in_weight,
    conv_weight,
    conv_bias,
    dt_bias,
    a_log,
    skip_gain,
    out_gain,
    out_weight,
    cotangent,
):
    seqs_here, slot_rows, width = tokens.shape
    row_count = seqs_here * slot_rows
    inner_width = out_gain.shape[0]
    channels = conv_bias.shape[0]
    bc_width = channels - inner_width
    state_size = bc_width // 2
    head_count = dt_bias.shape[0]
    head_size = inner_width // head_count
    seq_devices = lax.axis_size("seq")
    group_devices = lax.axis_size("wa")
    seq_index = lax.axis_index("seq")
    length = seq_devices * slot_rows
    local_heads = head_count // seq_devices
    local_width = local_heads * head_size
    channel_start = seq_index * local_width
    head_start = seq_index * local_heads
    bf16, f32 = jnp.bfloat16, jnp.float32

    def take(array, start, size, axis):
        return lax.dynamic_slice_in_dim(array, start, size, axis)

    positions = seq_index * slot_rows + jnp.arange(slot_rows)
    valid_rows = (positions[None, :] < lengths[:, None]).astype(f32).reshape(row_count, 1)
    flat_tokens = tokens.reshape(row_count, width).astype(f32)
    in_scale = row_scale(flat_tokens)
    normed = (flat_tokens * in_scale * norm_gain).astype(bf16)
    cot_rows = cotangent.reshape(row_count, width)

    blocks = (seq_devices, seqs_here, slot_rows)
    params = jnp.pad(jnp.stack([dt_bias, a_log, skip_gain]), ((0, 5), (0, 128 - head_count)))
    spread, fold, tri, upper = scan_tables(slot_rows, local_width, head_size)
    widths = (local_width, bc_width)
    per_owner = seq_devices // group_devices
    (
        normed_all,
        in_columns,
        projected,
        y_heads,
        entering,
        normed_out,
        turned_out,
        gated_grad,
        gain_sum,
        taps,
        heads,
        wide,
        branch_grad,
        out_full,
    ) = front(
        normed,
        in_weight.T,
        cot_rows * valid_rows.astype(bf16),
        out_weight.reshape(per_owner, local_width, width),
        (conv_weight, conv_bias[None], params, out_gain[None], spread, tri),
        inner_width,
        widths,
        head_size,
        0,
    )
    branch_grad = branch_grad.reshape(-1, width)
    proj_grad, turned_grad, taps_sum, _, head_sum, swapped = scan_backward(
        projected,
        y_heads,
        entering,
        gated_grad,
        taps,
        heads,
        wide,
        spread,
        fold,
        tri,
        upper,
        normed_out,
        widths,
        head_size,
        1,
    )
    swapped = swapped.reshape(seq_devices, row_count, local_width)
    columns_here = proj_grad.shape[3]
    proj_grad = proj_grad.reshape(-1, columns_here)
    in_rows = in_weight.shape[0]
    shared_count = bc_width + head_count
    shared_rows = shared_count // seq_devices
    normed_grad, gathered, _, owned, shared_all, small_all, branch, _ = finish(
        proj_grad.reshape(blocks + (columns_here,)),
        in_columns,
        normed_all.reshape(blocks + (width,)),
        turned_grad,
        turned_out,
        branch_grad,
        tokens,
        jnp.broadcast_to(in_scale.reshape(seqs_here, slot_rows, 1), (seqs_here, slot_rows, 128)),
        taps_sum,
        gain_sum,
        head_sum,
        swapped,
        out_weight.reshape(per_owner, local_width, width),
        out_full,
        (2 * local_width, shared_count),
        2,
    )
    normed_grad = normed_grad.reshape(row_count, width)
    token_grad = norm_backward(flat_tokens, in_scale, norm_gain, normed_grad)
    token_grad = token_grad + cot_rows.astype(f32)
    owned = owned.reshape(
        group_devices, per_owner, local_width // group_devices, width
    )
    shared_all = shared_all.reshape(seq_devices, 2, shared_rows, in_rows // 2)
    small_all = small_all.reshape(seq_devices, -1, 128)
    mixed_out = (flat_tokens + valid_rows * branch).astype(bf16).reshape(tokens.shape)
    tail = jnp.transpose(shared_all, (0, 2, 1, 3)).reshape(shared_count, in_rows)
    in_weight_grad = assemble_in(gathered, tail).T
    out_weight_grad, conv_weight_grad, conv_bias_grad, gain_grad, head_all, norm_grad = (
        assemble_out(owned, small_all, widths, local_heads)
    )
    return (
        mixed_out,
        token_grad.reshape(tokens.shape),
        norm_grad[0],
        in_weight_grad,
        conv_weight_grad,
        conv_bias_grad[0],
        head_all[0, :head_count],
        head_all[1, :head_count],
        head_all[2, :head_count],
        gain_grad[0],
        out_weight_grad,
    )


def solution(mesh):
    placed = (
        P("wa", "seq", None),
        P("wa"),
        P(),
        P("wa", None),
        P(),
        P(),
        P(),
        P(),
        P(),
        P(),
        P("wa", None),
        P("wa", "seq", None),
    )
    return jax.shard_map(
        body,
        mesh=mesh,
        in_specs=placed,
        out_specs=(
            P("wa", "seq", None),
            P("wa", "seq", None),
            P(),
            P("wa", None),
            P(),
            P(),
            P(),
            P(),
            P(),
            P(),
            P("wa", None),
        ),
        check_vma=False,
    )
```

```python
import functools

import jax
import jax.numpy as jnp
import numpy as np
from jax import lax
from jax.experimental import pallas as pl
from jax.experimental.pallas import tpu as pltpu
from jax.sharding import PartitionSpec as P

KW = 4
EPS = 1e-05
HIGHEST = lax.Precision.HIGHEST
MESH = pl.DeviceIdType.MESH


def row_scale(values):
    return lax.rsqrt(jnp.mean(values * values, axis=-1, keepdims=True) + EPS)


def norm_backward(values, row_scales, gain_vec, grad_out):
    weighted = grad_out * gain_vec
    return row_scales * weighted - values * row_scales**3 * jnp.mean(
        weighted * values, axis=-1, keepdims=True
    )


def dot(a, b, ca, cb, precision=None):
    return lax.dot_general(
        a, b, (((ca,), (cb,)), ((), ())), precision=precision, preferred_element_type=jnp.float32
    )


def chunk_front(proj_ref, ext, taps_ref, heads_ref, tri_ref, widths, head_start):
    lw, bc = widths
    rows = proj_ref.shape[2]
    ext[8:, :] = proj_ref[0, 0, :, lw : 2 * lw + bc].astype(jnp.float32)
    conv = taps_ref[KW : KW + 1, :]
    for k in range(KW):
        conv = conv + taps_ref[k : k + 1, :] * ext[5 + k : 5 + k + rows, :]
    conv_sig = lax.logistic(conv)
    act = conv * conv_sig
    raw = proj_ref[0, 0, :, 2 * lw + bc :].astype(jnp.float32)
    step_in = pltpu.roll(raw, lax.rem(128 - head_start, 128), 1) + heads_ref[0:1, :]
    steps = jnp.maximum(step_in, 0.0) + jnp.log1p(jnp.exp(-jnp.abs(step_in)))
    rates = heads_ref[1:2, :] * steps
    cum = dot(tri_ref[...], rates, 1, 0, HIGHEST)
    return conv, conv_sig, act, step_in, steps, rates, cum


def head_masks(rows, head_size):
    lane = lax.broadcasted_iota(jnp.int32, (rows, 128), 1)
    row = lax.broadcasted_iota(jnp.int32, (rows, rows), 0)
    col = lax.broadcasted_iota(jnp.int32, (rows, rows), 1)
    return lane, row >= col


def forward_chunk(
    widths,
    head_size,
    head_start,
    start,
    proj_ref,
    taps_ref,
    heads_ref,
    wide_ref,
    spread_ref,
    tri_ref,
    gated_ref,
    y_ref,
    enter_ref,
    state,
    ext,
    halo,
):
    lw, bc = widths
    bf16, f32 = jnp.bfloat16, jnp.float32
    rows = proj_ref.shape[2]
    per_tile = 128 // head_size

    @pl.when(start)
    def _():
        state[...] = jnp.zeros_like(state)
        halo[...] = jnp.zeros_like(halo)

    ext[0:8, :] = halo[...]
    _, _, act, _, steps, _, cum = chunk_front(
        proj_ref, ext, taps_ref, heads_ref, tri_ref, widths, head_start
    )
    halo[...] = ext[rows : rows + 8, :]
    x = act[:, :lw]
    xb = x.astype(bf16)
    b_rows = act[:, lw : lw + bc // 2].astype(bf16)
    c_rows = act[:, lw + bc // 2 :].astype(bf16)
    cum_t, steps_t = cum.T, steps.T
    last = cum[rows - 1 : rows, :]
    grow = dot(jnp.exp(cum).astype(bf16), spread_ref[...], 1, 0)
    tail = dot((jnp.exp(last - cum) * steps).astype(bf16), spread_ref[...], 1, 0)
    scores = dot(c_rows, b_rows, 1, 1)
    entering = state[...].astype(bf16)
    enter_ref[0, 0] = entering
    y = dot(c_rows, entering, 1, 1) * grow + wide_ref[1:2, :] * x
    added = dot((x * tail).astype(bf16), b_rows, 0, 0)
    lane, causal = head_masks(rows, head_size)
    gate = proj_ref[0, 0, :, :lw].astype(f32)
    silu_gate = gate * lax.logistic(gate)
    for tile in range(lw // 128):
        cols = slice(tile * 128, (tile + 1) * 128)
        inner = None
        for sub in range(per_tile):
            head = tile * per_tile + sub
            log_decay = cum[:, head : head + 1] - cum_t[head : head + 1, :]
            decay = jnp.exp(jnp.where(causal, log_decay, -1e30))
            weights = (scores * decay * steps_t[head : head + 1, :]).astype(bf16)
            part = dot(weights, xb[:, cols], 1, 0)
            inner = part if inner is None else jnp.where(lane >= sub * head_size, part, inner)
            span = slice(head * head_size, (head + 1) * head_size)
            state[span, :] = (
                jnp.exp(cum[rows - 1 : rows, head : head + 1]) * state[span, :] + added[span, :]
            )
        y_tile = y[:, cols] + inner
        y_ref[0, 0, :, cols] = y_tile.astype(bf16)
        gated_ref[:, cols] = (y_tile * silu_gate[:, cols]).astype(bf16)


def backward_kernel(
    widths,
    head_size,
    chunks,
    proj_ref,
    before_ref,
    y_ref,
    enter_ref,
    grad_ref,
    taps_ref,
    heads_ref,
    wide_ref,
    spread_ref,
    fold_ref,
    tri_ref,
    upper_ref,
    normed_ref,
    out_ref,
    turned_ref,
    taps_acc,
    skip_acc,
    head_acc,
    swapped_ref,
    lam,
    ext,
    later,
    after,
    swap_send,
    swap_recv,
    swap_local,
):
    lw, bc = widths
    state_size = bc // 2
    bf16, f32 = jnp.bfloat16, jnp.float32
    rows = proj_ref.shape[2]
    per_tile = 128 // head_size
    chunk = chunks - 1 - pl.program_id(1)
    head_start = lax.axis_index("seq") * (lw // head_size)

    me, group = lax.axis_index("seq"), lax.axis_index("wa")
    swaps = [
        push(
            normed_ref.at[other],
            swapped_ref.at[me],
            swap_send.at[k],
            swap_recv.at[k],
            (other, group),
        )
        for k, other in enumerate(others(me, chunks))
    ]
    swap_kept = pltpu.make_async_copy(normed_ref.at[me], swapped_ref.at[me], swap_local)

    @pl.when((pl.program_id(0) == 0) & (pl.program_id(1) == 0))
    def _():
        greet([(other, group) for other in others(me, chunks)])
        for copy in swaps:
            copy.start()
        swap_kept.start()
        taps_acc[...] = jnp.zeros_like(taps_acc)
        skip_acc[...] = jnp.zeros_like(skip_acc)
        head_acc[...] = jnp.zeros_like(head_acc)

    @pl.when(pl.program_id(1) == 0)
    def _():
        lam[...] = jnp.zeros_like(lam)
        after[...] = jnp.zeros_like(after)

    ext[0:8, :] = jnp.where(
        chunk > 0, before_ref[0, 0, 8:16, lw : 2 * lw + bc].astype(f32), 0.0
    )
    conv, conv_sig, act, step_in, steps, rates, cum = chunk_front(
        proj_ref, ext, taps_ref, heads_ref, tri_ref, widths, head_start
    )
    x = act[:, :lw]
    xb = x.astype(bf16)
    b_rows = act[:, lw : lw + state_size].astype(bf16)
    c_rows = act[:, lw + state_size :].astype(bf16)
    cum_t, steps_t = cum.T, steps.T
    last = cum[rows - 1 : rows, :]
    to_end = jnp.exp(last - cum)
    tail_heads = to_end * steps
    grow = dot(jnp.exp(cum).astype(bf16), spread_ref[...], 1, 0)
    tail = dot(tail_heads.astype(bf16), spread_ref[...], 1, 0)
    scores = dot(c_rows, b_rows, 1, 1)

    gate = proj_ref[0, 0, :, :lw].astype(f32)
    gate_sig = lax.logistic(gate)
    grad = grad_ref[0, 0].astype(f32)
    y_grad = grad * gate * gate_sig
    out_ref[0, 0, :, :lw] = (
        grad * y_ref[0, 0].astype(f32) * (gate_sig * (1.0 + gate * (1.0 - gate_sig)))
    ).astype(bf16)
    yb = y_grad.astype(bf16)

    entering = enter_ref[0, 0]
    grown = y_grad * grow
    grown_b = grown.astype(bf16)
    c_grad = dot(grown_b, entering, 1, 0)
    carried = dot((grown * dot(c_rows, entering, 1, 1)).astype(bf16), fold_ref[...], 1, 0)
    lam_now = lam[...]
    lam_b = lam_now.astype(bf16)
    from_lam = dot(b_rows, lam_b, 1, 1)
    b_grad = dot((x * tail).astype(bf16), lam_b, 1, 0)
    x_lam = dot((x * from_lam).astype(bf16), fold_ref[...], 1, 0)
    x_grad = wide_ref[1:2, :] * y_grad + tail * from_lam
    skip_acc[0:1, :] += jnp.sum(y_grad * x, axis=0, keepdims=True)
    ones = jnp.ones((8, state_size), bf16)
    kept = dot(
        dot(ones, (lam_now * entering.astype(f32)).astype(bf16), 1, 1),
        fold_ref[...].astype(f32),
        1,
        0,
        HIGHEST,
    )
    through = jnp.exp(last) * kept[0:1, :]
    lam_add = dot(grown_b, c_rows, 0, 0)

    lane, causal = head_masks(rows, head_size)
    score_grad = None
    row_sums = jnp.zeros((rows, 128), f32)
    col_sums = []
    x_tiles = []
    for tile in range(lw // 128):
        cols = slice(tile * 128, (tile + 1) * 128)
        inner = None
        for sub in range(per_tile):
            head = tile * per_tile + sub
            log_decay = cum[:, head : head + 1] - cum_t[head : head + 1, :]
            decay = jnp.exp(jnp.where(causal, log_decay, -1e30))
            step_row = steps_t[head : head + 1, :]
            weights = (scores * decay * step_row).astype(bf16)
            inside = (lane >= sub * head_size) & (lane < (sub + 1) * head_size)
            y_head = jnp.where(inside, yb[:, cols], jnp.zeros_like(yb[:, cols]))
            weights_grad = dot(y_head, xb[:, cols], 1, 1)
            part = dot(weights, yb[:, cols], 0, 0)
            inner = part if inner is None else jnp.where(lane >= sub * head_size, part, inner)
            decayed = weights_grad * decay
            stepped = decayed * step_row
            score_grad = stepped if score_grad is None else score_grad + stepped
            col_sums.append(jnp.sum(decayed * scores, axis=0, keepdims=True))
            row_sum = jnp.sum(stepped * scores, axis=1, keepdims=True)
            row_sums = row_sums + jnp.where(lane == head, row_sum, 0.0)
            span = slice(head * head_size, (head + 1) * head_size)
            lam[span, :] = (
                jnp.exp(cum[rows - 1 : rows, head : head + 1]) * lam_now[span, :] + lam_add[span, :]
            )
        x_tiles.append(x_grad[:, cols] + inner)
    col_sums.append(jnp.zeros((rows - len(col_sums), rows), f32))
    col_sum = jnp.concatenate(col_sums, axis=0).T
    source = row_sums - steps * col_sum + carried
    rates_grad = (
        dot(upper_ref[...], source, 1, 0, HIGHEST)
        + dot(1.0 - upper_ref[...], tail_heads * x_lam, 1, 0, HIGHEST)
        + through
    )
    steps_grad = col_sum + to_end * x_lam + rates_grad * heads_ref[1:2, :]
    raw_grad = steps_grad * lax.logistic(step_in)
    out_ref[0, 0, :, 2 * lw + bc :] = pltpu.roll(raw_grad, head_start, 1).astype(bf16)
    head_acc[0:1, :] += jnp.sum(raw_grad, axis=0, keepdims=True)
    head_acc[1:2, :] += jnp.sum(rates_grad * rates, axis=0, keepdims=True)
    score_b = score_grad.astype(bf16)
    c_grad = c_grad + dot(score_b, b_rows, 1, 0)
    b_grad = b_grad + dot(score_b, c_rows, 0, 0)
    act_grad = jnp.concatenate(x_tiles + [b_grad, c_grad], axis=1)
    conv_grad = act_grad * (conv_sig * (1.0 + conv * (1.0 - conv_sig)))
    later[0:rows, :] = conv_grad
    later[rows : rows + 8, :] = after[...]
    after[...] = conv_grad[0:8, :]
    total = None
    for k in range(KW):
        term = taps_ref[k : k + 1, :] * later[3 - k : 3 - k + rows, :]
        total = term if total is None else total + term
        taps_acc[k : k + 1, :] += jnp.sum(conv_grad * ext[5 + k : 5 + k + rows, :], axis=0, keepdims=True)
    taps_acc[KW : KW + 1, :] += jnp.sum(conv_grad, axis=0, keepdims=True)

    @pl.when((pl.program_id(0) == pl.num_programs(0) - 1) & (chunk == 0))
    def _():
        head_acc[2:3, :] = dot(
            skip_acc[...], fold_ref[...].astype(f32), 1, 0, HIGHEST
        )[0:1, :]
        for copy in swaps:
            copy.wait()
        swap_kept.wait()
    out_ref[0, 0, :, lw : 2 * lw + bc] = total.astype(bf16)
    turned_ref[...] = out_ref[0, 0].T


def whole_spec(array):
    return pl.BlockSpec(array.shape, lambda q, c: (0,) * array.ndim)


def scan_tables(rows, local_width, head_size):
    head_of = np.arange(local_width) // head_size
    spread = (np.arange(128)[:, None] == head_of[None, :]).astype(jnp.bfloat16)
    tri = (np.arange(rows)[:, None] >= np.arange(rows)[None, :]).astype(np.float32)
    return [jnp.asarray(t) for t in (spread, spread.T.copy(), tri, tri.T.copy())]


def scan_backward(
    proj, y, enter, grad, taps, heads, wide, spread, fold, tri, upper, normed, widths, head_size, collective_id
):
    chunks, seqs, rows, cols = proj.shape
    lw, bc = widths
    block = lambda *tail: pl.BlockSpec((1, 1) + tail, lambda q, c: (chunks - 1 - c, q, 0, 0))
    before = pl.BlockSpec(
        (1, 1, 16, cols),
        lambda q, c: (jnp.maximum(chunks - 2 - c, 0), q, rows // 16 - 1, 0),
    )
    tables = (taps, heads, wide, spread, fold, tri, upper)
    sums = [(8, lw + bc), (8, lw), (8, 128)]
    return pl.pallas_call(
        functools.partial(backward_kernel, widths, head_size, chunks),
        grid=(seqs, chunks),
        in_specs=[block(rows, cols), before, block(rows, lw), block(lw, bc // 2), block(rows, lw)]
        + [whole_spec(t) for t in tables]
        + [ANY],
        out_specs=[
            block(rows, cols),
            pl.BlockSpec((cols, rows), lambda q, c: (0, (chunks - 1 - c) * seqs + q)),
        ]
        + [pl.BlockSpec(s, lambda q, c: (0, 0)) for s in sums]
        + [ANY],
        out_shape=[
            jax.ShapeDtypeStruct(proj.shape, jnp.bfloat16),
            jax.ShapeDtypeStruct((cols, chunks * seqs * rows), jnp.bfloat16),
        ]
        + [jax.ShapeDtypeStruct(s, jnp.float32) for s in sums]
        + [jax.ShapeDtypeStruct(normed.shape, normed.dtype)],
        scratch_shapes=[
            pltpu.VMEM((lw, bc // 2), jnp.float32),
            pltpu.VMEM((rows + 8, lw + bc), jnp.float32),
            pltpu.VMEM((rows + 8, lw + bc), jnp.float32),
            pltpu.VMEM((8, lw + bc), jnp.float32),
            pltpu.SemaphoreType.DMA((chunks - 1,)),
            pltpu.SemaphoreType.DMA((chunks - 1,)),
            pltpu.SemaphoreType.DMA,
        ],
        compiler_params=comm_params(collective_id, 60),
        name="scan_backward",
    )(proj, proj, y, enter, grad, *tables, normed)


def ring_pos(index, size):
    row, side = index // 2, index % 2
    return row + side * (size - 1 - 2 * row)


def ring_index(pos, size):
    side = pos // (size // 2)
    row = pos + side * (size - 1 - 2 * pos)
    return row * 2 + side


def greet(peers):
    barrier = pltpu.get_barrier_semaphore()
    for peer in peers:
        pl.semaphore_signal(barrier, inc=1, device_id=peer, device_id_type=MESH)
    pl.semaphore_wait(barrier, len(peers))


def push(source, target, send_sem, recv_sem, peer):
    return pltpu.make_async_remote_copy(
        source, target, send_sem, recv_sem, device_id=peer, device_id_type=MESH
    )


def neighbours(size):
    me, group = lax.axis_index("seq"), lax.axis_index("wa")
    pos = ring_pos(me, size)
    right = (ring_index((pos + 1) % size, size), group)
    left = (ring_index((pos + size - 1) % size, size), group)
    return me, group, pos, right, left


def others(index, size):
    return [(index + offset) % size for offset in range(1, size)]


ANY = pl.BlockSpec(memory_space=pl.ANY)
VMEM = pl.BlockSpec(memory_space=pltpu.VMEM)


def comm_params(collective_id, megabytes=None):
    limit = None if megabytes is None else megabytes * 2**20
    return pltpu.CompilerParams(
        collective_id=collective_id, has_side_effects=True, vmem_limit_bytes=limit
    )


class RingGather:
    def __init__(self, size, x_ref, o_ref, send_sem, recv_sem, local_sem):
        self.size, self.x, self.o = size, x_ref, o_ref
        self.send, self.recv, self.local = send_sem, recv_sem, local_sem
        self.chunks = x_ref.shape[1]
        self.me, _, self.pos, self.right, self.left = neighbours(size)

    def copy(self, step, chunk, way, first=False):
        size = self.size
        if way == 0:
            block, peer = ring_index((self.pos - step + size) % size, size), self.right
        else:
            block, peer = ring_index((self.pos + step) % size, size), self.left
        source = self.x.at[way, chunk] if first else self.o.at[block, way, chunk]
        return push(
            source,
            self.o.at[block, way, chunk],
            self.send.at[step, chunk, way],
            self.recv.at[step, chunk, way],
            peer,
        )

    def kept(self):
        return pltpu.make_async_copy(self.x, self.o.at[self.me], self.local)

    def start(self):
        self.kept().start()
        for chunk in range(self.chunks):
            for way in range(2):
                self.copy(0, chunk, way, True).start()

    def advance(self, step):
        for chunk in range(self.chunks):
            for way in range(2):
                self.copy(step - 1, chunk, way).wait_recv()
                self.copy(step, chunk, way).start()

    def arrive(self):
        last = self.size - 2
        for chunk in range(self.chunks):
            for way in range(2):
                self.copy(last, chunk, way).wait_recv()

    def finish(self):
        self.arrive()
        self.settle()

    def settle(self):
        def drain(step, carry):
            for chunk in range(self.chunks):
                for way in range(2):
                    self.copy(step, chunk, way).wait_send()
            return carry

        lax.fori_loop(0, self.size - 1, drain, 0)
        self.kept().wait()


def ring_parts(x, chunks):
    return x.reshape(2, chunks, x.shape[0] // (2 * chunks), x.shape[1])


def ring_sems(size, chunks):
    return [
        pltpu.SemaphoreType.DMA((size - 1, chunks, 2)),
        pltpu.SemaphoreType.DMA((size - 1, chunks, 2)),
        pltpu.SemaphoreType.DMA,
    ]


def front_kernel(
    widths,
    head_size,
    size,
    groups,
    inner,
    x_ref,
    w_ref,
    cot_ref,
    shard_ref,
    conv_ref,
    conv_bias_ref,
    params_ref,
    out_gain_ref,
    spread_ref,
    tri_ref,
    rows_ref,
    weights_ref,
    proj_ref,
    y_ref,
    enter_ref,
    normed_ref,
    turned_ref,
    grad_ref,
    gain_acc,
    taps_ref,
    heads_ref,
    wide_ref,
    branch_ref,
    part_ref,
    weights,
    projected,
    taken,
    state,
    ext,
    halo,
    gated,
    out_grad,
    y_held,
    enter_held,
    out_rows,
    out_turned,
    sums,
    landing,
    normed_held,
    turned_held,
    grad_held,
    result_sem,
    weight_send,
    weight_recv,
    weight_local,
    take_sem,
    proj_sem,
    held_sem,
    shard_send,
    shard_recv,
    shard_local,
    pair_send,
    pair_recv,
    *ring_refs,
):
    bf16, f32 = jnp.bfloat16, jnp.float32
    me, group, pos, right, left = neighbours(size)
    rows, lw = gated.shape[2:]
    depth = weights.shape[2]
    peers = [(other, group) for other in others(me, size)]
    mates = [(me, other) for other in others(group, groups)]
    sibling = (me, group + 1 - 2 * lax.rem(group, 2))
    across = (me, lax.rem(group + 2, groups))
    per_owner = size // groups
    chosen = lax.rem(me, per_owner)
    owner = me // per_owner
    greet(mates + peers)
    ring = RingGather(size, x_ref, rows_ref, *ring_refs[0:3])
    cot_ring = RingGather(size, cot_ref, branch_ref, *ring_refs[3:6])
    ring.start()
    bc = widths[1]
    used = w_ref.shape[0] - 2 * inner
    lane_at = pl.multiple_of(me * lw, 128)
    spans = (
        (pl.ds(lane_at, lw), pl.ds(0, lw)),
        (pl.ds(pl.multiple_of(inner + me * lw, 128), lw), pl.ds(lw, lw)),
        (pl.ds(2 * inner, used), pl.ds(2 * lw, used)),
    )
    sent = [
        push(
            w_ref.at[here],
            weights.at[group, there],
            weight_send.at[k, part],
            weight_recv.at[k, part],
            mate,
        )
        for k, mate in enumerate(mates)
        for part, (here, there) in enumerate(spans)
    ]
    for copy in sent:
        copy.start()
    kept = [
        pltpu.make_async_copy(w_ref.at[here], weights.at[group, there], weight_local.at[part])
        for part, (here, there) in enumerate(spans)
    ]
    for copy in kept:
        copy.start()
    blank = weights.shape[1] - 2 * lw - used
    for part in range(groups):
        weights[part, 2 * lw + used :, :] = jnp.zeros((blank, depth), bf16)
    heads_here = lw // head_size
    head_start = me * heads_here
    taps_ref[...] = jnp.zeros_like(taps_ref)
    taps_ref[0:KW, :lw] = conv_ref[:, pl.ds(lane_at, lw)]
    taps_ref[0:KW, lw:] = conv_ref[:, inner:]
    taps_ref[KW : KW + 1, :lw] = conv_bias_ref[:, pl.ds(lane_at, lw)]
    taps_ref[KW : KW + 1, lw:] = conv_bias_ref[:, inner:]
    params = pltpu.roll(params_ref[...], lax.rem(128 - head_start, 128), 1)
    params = jnp.where(
        lax.broadcasted_iota(jnp.int32, params.shape, 1) < heads_here, params, 0.0
    )
    at_row = lax.broadcasted_iota(jnp.int32, params.shape, 0)
    at_lane = lax.broadcasted_iota(jnp.int32, params.shape, 1)
    slopes = jnp.where(at_lane < heads_here, -jnp.exp(params), 0.0)
    heads_ref[...] = jnp.where(at_row == 1, slopes, params)
    wide_ref[...] = jnp.zeros_like(wide_ref)
    wide_ref[0:1, :] = out_gain_ref[:, pl.ds(lane_at, lw)]
    wide_ref[1:2, :] = dot(params, spread_ref[...].astype(f32), 1, 0, HIGHEST)[2:3, :]

    def shards(step, offset=0):
        at = lax.rem(chosen + offset, per_owner)
        held_by = across[1] if step == 2 else group
        source = part_ref.at[held_by, at] if step == 2 else shard_ref.at[at]
        return push(
            source,
            part_ref.at[held_by, at],
            shard_send.at[step, offset],
            shard_recv.at[step, offset],
            across if step == 0 else sibling,
        )

    def block_of(pair, way):
        return ring_index((pos - pair + size) % size if way == 0 else (pos + pair) % size, size)

    def stream(source_ref, landed_ref, low, high, compute, own=False):
        def take(pair, slot, way):
            source = source_ref.at[way] if own else landed_ref.at[block_of(pair, way), way]
            return pltpu.make_async_copy(source, taken.at[slot, way], take_sem.at[slot, way])

        for way in range(2):
            take(low, lax.rem(low, 2), way).start()

        def one(pair, carry):
            slot = lax.rem(pair, 2)
            for way in range(2):
                take(pair, slot, way).wait()

            @pl.when(pair + 1 < high)
            def _():
                for way in range(2):
                    take(pair + 1, 1 - slot, way).start()

            compute(pair, slot)
            return carry

        lax.fori_loop(low, high, one, 0)

    def put(pair, way):
        block = block_of(pair, way)
        return pltpu.make_async_copy(
            projected.at[block, way], proj_ref.at[block, way], proj_sem.at[pair, way]
        )

    def project(pair, slot):
        for way in range(2):
            x = taken[slot, way].reshape(rows, taken.shape[4])
            total = None
            for part in range(groups):
                term = dot(x[:, part * depth : (part + 1) * depth], weights[part], 1, 1)
                total = term if total is None else total + term
            projected[block_of(pair, way), way] = total.astype(bf16)
            put(pair, way).start()

    def advance(step, carry):
        ring.advance(step)
        return carry

    def turns(turn, count):
        return 1 + (turn * (size - 2)) // count, 1 + ((turn + 1) * (size - 2)) // count

    middle = size // 2 + 1
    lax.fori_loop(1, middle, advance, 0)
    for copy in kept:
        copy.wait()
    for copy in sent:
        copy.wait_recv()
    flushed = pltpu.make_async_copy(weights, weights_ref, weight_local.at[0])
    flushed.start()
    shards(0).start()
    shards(1).start()
    stream(x_ref, rows_ref, 0, 1, project, own=True)

    def late(step, carry):
        ring.advance(step)
        stream(x_ref, rows_ref, *turns(step - middle, size - 1 - middle), project)
        return carry

    lax.fori_loop(middle, size - 2, late, 0)
    ring.advance(size - 2)
    cot_ring.start()
    stream(x_ref, rows_ref, *turns(size - 2 - middle, size - 1 - middle), project)
    ring.arrive()
    stream(x_ref, rows_ref, size - 1, size, project)
    cot_ring.advance(1)

    def keep(index, slot):
        seq, chunk = index // size, lax.rem(index, size)
        return [
            pltpu.make_async_copy(y_held.at[slot, 0], y_ref.at[chunk, seq], held_sem.at[slot, 0]),
            pltpu.make_async_copy(
                enter_held.at[slot, 0], enter_ref.at[chunk, seq], held_sem.at[slot, 1]
            ),
        ]

    def scan(index, carry):
        seq, chunk = index // size, lax.rem(index, size)
        slot = lax.rem(index, 2)

        @pl.when(index >= 2)
        def _():
            for copy in keep(index - 2, slot):
                copy.wait()

        forward_chunk(
            widths,
            head_size,
            head_start,
            chunk == 0,
            projected.at[pl.ds(chunk, 1), pl.ds(seq, 1)],
            taps_ref,
            heads_ref,
            wide_ref,
            spread_ref,
            tri_ref,
            gated.at[chunk, seq],
            y_held.at[pl.ds(slot, 1)],
            enter_held.at[pl.ds(slot, 1)],
            state,
            ext,
            halo,
        )
        for copy in keep(index, slot):
            copy.start()

        @pl.when(index == size + 2)
        def _():
            cot_ring.advance(2)

        return carry

    lax.fori_loop(0, 2 * size, scan, 0)
    first, second, third = (shards(step) for step in range(3))
    first.wait_recv()
    third.start()
    for offset in range(1, per_owner):
        shards(0, offset).start()
        shards(1, offset).start()
    second.wait_recv()
    cot_ring.advance(3)
    third.wait_recv()

    @pl.when(owner == group)
    def _():
        loaded = pltpu.make_async_copy(shard_ref.at[chosen], out_rows, shard_local)
        loaded.start()
        loaded.wait()

    @pl.when(owner != group)
    def _():
        loaded = pltpu.make_async_copy(part_ref.at[owner, chosen], out_rows, shard_local)
        loaded.start()
        loaded.wait()

    out_turned[...] = out_rows[...].T
    ones = jnp.ones((8, lw), bf16)

    def compute(pair, slot):
        for way in range(2):
            block = block_of(pair, way)
            values = dot(taken[slot, way].reshape(rows, taken.shape[4]), out_turned[...], 1, 0)
            out_grad[block, way] = values
            here = gated[block, way].astype(f32)
            weighted = values * wide_ref[0:1, :] * here
            at = pl.ds(block * 2 + way, 1)
            sums[0, at, :] = dot(ones, (here * here).astype(bf16), 1, 1)[0:1, :]
            sums[1, at, :] = dot(ones, weighted.astype(bf16), 1, 1)[0:1, :]

    stream(cot_ref, branch_ref, 0, 1, compute, own=True)
    stream(cot_ref, branch_ref, *turns(0, size - 4), compute)

    def cot_late(step, carry):
        cot_ring.advance(step)
        stream(cot_ref, branch_ref, *turns(step - 3, size - 4), compute)
        return carry

    lax.fori_loop(4, size - 1, cot_late, 0)
    cot_ring.arrive()
    stream(cot_ref, branch_ref, size - 1, size, compute)
    copies = [
        push(sums, landing.at[k], pair_send.at[k], pair_recv.at[k], peer)
        for k, peer in enumerate(peers)
    ]
    for copy in copies:
        copy.start()
    total = sums[...]
    for k, copy in enumerate(copies):
        copy.wait_recv()
        total = total + landing[k]
    scale = lax.rsqrt(total[0] / inner + EPS)
    pull = scale * scale * scale * (total[1] / inner)
    fill = jnp.zeros((128 - 2 * size, rows), f32)
    scale_turned = jnp.concatenate([scale, fill]).T
    pull_turned = jnp.concatenate([pull, fill]).T
    lane = lax.broadcasted_iota(jnp.int32, (rows, 128), 1)
    gain_acc[...] = jnp.zeros_like(gain_acc)

    def results(block):
        pairs = ((normed_held, normed_ref), (turned_held, turned_ref), (grad_held, grad_ref))
        return [
            pltpu.make_async_copy(held.at[block], out.at[block], result_sem.at[k, block])
            for k, (held, out) in enumerate(pairs)
        ]

    def finish(block, carry):
        for way in range(2):
            mask = lane == block * 2 + way
            by = jnp.sum(jnp.where(mask, scale_turned, 0.0), axis=1, keepdims=True)
            less = jnp.sum(jnp.where(mask, pull_turned, 0.0), axis=1, keepdims=True)
            here = gated[block, way].astype(f32)
            values = out_grad[block, way]
            scaled = here * by
            normed = (scaled * wide_ref[0:1, :]).astype(bf16)
            normed_held[block, way] = normed
            turned_held[block, :, way * rows : (way + 1) * rows] = normed.T
            grad_held[block, way] = (values * wide_ref[0:1, :] * by - here * less).astype(bf16)
            gain_acc[0:1, :] += jnp.sum(values * scaled, axis=0, keepdims=True)
        for copy in results(block):
            copy.start()
        return carry

    lax.fori_loop(0, size, finish, 0)
    for offset in range(1, per_owner):
        shards(0, offset).wait_recv()
        shards(2, offset).start()
    for copy in sent + copies + [first, second, third]:
        copy.wait_send()
    flushed.wait()
    for index in (2 * size - 2, 2 * size - 1):
        for copy in keep(index, index % 2):
            copy.wait()

    def settle(pair, carry):
        for way in range(2):
            put(pair, way).wait()
        for copy in results(pair):
            copy.wait()
        return carry

    lax.fori_loop(0, size, settle, 0)
    ring.settle()
    cot_ring.settle()
    for offset in range(1, per_owner):
        shards(1, offset).wait_recv()
        shards(2, offset).wait_recv()
        for step in range(3):
            shards(step, offset).wait_send()


def front(x, weight, cot, shard, params, inner, widths, head_size, collective_id):
    size, groups = lax.axis_size("seq"), lax.axis_size("wa")
    parts, cot_parts = ring_parts(x, 2), ring_parts(cot, 2)
    depth = weight.shape[1]
    rows = x.shape[0] // 2
    width = x.shape[1]
    lw, bc = widths
    cols = 2 * lw + bc + 128
    per_owner = size // groups
    bf16, f32, DMA, vmem = jnp.bfloat16, jnp.float32, pltpu.SemaphoreType.DMA, pltpu.VMEM
    whole = (size, 2, rows, lw)
    shape = jax.ShapeDtypeStruct
    return pl.pallas_call(
        functools.partial(front_kernel, widths, head_size, size, groups, inner),
        out_shape=[
            shape((size,) + parts.shape, bf16),
            shape((groups, cols, depth), bf16),
            shape((size, 2, rows, cols), bf16),
            shape(whole, bf16),
            shape((size, 2, lw, bc // 2), bf16),
            shape(whole, bf16),
            shape((size, lw, 2 * rows), bf16),
            shape(whole, bf16),
            shape((8, lw), f32),
            shape((8, lw + bc), f32),
            shape((8, 128), f32),
            shape((8, lw), f32),
            shape((size,) + parts.shape, bf16),
            shape((groups, per_owner, lw, width), bf16),
        ],
        in_specs=[ANY] * 4 + [VMEM] * 6,
        out_specs=[ANY] * 8 + [VMEM] * 4 + [ANY] * 2,
        scratch_shapes=[
            vmem((groups, cols, depth), bf16),
            vmem((size, 2, rows, cols), bf16),
            vmem((2,) + parts.shape, bf16),
            vmem((lw, bc // 2), f32),
            vmem((rows + 8, lw + bc), f32),
            vmem((8, lw + bc), f32),
            vmem(whole, bf16),
            vmem(whole, f32),
            vmem((2, 1, rows, lw), bf16),
            vmem((2, 1, lw, bc // 2), bf16),
            vmem((lw, width), bf16),
            vmem((width, lw), bf16),
            vmem((2, 2 * size, rows), f32),
            vmem((size - 1, 2, 2 * size, rows), f32),
            vmem(whole, bf16),
            vmem((size, lw, 2 * rows), bf16),
            vmem(whole, bf16),
            DMA((3, size)),
            DMA((groups - 1, 3)),
            DMA((groups - 1, 3)),
            DMA((3,)),
            DMA((2, 2)),
            DMA((size, 2)),
            DMA((2, 2)),
            DMA((3, per_owner)),
            DMA((3, per_owner)),
            DMA,
            DMA((size - 1,)),
            DMA((size - 1,)),
        ]
        + ring_sems(size, 2)
        + ring_sems(size, 2),
        compiler_params=comm_params(collective_id, 62),
        name="front",
    )(parts, weight, cot_parts, shard, *params)


def finish_kernel(
    size,
    groups,
    counts,
    grad_ref,
    weight_ref,
    normed_ref,
    turned_ref,
    out_ref,
    branch_grad_ref,
    tokens_ref,
    scale_ref,
    taps_ref,
    gain_ref,
    heads_ref,
    swapped_ref,
    shard_ref,
    out_full_ref,
    rows_ref,
    gathered_ref,
    pieces_ref,
    owned_ref,
    shared_out,
    small_out,
    branch_ref,
    landing,
    slots,
    first,
    parts,
    total,
    taken,
    turned,
    out_total,
    out_parts,
    out_landing,
    out_taken,
    piece,
    main,
    shared,
    shared_land,
    shared_sum,
    small,
    small_land,
    send_sem,
    recv_sem,
    part_send,
    part_recv,
    take_sem,
    out_send,
    out_recv,
    owned_send,
    owned_recv,
    owned_local,
    pair_send,
    pair_recv,
    mate_send,
    mate_recv,
    *ring_refs,
):
    me, group, pos, right, left = neighbours(size)
    mates = [(me, index) for index in others(group, groups)]
    peers = [(index, group) for index in others(me, size)]
    tiles, rows, tile = slots.shape[2:]
    cols = total.shape[0]
    bf16, f32 = jnp.bfloat16, jnp.float32
    out_ring = RingGather(size, piece, pieces_ref, *ring_refs[0:3])
    main_ring = RingGather(size, main, gathered_ref, *ring_refs[3:6])
    shared_ring = RingGather(size, shared_sum, shared_out, *ring_refs[6:9])
    small_ring = RingGather(size, small, small_out, *ring_refs[9:12])
    fetch_sem, weights_taken, held, held_sem, out_turned = ring_refs[12:17]
    weight_held, swapped_held, load_sem = ring_refs[17:20]
    loads = [
        pltpu.make_async_copy(weight_ref.at[part], weight_held.at[part], load_sem.at[part])
        for part in range(groups)
    ]
    swapped_load = pltpu.make_async_copy(swapped_ref, swapped_held, load_sem.at[groups])

    def target(step, way):
        shift = (pos - 1 - step + 2 * size) if way == 0 else (pos + 1 + step)
        return ring_index(shift % size, size)

    def fetch(step, way):
        slot = lax.rem(step, 2)
        return pltpu.make_async_copy(
            grad_ref.at[target(step, way), way], held.at[slot, way], held_sem.at[slot, way]
        )

    def term(step, way, at):
        return dot(held[lax.rem(step, 2), way], weight_held[at], 1, 0)

    def hop(step, way, at, source):
        return push(
            source,
            slots.at[step, way, at],
            send_sem.at[step, way, at],
            recv_sem.at[step, way, at],
            right if way == 0 else left,
        )

    def begin(at, carry):
        for way in range(2):
            first[way, at] = term(0, way, at).astype(bf16)
            hop(0, way, at, first.at[way, at]).start()
        return carry

    for way in range(2):
        fetch(0, way).start()
    for copy in loads:
        copy.start()
    for way in range(2):
        fetch(1, way).start()
    swapped_load.start()
    greet(mates + peers)
    for way in range(2):
        fetch(0, way).wait()
    for part in range(groups):
        loads[part].wait()
        begin(part, 0)

    def mate_of(offset):
        return lax.rem(group + offset, groups)

    def send_part(offset):
        return push(
            parts.at[offset - 1],
            landing.at[offset - 1],
            part_send.at[offset - 1],
            part_recv.at[offset - 1],
            (me, mate_of(offset)),
        )

    def send_out(offset):
        return push(
            out_parts.at[mate_of(offset)],
            out_landing.at[offset - 1],
            out_send.at[offset - 1],
            out_recv.at[offset - 1],
            (me, mate_of(offset)),
        )

    def stream(count, take, use):
        for copy in take(0, 0):
            copy.start()

        def one(block, carry):
            slot = lax.rem(block, 2)

            @pl.when(block + 1 < count)
            def _():
                for copy in take(block + 1, 1 - slot):
                    copy.start()

            for copy in take(block, slot):
                copy.wait()
            use(block, slot)
            return carry

        lax.fori_loop(0, count, one, 0)

    def tokens_of(block):
        return pl.ds(pl.multiple_of(block * 2 * rows, 2 * rows), 2 * rows)

    def weight_part(offset):
        columns = pl.ds(pl.multiple_of(mate_of(offset) * tile, tile), tile)

        def take(block, slot):
            return [
                pltpu.make_async_copy(
                    normed_ref.at[block, :, :, columns], taken.at[slot], take_sem.at[slot, 0]
                ),
                pltpu.make_async_copy(
                    turned_ref.at[:, tokens_of(block)], turned.at[slot], take_sem.at[slot, 1]
                ),
            ]

        def use(block, slot):
            values = dot(turned[slot], taken[slot].reshape(2 * rows, tile), 1, 0)

            @pl.when(block == 0)
            def _():
                total[...] = values

            @pl.when(block > 0)
            def _():
                total[...] += values

        stream(size, take, use)

    def out_part(low, count):
        piece_rows = out_parts.shape[1]

        def take(block, slot):
            return [
                pltpu.make_async_copy(
                    branch_grad_ref.at[tokens_of(low + block)],
                    out_taken.at[slot],
                    take_sem.at[slot, 0],
                ),
                pltpu.make_async_copy(
                    out_ref.at[low + block], out_turned.at[slot], take_sem.at[slot, 1]
                ),
            ]

        def use(block, slot):
            values = dot(out_turned[slot], out_taken[slot], 1, 0)

            @pl.when(low + block == 0)
            def _():
                out_total[...] = values

            @pl.when(low + block > 0)
            def _():
                out_total[...] += values

        stream(count, take, use)

    def out_sends():
        piece_rows = out_parts.shape[1]
        for index in range(groups):
            out_parts[index] = out_total[index * piece_rows : (index + 1) * piece_rows].astype(bf16)
        for offset in range(1, groups):
            send_out(offset).start()

    def advance(step, carry):
        for way in range(2):
            fetch(step + 1, way).start()
        for way in range(2):
            fetch(step, way).wait()

        def one(at, inner):
            for way in range(2):
                own = term(step, way, at)
                hop(step - 1, way, at, first.at[way, at]).wait_recv()
                slots[step - 1, way, at] = (slots[step - 1, way, at].astype(f32) + own).astype(bf16)
                hop(step, way, at, slots.at[step - 1, way, at]).start()
            return inner

        lax.fori_loop(0, tiles, one, 0)

        @pl.when(step < 3)
        def _():
            out_part((step - 1) * (size // 2), size // 2)

        @pl.when(step == 2)
        def _():
            out_sends()

        @pl.when((step > 2) & (step <= groups + 1))
        def _():
            weight_part(step - 2)
            parts[step - 3] = total[...].astype(bf16)
            send_part(step - 2).start()

        return carry

    lax.fori_loop(1, size - 1, advance, 0)
    for offset in range(1, groups):
        send_out(offset).wait_recv()
    summed = out_parts[group].astype(f32)
    for offset in range(1, groups):
        summed = summed + out_landing[offset - 1].astype(f32)
    piece[...] = summed.astype(bf16).reshape(piece.shape)
    out_ring.start()

    for way in range(2):
        fetch(size - 1, way).wait()

    def end(at, carry):
        columns = pl.ds(pl.multiple_of(at * tile, tile), tile)
        for way in range(2):
            own = term(size - 1, way, at)
            hop(size - 2, way, at, first.at[way, at]).wait_recv()
            rows_ref[way, :, columns] = slots[size - 2, way, at].astype(f32) + own
        return carry

    lax.fori_loop(0, tiles, end, 0)
    width = rows_ref.shape[2]
    own_width = gain_ref.shape[1]
    flat = jnp.zeros((1, width), f32)
    for way in range(2):
        values = tokens_ref[way].astype(f32) * scale_ref[way, :, 0:1]
        flat = flat + jnp.sum(rows_ref[way] * values, axis=0, keepdims=True)
    half = small.shape[2]
    listed = [
        taps_ref[k : k + 1, at : at + 128] for k in range(KW + 1) for at in range(0, own_width, 128)
    ]
    listed += [gain_ref[0:1, at : at + 128] for at in range(0, own_width, 128)]
    listed += [heads_ref[k : k + 1, :] for k in range(3)]
    listed += [
        taps_ref[k : k + 1, at : at + 128]
        for k in range(KW + 1)
        for at in range(own_width, taps_ref.shape[1], 128)
    ]
    listed += [flat[:, at : at + 128] for at in range(0, width, 128)]
    for at, row in enumerate(listed):
        small[at // half, 0, at % half : at % half + 1, :] = row
    small_in = [
        push(small, small_land.at[k], mate_send.at[k], mate_recv.at[k], mate)
        for k, mate in enumerate(mates)
    ]
    for copy in small_in:
        copy.start()

    def out_advance(step, carry):
        out_ring.advance(step)
        return carry

    lax.fori_loop(1, 2, out_advance, 0)
    weight_part(groups)
    lax.fori_loop(2, size // 2, out_advance, 0)
    fetched = []
    for offset in range(1, groups):
        send_part(offset).wait()
        fetched.append(
            pltpu.make_async_copy(
                landing.at[offset - 1], parts.at[offset - 1], fetch_sem.at[offset - 1]
            )
        )
        fetched[-1].start()
    for copy, part in zip(fetched, range(groups - 1)):
        copy.wait()
        total[...] += parts[part].astype(f32)
    main[...] = total[: counts[0]].astype(bf16).reshape(main.shape)
    shared[...] = total[counts[0] : counts[0] + counts[1]].astype(bf16).reshape(shared.shape)
    shared_in = [
        push(shared.at[peer[0]], shared_land.at[k], pair_send.at[k], pair_recv.at[k], peer)
        for k, peer in enumerate(peers)
    ]
    for copy in shared_in:
        copy.start()
    lax.fori_loop(size // 2, size - 1, out_advance, 0)
    main_ring.start()
    for copy in small_in + shared_in:
        copy.wait()
    values = small[...]
    for k in range(groups - 1):
        values = values + small_land[k]
    small[...] = values
    values = shared[me].astype(f32)
    for k in range(size - 1):
        values = values + shared_land[k].astype(f32)
    across = shared_sum.shape[3]
    for way in range(2):
        shared_sum[way, 0] = values[:, way * across : (way + 1) * across].astype(bf16)
    small_ring.start()
    shared_ring.start()
    out_ring.finish()
    owned = [
        push(pieces_by_owner(pieces_ref, mate[1], groups), owned_ref.at[group], owned_send.at[k], owned_recv.at[k], mate)
        for k, mate in enumerate(mates)
    ]
    kept = pltpu.make_async_copy(
        pieces_by_owner(pieces_ref, group, groups), owned_ref.at[group], owned_local
    )
    for copy in owned:
        copy.start()
    kept.start()
    branch_ref[...] = jnp.zeros_like(branch_ref)

    per_owner = size // groups

    def weight_take(block, slot):
        owner, at = block // per_owner, lax.rem(block, per_owner)

        @pl.when(owner == group)
        def _():
            pltpu.make_async_copy(
                shard_ref.at[at], weights_taken.at[slot], take_sem.at[slot, 0]
            ).start()

        @pl.when(owner != group)
        def _():
            pltpu.make_async_copy(
                out_full_ref.at[owner, at], weights_taken.at[slot], take_sem.at[slot, 0]
            ).start()

    def multiply(block, carry):
        slot = lax.rem(block, 2)

        @pl.when(block + 1 < size)
        def _():
            weight_take(block + 1, 1 - slot)

        pltpu.make_async_copy(
            shard_ref.at[0], weights_taken.at[slot], take_sem.at[slot, 0]
        ).wait()
        branch_ref[...] += dot(swapped_held[block], weights_taken[slot], 1, 0)
        return carry

    weight_take(0, 0)
    swapped_load.wait()
    count = size - 2

    def main_advance(step, carry):
        main_ring.advance(step)
        small_ring.advance(step)
        shared_ring.advance(step)
        lax.fori_loop(((step - 1) * size) // count, (step * size) // count, multiply, 0)
        return carry

    lax.fori_loop(1, size - 1, main_advance, 0)

    def drain(step, carry):
        def one(at, inner):
            for way in range(2):
                hop(step, way, at, first.at[way, at]).wait_send()
            return inner

        return lax.fori_loop(0, tiles, one, carry)

    lax.fori_loop(0, size - 1, drain, 0)
    for offset in range(1, groups):
        send_out(offset).wait_send()
    main_ring.finish()
    small_ring.finish()
    shared_ring.finish()
    for copy in owned:
        copy.wait()
    kept.wait()


def pieces_by_owner(pieces_ref, owner, groups):
    count = pieces_ref.shape[0] // groups
    return pieces_ref.at[pl.ds(owner * count, count)]


def finish(
    grad,
    weight,
    normed,
    turned,
    out,
    branch_grad,
    tokens,
    scale,
    taps,
    gain,
    heads,
    swapped,
    shard,
    out_full,
    counts,
    collective_id,
):
    size, groups = lax.axis_size("seq"), lax.axis_size("wa")
    _, ways, rows, cols = grad.shape
    tile, tiles = weight.shape[2], groups
    width = tiles * tile
    lw = out.shape[1]
    bc = taps.shape[1] - lw
    piece_rows = lw // groups
    per_owner = size // groups
    bf16, f32, DMA = jnp.bfloat16, jnp.float32, pltpu.SemaphoreType.DMA
    total_small = ((KW + 2) * lw + (KW + 1) * bc + width) // 128 + 3
    half = -(-total_small // 16) * 8
    piece = (2, 2, piece_rows // 4, width)
    main = (2, 2, counts[0] // 4, tile)
    shared_rows = counts[1] // size
    both = (2, 1, shared_rows, tile // 2)
    small_shape = (2, 1, half, 128)
    vmem = pltpu.VMEM
    return pl.pallas_call(
        functools.partial(finish_kernel, size, groups, counts),
        out_shape=[
            jax.ShapeDtypeStruct((ways, rows, width), f32),
            jax.ShapeDtypeStruct((size,) + main, bf16),
            jax.ShapeDtypeStruct((size,) + piece, bf16),
            jax.ShapeDtypeStruct((groups, per_owner) + piece, bf16),
            jax.ShapeDtypeStruct((size,) + both, bf16),
            jax.ShapeDtypeStruct((size,) + small_shape, f32),
            jax.ShapeDtypeStruct((ways * rows, width), f32),
            jax.ShapeDtypeStruct((groups - 1, cols, tile), bf16),
        ],
        in_specs=[ANY] * 6 + [VMEM] * 5 + [ANY] * 3,
        out_specs=[VMEM, ANY, ANY, ANY, ANY, ANY, VMEM, ANY],
        scratch_shapes=[
            vmem((size - 1, 2, tiles, rows, tile), bf16),
            vmem((2, tiles, rows, tile), bf16),
            vmem((groups - 1, cols, tile), bf16),
            vmem((cols, tile), f32),
            vmem((2, ways, rows, tile), bf16),
            vmem((2, cols, 2 * rows), bf16),
            vmem((lw, width), f32),
            vmem((groups, piece_rows, width), bf16),
            vmem((groups - 1, piece_rows, width), bf16),
            vmem((2, 2 * rows, width), bf16),
            vmem(piece, bf16),
            vmem(main, bf16),
            vmem((size, shared_rows, tile), bf16),
            vmem((size - 1, shared_rows, tile), bf16),
            vmem(both, bf16),
            vmem(small_shape, f32),
            vmem((groups - 1,) + small_shape, f32),
            DMA((size - 1, 2, tiles)),
            DMA((size - 1, 2, tiles)),
            DMA((groups - 1,)),
            DMA((groups - 1,)),
            DMA((2, 2)),
            DMA((groups - 1,)),
            DMA((groups - 1,)),
            DMA((groups - 1,)),
            DMA((groups - 1,)),
            DMA,
            DMA((size - 1,)),
            DMA((size - 1,)),
            DMA((groups - 1,)),
            DMA((groups - 1,)),
        ]
        + ring_sems(size, 2)
        + ring_sems(size, 2)
        + ring_sems(size, 1)
        + ring_sems(size, 1)
        + [DMA((groups - 1,)), vmem((2, lw, width), bf16)]
        + [vmem((2, 2, rows, cols), bf16), DMA((2, 2)), vmem((2, lw, 2 * rows), bf16)]
        + [vmem(weight.shape, bf16), vmem(swapped.shape, bf16), DMA((groups + 1,))],
        compiler_params=comm_params(collective_id, 63),
        name="finish",
    )(
        grad,
        weight,
        normed,
        turned,
        out,
        branch_grad,
        tokens,
        scale,
        taps,
        gain,
        heads,
        swapped,
        shard,
        out_full,
    )


def assemble_kernel(blocks, gathered_ref, tail_ref, o_ref):
    @pl.when(pl.program_id(0) < blocks)
    def _():
        o_ref[...] = gathered_ref[0, 0].reshape(o_ref.shape).astype(jnp.float32)

    @pl.when(pl.program_id(0) == blocks)
    def _():
        o_ref[...] = tail_ref[...].astype(jnp.float32)


def assemble_in(gathered, tail):
    size, ways, chunks, rows, width = gathered.shape
    step = chunks * rows
    blocks = size * ways
    total = blocks * step + tail.shape[0]
    steps = blocks + 1
    pad = -tail.shape[0] % step
    if tail.shape[0] > step:
        out = jnp.swapaxes(gathered, 0, 1).reshape(blocks * step, width)
        return jnp.concatenate([out, tail]).astype(jnp.float32)
    return pl.pallas_call(
        functools.partial(assemble_kernel, blocks),
        grid=(steps,),
        in_specs=[
            pl.BlockSpec(
                (1, 1, chunks, rows, width),
                lambda i: (lax.rem(i, size), jnp.minimum(i // size, ways - 1), 0, 0, 0),
            ),
            pl.BlockSpec((step, width), lambda i: (0, 0)),
        ],
        out_specs=pl.BlockSpec((step, width), lambda i: (i, 0)),
        out_shape=jax.ShapeDtypeStruct((total, width), jnp.float32),
        compiler_params=pltpu.CompilerParams(vmem_limit_bytes=32 * 2**20),
        name="assemble_in",
    )(gathered, jnp.pad(tail, ((0, pad), (0, 0))))


def widen_kernel(
    widths, heads, x_ref, small_ref, o_ref, conv_ref, bias_ref, gain_ref, heads_ref, norm_ref
):
    o_ref[...] = x_ref[0, 0].astype(jnp.float32)

    @pl.when((pl.program_id(0) == 0) & (pl.program_id(1) == 0))
    def _():
        lw, bc = widths
        size = small_ref.shape[0]
        tiles, shared = lw // 128, bc // 128
        inner = size * lw
        found = jnp.zeros((8, 128), jnp.float32)
        first = (KW + 2) * tiles
        for block in range(size):
            for tile in range(tiles):
                at = slice(block * lw + tile * 128, block * lw + (tile + 1) * 128)
                for k in range(KW):
                    row = k * tiles + tile
                    conv_ref[k : k + 1, at] = small_ref[block, row : row + 1, :]
                row = KW * tiles + tile
                bias_ref[:, at] = small_ref[block, row : row + 1, :]
                row = (KW + 1) * tiles + tile
                gain_ref[:, at] = small_ref[block, row : row + 1, :]
            found = found + pltpu.roll(small_ref[block, first : first + 8, :], block * heads, 1)
        heads_ref[...] = found
        total = small_ref[0]
        for block in range(1, size):
            total = total + small_ref[block]
        row = first + 3
        for k in range(KW + 1):
            for tile in range(shared):
                at = slice(inner + tile * 128, inner + (tile + 1) * 128)
                if k < KW:
                    conv_ref[k : k + 1, at] = total[row : row + 1, :]
                else:
                    bias_ref[:, at] = total[row : row + 1, :]
                row += 1
        for tile in range(norm_ref.shape[1] // 128):
            norm_ref[:, tile * 128 : (tile + 1) * 128] = total[row : row + 1, :]
            row += 1


def assemble_out(owned, small, widths, heads):
    groups, count, rows, width = owned.shape
    size = small.shape[0]
    lw, bc = widths
    inner = size * lw
    f32 = jnp.float32
    shapes = [(KW, inner + bc), (1, inner + bc), (1, inner), (8, 128), (1, width)]
    return pl.pallas_call(
        functools.partial(widen_kernel, widths, heads),
        grid=(count, groups),
        in_specs=[
            pl.BlockSpec((1, 1, rows, width), lambda t, g: (g, t, 0, 0)),
            pl.BlockSpec(small.shape, lambda t, g: (0, 0, 0)),
        ],
        out_specs=[pl.BlockSpec((rows, width), lambda t, g: (t * groups + g, 0))]
        + [pl.BlockSpec(s, lambda t, g: (0, 0)) for s in shapes],
        out_shape=[jax.ShapeDtypeStruct((groups * count * rows, width), f32)]
        + [jax.ShapeDtypeStruct(s, f32) for s in shapes],
        name="assemble_out",
    )(owned, small)


def body(
    tokens,
    lengths,
    norm_gain,
    in_weight,
    conv_weight,
    conv_bias,
    dt_bias,
    a_log,
    skip_gain,
    out_gain,
    out_weight,
    cotangent,
):
    seqs_here, slot_rows, width = tokens.shape
    row_count = seqs_here * slot_rows
    inner_width = out_gain.shape[0]
    channels = conv_bias.shape[0]
    bc_width = channels - inner_width
    state_size = bc_width // 2
    head_count = dt_bias.shape[0]
    head_size = inner_width // head_count
    seq_devices = lax.axis_size("seq")
    group_devices = lax.axis_size("wa")
    seq_index = lax.axis_index("seq")
    length = seq_devices * slot_rows
    local_heads = head_count // seq_devices
    local_width = local_heads * head_size
    channel_start = seq_index * local_width
    head_start = seq_index * local_heads
    bf16, f32 = jnp.bfloat16, jnp.float32

    def take(array, start, size, axis):
        return lax.dynamic_slice_in_dim(array, start, size, axis)

    positions = seq_index * slot_rows + jnp.arange(slot_rows)
    valid_rows = (positions[None, :] < lengths[:, None]).astype(f32).reshape(row_count, 1)
    flat_tokens = tokens.reshape(row_count, width).astype(f32)
    in_scale = row_scale(flat_tokens)
    normed = (flat_tokens * in_scale * norm_gain).astype(bf16)
    cot_rows = cotangent.reshape(row_count, width)

    blocks = (seq_devices, seqs_here, slot_rows)
    params = jnp.pad(jnp.stack([dt_bias, a_log, skip_gain]), ((0, 5), (0, 128 - head_count)))
    spread, fold, tri, upper = scan_tables(slot_rows, local_width, head_size)
    widths = (local_width, bc_width)
    per_owner = seq_devices // group_devices
    (
        normed_all,
        in_columns,
        projected,
        y_heads,
        entering,
        normed_out,
        turned_out,
        gated_grad,
        gain_sum,
        taps,
        heads,
        wide,
        branch_grad,
        out_full,
    ) = front(
        normed,
        in_weight.T,
        cot_rows * valid_rows.astype(bf16),
        out_weight.reshape(per_owner, local_width, width),
        (conv_weight, conv_bias[None], params, out_gain[None], spread, tri),
        inner_width,
        widths,
        head_size,
        0,
    )
    branch_grad = branch_grad.reshape(-1, width)
    proj_grad, turned_grad, taps_sum, _, head_sum, swapped = scan_backward(
        projected,
        y_heads,
        entering,
        gated_grad,
        taps,
        heads,
        wide,
        spread,
        fold,
        tri,
        upper,
        normed_out,
        widths,
        head_size,
        1,
    )
    swapped = swapped.reshape(seq_devices, row_count, local_width)
    columns_here = proj_grad.shape[3]
    proj_grad = proj_grad.reshape(-1, columns_here)
    in_rows = in_weight.shape[0]
    shared_count = bc_width + head_count
    shared_rows = shared_count // seq_devices
    normed_grad, gathered, _, owned, shared_all, small_all, branch, _ = finish(
        proj_grad.reshape(blocks + (columns_here,)),
        in_columns,
        normed_all.reshape(blocks + (width,)),
        turned_grad,
        turned_out,
        branch_grad,
        tokens,
        jnp.broadcast_to(in_scale.reshape(seqs_here, slot_rows, 1), (seqs_here, slot_rows, 128)),
        taps_sum,
        gain_sum,
        head_sum,
        swapped,
        out_weight.reshape(per_owner, local_width, width),
        out_full,
        (2 * local_width, shared_count),
        2,
    )
    normed_grad = normed_grad.reshape(row_count, width)
    token_grad = norm_backward(flat_tokens, in_scale, norm_gain, normed_grad)
    token_grad = token_grad + cot_rows.astype(f32)
    owned = owned.reshape(
        group_devices, per_owner, local_width // group_devices, width
    )
    shared_all = shared_all.reshape(seq_devices, 2, shared_rows, in_rows // 2)
    small_all = small_all.reshape(seq_devices, -1, 128)
    mixed_out = (flat_tokens + valid_rows * branch).astype(bf16).reshape(tokens.shape)
    tail = jnp.transpose(shared_all, (0, 2, 1, 3)).reshape(shared_count, in_rows)
    in_weight_grad = assemble_in(gathered, tail).T
    out_weight_grad, conv_weight_grad, conv_bias_grad, gain_grad, head_all, norm_grad = (
        assemble_out(owned, small_all, widths, local_heads)
    )
    return (
        mixed_out,
        token_grad.reshape(tokens.shape),
        norm_grad[0],
        in_weight_grad,
        conv_weight_grad,
        conv_bias_grad[0],
        head_all[0, :head_count],
        head_all[1, :head_count],
        head_all[2, :head_count],
        gain_grad[0],
        out_weight_grad,
    )


def solution(mesh):
    placed = (
        P("wa", "seq", None),
        P("wa"),
        P(),
        P("wa", None),
        P(),
        P(),
        P(),
        P(),
        P(),
        P(),
        P("wa", None),
        P("wa", "seq", None),
    )
    return jax.shard_map(
        body,
        mesh=mesh,
        in_specs=placed,
        out_specs=(
            P("wa", "seq", None),
            P("wa", "seq", None),
            P(),
            P("wa", None),
            P(),
            P(),
            P(),
            P(),
            P(),
            P(),
            P("wa", None),
        ),
        check_vma=False,
    )
```

```python
import functools

import jax
import jax.numpy as jnp
import numpy as np
from jax import lax
from jax.experimental import pallas as pl
from jax.experimental.pallas import tpu as pltpu
from jax.sharding import PartitionSpec as P

KW = 4
EPS = 1e-05
HIGHEST = lax.Precision.HIGHEST
MESH = pl.DeviceIdType.MESH


def row_scale(values):
    return lax.rsqrt(jnp.mean(values * values, axis=-1, keepdims=True) + EPS)


def norm_backward(values, row_scales, gain_vec, grad_out):
    weighted = grad_out * gain_vec
    return row_scales * weighted - values * row_scales**3 * jnp.mean(
        weighted * values, axis=-1, keepdims=True
    )


def dot(a, b, ca, cb, precision=None):
    return lax.dot_general(
        a, b, (((ca,), (cb,)), ((), ())), precision=precision, preferred_element_type=jnp.float32
    )


def chunk_front(proj_ref, ext, taps_ref, heads_ref, tri_ref, widths, head_start):
    lw, bc = widths
    rows = proj_ref.shape[2]
    ext[8:, :] = proj_ref[0, 0, :, lw : 2 * lw + bc].astype(jnp.float32)
    conv = taps_ref[KW : KW + 1, :]
    for k in range(KW):
        conv = conv + taps_ref[k : k + 1, :] * ext[5 + k : 5 + k + rows, :]
    conv_sig = lax.logistic(conv)
    act = conv * conv_sig
    raw = proj_ref[0, 0, :, 2 * lw + bc :].astype(jnp.float32)
    step_in = pltpu.roll(raw, lax.rem(128 - head_start, 128), 1) + heads_ref[0:1, :]
    steps = jnp.maximum(step_in, 0.0) + jnp.log1p(jnp.exp(-jnp.abs(step_in)))
    rates = heads_ref[1:2, :] * steps
    cum = dot(tri_ref[...], rates, 1, 0, HIGHEST)
    return conv, conv_sig, act, step_in, steps, rates, cum


def head_masks(rows, head_size):
    lane = lax.broadcasted_iota(jnp.int32, (rows, 128), 1)
    row = lax.broadcasted_iota(jnp.int32, (rows, rows), 0)
    col = lax.broadcasted_iota(jnp.int32, (rows, rows), 1)
    return lane, row >= col


def forward_chunk(
    widths,
    head_size,
    head_start,
    start,
    proj_ref,
    taps_ref,
    heads_ref,
    wide_ref,
    spread_ref,
    tri_ref,
    gated_ref,
    y_ref,
    enter_ref,
    state,
    ext,
    halo,
):
    lw, bc = widths
    bf16, f32 = jnp.bfloat16, jnp.float32
    rows = proj_ref.shape[2]
    per_tile = 128 // head_size

    @pl.when(start)
    def _():
        state[...] = jnp.zeros_like(state)
        halo[...] = jnp.zeros_like(halo)

    ext[0:8, :] = halo[...]
    _, _, act, _, steps, _, cum = chunk_front(
        proj_ref, ext, taps_ref, heads_ref, tri_ref, widths, head_start
    )
    halo[...] = ext[rows : rows + 8, :]
    x = act[:, :lw]
    xb = x.astype(bf16)
    b_rows = act[:, lw : lw + bc // 2].astype(bf16)
    c_rows = act[:, lw + bc // 2 :].astype(bf16)
    cum_t, steps_t = cum.T, steps.T
    last = cum[rows - 1 : rows, :]
    grow = dot(jnp.exp(cum).astype(bf16), spread_ref[...], 1, 0)
    tail = dot((jnp.exp(last - cum) * steps).astype(bf16), spread_ref[...], 1, 0)
    scores = dot(c_rows, b_rows, 1, 1)
    entering = state[...].astype(bf16)
    enter_ref[0, 0] = entering
    y = dot(c_rows, entering, 1, 1) * grow + wide_ref[1:2, :] * x
    added = dot((x * tail).astype(bf16), b_rows, 0, 0)
    lane, causal = head_masks(rows, head_size)
    gate = proj_ref[0, 0, :, :lw].astype(f32)
    silu_gate = gate * lax.logistic(gate)
    for tile in range(lw // 128):
        cols = slice(tile * 128, (tile + 1) * 128)
        inner = None
        for sub in range(per_tile):
            head = tile * per_tile + sub
            log_decay = cum[:, head : head + 1] - cum_t[head : head + 1, :]
            decay = jnp.exp(jnp.where(causal, log_decay, -1e30))
            weights = (scores * decay * steps_t[head : head + 1, :]).astype(bf16)
            part = dot(weights, xb[:, cols], 1, 0)
            inner = part if inner is None else jnp.where(lane >= sub * head_size, part, inner)
            span = slice(head * head_size, (head + 1) * head_size)
            state[span, :] = (
                jnp.exp(cum[rows - 1 : rows, head : head + 1]) * state[span, :] + added[span, :]
            )
        y_tile = y[:, cols] + inner
        y_ref[0, 0, :, cols] = y_tile.astype(bf16)
        gated_ref[:, cols] = (y_tile * silu_gate[:, cols]).astype(bf16)


def backward_kernel(
    widths,
    head_size,
    chunks,
    proj_ref,
    before_ref,
    y_ref,
    enter_ref,
    grad_ref,
    taps_ref,
    heads_ref,
    wide_ref,
    spread_ref,
    fold_ref,
    tri_ref,
    upper_ref,
    normed_ref,
    out_ref,
    turned_ref,
    taps_acc,
    skip_acc,
    head_acc,
    swapped_ref,
    lam,
    ext,
    later,
    after,
    swap_send,
    swap_recv,
    swap_local,
):
    lw, bc = widths
    state_size = bc // 2
    bf16, f32 = jnp.bfloat16, jnp.float32
    rows = proj_ref.shape[2]
    per_tile = 128 // head_size
    chunk = chunks - 1 - pl.program_id(1)
    head_start = lax.axis_index("seq") * (lw // head_size)

    me, group = lax.axis_index("seq"), lax.axis_index("wa")
    swaps = [
        push(
            normed_ref.at[other],
            swapped_ref.at[me],
            swap_send.at[k],
            swap_recv.at[k],
            (other, group),
        )
        for k, other in enumerate(others(me, chunks))
    ]
    swap_kept = pltpu.make_async_copy(normed_ref.at[me], swapped_ref.at[me], swap_local)

    @pl.when((pl.program_id(0) == 0) & (pl.program_id(1) == 0))
    def _():
        greet([(other, group) for other in others(me, chunks)])
        for copy in swaps:
            copy.start()
        swap_kept.start()
        taps_acc[...] = jnp.zeros_like(taps_acc)
        skip_acc[...] = jnp.zeros_like(skip_acc)
        head_acc[...] = jnp.zeros_like(head_acc)

    @pl.when(pl.program_id(1) == 0)
    def _():
        lam[...] = jnp.zeros_like(lam)
        after[...] = jnp.zeros_like(after)

    ext[0:8, :] = jnp.where(
        chunk > 0, before_ref[0, 0, 8:16, lw : 2 * lw + bc].astype(f32), 0.0
    )
    conv, conv_sig, act, step_in, steps, rates, cum = chunk_front(
        proj_ref, ext, taps_ref, heads_ref, tri_ref, widths, head_start
    )
    x = act[:, :lw]
    xb = x.astype(bf16)
    b_rows = act[:, lw : lw + state_size].astype(bf16)
    c_rows = act[:, lw + state_size :].astype(bf16)
    cum_t, steps_t = cum.T, steps.T
    last = cum[rows - 1 : rows, :]
    to_end = jnp.exp(last - cum)
    tail_heads = to_end * steps
    grow = dot(jnp.exp(cum).astype(bf16), spread_ref[...], 1, 0)
    tail = dot(tail_heads.astype(bf16), spread_ref[...], 1, 0)
    scores = dot(c_rows, b_rows, 1, 1)

    gate = proj_ref[0, 0, :, :lw].astype(f32)
    gate_sig = lax.logistic(gate)
    grad = grad_ref[0, 0].astype(f32)
    y_grad = grad * gate * gate_sig
    out_ref[0, 0, :, :lw] = (
        grad * y_ref[0, 0].astype(f32) * (gate_sig * (1.0 + gate * (1.0 - gate_sig)))
    ).astype(bf16)
    yb = y_grad.astype(bf16)

    entering = enter_ref[0, 0]
    grown = y_grad * grow
    grown_b = grown.astype(bf16)
    c_grad = dot(grown_b, entering, 1, 0)
    carried = dot((grown * dot(c_rows, entering, 1, 1)).astype(bf16), fold_ref[...], 1, 0)
    lam_now = lam[...]
    lam_b = lam_now.astype(bf16)
    from_lam = dot(b_rows, lam_b, 1, 1)
    b_grad = dot((x * tail).astype(bf16), lam_b, 1, 0)
    x_lam = dot((x * from_lam).astype(bf16), fold_ref[...], 1, 0)
    x_grad = wide_ref[1:2, :] * y_grad + tail * from_lam
    skip_acc[0:1, :] += jnp.sum(y_grad * x, axis=0, keepdims=True)
    ones = jnp.ones((8, state_size), bf16)
    kept = dot(
        dot(ones, (lam_now * entering.astype(f32)).astype(bf16), 1, 1),
        fold_ref[...].astype(f32),
        1,
        0,
        HIGHEST,
    )
    through = jnp.exp(last) * kept[0:1, :]
    lam_add = dot(grown_b, c_rows, 0, 0)

    lane, causal = head_masks(rows, head_size)
    score_grad = None
    row_sums = jnp.zeros((rows, 128), f32)
    col_sums = []
    x_tiles = []
    for tile in range(lw // 128):
        cols = slice(tile * 128, (tile + 1) * 128)
        inner = None
        for sub in range(per_tile):
            head = tile * per_tile + sub
            log_decay = cum[:, head : head + 1] - cum_t[head : head + 1, :]
            decay = jnp.exp(jnp.where(causal, log_decay, -1e30))
            step_row = steps_t[head : head + 1, :]
            weights = (scores * decay * step_row).astype(bf16)
            inside = (lane >= sub * head_size) & (lane < (sub + 1) * head_size)
            y_head = jnp.where(inside, yb[:, cols], jnp.zeros_like(yb[:, cols]))
            weights_grad = dot(y_head, xb[:, cols], 1, 1)
            part = dot(weights, yb[:, cols], 0, 0)
            inner = part if inner is None else jnp.where(lane >= sub * head_size, part, inner)
            decayed = weights_grad * decay
            stepped = decayed * step_row
            score_grad = stepped if score_grad is None else score_grad + stepped
            col_sums.append(jnp.sum(decayed * scores, axis=0, keepdims=True))
            row_sum = jnp.sum(stepped * scores, axis=1, keepdims=True)
            row_sums = row_sums + jnp.where(lane == head, row_sum, 0.0)
            span = slice(head * head_size, (head + 1) * head_size)
            lam[span, :] = (
                jnp.exp(cum[rows - 1 : rows, head : head + 1]) * lam_now[span, :] + lam_add[span, :]
            )
        x_tiles.append(x_grad[:, cols] + inner)
    col_sums.append(jnp.zeros((rows - len(col_sums), rows), f32))
    col_sum = jnp.concatenate(col_sums, axis=0).T
    source = row_sums - steps * col_sum + carried
    rates_grad = (
        dot(upper_ref[...], source, 1, 0, HIGHEST)
        + dot(1.0 - upper_ref[...], tail_heads * x_lam, 1, 0, HIGHEST)
        + through
    )
    steps_grad = col_sum + to_end * x_lam + rates_grad * heads_ref[1:2, :]
    raw_grad = steps_grad * lax.logistic(step_in)
    out_ref[0, 0, :, 2 * lw + bc :] = pltpu.roll(raw_grad, head_start, 1).astype(bf16)
    head_acc[0:1, :] += jnp.sum(raw_grad, axis=0, keepdims=True)
    head_acc[1:2, :] += jnp.sum(rates_grad * rates, axis=0, keepdims=True)
    score_b = score_grad.astype(bf16)
    c_grad = c_grad + dot(score_b, b_rows, 1, 0)
    b_grad = b_grad + dot(score_b, c_rows, 0, 0)
    act_grad = jnp.concatenate(x_tiles + [b_grad, c_grad], axis=1)
    conv_grad = act_grad * (conv_sig * (1.0 + conv * (1.0 - conv_sig)))
    later[0:rows, :] = conv_grad
    later[rows : rows + 8, :] = after[...]
    after[...] = conv_grad[0:8, :]
    total = None
    for k in range(KW):
        term = taps_ref[k : k + 1, :] * later[3 - k : 3 - k + rows, :]
        total = term if total is None else total + term
        taps_acc[k : k + 1, :] += jnp.sum(conv_grad * ext[5 + k : 5 + k + rows, :], axis=0, keepdims=True)
    taps_acc[KW : KW + 1, :] += jnp.sum(conv_grad, axis=0, keepdims=True)

    @pl.when((pl.program_id(0) == pl.num_programs(0) - 1) & (chunk == 0))
    def _():
        head_acc[2:3, :] = dot(
            skip_acc[...], fold_ref[...].astype(f32), 1, 0, HIGHEST
        )[0:1, :]
        for copy in swaps:
            copy.wait()
        swap_kept.wait()
    out_ref[0, 0, :, lw : 2 * lw + bc] = total.astype(bf16)
    turned_ref[...] = out_ref[0, 0].T


def whole_spec(array):
    return pl.BlockSpec(array.shape, lambda q, c: (0,) * array.ndim)


def scan_tables(rows, local_width, head_size):
    head_of = np.arange(local_width) // head_size
    spread = (np.arange(128)[:, None] == head_of[None, :]).astype(jnp.bfloat16)
    tri = (np.arange(rows)[:, None] >= np.arange(rows)[None, :]).astype(np.float32)
    return [jnp.asarray(t) for t in (spread, spread.T.copy(), tri, tri.T.copy())]


def scan_backward(
    proj, y, enter, grad, taps, heads, wide, spread, fold, tri, upper, normed, widths, head_size, collective_id
):
    chunks, seqs, rows, cols = proj.shape
    lw, bc = widths
    block = lambda *tail: pl.BlockSpec((1, 1) + tail, lambda q, c: (chunks - 1 - c, q, 0, 0))
    before = pl.BlockSpec(
        (1, 1, 16, cols),
        lambda q, c: (jnp.maximum(chunks - 2 - c, 0), q, rows // 16 - 1, 0),
    )
    tables = (taps, heads, wide, spread, fold, tri, upper)
    sums = [(8, lw + bc), (8, lw), (8, 128)]
    return pl.pallas_call(
        functools.partial(backward_kernel, widths, head_size, chunks),
        grid=(seqs, chunks),
        in_specs=[block(rows, cols), before, block(rows, lw), block(lw, bc // 2), block(rows, lw)]
        + [whole_spec(t) for t in tables]
        + [ANY],
        out_specs=[
            block(rows, cols),
            pl.BlockSpec((cols, rows), lambda q, c: (0, (chunks - 1 - c) * seqs + q)),
        ]
        + [pl.BlockSpec(s, lambda q, c: (0, 0)) for s in sums]
        + [ANY],
        out_shape=[
            jax.ShapeDtypeStruct(proj.shape, jnp.bfloat16),
            jax.ShapeDtypeStruct((cols, chunks * seqs * rows), jnp.bfloat16),
        ]
        + [jax.ShapeDtypeStruct(s, jnp.float32) for s in sums]
        + [jax.ShapeDtypeStruct(normed.shape, normed.dtype)],
        scratch_shapes=[
            pltpu.VMEM((lw, bc // 2), jnp.float32),
            pltpu.VMEM((rows + 8, lw + bc), jnp.float32),
            pltpu.VMEM((rows + 8, lw + bc), jnp.float32),
            pltpu.VMEM((8, lw + bc), jnp.float32),
            pltpu.SemaphoreType.DMA((chunks - 1,)),
            pltpu.SemaphoreType.DMA((chunks - 1,)),
            pltpu.SemaphoreType.DMA,
        ],
        compiler_params=comm_params(collective_id, 60),
        name="scan_backward",
    )(proj, proj, y, enter, grad, *tables, normed)


def ring_pos(index, size):
    row, side = index // 2, index % 2
    return row + side * (size - 1 - 2 * row)


def ring_index(pos, size):
    side = pos // (size // 2)
    row = pos + side * (size - 1 - 2 * pos)
    return row * 2 + side


def greet(peers):
    barrier = pltpu.get_barrier_semaphore()
    for peer in peers:
        pl.semaphore_signal(barrier, inc=1, device_id=peer, device_id_type=MESH)
    pl.semaphore_wait(barrier, len(peers))


def push(source, target, send_sem, recv_sem, peer):
    return pltpu.make_async_remote_copy(
        source, target, send_sem, recv_sem, device_id=peer, device_id_type=MESH
    )


def neighbours(size):
    me, group = lax.axis_index("seq"), lax.axis_index("wa")
    pos = ring_pos(me, size)
    right = (ring_index((pos + 1) % size, size), group)
    left = (ring_index((pos + size - 1) % size, size), group)
    return me, group, pos, right, left


def others(index, size):
    return [(index + offset) % size for offset in range(1, size)]


ANY = pl.BlockSpec(memory_space=pl.ANY)
VMEM = pl.BlockSpec(memory_space=pltpu.VMEM)


def comm_params(collective_id, megabytes=None):
    limit = None if megabytes is None else megabytes * 2**20
    return pltpu.CompilerParams(
        collective_id=collective_id, has_side_effects=True, vmem_limit_bytes=limit
    )


class RingGather:
    def __init__(self, size, x_ref, o_ref, send_sem, recv_sem, local_sem):
        self.size, self.x, self.o = size, x_ref, o_ref
        self.send, self.recv, self.local = send_sem, recv_sem, local_sem
        self.chunks = x_ref.shape[1]
        self.me, _, self.pos, self.right, self.left = neighbours(size)

    def copy(self, step, chunk, way, first=False):
        size = self.size
        if way == 0:
            block, peer = ring_index((self.pos - step + size) % size, size), self.right
        else:
            block, peer = ring_index((self.pos + step) % size, size), self.left
        source = self.x.at[way, chunk] if first else self.o.at[block, way, chunk]
        return push(
            source,
            self.o.at[block, way, chunk],
            self.send.at[step, chunk, way],
            self.recv.at[step, chunk, way],
            peer,
        )

    def kept(self):
        return pltpu.make_async_copy(self.x, self.o.at[self.me], self.local)

    def start(self):
        self.kept().start()
        for chunk in range(self.chunks):
            for way in range(2):
                self.copy(0, chunk, way, True).start()

    def advance(self, step):
        for chunk in range(self.chunks):
            for way in range(2):
                self.copy(step - 1, chunk, way).wait_recv()
                self.copy(step, chunk, way).start()

    def arrive(self):
        last = self.size - 2
        for chunk in range(self.chunks):
            for way in range(2):
                self.copy(last, chunk, way).wait_recv()

    def finish(self):
        self.arrive()
        self.settle()

    def settle(self):
        def drain(step, carry):
            for chunk in range(self.chunks):
                for way in range(2):
                    self.copy(step, chunk, way).wait_send()
            return carry

        lax.fori_loop(0, self.size - 1, drain, 0)
        self.kept().wait()


def ring_parts(x, chunks):
    return x.reshape(2, chunks, x.shape[0] // (2 * chunks), x.shape[1])


def ring_sems(size, chunks):
    return [
        pltpu.SemaphoreType.DMA((size - 1, chunks, 2)),
        pltpu.SemaphoreType.DMA((size - 1, chunks, 2)),
        pltpu.SemaphoreType.DMA,
    ]


def front_kernel(
    widths,
    head_size,
    size,
    groups,
    inner,
    x_ref,
    w_ref,
    cot_ref,
    shard_ref,
    conv_ref,
    conv_bias_ref,
    params_ref,
    out_gain_ref,
    spread_ref,
    tri_ref,
    rows_ref,
    weights_ref,
    proj_ref,
    y_ref,
    enter_ref,
    normed_ref,
    turned_ref,
    grad_ref,
    gain_acc,
    taps_ref,
    heads_ref,
    wide_ref,
    branch_ref,
    part_ref,
    weights,
    projected,
    taken,
    state,
    ext,
    halo,
    gated,
    out_grad,
    y_held,
    enter_held,
    out_rows,
    out_turned,
    sums,
    landing,
    normed_held,
    turned_held,
    grad_held,
    result_sem,
    weight_send,
    weight_recv,
    weight_local,
    take_sem,
    proj_sem,
    held_sem,
    shard_send,
    shard_recv,
    shard_local,
    pair_send,
    pair_recv,
    *ring_refs,
):
    bf16, f32 = jnp.bfloat16, jnp.float32
    me, group, pos, right, left = neighbours(size)
    rows, lw = gated.shape[2:]
    depth = weights.shape[2]
    peers = [(other, group) for other in others(me, size)]
    mates = [(me, other) for other in others(group, groups)]
    sibling = (me, group + 1 - 2 * lax.rem(group, 2))
    across = (me, lax.rem(group + 2, groups))
    per_owner = size // groups
    chosen = lax.rem(me, per_owner)
    owner = me // per_owner
    greet(mates + peers)
    ring = RingGather(size, x_ref, rows_ref, *ring_refs[0:3])
    cot_ring = RingGather(size, cot_ref, branch_ref, *ring_refs[3:6])
    ring.start()
    bc = widths[1]
    used = w_ref.shape[0] - 2 * inner
    lane_at = pl.multiple_of(me * lw, 128)
    spans = (
        (pl.ds(lane_at, lw), pl.ds(0, lw)),
        (pl.ds(pl.multiple_of(inner + me * lw, 128), lw), pl.ds(lw, lw)),
        (pl.ds(2 * inner, used), pl.ds(2 * lw, used)),
    )
    sent = [
        push(
            w_ref.at[here],
            weights.at[group, there],
            weight_send.at[k, part],
            weight_recv.at[k, part],
            mate,
        )
        for k, mate in enumerate(mates)
        for part, (here, there) in enumerate(spans)
    ]
    for copy in sent:
        copy.start()
    kept = [
        pltpu.make_async_copy(w_ref.at[here], weights.at[group, there], weight_local.at[part])
        for part, (here, there) in enumerate(spans)
    ]
    for copy in kept:
        copy.start()
    blank = weights.shape[1] - 2 * lw - used
    for part in range(groups):
        weights[part, 2 * lw + used :, :] = jnp.zeros((blank, depth), bf16)
    heads_here = lw // head_size
    head_start = me * heads_here
    taps_ref[...] = jnp.zeros_like(taps_ref)
    taps_ref[0:KW, :lw] = conv_ref[:, pl.ds(lane_at, lw)]
    taps_ref[0:KW, lw:] = conv_ref[:, inner:]
    taps_ref[KW : KW + 1, :lw] = conv_bias_ref[:, pl.ds(lane_at, lw)]
    taps_ref[KW : KW + 1, lw:] = conv_bias_ref[:, inner:]
    params = pltpu.roll(params_ref[...], lax.rem(128 - head_start, 128), 1)
    params = jnp.where(
        lax.broadcasted_iota(jnp.int32, params.shape, 1) < heads_here, params, 0.0
    )
    at_row = lax.broadcasted_iota(jnp.int32, params.shape, 0)
    at_lane = lax.broadcasted_iota(jnp.int32, params.shape, 1)
    slopes = jnp.where(at_lane < heads_here, -jnp.exp(params), 0.0)
    heads_ref[...] = jnp.where(at_row == 1, slopes, params)
    wide_ref[...] = jnp.zeros_like(wide_ref)
    wide_ref[0:1, :] = out_gain_ref[:, pl.ds(lane_at, lw)]
    wide_ref[1:2, :] = dot(params, spread_ref[...].astype(f32), 1, 0, HIGHEST)[2:3, :]

    def shards(step, offset=0):
        at = lax.rem(chosen + offset, per_owner)
        held_by = across[1] if step == 2 else group
        source = part_ref.at[held_by, at] if step == 2 else shard_ref.at[at]
        return push(
            source,
            part_ref.at[held_by, at],
            shard_send.at[step, offset],
            shard_recv.at[step, offset],
            across if step == 0 else sibling,
        )

    def block_of(pair, way):
        return ring_index((pos - pair + size) % size if way == 0 else (pos + pair) % size, size)

    def stream(source_ref, landed_ref, low, high, compute, own=False):
        def take(pair, slot, way):
            source = source_ref.at[way] if own else landed_ref.at[block_of(pair, way), way]
            return pltpu.make_async_copy(source, taken.at[slot, way], take_sem.at[slot, way])

        for way in range(2):
            take(low, lax.rem(low, 2), way).start()

        def one(pair, carry):
            slot = lax.rem(pair, 2)
            for way in range(2):
                take(pair, slot, way).wait()

            @pl.when(pair + 1 < high)
            def _():
                for way in range(2):
                    take(pair + 1, 1 - slot, way).start()

            compute(pair, slot)
            return carry

        lax.fori_loop(low, high, one, 0)

    def put(pair, way):
        block = block_of(pair, way)
        return pltpu.make_async_copy(
            projected.at[block, way], proj_ref.at[block, way], proj_sem.at[pair, way]
        )

    def project(pair, slot):
        for way in range(2):
            x = taken[slot, way].reshape(rows, taken.shape[4])
            total = None
            for part in range(groups):
                term = dot(x[:, part * depth : (part + 1) * depth], weights[part], 1, 1)
                total = term if total is None else total + term
            projected[block_of(pair, way), way] = total.astype(bf16)
            put(pair, way).start()

    def advance(step, carry):
        ring.advance(step)
        return carry

    def turns(turn, count):
        return 1 + (turn * (size - 2)) // count, 1 + ((turn + 1) * (size - 2)) // count

    middle = size // 2 + 1
    lax.fori_loop(1, middle, advance, 0)
    for copy in kept:
        copy.wait()
    for copy in sent:
        copy.wait_recv()
    flushed = pltpu.make_async_copy(weights, weights_ref, weight_local.at[0])
    flushed.start()
    shards(0).start()
    shards(1).start()
    stream(x_ref, rows_ref, 0, 1, project, own=True)

    def late(step, carry):
        ring.advance(step)
        stream(x_ref, rows_ref, *turns(step - middle, size - 1 - middle), project)
        return carry

    lax.fori_loop(middle, size - 2, late, 0)
    ring.advance(size - 2)
    cot_ring.start()
    stream(x_ref, rows_ref, *turns(size - 2 - middle, size - 1 - middle), project)
    ring.arrive()
    stream(x_ref, rows_ref, size - 1, size, project)
    cot_ring.advance(1)

    def keep(index, slot):
        seq, chunk = index // size, lax.rem(index, size)
        return [
            pltpu.make_async_copy(y_held.at[slot, 0], y_ref.at[chunk, seq], held_sem.at[slot, 0]),
            pltpu.make_async_copy(
                enter_held.at[slot, 0], enter_ref.at[chunk, seq], held_sem.at[slot, 1]
            ),
        ]

    def scan(index, carry):
        seq, chunk = index // size, lax.rem(index, size)
        slot = lax.rem(index, 2)

        @pl.when(index >= 2)
        def _():
            for copy in keep(index - 2, slot):
                copy.wait()

        forward_chunk(
            widths,
            head_size,
            head_start,
            chunk == 0,
            projected.at[pl.ds(chunk, 1), pl.ds(seq, 1)],
            taps_ref,
            heads_ref,
            wide_ref,
            spread_ref,
            tri_ref,
            gated.at[chunk, seq],
            y_held.at[pl.ds(slot, 1)],
            enter_held.at[pl.ds(slot, 1)],
            state,
            ext,
            halo,
        )
        for copy in keep(index, slot):
            copy.start()

        @pl.when(index == size + 2)
        def _():
            cot_ring.advance(2)

        return carry

    lax.fori_loop(0, 2 * size, scan, 0)
    first, second, third = (shards(step) for step in range(3))
    first.wait_recv()
    third.start()
    for offset in range(1, per_owner):
        shards(0, offset).start()
        shards(1, offset).start()
    second.wait_recv()
    cot_ring.advance(3)
    third.wait_recv()

    @pl.when(owner == group)
    def _():
        loaded = pltpu.make_async_copy(shard_ref.at[chosen], out_rows, shard_local)
        loaded.start()
        loaded.wait()

    @pl.when(owner != group)
    def _():
        loaded = pltpu.make_async_copy(part_ref.at[owner, chosen], out_rows, shard_local)
        loaded.start()
        loaded.wait()

    out_turned[...] = out_rows[...].T
    ones = jnp.ones((8, lw), bf16)

    def compute(pair, slot):
        for way in range(2):
            block = block_of(pair, way)
            values = dot(taken[slot, way].reshape(rows, taken.shape[4]), out_turned[...], 1, 0)
            out_grad[block, way] = values
            here = gated[block, way].astype(f32)
            weighted = values * wide_ref[0:1, :] * here
            at = pl.ds(block * 2 + way, 1)
            sums[0, at, :] = dot(ones, (here * here).astype(bf16), 1, 1)[0:1, :]
            sums[1, at, :] = dot(ones, weighted.astype(bf16), 1, 1)[0:1, :]

    stream(cot_ref, branch_ref, 0, 1, compute, own=True)
    stream(cot_ref, branch_ref, *turns(0, size - 4), compute)

    def cot_late(step, carry):
        cot_ring.advance(step)
        stream(cot_ref, branch_ref, *turns(step - 3, size - 4), compute)
        return carry

    lax.fori_loop(4, size - 1, cot_late, 0)
    cot_ring.arrive()
    stream(cot_ref, branch_ref, size - 1, size, compute)
    copies = [
        push(sums, landing.at[k], pair_send.at[k], pair_recv.at[k], peer)
        for k, peer in enumerate(peers)
    ]
    for copy in copies:
        copy.start()
    total = sums[...]
    for k, copy in enumerate(copies):
        copy.wait_recv()
        total = total + landing[k]
    scale = lax.rsqrt(total[0] / inner + EPS)
    pull = scale * scale * scale * (total[1] / inner)
    fill = jnp.zeros((128 - 2 * size, rows), f32)
    scale_turned = jnp.concatenate([scale, fill]).T
    pull_turned = jnp.concatenate([pull, fill]).T
    lane = lax.broadcasted_iota(jnp.int32, (rows, 128), 1)
    gain_acc[...] = jnp.zeros_like(gain_acc)

    def results(block):
        pairs = ((normed_held, normed_ref), (turned_held, turned_ref), (grad_held, grad_ref))
        return [
            pltpu.make_async_copy(held.at[block], out.at[block], result_sem.at[k, block])
            for k, (held, out) in enumerate(pairs)
        ]

    def finish(block, carry):
        for way in range(2):
            mask = lane == block * 2 + way
            by = jnp.sum(jnp.where(mask, scale_turned, 0.0), axis=1, keepdims=True)
            less = jnp.sum(jnp.where(mask, pull_turned, 0.0), axis=1, keepdims=True)
            here = gated[block, way].astype(f32)
            values = out_grad[block, way]
            scaled = here * by
            normed = (scaled * wide_ref[0:1, :]).astype(bf16)
            normed_held[block, way] = normed
            turned_held[block, :, way * rows : (way + 1) * rows] = normed.T
            grad_held[block, way] = (values * wide_ref[0:1, :] * by - here * less).astype(bf16)
            gain_acc[0:1, :] += jnp.sum(values * scaled, axis=0, keepdims=True)
        for copy in results(block):
            copy.start()
        return carry

    lax.fori_loop(0, size, finish, 0)
    for offset in range(1, per_owner):
        shards(0, offset).wait_recv()
        shards(2, offset).start()
    for copy in sent + copies + [first, second, third]:
        copy.wait_send()
    flushed.wait()
    for index in (2 * size - 2, 2 * size - 1):
        for copy in keep(index, index % 2):
            copy.wait()

    def settle(pair, carry):
        for way in range(2):
            put(pair, way).wait()
        for copy in results(pair):
            copy.wait()
        return carry

    lax.fori_loop(0, size, settle, 0)
    ring.settle()
    cot_ring.settle()
    for offset in range(1, per_owner):
        shards(1, offset).wait_recv()
        shards(2, offset).wait_recv()
        for step in range(3):
            shards(step, offset).wait_send()


def front(x, weight, cot, shard, params, inner, widths, head_size, collective_id):
    size, groups = lax.axis_size("seq"), lax.axis_size("wa")
    parts, cot_parts = ring_parts(x, 2), ring_parts(cot, 2)
    depth = weight.shape[1]
    rows = x.shape[0] // 2
    width = x.shape[1]
    lw, bc = widths
    cols = 2 * lw + bc + 128
    per_owner = size // groups
    bf16, f32, DMA, vmem = jnp.bfloat16, jnp.float32, pltpu.SemaphoreType.DMA, pltpu.VMEM
    whole = (size, 2, rows, lw)
    shape = jax.ShapeDtypeStruct
    return pl.pallas_call(
        functools.partial(front_kernel, widths, head_size, size, groups, inner),
        out_shape=[
            shape((size,) + parts.shape, bf16),
            shape((groups, cols, depth), bf16),
            shape((size, 2, rows, cols), bf16),
            shape(whole, bf16),
            shape((size, 2, lw, bc // 2), bf16),
            shape(whole, bf16),
            shape((size, lw, 2 * rows), bf16),
            shape(whole, bf16),
            shape((8, lw), f32),
            shape((8, lw + bc), f32),
            shape((8, 128), f32),
            shape((8, lw), f32),
            shape((size,) + parts.shape, bf16),
            shape((groups, per_owner, lw, width), bf16),
        ],
        in_specs=[ANY] * 4 + [VMEM] * 6,
        out_specs=[ANY] * 8 + [VMEM] * 4 + [ANY] * 2,
        scratch_shapes=[
            vmem((groups, cols, depth), bf16),
            vmem((size, 2, rows, cols), bf16),
            vmem((2,) + parts.shape, bf16),
            vmem((lw, bc // 2), f32),
            vmem((rows + 8, lw + bc), f32),
            vmem((8, lw + bc), f32),
            vmem(whole, bf16),
            vmem(whole, f32),
            vmem((2, 1, rows, lw), bf16),
            vmem((2, 1, lw, bc // 2), bf16),
            vmem((lw, width), bf16),
            vmem((width, lw), bf16),
            vmem((2, 2 * size, rows), f32),
            vmem((size - 1, 2, 2 * size, rows), f32),
            vmem(whole, bf16),
            vmem((size, lw, 2 * rows), bf16),
            vmem(whole, bf16),
            DMA((3, size)),
            DMA((groups - 1, 3)),
            DMA((groups - 1, 3)),
            DMA((3,)),
            DMA((2, 2)),
            DMA((size, 2)),
            DMA((2, 2)),
            DMA((3, per_owner)),
            DMA((3, per_owner)),
            DMA,
            DMA((size - 1,)),
            DMA((size - 1,)),
        ]
        + ring_sems(size, 2)
        + ring_sems(size, 2),
        compiler_params=comm_params(collective_id, 62),
        name="front",
    )(parts, weight, cot_parts, shard, *params)


def finish_kernel(
    size,
    groups,
    counts,
    grad_ref,
    weight_ref,
    normed_ref,
    turned_ref,
    out_ref,
    branch_grad_ref,
    tokens_ref,
    scale_ref,
    taps_ref,
    gain_ref,
    heads_ref,
    swapped_ref,
    shard_ref,
    out_full_ref,
    rows_ref,
    gathered_ref,
    pieces_ref,
    owned_ref,
    shared_out,
    small_out,
    branch_ref,
    landing,
    slots,
    first,
    parts,
    total,
    taken,
    turned,
    out_total,
    out_parts,
    out_landing,
    out_taken,
    piece,
    main,
    shared,
    shared_land,
    shared_sum,
    small,
    small_land,
    send_sem,
    recv_sem,
    part_send,
    part_recv,
    take_sem,
    out_send,
    out_recv,
    owned_send,
    owned_recv,
    owned_local,
    pair_send,
    pair_recv,
    mate_send,
    mate_recv,
    *ring_refs,
):
    me, group, pos, right, left = neighbours(size)
    mates = [(me, index) for index in others(group, groups)]
    peers = [(index, group) for index in others(me, size)]
    tiles, rows, tile = slots.shape[2:]
    cols = total.shape[0]
    bf16, f32 = jnp.bfloat16, jnp.float32
    out_ring = RingGather(size, piece, pieces_ref, *ring_refs[0:3])
    main_ring = RingGather(size, main, gathered_ref, *ring_refs[3:6])
    shared_ring = RingGather(size, shared_sum, shared_out, *ring_refs[6:9])
    small_ring = RingGather(size, small, small_out, *ring_refs[9:12])
    fetch_sem, weights_taken, held, held_sem, out_turned = ring_refs[12:17]
    weight_held, swapped_held, load_sem = ring_refs[17:20]
    loads = [
        pltpu.make_async_copy(weight_ref.at[part], weight_held.at[part], load_sem.at[part])
        for part in range(groups)
    ]
    swapped_load = pltpu.make_async_copy(swapped_ref, swapped_held, load_sem.at[groups])

    def target(step, way):
        shift = (pos - 1 - step + 2 * size) if way == 0 else (pos + 1 + step)
        return ring_index(shift % size, size)

    def fetch(step, way):
        slot = lax.rem(step, 2)
        return pltpu.make_async_copy(
            grad_ref.at[target(step, way), way], held.at[slot, way], held_sem.at[slot, way]
        )

    def term(step, way, at):
        return dot(held[lax.rem(step, 2), way], weight_held[at], 1, 0)

    def hop(step, way, at, source):
        return push(
            source,
            slots.at[step, way, at],
            send_sem.at[step, way, at],
            recv_sem.at[step, way, at],
            right if way == 0 else left,
        )

    def begin(at, carry):
        for way in range(2):
            first[way, at] = term(0, way, at).astype(bf16)
            hop(0, way, at, first.at[way, at]).start()
        return carry

    for way in range(2):
        fetch(0, way).start()
    for copy in loads:
        copy.start()
    for way in range(2):
        fetch(1, way).start()
    swapped_load.start()
    greet(mates + peers)
    for way in range(2):
        fetch(0, way).wait()
    for part in range(groups):
        loads[part].wait()
        begin(part, 0)

    def mate_of(offset):
        return lax.rem(group + offset, groups)

    def send_part(offset):
        return push(
            parts.at[offset - 1],
            landing.at[offset - 1],
            part_send.at[offset - 1],
            part_recv.at[offset - 1],
            (me, mate_of(offset)),
        )

    def send_out(offset):
        return push(
            out_parts.at[mate_of(offset)],
            out_landing.at[offset - 1],
            out_send.at[offset - 1],
            out_recv.at[offset - 1],
            (me, mate_of(offset)),
        )

    def stream(count, take, use):
        for copy in take(0, 0):
            copy.start()

        def one(block, carry):
            slot = lax.rem(block, 2)

            @pl.when(block + 1 < count)
            def _():
                for copy in take(block + 1, 1 - slot):
                    copy.start()

            for copy in take(block, slot):
                copy.wait()
            use(block, slot)
            return carry

        lax.fori_loop(0, count, one, 0)

    def tokens_of(block):
        return pl.ds(pl.multiple_of(block * 2 * rows, 2 * rows), 2 * rows)

    def weight_part(offset):
        columns = pl.ds(pl.multiple_of(mate_of(offset) * tile, tile), tile)

        def take(block, slot):
            return [
                pltpu.make_async_copy(
                    normed_ref.at[block, :, :, columns], taken.at[slot], take_sem.at[slot, 0]
                ),
                pltpu.make_async_copy(
                    turned_ref.at[:, tokens_of(block)], turned.at[slot], take_sem.at[slot, 1]
                ),
            ]

        def use(block, slot):
            values = dot(turned[slot], taken[slot].reshape(2 * rows, tile), 1, 0)

            @pl.when(block == 0)
            def _():
                total[...] = values

            @pl.when(block > 0)
            def _():
                total[...] += values

        stream(size, take, use)

    def out_part(low, count):
        piece_rows = out_parts.shape[1]

        def take(block, slot):
            return [
                pltpu.make_async_copy(
                    branch_grad_ref.at[tokens_of(low + block)],
                    out_taken.at[slot],
                    take_sem.at[slot, 0],
                ),
                pltpu.make_async_copy(
                    out_ref.at[low + block], out_turned.at[slot], take_sem.at[slot, 1]
                ),
            ]

        def use(block, slot):
            values = dot(out_turned[slot], out_taken[slot], 1, 0)

            @pl.when(low + block == 0)
            def _():
                out_total[...] = values

            @pl.when(low + block > 0)
            def _():
                out_total[...] += values

        stream(count, take, use)

    def out_sends():
        piece_rows = out_parts.shape[1]
        for index in range(groups):
            out_parts[index] = out_total[index * piece_rows : (index + 1) * piece_rows].astype(bf16)
        for offset in range(1, groups):
            send_out(offset).start()

    def advance(step, carry):
        for way in range(2):
            fetch(step + 1, way).start()
        for way in range(2):
            fetch(step, way).wait()

        def one(at, inner):
            for way in range(2):
                own = term(step, way, at)
                hop(step - 1, way, at, first.at[way, at]).wait_recv()
                slots[step - 1, way, at] = (slots[step - 1, way, at].astype(f32) + own).astype(bf16)
                hop(step, way, at, slots.at[step - 1, way, at]).start()
            return inner

        lax.fori_loop(0, tiles, one, 0)

        @pl.when(step < 3)
        def _():
            out_part((step - 1) * (size // 2), size // 2)

        @pl.when(step == 2)
        def _():
            out_sends()

        @pl.when((step > 2) & (step <= groups + 1))
        def _():
            weight_part(step - 2)
            parts[step - 3] = total[...].astype(bf16)
            send_part(step - 2).start()

        return carry

    lax.fori_loop(1, size - 1, advance, 0)
    for offset in range(1, groups):
        send_out(offset).wait_recv()
    summed = out_parts[group].astype(f32)
    for offset in range(1, groups):
        summed = summed + out_landing[offset - 1].astype(f32)
    piece[...] = summed.astype(bf16).reshape(piece.shape)
    out_ring.start()

    for way in range(2):
        fetch(size - 1, way).wait()

    def end(at, carry):
        columns = pl.ds(pl.multiple_of(at * tile, tile), tile)
        for way in range(2):
            own = term(size - 1, way, at)
            hop(size - 2, way, at, first.at[way, at]).wait_recv()
            rows_ref[way, :, columns] = slots[size - 2, way, at].astype(f32) + own
        return carry

    lax.fori_loop(0, tiles, end, 0)
    width = rows_ref.shape[2]
    own_width = gain_ref.shape[1]
    flat = jnp.zeros((1, width), f32)
    for way in range(2):
        values = tokens_ref[way].astype(f32) * scale_ref[way, :, 0:1]
        flat = flat + jnp.sum(rows_ref[way] * values, axis=0, keepdims=True)
    half = small.shape[2]
    listed = [
        taps_ref[k : k + 1, at : at + 128] for k in range(KW + 1) for at in range(0, own_width, 128)
    ]
    listed += [gain_ref[0:1, at : at + 128] for at in range(0, own_width, 128)]
    listed += [heads_ref[k : k + 1, :] for k in range(3)]
    listed += [
        taps_ref[k : k + 1, at : at + 128]
        for k in range(KW + 1)
        for at in range(own_width, taps_ref.shape[1], 128)
    ]
    listed += [flat[:, at : at + 128] for at in range(0, width, 128)]
    for at, row in enumerate(listed):
        small[at // half, 0, at % half : at % half + 1, :] = row
    small_in = [
        push(small, small_land.at[k], mate_send.at[k], mate_recv.at[k], mate)
        for k, mate in enumerate(mates)
    ]
    for copy in small_in:
        copy.start()

    def out_advance(step, carry):
        out_ring.advance(step)
        return carry

    lax.fori_loop(1, 2, out_advance, 0)
    weight_part(groups)
    lax.fori_loop(2, size - 2, out_advance, 0)
    fetched = []
    for offset in range(1, groups):
        send_part(offset).wait()
        fetched.append(
            pltpu.make_async_copy(
                landing.at[offset - 1], parts.at[offset - 1], fetch_sem.at[offset - 1]
            )
        )
        fetched[-1].start()
    for copy, part in zip(fetched, range(groups - 1)):
        copy.wait()
        total[...] += parts[part].astype(f32)
    main[...] = total[: counts[0]].astype(bf16).reshape(main.shape)
    shared[...] = total[counts[0] : counts[0] + counts[1]].astype(bf16).reshape(shared.shape)
    shared_in = [
        push(shared.at[peer[0]], shared_land.at[k], pair_send.at[k], pair_recv.at[k], peer)
        for k, peer in enumerate(peers)
    ]
    for copy in shared_in:
        copy.start()
    lax.fori_loop(size - 2, size - 1, out_advance, 0)
    main_ring.start()
    for copy in small_in + shared_in:
        copy.wait()
    values = small[...]
    for k in range(groups - 1):
        values = values + small_land[k]
    small[...] = values
    values = shared[me].astype(f32)
    for k in range(size - 1):
        values = values + shared_land[k].astype(f32)
    across = shared_sum.shape[3]
    for way in range(2):
        shared_sum[way, 0] = values[:, way * across : (way + 1) * across].astype(bf16)
    small_ring.start()
    shared_ring.start()
    out_ring.finish()
    owned = [
        push(pieces_by_owner(pieces_ref, mate[1], groups), owned_ref.at[group], owned_send.at[k], owned_recv.at[k], mate)
        for k, mate in enumerate(mates)
    ]
    kept = pltpu.make_async_copy(
        pieces_by_owner(pieces_ref, group, groups), owned_ref.at[group], owned_local
    )
    for copy in owned:
        copy.start()
    kept.start()
    branch_ref[...] = jnp.zeros_like(branch_ref)

    per_owner = size // groups

    def weight_take(block, slot):
        owner, at = block // per_owner, lax.rem(block, per_owner)

        @pl.when(owner == group)
        def _():
            pltpu.make_async_copy(
                shard_ref.at[at], weights_taken.at[slot], take_sem.at[slot, 0]
            ).start()

        @pl.when(owner != group)
        def _():
            pltpu.make_async_copy(
                out_full_ref.at[owner, at], weights_taken.at[slot], take_sem.at[slot, 0]
            ).start()

    def multiply(block, carry):
        slot = lax.rem(block, 2)

        @pl.when(block + 1 < size)
        def _():
            weight_take(block + 1, 1 - slot)

        pltpu.make_async_copy(
            shard_ref.at[0], weights_taken.at[slot], take_sem.at[slot, 0]
        ).wait()
        branch_ref[...] += dot(swapped_held[block], weights_taken[slot], 1, 0)
        return carry

    weight_take(0, 0)
    swapped_load.wait()
    count = size - 2

    def main_advance(step, carry):
        main_ring.advance(step)
        small_ring.advance(step)
        shared_ring.advance(step)
        lax.fori_loop(((step - 1) * size) // count, (step * size) // count, multiply, 0)
        return carry

    lax.fori_loop(1, size - 1, main_advance, 0)

    def drain(step, carry):
        def one(at, inner):
            for way in range(2):
                hop(step, way, at, first.at[way, at]).wait_send()
            return inner

        return lax.fori_loop(0, tiles, one, carry)

    lax.fori_loop(0, size - 1, drain, 0)
    for offset in range(1, groups):
        send_out(offset).wait_send()
    main_ring.finish()
    small_ring.finish()
    shared_ring.finish()
    for copy in owned:
        copy.wait()
    kept.wait()


def pieces_by_owner(pieces_ref, owner, groups):
    count = pieces_ref.shape[0] // groups
    return pieces_ref.at[pl.ds(owner * count, count)]


def finish(
    grad,
    weight,
    normed,
    turned,
    out,
    branch_grad,
    tokens,
    scale,
    taps,
    gain,
    heads,
    swapped,
    shard,
    out_full,
    counts,
    collective_id,
):
    size, groups = lax.axis_size("seq"), lax.axis_size("wa")
    _, ways, rows, cols = grad.shape
    tile, tiles = weight.shape[2], groups
    width = tiles * tile
    lw = out.shape[1]
    bc = taps.shape[1] - lw
    piece_rows = lw // groups
    per_owner = size // groups
    bf16, f32, DMA = jnp.bfloat16, jnp.float32, pltpu.SemaphoreType.DMA
    total_small = ((KW + 2) * lw + (KW + 1) * bc + width) // 128 + 3
    half = -(-total_small // 16) * 8
    piece = (2, 2, piece_rows // 4, width)
    main = (2, 2, counts[0] // 4, tile)
    shared_rows = counts[1] // size
    both = (2, 1, shared_rows, tile // 2)
    small_shape = (2, 1, half, 128)
    vmem = pltpu.VMEM
    return pl.pallas_call(
        functools.partial(finish_kernel, size, groups, counts),
        out_shape=[
            jax.ShapeDtypeStruct((ways, rows, width), f32),
            jax.ShapeDtypeStruct((size,) + main, bf16),
            jax.ShapeDtypeStruct((size,) + piece, bf16),
            jax.ShapeDtypeStruct((groups, per_owner) + piece, bf16),
            jax.ShapeDtypeStruct((size,) + both, bf16),
            jax.ShapeDtypeStruct((size,) + small_shape, f32),
            jax.ShapeDtypeStruct((ways * rows, width), f32),
            jax.ShapeDtypeStruct((groups - 1, cols, tile), bf16),
        ],
        in_specs=[ANY] * 6 + [VMEM] * 5 + [ANY] * 3,
        out_specs=[VMEM, ANY, ANY, ANY, ANY, ANY, VMEM, ANY],
        scratch_shapes=[
            vmem((size - 1, 2, tiles, rows, tile), bf16),
            vmem((2, tiles, rows, tile), bf16),
            vmem((groups - 1, cols, tile), bf16),
            vmem((cols, tile), f32),
            vmem((2, ways, rows, tile), bf16),
            vmem((2, cols, 2 * rows), bf16),
            vmem((lw, width), f32),
            vmem((groups, piece_rows, width), bf16),
            vmem((groups - 1, piece_rows, width), bf16),
            vmem((2, 2 * rows, width), bf16),
            vmem(piece, bf16),
            vmem(main, bf16),
            vmem((size, shared_rows, tile), bf16),
            vmem((size - 1, shared_rows, tile), bf16),
            vmem(both, bf16),
            vmem(small_shape, f32),
            vmem((groups - 1,) + small_shape, f32),
            DMA((size - 1, 2, tiles)),
            DMA((size - 1, 2, tiles)),
            DMA((groups - 1,)),
            DMA((groups - 1,)),
            DMA((2, 2)),
            DMA((groups - 1,)),
            DMA((groups - 1,)),
            DMA((groups - 1,)),
            DMA((groups - 1,)),
            DMA,
            DMA((size - 1,)),
            DMA((size - 1,)),
            DMA((groups - 1,)),
            DMA((groups - 1,)),
        ]
        + ring_sems(size, 2)
        + ring_sems(size, 2)
        + ring_sems(size, 1)
        + ring_sems(size, 1)
        + [DMA((groups - 1,)), vmem((2, lw, width), bf16)]
        + [vmem((2, 2, rows, cols), bf16), DMA((2, 2)), vmem((2, lw, 2 * rows), bf16)]
        + [vmem(weight.shape, bf16), vmem(swapped.shape, bf16), DMA((groups + 1,))],
        compiler_params=comm_params(collective_id, 63),
        name="finish",
    )(
        grad,
        weight,
        normed,
        turned,
        out,
        branch_grad,
        tokens,
        scale,
        taps,
        gain,
        heads,
        swapped,
        shard,
        out_full,
    )


def assemble_kernel(blocks, gathered_ref, tail_ref, o_ref):
    @pl.when(pl.program_id(0) < blocks)
    def _():
        o_ref[...] = gathered_ref[0, 0].reshape(o_ref.shape).astype(jnp.float32)

    @pl.when(pl.program_id(0) == blocks)
    def _():
        o_ref[...] = tail_ref[...].astype(jnp.float32)


def assemble_in(gathered, tail):
    size, ways, chunks, rows, width = gathered.shape
    step = chunks * rows
    blocks = size * ways
    total = blocks * step + tail.shape[0]
    steps = blocks + 1
    pad = -tail.shape[0] % step
    if tail.shape[0] > step:
        out = jnp.swapaxes(gathered, 0, 1).reshape(blocks * step, width)
        return jnp.concatenate([out, tail]).astype(jnp.float32)
    return pl.pallas_call(
        functools.partial(assemble_kernel, blocks),
        grid=(steps,),
        in_specs=[
            pl.BlockSpec(
                (1, 1, chunks, rows, width),
                lambda i: (lax.rem(i, size), jnp.minimum(i // size, ways - 1), 0, 0, 0),
            ),
            pl.BlockSpec((step, width), lambda i: (0, 0)),
        ],
        out_specs=pl.BlockSpec((step, width), lambda i: (i, 0)),
        out_shape=jax.ShapeDtypeStruct((total, width), jnp.float32),
        compiler_params=pltpu.CompilerParams(vmem_limit_bytes=32 * 2**20),
        name="assemble_in",
    )(gathered, jnp.pad(tail, ((0, pad), (0, 0))))


def widen_kernel(
    widths, heads, x_ref, small_ref, o_ref, conv_ref, bias_ref, gain_ref, heads_ref, norm_ref
):
    o_ref[...] = x_ref[0, 0].astype(jnp.float32)

    @pl.when((pl.program_id(0) == 0) & (pl.program_id(1) == 0))
    def _():
        lw, bc = widths
        size = small_ref.shape[0]
        tiles, shared = lw // 128, bc // 128
        inner = size * lw
        found = jnp.zeros((8, 128), jnp.float32)
        first = (KW + 2) * tiles
        for block in range(size):
            for tile in range(tiles):
                at = slice(block * lw + tile * 128, block * lw + (tile + 1) * 128)
                for k in range(KW):
                    row = k * tiles + tile
                    conv_ref[k : k + 1, at] = small_ref[block, row : row + 1, :]
                row = KW * tiles + tile
                bias_ref[:, at] = small_ref[block, row : row + 1, :]
                row = (KW + 1) * tiles + tile
                gain_ref[:, at] = small_ref[block, row : row + 1, :]
            found = found + pltpu.roll(small_ref[block, first : first + 8, :], block * heads, 1)
        heads_ref[...] = found
        total = small_ref[0]
        for block in range(1, size):
            total = total + small_ref[block]
        row = first + 3
        for k in range(KW + 1):
            for tile in range(shared):
                at = slice(inner + tile * 128, inner + (tile + 1) * 128)
                if k < KW:
                    conv_ref[k : k + 1, at] = total[row : row + 1, :]
                else:
                    bias_ref[:, at] = total[row : row + 1, :]
                row += 1
        for tile in range(norm_ref.shape[1] // 128):
            norm_ref[:, tile * 128 : (tile + 1) * 128] = total[row : row + 1, :]
            row += 1


def assemble_out(owned, small, widths, heads):
    groups, count, rows, width = owned.shape
    size = small.shape[0]
    lw, bc = widths
    inner = size * lw
    f32 = jnp.float32
    shapes = [(KW, inner + bc), (1, inner + bc), (1, inner), (8, 128), (1, width)]
    return pl.pallas_call(
        functools.partial(widen_kernel, widths, heads),
        grid=(count, groups),
        in_specs=[
            pl.BlockSpec((1, 1, rows, width), lambda t, g: (g, t, 0, 0)),
            pl.BlockSpec(small.shape, lambda t, g: (0, 0, 0)),
        ],
        out_specs=[pl.BlockSpec((rows, width), lambda t, g: (t * groups + g, 0))]
        + [pl.BlockSpec(s, lambda t, g: (0, 0)) for s in shapes],
        out_shape=[jax.ShapeDtypeStruct((groups * count * rows, width), f32)]
        + [jax.ShapeDtypeStruct(s, f32) for s in shapes],
        name="assemble_out",
    )(owned, small)


def body(
    tokens,
    lengths,
    norm_gain,
    in_weight,
    conv_weight,
    conv_bias,
    dt_bias,
    a_log,
    skip_gain,
    out_gain,
    out_weight,
    cotangent,
):
    seqs_here, slot_rows, width = tokens.shape
    row_count = seqs_here * slot_rows
    inner_width = out_gain.shape[0]
    channels = conv_bias.shape[0]
    bc_width = channels - inner_width
    state_size = bc_width // 2
    head_count = dt_bias.shape[0]
    head_size = inner_width // head_count
    seq_devices = lax.axis_size("seq")
    group_devices = lax.axis_size("wa")
    seq_index = lax.axis_index("seq")
    length = seq_devices * slot_rows
    local_heads = head_count // seq_devices
    local_width = local_heads * head_size
    channel_start = seq_index * local_width
    head_start = seq_index * local_heads
    bf16, f32 = jnp.bfloat16, jnp.float32

    def take(array, start, size, axis):
        return lax.dynamic_slice_in_dim(array, start, size, axis)

    positions = seq_index * slot_rows + jnp.arange(slot_rows)
    valid_rows = (positions[None, :] < lengths[:, None]).astype(f32).reshape(row_count, 1)
    flat_tokens = tokens.reshape(row_count, width).astype(f32)
    in_scale = row_scale(flat_tokens)
    normed = (flat_tokens * in_scale * norm_gain).astype(bf16)
    cot_rows = cotangent.reshape(row_count, width)

    blocks = (seq_devices, seqs_here, slot_rows)
    params = jnp.pad(jnp.stack([dt_bias, a_log, skip_gain]), ((0, 5), (0, 128 - head_count)))
    spread, fold, tri, upper = scan_tables(slot_rows, local_width, head_size)
    widths = (local_width, bc_width)
    per_owner = seq_devices // group_devices
    (
        normed_all,
        in_columns,
        projected,
        y_heads,
        entering,
        normed_out,
        turned_out,
        gated_grad,
        gain_sum,
        taps,
        heads,
        wide,
        branch_grad,
        out_full,
    ) = front(
        normed,
        in_weight.T,
        cot_rows * valid_rows.astype(bf16),
        out_weight.reshape(per_owner, local_width, width),
        (conv_weight, conv_bias[None], params, out_gain[None], spread, tri),
        inner_width,
        widths,
        head_size,
        0,
    )
    branch_grad = branch_grad.reshape(-1, width)
    proj_grad, turned_grad, taps_sum, _, head_sum, swapped = scan_backward(
        projected,
        y_heads,
        entering,
        gated_grad,
        taps,
        heads,
        wide,
        spread,
        fold,
        tri,
        upper,
        normed_out,
        widths,
        head_size,
        1,
    )
    swapped = swapped.reshape(seq_devices, row_count, local_width)
    columns_here = proj_grad.shape[3]
    proj_grad = proj_grad.reshape(-1, columns_here)
    in_rows = in_weight.shape[0]
    shared_count = bc_width + head_count
    shared_rows = shared_count // seq_devices
    normed_grad, gathered, _, owned, shared_all, small_all, branch, _ = finish(
        proj_grad.reshape(blocks + (columns_here,)),
        in_columns,
        normed_all.reshape(blocks + (width,)),
        turned_grad,
        turned_out,
        branch_grad,
        tokens,
        jnp.broadcast_to(in_scale.reshape(seqs_here, slot_rows, 1), (seqs_here, slot_rows, 128)),
        taps_sum,
        gain_sum,
        head_sum,
        swapped,
        out_weight.reshape(per_owner, local_width, width),
        out_full,
        (2 * local_width, shared_count),
        2,
    )
    normed_grad = normed_grad.reshape(row_count, width)
    token_grad = norm_backward(flat_tokens, in_scale, norm_gain, normed_grad)
    token_grad = token_grad + cot_rows.astype(f32)
    owned = owned.reshape(
        group_devices, per_owner, local_width // group_devices, width
    )
    shared_all = shared_all.reshape(seq_devices, 2, shared_rows, in_rows // 2)
    small_all = small_all.reshape(seq_devices, -1, 128)
    mixed_out = (flat_tokens + valid_rows * branch).astype(bf16).reshape(tokens.shape)
    tail = jnp.transpose(shared_all, (0, 2, 1, 3)).reshape(shared_count, in_rows)
    in_weight_grad = assemble_in(gathered, tail).T
    out_weight_grad, conv_weight_grad, conv_bias_grad, gain_grad, head_all, norm_grad = (
        assemble_out(owned, small_all, widths, local_heads)
    )
    return (
        mixed_out,
        token_grad.reshape(tokens.shape),
        norm_grad[0],
        in_weight_grad,
        conv_weight_grad,
        conv_bias_grad[0],
        head_all[0, :head_count],
        head_all[1, :head_count],
        head_all[2, :head_count],
        gain_grad[0],
        out_weight_grad,
    )


def solution(mesh):
    placed = (
        P("wa", "seq", None),
        P("wa"),
        P(),
        P("wa", None),
        P(),
        P(),
        P(),
        P(),
        P(),
        P(),
        P("wa", None),
        P("wa", "seq", None),
    )
    return jax.shard_map(
        body,
        mesh=mesh,
        in_specs=placed,
        out_specs=(
            P("wa", "seq", None),
            P("wa", "seq", None),
            P(),
            P("wa", None),
            P(),
            P(),
            P(),
            P(),
            P(),
            P(),
            P("wa", None),
        ),
        check_vma=False,
    )
```

```python
import functools

import jax
import jax.numpy as jnp
import numpy as np
from jax import lax
from jax.experimental import pallas as pl
from jax.experimental.pallas import tpu as pltpu
from jax.sharding import PartitionSpec as P

KW = 4
EPS = 1e-05
HIGHEST = lax.Precision.HIGHEST
MESH = pl.DeviceIdType.MESH


def row_scale(values):
    return lax.rsqrt(jnp.mean(values * values, axis=-1, keepdims=True) + EPS)


def norm_backward(values, row_scales, gain_vec, grad_out):
    weighted = grad_out * gain_vec
    return row_scales * weighted - values * row_scales**3 * jnp.mean(
        weighted * values, axis=-1, keepdims=True
    )


def dot(a, b, ca, cb, precision=None):
    return lax.dot_general(
        a, b, (((ca,), (cb,)), ((), ())), precision=precision, preferred_element_type=jnp.float32
    )


def chunk_front(proj_ref, ext, taps_ref, heads_ref, tri_ref, widths, head_start):
    lw, bc = widths
    rows = proj_ref.shape[2]
    ext[8:, :] = proj_ref[0, 0, :, lw : 2 * lw + bc].astype(jnp.float32)
    conv = taps_ref[KW : KW + 1, :]
    for k in range(KW):
        conv = conv + taps_ref[k : k + 1, :] * ext[5 + k : 5 + k + rows, :]
    conv_sig = lax.logistic(conv)
    act = conv * conv_sig
    raw = proj_ref[0, 0, :, 2 * lw + bc :].astype(jnp.float32)
    step_in = pltpu.roll(raw, lax.rem(128 - head_start, 128), 1) + heads_ref[0:1, :]
    steps = jnp.maximum(step_in, 0.0) + jnp.log1p(jnp.exp(-jnp.abs(step_in)))
    rates = heads_ref[1:2, :] * steps
    cum = dot(tri_ref[...], rates, 1, 0, HIGHEST)
    return conv, conv_sig, act, step_in, steps, rates, cum


def head_masks(rows, head_size):
    lane = lax.broadcasted_iota(jnp.int32, (rows, 128), 1)
    row = lax.broadcasted_iota(jnp.int32, (rows, rows), 0)
    col = lax.broadcasted_iota(jnp.int32, (rows, rows), 1)
    return lane, row >= col


def forward_chunk(
    widths,
    head_size,
    head_start,
    start,
    proj_ref,
    taps_ref,
    heads_ref,
    wide_ref,
    spread_ref,
    tri_ref,
    gated_ref,
    y_ref,
    enter_ref,
    state,
    ext,
    halo,
):
    lw, bc = widths
    bf16, f32 = jnp.bfloat16, jnp.float32
    rows = proj_ref.shape[2]
    per_tile = 128 // head_size

    @pl.when(start)
    def _():
        state[...] = jnp.zeros_like(state)
        halo[...] = jnp.zeros_like(halo)

    ext[0:8, :] = halo[...]
    _, _, act, _, steps, _, cum = chunk_front(
        proj_ref, ext, taps_ref, heads_ref, tri_ref, widths, head_start
    )
    halo[...] = ext[rows : rows + 8, :]
    x = act[:, :lw]
    xb = x.astype(bf16)
    b_rows = act[:, lw : lw + bc // 2].astype(bf16)
    c_rows = act[:, lw + bc // 2 :].astype(bf16)
    cum_t, steps_t = cum.T, steps.T
    last = cum[rows - 1 : rows, :]
    grow = dot(jnp.exp(cum).astype(bf16), spread_ref[...], 1, 0)
    tail = dot((jnp.exp(last - cum) * steps).astype(bf16), spread_ref[...], 1, 0)
    scores = dot(c_rows, b_rows, 1, 1)
    entering = state[...].astype(bf16)
    enter_ref[0, 0] = entering
    y = dot(c_rows, entering, 1, 1) * grow + wide_ref[1:2, :] * x
    added = dot((x * tail).astype(bf16), b_rows, 0, 0)
    lane, causal = head_masks(rows, head_size)
    gate = proj_ref[0, 0, :, :lw].astype(f32)
    silu_gate = gate * lax.logistic(gate)
    for tile in range(lw // 128):
        cols = slice(tile * 128, (tile + 1) * 128)
        inner = None
        for sub in range(per_tile):
            head = tile * per_tile + sub
            log_decay = cum[:, head : head + 1] - cum_t[head : head + 1, :]
            decay = jnp.exp(jnp.where(causal, log_decay, -1e30))
            weights = (scores * decay * steps_t[head : head + 1, :]).astype(bf16)
            part = dot(weights, xb[:, cols], 1, 0)
            inner = part if inner is None else jnp.where(lane >= sub * head_size, part, inner)
            span = slice(head * head_size, (head + 1) * head_size)
            state[span, :] = (
                jnp.exp(cum[rows - 1 : rows, head : head + 1]) * state[span, :] + added[span, :]
            )
        y_tile = y[:, cols] + inner
        y_ref[0, 0, :, cols] = y_tile.astype(bf16)
        gated_ref[:, cols] = (y_tile * silu_gate[:, cols]).astype(bf16)


def backward_kernel(
    widths,
    head_size,
    chunks,
    proj_ref,
    before_ref,
    y_ref,
    enter_ref,
    grad_ref,
    taps_ref,
    heads_ref,
    wide_ref,
    spread_ref,
    fold_ref,
    tri_ref,
    upper_ref,
    normed_ref,
    out_ref,
    turned_ref,
    taps_acc,
    skip_acc,
    head_acc,
    swapped_ref,
    lam,
    ext,
    later,
    after,
    swap_send,
    swap_recv,
    swap_local,
):
    lw, bc = widths
    state_size = bc // 2
    bf16, f32 = jnp.bfloat16, jnp.float32
    rows = proj_ref.shape[2]
    per_tile = 128 // head_size
    chunk = chunks - 1 - pl.program_id(1)
    head_start = lax.axis_index("seq") * (lw // head_size)

    me, group = lax.axis_index("seq"), lax.axis_index("wa")
    swaps = [
        push(
            normed_ref.at[other],
            swapped_ref.at[me],
            swap_send.at[k],
            swap_recv.at[k],
            (other, group),
        )
        for k, other in enumerate(others(me, chunks))
    ]
    swap_kept = pltpu.make_async_copy(normed_ref.at[me], swapped_ref.at[me], swap_local)

    @pl.when((pl.program_id(0) == 0) & (pl.program_id(1) == 0))
    def _():
        greet([(other, group) for other in others(me, chunks)])
        for copy in swaps:
            copy.start()
        swap_kept.start()
        taps_acc[...] = jnp.zeros_like(taps_acc)
        skip_acc[...] = jnp.zeros_like(skip_acc)
        head_acc[...] = jnp.zeros_like(head_acc)

    @pl.when(pl.program_id(1) == 0)
    def _():
        lam[...] = jnp.zeros_like(lam)
        after[...] = jnp.zeros_like(after)

    ext[0:8, :] = jnp.where(
        chunk > 0, before_ref[0, 0, 8:16, lw : 2 * lw + bc].astype(f32), 0.0
    )
    conv, conv_sig, act, step_in, steps, rates, cum = chunk_front(
        proj_ref, ext, taps_ref, heads_ref, tri_ref, widths, head_start
    )
    x = act[:, :lw]
    xb = x.astype(bf16)
    b_rows = act[:, lw : lw + state_size].astype(bf16)
    c_rows = act[:, lw + state_size :].astype(bf16)
    cum_t, steps_t = cum.T, steps.T
    last = cum[rows - 1 : rows, :]
    to_end = jnp.exp(last - cum)
    tail_heads = to_end * steps
    grow = dot(jnp.exp(cum).astype(bf16), spread_ref[...], 1, 0)
    tail = dot(tail_heads.astype(bf16), spread_ref[...], 1, 0)
    scores = dot(c_rows, b_rows, 1, 1)

    gate = proj_ref[0, 0, :, :lw].astype(f32)
    gate_sig = lax.logistic(gate)
    grad = grad_ref[0, 0].astype(f32)
    y_grad = grad * gate * gate_sig
    out_ref[0, 0, :, :lw] = (
        grad * y_ref[0, 0].astype(f32) * (gate_sig * (1.0 + gate * (1.0 - gate_sig)))
    ).astype(bf16)
    yb = y_grad.astype(bf16)

    entering = enter_ref[0, 0]
    grown = y_grad * grow
    grown_b = grown.astype(bf16)
    c_grad = dot(grown_b, entering, 1, 0)
    carried = dot((grown * dot(c_rows, entering, 1, 1)).astype(bf16), fold_ref[...], 1, 0)
    lam_now = lam[...]
    lam_b = lam_now.astype(bf16)
    from_lam = dot(b_rows, lam_b, 1, 1)
    b_grad = dot((x * tail).astype(bf16), lam_b, 1, 0)
    x_lam = dot((x * from_lam).astype(bf16), fold_ref[...], 1, 0)
    x_grad = wide_ref[1:2, :] * y_grad + tail * from_lam
    skip_acc[0:1, :] += jnp.sum(y_grad * x, axis=0, keepdims=True)
    ones = jnp.ones((8, state_size), bf16)
    kept = dot(
        dot(ones, (lam_now * entering.astype(f32)).astype(bf16), 1, 1),
        fold_ref[...].astype(f32),
        1,
        0,
        HIGHEST,
    )
    through = jnp.exp(last) * kept[0:1, :]
    lam_add = dot(grown_b, c_rows, 0, 0)

    lane, causal = head_masks(rows, head_size)
    score_grad = None
    row_sums = jnp.zeros((rows, 128), f32)
    col_sums = []
    x_tiles = []
    for tile in range(lw // 128):
        cols = slice(tile * 128, (tile + 1) * 128)
        inner = None
        for sub in range(per_tile):
            head = tile * per_tile + sub
            log_decay = cum[:, head : head + 1] - cum_t[head : head + 1, :]
            decay = jnp.exp(jnp.where(causal, log_decay, -1e30))
            step_row = steps_t[head : head + 1, :]
            weights = (scores * decay * step_row).astype(bf16)
            inside = (lane >= sub * head_size) & (lane < (sub + 1) * head_size)
            y_head = jnp.where(inside, yb[:, cols], jnp.zeros_like(yb[:, cols]))
            weights_grad = dot(y_head, xb[:, cols], 1, 1)
            part = dot(weights, yb[:, cols], 0, 0)
            inner = part if inner is None else jnp.where(lane >= sub * head_size, part, inner)
            decayed = weights_grad * decay
            stepped = decayed * step_row
            score_grad = stepped if score_grad is None else score_grad + stepped
            col_sums.append(jnp.sum(decayed * scores, axis=0, keepdims=True))
            row_sum = jnp.sum(stepped * scores, axis=1, keepdims=True)
            row_sums = row_sums + jnp.where(lane == head, row_sum, 0.0)
            span = slice(head * head_size, (head + 1) * head_size)
            lam[span, :] = (
                jnp.exp(cum[rows - 1 : rows, head : head + 1]) * lam_now[span, :] + lam_add[span, :]
            )
        x_tiles.append(x_grad[:, cols] + inner)
    col_sums.append(jnp.zeros((rows - len(col_sums), rows), f32))
    col_sum = jnp.concatenate(col_sums, axis=0).T
    source = row_sums - steps * col_sum + carried
    rates_grad = (
        dot(upper_ref[...], source, 1, 0, HIGHEST)
        + dot(1.0 - upper_ref[...], tail_heads * x_lam, 1, 0, HIGHEST)
        + through
    )
    steps_grad = col_sum + to_end * x_lam + rates_grad * heads_ref[1:2, :]
    raw_grad = steps_grad * lax.logistic(step_in)
    out_ref[0, 0, :, 2 * lw + bc :] = pltpu.roll(raw_grad, head_start, 1).astype(bf16)
    head_acc[0:1, :] += jnp.sum(raw_grad, axis=0, keepdims=True)
    head_acc[1:2, :] += jnp.sum(rates_grad * rates, axis=0, keepdims=True)
    score_b = score_grad.astype(bf16)
    c_grad = c_grad + dot(score_b, b_rows, 1, 0)
    b_grad = b_grad + dot(score_b, c_rows, 0, 0)
    act_grad = jnp.concatenate(x_tiles + [b_grad, c_grad], axis=1)
    conv_grad = act_grad * (conv_sig * (1.0 + conv * (1.0 - conv_sig)))
    later[0:rows, :] = conv_grad
    later[rows : rows + 8, :] = after[...]
    after[...] = conv_grad[0:8, :]
    total = None
    for k in range(KW):
        term = taps_ref[k : k + 1, :] * later[3 - k : 3 - k + rows, :]
        total = term if total is None else total + term
        taps_acc[k : k + 1, :] += jnp.sum(conv_grad * ext[5 + k : 5 + k + rows, :], axis=0, keepdims=True)
    taps_acc[KW : KW + 1, :] += jnp.sum(conv_grad, axis=0, keepdims=True)

    @pl.when((pl.program_id(0) == pl.num_programs(0) - 1) & (chunk == 0))
    def _():
        head_acc[2:3, :] = dot(
            skip_acc[...], fold_ref[...].astype(f32), 1, 0, HIGHEST
        )[0:1, :]
        for copy in swaps:
            copy.wait()
        swap_kept.wait()
    out_ref[0, 0, :, lw : 2 * lw + bc] = total.astype(bf16)
    turned_ref[...] = out_ref[0, 0].T


def whole_spec(array):
    return pl.BlockSpec(array.shape, lambda q, c: (0,) * array.ndim)


def scan_tables(rows, local_width, head_size):
    head_of = np.arange(local_width) // head_size
    spread = (np.arange(128)[:, None] == head_of[None, :]).astype(jnp.bfloat16)
    tri = (np.arange(rows)[:, None] >= np.arange(rows)[None, :]).astype(np.float32)
    return [jnp.asarray(t) for t in (spread, spread.T.copy(), tri, tri.T.copy())]


def scan_backward(
    proj, y, enter, grad, taps, heads, wide, spread, fold, tri, upper, normed, widths, head_size, collective_id
):
    chunks, seqs, rows, cols = proj.shape
    lw, bc = widths
    block = lambda *tail: pl.BlockSpec((1, 1) + tail, lambda q, c: (chunks - 1 - c, q, 0, 0))
    before = pl.BlockSpec(
        (1, 1, 16, cols),
        lambda q, c: (jnp.maximum(chunks - 2 - c, 0), q, rows // 16 - 1, 0),
    )
    tables = (taps, heads, wide, spread, fold, tri, upper)
    sums = [(8, lw + bc), (8, lw), (8, 128)]
    return pl.pallas_call(
        functools.partial(backward_kernel, widths, head_size, chunks),
        grid=(seqs, chunks),
        in_specs=[block(rows, cols), before, block(rows, lw), block(lw, bc // 2), block(rows, lw)]
        + [whole_spec(t) for t in tables]
        + [ANY],
        out_specs=[
            block(rows, cols),
            pl.BlockSpec((cols, rows), lambda q, c: (0, (chunks - 1 - c) * seqs + q)),
        ]
        + [pl.BlockSpec(s, lambda q, c: (0, 0)) for s in sums]
        + [ANY],
        out_shape=[
            jax.ShapeDtypeStruct(proj.shape, jnp.bfloat16),
            jax.ShapeDtypeStruct((cols, chunks * seqs * rows), jnp.bfloat16),
        ]
        + [jax.ShapeDtypeStruct(s, jnp.float32) for s in sums]
        + [jax.ShapeDtypeStruct(normed.shape, normed.dtype)],
        scratch_shapes=[
            pltpu.VMEM((lw, bc // 2), jnp.float32),
            pltpu.VMEM((rows + 8, lw + bc), jnp.float32),
            pltpu.VMEM((rows + 8, lw + bc), jnp.float32),
            pltpu.VMEM((8, lw + bc), jnp.float32),
            pltpu.SemaphoreType.DMA((chunks - 1,)),
            pltpu.SemaphoreType.DMA((chunks - 1,)),
            pltpu.SemaphoreType.DMA,
        ],
        compiler_params=comm_params(collective_id, 60),
        name="scan_backward",
    )(proj, proj, y, enter, grad, *tables, normed)


def ring_pos(index, size):
    row, side = index // 2, index % 2
    return row + side * (size - 1 - 2 * row)


def ring_index(pos, size):
    side = pos // (size // 2)
    row = pos + side * (size - 1 - 2 * pos)
    return row * 2 + side


def greet(peers):
    barrier = pltpu.get_barrier_semaphore()
    for peer in peers:
        pl.semaphore_signal(barrier, inc=1, device_id=peer, device_id_type=MESH)
    pl.semaphore_wait(barrier, len(peers))


def push(source, target, send_sem, recv_sem, peer):
    return pltpu.make_async_remote_copy(
        source, target, send_sem, recv_sem, device_id=peer, device_id_type=MESH
    )


def neighbours(size):
    me, group = lax.axis_index("seq"), lax.axis_index("wa")
    pos = ring_pos(me, size)
    right = (ring_index((pos + 1) % size, size), group)
    left = (ring_index((pos + size - 1) % size, size), group)
    return me, group, pos, right, left


def others(index, size):
    return [(index + offset) % size for offset in range(1, size)]


ANY = pl.BlockSpec(memory_space=pl.ANY)
VMEM = pl.BlockSpec(memory_space=pltpu.VMEM)


def comm_params(collective_id, megabytes=None):
    limit = None if megabytes is None else megabytes * 2**20
    return pltpu.CompilerParams(
        collective_id=collective_id, has_side_effects=True, vmem_limit_bytes=limit
    )


class RingGather:
    def __init__(self, size, x_ref, o_ref, send_sem, recv_sem, local_sem):
        self.size, self.x, self.o = size, x_ref, o_ref
        self.send, self.recv, self.local = send_sem, recv_sem, local_sem
        self.chunks = x_ref.shape[1]
        self.me, _, self.pos, self.right, self.left = neighbours(size)

    def copy(self, step, chunk, way, first=False):
        size = self.size
        if way == 0:
            block, peer = ring_index((self.pos - step + size) % size, size), self.right
        else:
            block, peer = ring_index((self.pos + step) % size, size), self.left
        source = self.x.at[way, chunk] if first else self.o.at[block, way, chunk]
        return push(
            source,
            self.o.at[block, way, chunk],
            self.send.at[step, chunk, way],
            self.recv.at[step, chunk, way],
            peer,
        )

    def kept(self):
        return pltpu.make_async_copy(self.x, self.o.at[self.me], self.local)

    def start(self):
        self.kept().start()
        for chunk in range(self.chunks):
            for way in range(2):
                self.copy(0, chunk, way, True).start()

    def advance(self, step):
        for chunk in range(self.chunks):
            for way in range(2):
                self.copy(step - 1, chunk, way).wait_recv()
                self.copy(step, chunk, way).start()

    def arrive(self):
        last = self.size - 2
        for chunk in range(self.chunks):
            for way in range(2):
                self.copy(last, chunk, way).wait_recv()

    def finish(self):
        self.arrive()
        self.settle()

    def settle(self):
        def drain(step, carry):
            for chunk in range(self.chunks):
                for way in range(2):
                    self.copy(step, chunk, way).wait_send()
            return carry

        lax.fori_loop(0, self.size - 1, drain, 0)
        self.kept().wait()


def ring_parts(x, chunks):
    return x.reshape(2, chunks, x.shape[0] // (2 * chunks), x.shape[1])


def ring_sems(size, chunks):
    return [
        pltpu.SemaphoreType.DMA((size - 1, chunks, 2)),
        pltpu.SemaphoreType.DMA((size - 1, chunks, 2)),
        pltpu.SemaphoreType.DMA,
    ]


def front_kernel(
    widths,
    head_size,
    size,
    groups,
    inner,
    x_ref,
    w_ref,
    cot_ref,
    shard_ref,
    conv_ref,
    conv_bias_ref,
    params_ref,
    out_gain_ref,
    spread_ref,
    tri_ref,
    rows_ref,
    weights_ref,
    proj_ref,
    y_ref,
    enter_ref,
    normed_ref,
    turned_ref,
    grad_ref,
    gain_acc,
    taps_ref,
    heads_ref,
    wide_ref,
    branch_ref,
    part_ref,
    weights,
    projected,
    taken,
    state,
    ext,
    halo,
    gated,
    out_grad,
    y_held,
    enter_held,
    out_rows,
    out_turned,
    sums,
    landing,
    normed_held,
    turned_held,
    grad_held,
    result_sem,
    weight_send,
    weight_recv,
    weight_local,
    take_sem,
    proj_sem,
    held_sem,
    shard_send,
    shard_recv,
    shard_local,
    pair_send,
    pair_recv,
    *ring_refs,
):
    bf16, f32 = jnp.bfloat16, jnp.float32
    me, group, pos, right, left = neighbours(size)
    rows, lw = gated.shape[2:]
    depth = weights.shape[2]
    peers = [(other, group) for other in others(me, size)]
    mates = [(me, other) for other in others(group, groups)]
    sibling = (me, group + 1 - 2 * lax.rem(group, 2))
    across = (me, lax.rem(group + 2, groups))
    per_owner = size // groups
    chosen = lax.rem(me, per_owner)
    owner = me // per_owner
    greet(mates + peers)
    ring = RingGather(size, x_ref, rows_ref, *ring_refs[0:3])
    cot_ring = RingGather(size, cot_ref, branch_ref, *ring_refs[3:6])
    ring.start()
    bc = widths[1]
    used = w_ref.shape[0] - 2 * inner
    lane_at = pl.multiple_of(me * lw, 128)
    spans = (
        (pl.ds(lane_at, lw), pl.ds(0, lw)),
        (pl.ds(pl.multiple_of(inner + me * lw, 128), lw), pl.ds(lw, lw)),
        (pl.ds(2 * inner, used), pl.ds(2 * lw, used)),
    )
    sent = [
        push(
            w_ref.at[here],
            weights.at[group, there],
            weight_send.at[k, part],
            weight_recv.at[k, part],
            mate,
        )
        for k, mate in enumerate(mates)
        for part, (here, there) in enumerate(spans)
    ]
    for copy in sent:
        copy.start()
    kept = [
        pltpu.make_async_copy(w_ref.at[here], weights.at[group, there], weight_local.at[part])
        for part, (here, there) in enumerate(spans)
    ]
    for copy in kept:
        copy.start()
    blank = weights.shape[1] - 2 * lw - used
    for part in range(groups):
        weights[part, 2 * lw + used :, :] = jnp.zeros((blank, depth), bf16)
    heads_here = lw // head_size
    head_start = me * heads_here
    taps_ref[...] = jnp.zeros_like(taps_ref)
    taps_ref[0:KW, :lw] = conv_ref[:, pl.ds(lane_at, lw)]
    taps_ref[0:KW, lw:] = conv_ref[:, inner:]
    taps_ref[KW : KW + 1, :lw] = conv_bias_ref[:, pl.ds(lane_at, lw)]
    taps_ref[KW : KW + 1, lw:] = conv_bias_ref[:, inner:]
    params = pltpu.roll(params_ref[...], lax.rem(128 - head_start, 128), 1)
    params = jnp.where(
        lax.broadcasted_iota(jnp.int32, params.shape, 1) < heads_here, params, 0.0
    )
    at_row = lax.broadcasted_iota(jnp.int32, params.shape, 0)
    at_lane = lax.broadcasted_iota(jnp.int32, params.shape, 1)
    slopes = jnp.where(at_lane < heads_here, -jnp.exp(params), 0.0)
    heads_ref[...] = jnp.where(at_row == 1, slopes, params)
    wide_ref[...] = jnp.zeros_like(wide_ref)
    wide_ref[0:1, :] = out_gain_ref[:, pl.ds(lane_at, lw)]
    wide_ref[1:2, :] = dot(params, spread_ref[...].astype(f32), 1, 0, HIGHEST)[2:3, :]

    def shards(step, offset=0):
        at = lax.rem(chosen + offset, per_owner)
        held_by = across[1] if step == 2 else group
        source = part_ref.at[held_by, at] if step == 2 else shard_ref.at[at]
        return push(
            source,
            part_ref.at[held_by, at],
            shard_send.at[step, offset],
            shard_recv.at[step, offset],
            across if step == 0 else sibling,
        )

    def block_of(pair, way):
        return ring_index((pos - pair + size) % size if way == 0 else (pos + pair) % size, size)

    def stream(source_ref, landed_ref, low, high, compute, own=False):
        def take(pair, slot, way):
            source = source_ref.at[way] if own else landed_ref.at[block_of(pair, way), way]
            return pltpu.make_async_copy(source, taken.at[slot, way], take_sem.at[slot, way])

        for way in range(2):
            take(low, lax.rem(low, 2), way).start()

        def one(pair, carry):
            slot = lax.rem(pair, 2)
            for way in range(2):
                take(pair, slot, way).wait()

            @pl.when(pair + 1 < high)
            def _():
                for way in range(2):
                    take(pair + 1, 1 - slot, way).start()

            compute(pair, slot)
            return carry

        lax.fori_loop(low, high, one, 0)

    def put(pair, way):
        block = block_of(pair, way)
        return pltpu.make_async_copy(
            projected.at[block, way], proj_ref.at[block, way], proj_sem.at[pair, way]
        )

    def project(pair, slot):
        for way in range(2):
            x = taken[slot, way].reshape(rows, taken.shape[4])
            total = None
            for part in range(groups):
                term = dot(x[:, part * depth : (part + 1) * depth], weights[part], 1, 1)
                total = term if total is None else total + term
            projected[block_of(pair, way), way] = total.astype(bf16)
            put(pair, way).start()

    def advance(step, carry):
        ring.advance(step)
        return carry

    def turns(turn, count):
        return 1 + (turn * (size - 2)) // count, 1 + ((turn + 1) * (size - 2)) // count

    middle = size // 2 + 1
    lax.fori_loop(1, middle, advance, 0)
    for copy in kept:
        copy.wait()
    for copy in sent:
        copy.wait_recv()
    flushed = pltpu.make_async_copy(weights, weights_ref, weight_local.at[0])
    flushed.start()
    shards(0).start()
    shards(1).start()
    stream(x_ref, rows_ref, 0, 1, project, own=True)

    def late(step, carry):
        ring.advance(step)
        stream(x_ref, rows_ref, *turns(step - middle, size - 1 - middle), project)
        return carry

    lax.fori_loop(middle, size - 2, late, 0)
    ring.advance(size - 2)
    cot_ring.start()
    stream(x_ref, rows_ref, *turns(size - 2 - middle, size - 1 - middle), project)
    ring.arrive()
    stream(x_ref, rows_ref, size - 1, size, project)
    cot_ring.advance(1)

    def keep(index, slot):
        seq, chunk = index // size, lax.rem(index, size)
        return [
            pltpu.make_async_copy(y_held.at[slot, 0], y_ref.at[chunk, seq], held_sem.at[slot, 0]),
            pltpu.make_async_copy(
                enter_held.at[slot, 0], enter_ref.at[chunk, seq], held_sem.at[slot, 1]
            ),
        ]

    def scan(index, carry):
        seq, chunk = index // size, lax.rem(index, size)
        slot = lax.rem(index, 2)

        @pl.when(index >= 2)
        def _():
            for copy in keep(index - 2, slot):
                copy.wait()

        forward_chunk(
            widths,
            head_size,
            head_start,
            chunk == 0,
            projected.at[pl.ds(chunk, 1), pl.ds(seq, 1)],
            taps_ref,
            heads_ref,
            wide_ref,
            spread_ref,
            tri_ref,
            gated.at[chunk, seq],
            y_held.at[pl.ds(slot, 1)],
            enter_held.at[pl.ds(slot, 1)],
            state,
            ext,
            halo,
        )
        for copy in keep(index, slot):
            copy.start()

        @pl.when(index == size + 2)
        def _():
            cot_ring.advance(2)

        return carry

    lax.fori_loop(0, 2 * size, scan, 0)
    first, second, third = (shards(step) for step in range(3))
    first.wait_recv()
    third.start()
    for offset in range(1, per_owner):
        shards(0, offset).start()
        shards(1, offset).start()
    second.wait_recv()
    cot_ring.advance(3)
    third.wait_recv()

    @pl.when(owner == group)
    def _():
        loaded = pltpu.make_async_copy(shard_ref.at[chosen], out_rows, shard_local)
        loaded.start()
        loaded.wait()

    @pl.when(owner != group)
    def _():
        loaded = pltpu.make_async_copy(part_ref.at[owner, chosen], out_rows, shard_local)
        loaded.start()
        loaded.wait()

    out_turned[...] = out_rows[...].T
    ones = jnp.ones((8, lw), bf16)

    def compute(pair, slot):
        for way in range(2):
            block = block_of(pair, way)
            values = dot(taken[slot, way].reshape(rows, taken.shape[4]), out_turned[...], 1, 0)
            out_grad[block, way] = values
            here = gated[block, way].astype(f32)
            weighted = values * wide_ref[0:1, :] * here
            at = pl.ds(block * 2 + way, 1)
            sums[0, at, :] = dot(ones, (here * here).astype(bf16), 1, 1)[0:1, :]
            sums[1, at, :] = dot(ones, weighted.astype(bf16), 1, 1)[0:1, :]

    stream(cot_ref, branch_ref, 0, 1, compute, own=True)
    stream(cot_ref, branch_ref, *turns(0, size - 4), compute)

    def cot_late(step, carry):
        cot_ring.advance(step)
        stream(cot_ref, branch_ref, *turns(step - 3, size - 4), compute)
        return carry

    lax.fori_loop(4, size - 1, cot_late, 0)
    cot_ring.arrive()
    stream(cot_ref, branch_ref, size - 1, size, compute)
    copies = [
        push(sums, landing.at[k], pair_send.at[k], pair_recv.at[k], peer)
        for k, peer in enumerate(peers)
    ]
    for copy in copies:
        copy.start()
    total = sums[...]
    for k, copy in enumerate(copies):
        copy.wait_recv()
        total = total + landing[k]
    scale = lax.rsqrt(total[0] / inner + EPS)
    pull = scale * scale * scale * (total[1] / inner)
    fill = jnp.zeros((128 - 2 * size, rows), f32)
    scale_turned = jnp.concatenate([scale, fill]).T
    pull_turned = jnp.concatenate([pull, fill]).T
    lane = lax.broadcasted_iota(jnp.int32, (rows, 128), 1)
    gain_acc[...] = jnp.zeros_like(gain_acc)

    def results(block):
        pairs = ((normed_held, normed_ref), (turned_held, turned_ref), (grad_held, grad_ref))
        return [
            pltpu.make_async_copy(held.at[block], out.at[block], result_sem.at[k, block])
            for k, (held, out) in enumerate(pairs)
        ]

    def finish(block, carry):
        for way in range(2):
            mask = lane == block * 2 + way
            by = jnp.sum(jnp.where(mask, scale_turned, 0.0), axis=1, keepdims=True)
            less = jnp.sum(jnp.where(mask, pull_turned, 0.0), axis=1, keepdims=True)
            here = gated[block, way].astype(f32)
            values = out_grad[block, way]
            scaled = here * by
            normed = (scaled * wide_ref[0:1, :]).astype(bf16)
            normed_held[block, way] = normed
            turned_held[block, :, way * rows : (way + 1) * rows] = normed.T
            grad_held[block, way] = (values * wide_ref[0:1, :] * by - here * less).astype(bf16)
            gain_acc[0:1, :] += jnp.sum(values * scaled, axis=0, keepdims=True)
        for copy in results(block):
            copy.start()
        return carry

    lax.fori_loop(0, size, finish, 0)
    for offset in range(1, per_owner):
        shards(0, offset).wait_recv()
        shards(2, offset).start()
    for copy in sent + copies + [first, second, third]:
        copy.wait_send()
    flushed.wait()
    for index in (2 * size - 2, 2 * size - 1):
        for copy in keep(index, index % 2):
            copy.wait()

    def settle(pair, carry):
        for way in range(2):
            put(pair, way).wait()
        for copy in results(pair):
            copy.wait()
        return carry

    lax.fori_loop(0, size, settle, 0)
    ring.settle()
    cot_ring.settle()
    for offset in range(1, per_owner):
        shards(1, offset).wait_recv()
        shards(2, offset).wait_recv()
        for step in range(3):
            shards(step, offset).wait_send()


def front(x, weight, cot, shard, params, inner, widths, head_size, collective_id):
    size, groups = lax.axis_size("seq"), lax.axis_size("wa")
    parts, cot_parts = ring_parts(x, 2), ring_parts(cot, 2)
    depth = weight.shape[1]
    rows = x.shape[0] // 2
    width = x.shape[1]
    lw, bc = widths
    cols = 2 * lw + bc + 128
    per_owner = size // groups
    bf16, f32, DMA, vmem = jnp.bfloat16, jnp.float32, pltpu.SemaphoreType.DMA, pltpu.VMEM
    whole = (size, 2, rows, lw)
    shape = jax.ShapeDtypeStruct
    return pl.pallas_call(
        functools.partial(front_kernel, widths, head_size, size, groups, inner),
        out_shape=[
            shape((size,) + parts.shape, bf16),
            shape((groups, cols, depth), bf16),
            shape((size, 2, rows, cols), bf16),
            shape(whole, bf16),
            shape((size, 2, lw, bc // 2), bf16),
            shape(whole, bf16),
            shape((size, lw, 2 * rows), bf16),
            shape(whole, bf16),
            shape((8, lw), f32),
            shape((8, lw + bc), f32),
            shape((8, 128), f32),
            shape((8, lw), f32),
            shape((size,) + parts.shape, bf16),
            shape((groups, per_owner, lw, width), bf16),
        ],
        in_specs=[ANY] * 4 + [VMEM] * 6,
        out_specs=[ANY] * 8 + [VMEM] * 4 + [ANY] * 2,
        scratch_shapes=[
            vmem((groups, cols, depth), bf16),
            vmem((size, 2, rows, cols), bf16),
            vmem((2,) + parts.shape, bf16),
            vmem((lw, bc // 2), f32),
            vmem((rows + 8, lw + bc), f32),
            vmem((8, lw + bc), f32),
            vmem(whole, bf16),
            vmem(whole, f32),
            vmem((2, 1, rows, lw), bf16),
            vmem((2, 1, lw, bc // 2), bf16),
            vmem((lw, width), bf16),
            vmem((width, lw), bf16),
            vmem((2, 2 * size, rows), f32),
            vmem((size - 1, 2, 2 * size, rows), f32),
            vmem(whole, bf16),
            vmem((size, lw, 2 * rows), bf16),
            vmem(whole, bf16),
            DMA((3, size)),
            DMA((groups - 1, 3)),
            DMA((groups - 1, 3)),
            DMA((3,)),
            DMA((2, 2)),
            DMA((size, 2)),
            DMA((2, 2)),
            DMA((3, per_owner)),
            DMA((3, per_owner)),
            DMA,
            DMA((size - 1,)),
            DMA((size - 1,)),
        ]
        + ring_sems(size, 2)
        + ring_sems(size, 2),
        compiler_params=comm_params(collective_id, 62),
        name="front",
    )(parts, weight, cot_parts, shard, *params)


def finish_kernel(
    size,
    groups,
    counts,
    grad_ref,
    weight_ref,
    normed_ref,
    turned_ref,
    out_ref,
    branch_grad_ref,
    tokens_ref,
    scale_ref,
    taps_ref,
    gain_ref,
    heads_ref,
    swapped_ref,
    shard_ref,
    out_full_ref,
    rows_out,
    gathered_ref,
    pieces_ref,
    owned_ref,
    shared_out,
    small_out,
    branch_out,
    landing,
    slots,
    first,
    parts,
    total,
    taken,
    turned,
    out_total,
    out_parts,
    out_landing,
    out_taken,
    piece,
    main,
    shared,
    shared_land,
    shared_sum,
    small,
    small_land,
    send_sem,
    recv_sem,
    part_send,
    part_recv,
    take_sem,
    out_send,
    out_recv,
    owned_send,
    owned_recv,
    owned_local,
    pair_send,
    pair_recv,
    mate_send,
    mate_recv,
    *ring_refs,
):
    me, group, pos, right, left = neighbours(size)
    mates = [(me, index) for index in others(group, groups)]
    peers = [(index, group) for index in others(me, size)]
    tiles, rows, tile = slots.shape[2:]
    cols = total.shape[0]
    bf16, f32 = jnp.bfloat16, jnp.float32
    out_ring = RingGather(size, piece, pieces_ref, *ring_refs[0:3])
    main_ring = RingGather(size, main, gathered_ref, *ring_refs[3:6])
    shared_ring = RingGather(size, shared_sum, shared_out, *ring_refs[6:9])
    small_ring = RingGather(size, small, small_out, *ring_refs[9:12])
    fetch_sem, weights_taken, held, held_sem, out_turned = ring_refs[12:17]
    weight_held, swapped_held, load_sem = ring_refs[17:20]
    rows_ref, branch_ref, result_sem = ring_refs[20:23]
    rows_kept = pltpu.make_async_copy(rows_ref, rows_out, result_sem.at[0])
    branch_kept = pltpu.make_async_copy(branch_ref, branch_out, result_sem.at[1])
    loads = [
        pltpu.make_async_copy(weight_ref.at[part], weight_held.at[part], load_sem.at[part])
        for part in range(groups)
    ]
    swapped_load = pltpu.make_async_copy(swapped_ref, swapped_held, load_sem.at[groups])

    def target(step, way):
        shift = (pos - 1 - step + 2 * size) if way == 0 else (pos + 1 + step)
        return ring_index(shift % size, size)

    def fetch(step, way):
        slot = lax.rem(step, 2)
        return pltpu.make_async_copy(
            grad_ref.at[target(step, way), way], held.at[slot, way], held_sem.at[slot, way]
        )

    def term(step, way, at):
        return dot(held[lax.rem(step, 2), way], weight_held[at], 1, 0)

    def hop(step, way, at, source):
        return push(
            source,
            slots.at[step, way, at],
            send_sem.at[step, way, at],
            recv_sem.at[step, way, at],
            right if way == 0 else left,
        )

    def begin(at, carry):
        for way in range(2):
            first[way, at] = term(0, way, at).astype(bf16)
            hop(0, way, at, first.at[way, at]).start()
        return carry

    for way in range(2):
        fetch(0, way).start()
    for copy in loads:
        copy.start()
    for way in range(2):
        fetch(1, way).start()
    swapped_load.start()
    greet(mates + peers)
    for way in range(2):
        fetch(0, way).wait()
    for part in range(groups):
        loads[part].wait()
        begin(part, 0)

    def mate_of(offset):
        return lax.rem(group + offset, groups)

    def send_part(offset):
        return push(
            parts.at[offset - 1],
            landing.at[offset - 1],
            part_send.at[offset - 1],
            part_recv.at[offset - 1],
            (me, mate_of(offset)),
        )

    def send_out(offset):
        return push(
            out_parts.at[mate_of(offset)],
            out_landing.at[offset - 1],
            out_send.at[offset - 1],
            out_recv.at[offset - 1],
            (me, mate_of(offset)),
        )

    def stream(count, take, use):
        for copy in take(0, 0):
            copy.start()

        def one(block, carry):
            slot = lax.rem(block, 2)

            @pl.when(block + 1 < count)
            def _():
                for copy in take(block + 1, 1 - slot):
                    copy.start()

            for copy in take(block, slot):
                copy.wait()
            use(block, slot)
            return carry

        lax.fori_loop(0, count, one, 0)

    def tokens_of(block):
        return pl.ds(pl.multiple_of(block * 2 * rows, 2 * rows), 2 * rows)

    def weight_part(offset):
        columns = pl.ds(pl.multiple_of(mate_of(offset) * tile, tile), tile)

        def take(block, slot):
            return [
                pltpu.make_async_copy(
                    normed_ref.at[block, :, :, columns], taken.at[slot], take_sem.at[slot, 0]
                ),
                pltpu.make_async_copy(
                    turned_ref.at[:, tokens_of(block)], turned.at[slot], take_sem.at[slot, 1]
                ),
            ]

        def use(block, slot):
            values = dot(turned[slot], taken[slot].reshape(2 * rows, tile), 1, 0)

            @pl.when(block == 0)
            def _():
                total[...] = values

            @pl.when(block > 0)
            def _():
                total[...] += values

        stream(size, take, use)

    def out_part(low, count):
        piece_rows = out_parts.shape[1]

        def take(block, slot):
            return [
                pltpu.make_async_copy(
                    branch_grad_ref.at[tokens_of(low + block)],
                    out_taken.at[slot],
                    take_sem.at[slot, 0],
                ),
                pltpu.make_async_copy(
                    out_ref.at[low + block], out_turned.at[slot], take_sem.at[slot, 1]
                ),
            ]

        def use(block, slot):
            values = dot(out_turned[slot], out_taken[slot], 1, 0)

            @pl.when(low + block == 0)
            def _():
                out_total[...] = values

            @pl.when(low + block > 0)
            def _():
                out_total[...] += values

        stream(count, take, use)

    def out_sends():
        piece_rows = out_parts.shape[1]
        for index in range(groups):
            out_parts[index] = out_total[index * piece_rows : (index + 1) * piece_rows].astype(bf16)
        for offset in range(1, groups):
            send_out(offset).start()

    def advance(step, carry):
        for way in range(2):
            fetch(step + 1, way).start()
        for way in range(2):
            fetch(step, way).wait()

        def one(at, inner):
            for way in range(2):
                own = term(step, way, at)
                hop(step - 1, way, at, first.at[way, at]).wait_recv()
                slots[step - 1, way, at] = (slots[step - 1, way, at].astype(f32) + own).astype(bf16)
                hop(step, way, at, slots.at[step - 1, way, at]).start()
            return inner

        lax.fori_loop(0, tiles, one, 0)

        @pl.when(step < 3)
        def _():
            out_part((step - 1) * (size // 2), size // 2)

        @pl.when(step == 2)
        def _():
            out_sends()

        @pl.when((step > 2) & (step <= groups + 1))
        def _():
            weight_part(step - 2)
            parts[step - 3] = total[...].astype(bf16)
            send_part(step - 2).start()

        return carry

    lax.fori_loop(1, size - 1, advance, 0)
    for offset in range(1, groups):
        send_out(offset).wait_recv()
    summed = out_parts[group].astype(f32)
    for offset in range(1, groups):
        summed = summed + out_landing[offset - 1].astype(f32)
    piece[...] = summed.astype(bf16).reshape(piece.shape)
    out_ring.start()

    for way in range(2):
        fetch(size - 1, way).wait()

    def end(at, carry):
        columns = pl.ds(pl.multiple_of(at * tile, tile), tile)
        for way in range(2):
            own = term(size - 1, way, at)
            hop(size - 2, way, at, first.at[way, at]).wait_recv()
            rows_ref[way, :, columns] = slots[size - 2, way, at].astype(f32) + own
        return carry

    lax.fori_loop(0, tiles, end, 0)
    rows_kept.start()
    width = rows_ref.shape[2]
    own_width = gain_ref.shape[1]
    flat = jnp.zeros((1, width), f32)
    for way in range(2):
        values = tokens_ref[way].astype(f32) * scale_ref[way, :, 0:1]
        flat = flat + jnp.sum(rows_ref[way] * values, axis=0, keepdims=True)
    half = small.shape[2]
    listed = [
        taps_ref[k : k + 1, at : at + 128] for k in range(KW + 1) for at in range(0, own_width, 128)
    ]
    listed += [gain_ref[0:1, at : at + 128] for at in range(0, own_width, 128)]
    listed += [heads_ref[k : k + 1, :] for k in range(3)]
    listed += [
        taps_ref[k : k + 1, at : at + 128]
        for k in range(KW + 1)
        for at in range(own_width, taps_ref.shape[1], 128)
    ]
    listed += [flat[:, at : at + 128] for at in range(0, width, 128)]
    for at, row in enumerate(listed):
        small[at // half, 0, at % half : at % half + 1, :] = row
    small_in = [
        push(small, small_land.at[k], mate_send.at[k], mate_recv.at[k], mate)
        for k, mate in enumerate(mates)
    ]
    for copy in small_in:
        copy.start()

    def out_advance(step, carry):
        out_ring.advance(step)
        return carry

    lax.fori_loop(1, 2, out_advance, 0)
    weight_part(groups)
    lax.fori_loop(2, size - 2, out_advance, 0)
    fetched = []
    for offset in range(1, groups):
        send_part(offset).wait()
        fetched.append(
            pltpu.make_async_copy(
                landing.at[offset - 1], parts.at[offset - 1], fetch_sem.at[offset - 1]
            )
        )
        fetched[-1].start()
    for copy, part in zip(fetched, range(groups - 1)):
        copy.wait()
        total[...] += parts[part].astype(f32)
    main[...] = total[: counts[0]].astype(bf16).reshape(main.shape)
    shared[...] = total[counts[0] : counts[0] + counts[1]].astype(bf16).reshape(shared.shape)
    shared_in = [
        push(shared.at[peer[0]], shared_land.at[k], pair_send.at[k], pair_recv.at[k], peer)
        for k, peer in enumerate(peers)
    ]
    for copy in shared_in:
        copy.start()
    lax.fori_loop(size - 2, size - 1, out_advance, 0)
    main_ring.start()
    for copy in small_in + shared_in:
        copy.wait()
    values = small[...]
    for k in range(groups - 1):
        values = values + small_land[k]
    small[...] = values
    values = shared[me].astype(f32)
    for k in range(size - 1):
        values = values + shared_land[k].astype(f32)
    across = shared_sum.shape[3]
    for way in range(2):
        shared_sum[way, 0] = values[:, way * across : (way + 1) * across].astype(bf16)
    small_ring.start()
    shared_ring.start()
    out_ring.finish()
    owned = [
        push(pieces_by_owner(pieces_ref, mate[1], groups), owned_ref.at[group], owned_send.at[k], owned_recv.at[k], mate)
        for k, mate in enumerate(mates)
    ]
    kept = pltpu.make_async_copy(
        pieces_by_owner(pieces_ref, group, groups), owned_ref.at[group], owned_local
    )
    for copy in owned:
        copy.start()
    kept.start()
    branch_ref[...] = jnp.zeros_like(branch_ref)

    per_owner = size // groups

    def weight_take(block, slot):
        owner, at = block // per_owner, lax.rem(block, per_owner)

        @pl.when(owner == group)
        def _():
            pltpu.make_async_copy(
                shard_ref.at[at], weights_taken.at[slot], take_sem.at[slot, 0]
            ).start()

        @pl.when(owner != group)
        def _():
            pltpu.make_async_copy(
                out_full_ref.at[owner, at], weights_taken.at[slot], take_sem.at[slot, 0]
            ).start()

    def multiply(block, carry):
        slot = lax.rem(block, 2)

        @pl.when(block + 1 < size)
        def _():
            weight_take(block + 1, 1 - slot)

        pltpu.make_async_copy(
            shard_ref.at[0], weights_taken.at[slot], take_sem.at[slot, 0]
        ).wait()
        branch_ref[...] += dot(swapped_held[block], weights_taken[slot], 1, 0)
        return carry

    weight_take(0, 0)
    swapped_load.wait()
    count = size - 2

    def main_advance(step, carry):
        main_ring.advance(step)
        small_ring.advance(step)
        shared_ring.advance(step)
        lax.fori_loop(((step - 1) * size) // count, (step * size) // count, multiply, 0)
        return carry

    lax.fori_loop(1, size - 1, main_advance, 0)
    branch_kept.start()

    def drain(step, carry):
        def one(at, inner):
            for way in range(2):
                hop(step, way, at, first.at[way, at]).wait_send()
            return inner

        return lax.fori_loop(0, tiles, one, carry)

    lax.fori_loop(0, size - 1, drain, 0)
    for offset in range(1, groups):
        send_out(offset).wait_send()
    main_ring.finish()
    rows_kept.wait()
    branch_kept.wait()
    small_ring.finish()
    shared_ring.finish()
    for copy in owned:
        copy.wait()
    kept.wait()


def pieces_by_owner(pieces_ref, owner, groups):
    count = pieces_ref.shape[0] // groups
    return pieces_ref.at[pl.ds(owner * count, count)]


def finish(
    grad,
    weight,
    normed,
    turned,
    out,
    branch_grad,
    tokens,
    scale,
    taps,
    gain,
    heads,
    swapped,
    shard,
    out_full,
    counts,
    collective_id,
):
    size, groups = lax.axis_size("seq"), lax.axis_size("wa")
    _, ways, rows, cols = grad.shape
    tile, tiles = weight.shape[2], groups
    width = tiles * tile
    lw = out.shape[1]
    bc = taps.shape[1] - lw
    piece_rows = lw // groups
    per_owner = size // groups
    bf16, f32, DMA = jnp.bfloat16, jnp.float32, pltpu.SemaphoreType.DMA
    total_small = ((KW + 2) * lw + (KW + 1) * bc + width) // 128 + 3
    half = -(-total_small // 16) * 8
    piece = (2, 2, piece_rows // 4, width)
    main = (2, 2, counts[0] // 4, tile)
    shared_rows = counts[1] // size
    both = (2, 1, shared_rows, tile // 2)
    small_shape = (2, 1, half, 128)
    vmem = pltpu.VMEM
    return pl.pallas_call(
        functools.partial(finish_kernel, size, groups, counts),
        out_shape=[
            jax.ShapeDtypeStruct((ways, rows, width), f32),
            jax.ShapeDtypeStruct((size,) + main, bf16),
            jax.ShapeDtypeStruct((size,) + piece, bf16),
            jax.ShapeDtypeStruct((groups, per_owner) + piece, bf16),
            jax.ShapeDtypeStruct((size,) + both, bf16),
            jax.ShapeDtypeStruct((size,) + small_shape, f32),
            jax.ShapeDtypeStruct((ways * rows, width), f32),
            jax.ShapeDtypeStruct((groups - 1, cols, tile), bf16),
        ],
        in_specs=[ANY] * 6 + [VMEM] * 5 + [ANY] * 3,
        out_specs=[ANY] * 8,
        scratch_shapes=[
            vmem((size - 1, 2, tiles, rows, tile), bf16),
            vmem((2, tiles, rows, tile), bf16),
            vmem((groups - 1, cols, tile), bf16),
            vmem((cols, tile), f32),
            vmem((2, ways, rows, tile), bf16),
            vmem((2, cols, 2 * rows), bf16),
            vmem((lw, width), f32),
            vmem((groups, piece_rows, width), bf16),
            vmem((groups - 1, piece_rows, width), bf16),
            vmem((2, 2 * rows, width), bf16),
            vmem(piece, bf16),
            vmem(main, bf16),
            vmem((size, shared_rows, tile), bf16),
            vmem((size - 1, shared_rows, tile), bf16),
            vmem(both, bf16),
            vmem(small_shape, f32),
            vmem((groups - 1,) + small_shape, f32),
            DMA((size - 1, 2, tiles)),
            DMA((size - 1, 2, tiles)),
            DMA((groups - 1,)),
            DMA((groups - 1,)),
            DMA((2, 2)),
            DMA((groups - 1,)),
            DMA((groups - 1,)),
            DMA((groups - 1,)),
            DMA((groups - 1,)),
            DMA,
            DMA((size - 1,)),
            DMA((size - 1,)),
            DMA((groups - 1,)),
            DMA((groups - 1,)),
        ]
        + ring_sems(size, 2)
        + ring_sems(size, 2)
        + ring_sems(size, 1)
        + ring_sems(size, 1)
        + [DMA((groups - 1,)), vmem((2, lw, width), bf16)]
        + [vmem((2, 2, rows, cols), bf16), DMA((2, 2)), vmem((2, lw, 2 * rows), bf16)]
        + [vmem(weight.shape, bf16), vmem(swapped.shape, bf16), DMA((groups + 1,))]
        + [vmem((ways, rows, width), f32), vmem((ways * rows, width), f32), DMA((2,))],
        compiler_params=comm_params(collective_id, 63),
        name="finish",
    )(
        grad,
        weight,
        normed,
        turned,
        out,
        branch_grad,
        tokens,
        scale,
        taps,
        gain,
        heads,
        swapped,
        shard,
        out_full,
    )


def assemble_kernel(blocks, gathered_ref, tail_ref, o_ref):
    @pl.when(pl.program_id(0) < blocks)
    def _():
        o_ref[...] = gathered_ref[0, 0].reshape(o_ref.shape).astype(jnp.float32)

    @pl.when(pl.program_id(0) == blocks)
    def _():
        o_ref[...] = tail_ref[...].astype(jnp.float32)


def assemble_in(gathered, tail):
    size, ways, chunks, rows, width = gathered.shape
    step = chunks * rows
    blocks = size * ways
    total = blocks * step + tail.shape[0]
    steps = blocks + 1
    pad = -tail.shape[0] % step
    if tail.shape[0] > step:
        out = jnp.swapaxes(gathered, 0, 1).reshape(blocks * step, width)
        return jnp.concatenate([out, tail]).astype(jnp.float32)
    return pl.pallas_call(
        functools.partial(assemble_kernel, blocks),
        grid=(steps,),
        in_specs=[
            pl.BlockSpec(
                (1, 1, chunks, rows, width),
                lambda i: (lax.rem(i, size), jnp.minimum(i // size, ways - 1), 0, 0, 0),
            ),
            pl.BlockSpec((step, width), lambda i: (0, 0)),
        ],
        out_specs=pl.BlockSpec((step, width), lambda i: (i, 0)),
        out_shape=jax.ShapeDtypeStruct((total, width), jnp.float32),
        compiler_params=pltpu.CompilerParams(vmem_limit_bytes=32 * 2**20),
        name="assemble_in",
    )(gathered, jnp.pad(tail, ((0, pad), (0, 0))))


def widen_kernel(
    widths, heads, x_ref, small_ref, o_ref, conv_ref, bias_ref, gain_ref, heads_ref, norm_ref
):
    o_ref[...] = x_ref[0, 0].astype(jnp.float32)

    @pl.when((pl.program_id(0) == 0) & (pl.program_id(1) == 0))
    def _():
        lw, bc = widths
        size = small_ref.shape[0]
        tiles, shared = lw // 128, bc // 128
        inner = size * lw
        found = jnp.zeros((8, 128), jnp.float32)
        first = (KW + 2) * tiles
        for block in range(size):
            for tile in range(tiles):
                at = slice(block * lw + tile * 128, block * lw + (tile + 1) * 128)
                for k in range(KW):
                    row = k * tiles + tile
                    conv_ref[k : k + 1, at] = small_ref[block, row : row + 1, :]
                row = KW * tiles + tile
                bias_ref[:, at] = small_ref[block, row : row + 1, :]
                row = (KW + 1) * tiles + tile
                gain_ref[:, at] = small_ref[block, row : row + 1, :]
            found = found + pltpu.roll(small_ref[block, first : first + 8, :], block * heads, 1)
        heads_ref[...] = found
        total = small_ref[0]
        for block in range(1, size):
            total = total + small_ref[block]
        row = first + 3
        for k in range(KW + 1):
            for tile in range(shared):
                at = slice(inner + tile * 128, inner + (tile + 1) * 128)
                if k < KW:
                    conv_ref[k : k + 1, at] = total[row : row + 1, :]
                else:
                    bias_ref[:, at] = total[row : row + 1, :]
                row += 1
        for tile in range(norm_ref.shape[1] // 128):
            norm_ref[:, tile * 128 : (tile + 1) * 128] = total[row : row + 1, :]
            row += 1


def assemble_out(owned, small, widths, heads):
    groups, count, rows, width = owned.shape
    size = small.shape[0]
    lw, bc = widths
    inner = size * lw
    f32 = jnp.float32
    shapes = [(KW, inner + bc), (1, inner + bc), (1, inner), (8, 128), (1, width)]
    return pl.pallas_call(
        functools.partial(widen_kernel, widths, heads),
        grid=(count, groups),
        in_specs=[
            pl.BlockSpec((1, 1, rows, width), lambda t, g: (g, t, 0, 0)),
            pl.BlockSpec(small.shape, lambda t, g: (0, 0, 0)),
        ],
        out_specs=[pl.BlockSpec((rows, width), lambda t, g: (t * groups + g, 0))]
        + [pl.BlockSpec(s, lambda t, g: (0, 0)) for s in shapes],
        out_shape=[jax.ShapeDtypeStruct((groups * count * rows, width), f32)]
        + [jax.ShapeDtypeStruct(s, f32) for s in shapes],
        name="assemble_out",
    )(owned, small)


def body(
    tokens,
    lengths,
    norm_gain,
    in_weight,
    conv_weight,
    conv_bias,
    dt_bias,
    a_log,
    skip_gain,
    out_gain,
    out_weight,
    cotangent,
):
    seqs_here, slot_rows, width = tokens.shape
    row_count = seqs_here * slot_rows
    inner_width = out_gain.shape[0]
    channels = conv_bias.shape[0]
    bc_width = channels - inner_width
    state_size = bc_width // 2
    head_count = dt_bias.shape[0]
    head_size = inner_width // head_count
    seq_devices = lax.axis_size("seq")
    group_devices = lax.axis_size("wa")
    seq_index = lax.axis_index("seq")
    length = seq_devices * slot_rows
    local_heads = head_count // seq_devices
    local_width = local_heads * head_size
    channel_start = seq_index * local_width
    head_start = seq_index * local_heads
    bf16, f32 = jnp.bfloat16, jnp.float32

    def take(array, start, size, axis):
        return lax.dynamic_slice_in_dim(array, start, size, axis)

    positions = seq_index * slot_rows + jnp.arange(slot_rows)
    valid_rows = (positions[None, :] < lengths[:, None]).astype(f32).reshape(row_count, 1)
    flat_tokens = tokens.reshape(row_count, width).astype(f32)
    in_scale = row_scale(flat_tokens)
    normed = (flat_tokens * in_scale * norm_gain).astype(bf16)
    cot_rows = cotangent.reshape(row_count, width)

    blocks = (seq_devices, seqs_here, slot_rows)
    params = jnp.pad(jnp.stack([dt_bias, a_log, skip_gain]), ((0, 5), (0, 128 - head_count)))
    spread, fold, tri, upper = scan_tables(slot_rows, local_width, head_size)
    widths = (local_width, bc_width)
    per_owner = seq_devices // group_devices
    (
        normed_all,
        in_columns,
        projected,
        y_heads,
        entering,
        normed_out,
        turned_out,
        gated_grad,
        gain_sum,
        taps,
        heads,
        wide,
        branch_grad,
        out_full,
    ) = front(
        normed,
        in_weight.T,
        cot_rows * valid_rows.astype(bf16),
        out_weight.reshape(per_owner, local_width, width),
        (conv_weight, conv_bias[None], params, out_gain[None], spread, tri),
        inner_width,
        widths,
        head_size,
        0,
    )
    branch_grad = branch_grad.reshape(-1, width)
    proj_grad, turned_grad, taps_sum, _, head_sum, swapped = scan_backward(
        projected,
        y_heads,
        entering,
        gated_grad,
        taps,
        heads,
        wide,
        spread,
        fold,
        tri,
        upper,
        normed_out,
        widths,
        head_size,
        1,
    )
    swapped = swapped.reshape(seq_devices, row_count, local_width)
    columns_here = proj_grad.shape[3]
    proj_grad = proj_grad.reshape(-1, columns_here)
    in_rows = in_weight.shape[0]
    shared_count = bc_width + head_count
    shared_rows = shared_count // seq_devices
    normed_grad, gathered, _, owned, shared_all, small_all, branch, _ = finish(
        proj_grad.reshape(blocks + (columns_here,)),
        in_columns,
        normed_all.reshape(blocks + (width,)),
        turned_grad,
        turned_out,
        branch_grad,
        tokens,
        jnp.broadcast_to(in_scale.reshape(seqs_here, slot_rows, 1), (seqs_here, slot_rows, 128)),
        taps_sum,
        gain_sum,
        head_sum,
        swapped,
        out_weight.reshape(per_owner, local_width, width),
        out_full,
        (2 * local_width, shared_count),
        2,
    )
    normed_grad = normed_grad.reshape(row_count, width)
    token_grad = norm_backward(flat_tokens, in_scale, norm_gain, normed_grad)
    token_grad = token_grad + cot_rows.astype(f32)
    owned = owned.reshape(
        group_devices, per_owner, local_width // group_devices, width
    )
    shared_all = shared_all.reshape(seq_devices, 2, shared_rows, in_rows // 2)
    small_all = small_all.reshape(seq_devices, -1, 128)
    mixed_out = (flat_tokens + valid_rows * branch).astype(bf16).reshape(tokens.shape)
    tail = jnp.transpose(shared_all, (0, 2, 1, 3)).reshape(shared_count, in_rows)
    in_weight_grad = assemble_in(gathered, tail).T
    out_weight_grad, conv_weight_grad, conv_bias_grad, gain_grad, head_all, norm_grad = (
        assemble_out(owned, small_all, widths, local_heads)
    )
    return (
        mixed_out,
        token_grad.reshape(tokens.shape),
        norm_grad[0],
        in_weight_grad,
        conv_weight_grad,
        conv_bias_grad[0],
        head_all[0, :head_count],
        head_all[1, :head_count],
        head_all[2, :head_count],
        gain_grad[0],
        out_weight_grad,
    )


def solution(mesh):
    placed = (
        P("wa", "seq", None),
        P("wa"),
        P(),
        P("wa", None),
        P(),
        P(),
        P(),
        P(),
        P(),
        P(),
        P("wa", None),
        P("wa", "seq", None),
    )
    return jax.shard_map(
        body,
        mesh=mesh,
        in_specs=placed,
        out_specs=(
            P("wa", "seq", None),
            P("wa", "seq", None),
            P(),
            P("wa", None),
            P(),
            P(),
            P(),
            P(),
            P(),
            P(),
            P("wa", None),
        ),
        check_vma=False,
    )
```
